32 devices in a mesh: seq: 16 (over z, y, x), wshard: 2 (over core).
Axes of the slice: x: 2, y: 2, z: 4, core: 2. Of those that a mesh axis runs over, the one named last changes fastest.
Arguments:
- tokens: bfloat16 [8, 2048, 1536], P('wshard', 'seq'), may hold values from -6 to 6
- segment_ids: int32 [8, 2048], P('wshard', 'seq'), may hold values from 0 to 7, never falling along the last dimension, each value on 1 to 512 neighbouring positions
- document_adapter: int32 [8, 8], P('wshard'), may hold values from 0 to 7
- out_cotangent: bfloat16 [8, 2048, 1536], P('wshard', 'seq'), may hold values from -6 to 6
- mixer_gain: float32 [1536], replicated, may hold values from 0.25 to 1.75
- feed_gain: float32 [1536], replicated, may hold values from 0.25 to 1.75
- filter_taps: float32 [4, 2048], replicated, may hold values from -3 to 3
- decay_param: float32 [2048], replicated
- branch_weight: bfloat16 [1536, 2048], P('wshard'), may hold values from -0.15625 to 0.15625
- recur_weight: bfloat16 [1536, 2048], P('wshard'), may hold values from -0.15625 to 0.15625
- decay_blocks: bfloat16 [16, 128, 128], P('wshard'), may hold values from -0.5 to 0.5
- inflow_blocks: bfloat16 [16, 128, 128], P('wshard'), may hold values from -0.5 to 0.5
- output_weight: bfloat16 [2048, 1536], P('wshard'), may hold values from -0.375 to 0.375
- gating_weight: bfloat16 [1536, 4608], P('wshard'), may hold values from -0.15625 to 0.15625
- upward_weight: bfloat16 [1536, 4608], P('wshard'), may hold values from -0.15625 to 0.15625
- downward_weight: bfloat16 [4608, 1536], P('wshard'), may hold values from -0.1875 to 0.1875
- branch_shrink: bfloat16 [128, 1536], P('wshard'), may hold values from -0.15625 to 0.15625
- branch_expand: bfloat16 [128, 2048], P('wshard'), may hold values from -0.75 to 0.75
- recur_shrink: bfloat16 [128, 1536], P('wshard'), may hold values from -0.15625 to 0.15625
- recur_expand: bfloat16 [128, 2048], P('wshard'), may hold values from -0.75 to 0.75
- decay_shrink: bfloat16 [128, 2048], P('wshard'), may hold values from -0.125 to 0.125
- decay_expand: bfloat16 [128, 2048], P('wshard'), may hold values from -0.75 to 0.75
- inflow_shrink: bfloat16 [128, 2048], P('wshard'), may hold values from -0.125 to 0.125
- inflow_expand: bfloat16 [128, 2048], P('wshard'), may hold values from -0.75 to 0.75
- output_shrink: bfloat16 [128, 2048], P('wshard'), may hold values from -0.125 to 0.125
- output_expand: bfloat16 [128, 1536], P('wshard'), may hold values from -0.75 to 0.75
- gating_shrink: bfloat16 [128, 1536], P('wshard'), may hold values from -0.15625 to 0.15625
- gating_expand: bfloat16 [128, 4608], P('wshard'), may hold values from -0.75 to 0.75
- upward_shrink: bfloat16 [128, 1536], P('wshard'), may hold values from -0.15625 to 0.15625
- upward_expand: bfloat16 [128, 4608], P('wshard'), may hold values from -0.75 to 0.75
- downward_shrink: bfloat16 [128, 4608], P('wshard'), may hold values from -0.09375 to 0.09375
- downward_expand: bfloat16 [128, 1536], P('wshard'), may hold values from -0.75 to 0.75
Outputs:
- output: bfloat16 [8, 2048, 1536], P('wshard', 'seq')
- grad_tokens: float32 [8, 2048, 1536], P('wshard', 'seq')
- branch_shrink_grad: float32 [128, 1536], P(('seq', 'wshard'))
- branch_expand_grad: float32 [128, 2048], P(('seq', 'wshard'))
- recur_shrink_grad: float32 [128, 1536], P(('seq', 'wshard'))
- recur_expand_grad: float32 [128, 2048], P(('seq', 'wshard'))
- decay_shrink_grad: float32 [128, 2048], P(('seq', 'wshard'))
- decay_expand_grad: float32 [128, 2048], P(('seq', 'wshard'))
- inflow_shrink_grad: float32 [128, 2048], P(('seq', 'wshard'))
- inflow_expand_grad: float32 [128, 2048], P(('seq', 'wshard'))
- output_shrink_grad: float32 [128, 2048], P(('seq', 'wshard'))
- output_expand_grad: float32 [128, 1536], P(('seq', 'wshard'))
- gating_shrink_grad: float32 [128, 1536], P(('seq', 'wshard'))
- gating_expand_grad: float32 [128, 4608], P(('seq', 'wshard'))
- upward_shrink_grad: float32 [128, 1536], P(('seq', 'wshard'))
- upward_expand_grad: float32 [128, 4608], P(('seq', 'wshard'))
- downward_shrink_grad: float32 [128, 4608], P(('seq', 'wshard'))
- downward_expand_grad: float32 [128, 1536], P(('seq', 'wshard'))
The draws below stay inside these ranges and needn't reach their ends.
Inputs may be any that keep to these rules, and one draw needn't show every extreme that they name: `segment_ids`: within each sequence the numbers never fall; each of the 8 documents holds 1 to 512 tokens, and one holds exactly 512.
All inputs are finite; a program needn't handle non-finite values.
Results may differ from the reference program's by a relative error of at most 0.015.
The reference program's roundings to bfloat16 on the way count: a program that leaves them out, or rounds other values in their place, can miss the bound.
Values may be sent and summed in bfloat16 or wider, within the bound.
A program may use at most 512 MiB of HBM per device.

```python
import math
import jax
import jax.numpy as jnp
import numpy as np
from jax import lax

D = 1536
LRU = 2048
FF = 4608
NBLOCK = 16
BLOCK = 128
TAPS = 4
RANK = 16
NADAPT = 8
RANKALL = 128
SEQS = 8
LEN = 2048
DOC_COUNT = 8
DOC_MOST = 512


def draw_decay_param(key, part):
    pick_key, slow_key, fast_key = jax.random.split(jax.random.fold_in(key, 17), 3)
    slow_share = 0.5
    slow = jax.random.bernoulli(pick_key, slow_share, (LRU,))
    slow_rate = jnp.exp(jax.random.uniform(slow_key, (LRU,), jnp.float32, jnp.log(0.5), jnp.log(2.0))) / (8.0 * LEN)
    fast_rate = jnp.exp(jax.random.uniform(fast_key, (LRU,), jnp.float32, jnp.log(1.0 / 30.0), jnp.log(1.0 / 8.0))) / 8.0
    rate = jnp.where(slow, slow_rate, fast_rate)
    return (-jnp.log(jnp.expm1(rate))).astype(jnp.float32)


def place_ends(values, key, low, top_value):
    dims = values.shape
    index_at = [jax.random.randint(jax.random.fold_in(key, axis), (), 0, dims[axis]) for axis in range(len(dims))]
    values = values.at[tuple(index_at)].set(low)
    longest = dims.index(max(dims))
    index_at[longest] = (index_at[longest] + 1) % dims[longest]
    return values.at[tuple(index_at)].set(top_value)


def levels(rng, shape, shards, least, top_value):
    def one(axis_at, blocks):
        draws = jax.random.uniform(jax.random.fold_in(jax.random.fold_in(rng, 6), axis_at), (blocks,), jnp.float32, least / len(shards), top_value / len(shards))
        return jnp.repeat(jnp.exp(draws), shape[axis_at] // blocks).reshape((-1,) + (1,) * (len(shape) - axis_at - 1))

    factor_of = one(*shards[0])
    for cut in shards[1:]:
        factor_of = factor_of * one(*cut)
    return factor_of


def length_profile(amount, total, reach, skew):
    weights = [(1 << 20) // math.isqrt(rank ** skew) + 1 for rank in range(2, amount + 1)]
    rest, counts = total - reach - (amount - 1), [1] * (amount - 1)
    while rest > 0:
        candidates = [i for i in range(amount - 1) if counts[i] < reach]
        mass, left = sum([weights[i] for i in candidates]), rest
        for i in candidates:
            extra = min(reach - counts[i], max(1, left * weights[i] // mass), rest)
            counts[i] = counts[i] + extra
            rest = rest - extra
    return np.array([reach] + counts)


def ragged_sizes(stream_key, number_of, total, bound, slope):
    if number_of == 2:
        one = jax.random.randint(stream_key, (), max(1, total - bound), min(bound, total - 1) + 1)
        return jnp.stack([one, total - one])
    lengths = jnp.asarray(length_profile(number_of, total, bound, slope), jnp.int32)
    pairs = (number_of - 1) // 2
    giver, receiver = lengths[1:1 + 2 * pairs:2], lengths[2:2 + 2 * pairs:2]
    room = jnp.minimum(giver - 1, bound - receiver)
    moved = jax.random.randint(jax.random.fold_in(stream_key, 1), (pairs,), 0, 1 << 20) % (room + 1)
    lengths = lengths.at[1:1 + 2 * pairs:2].set(giver - moved).at[2:2 + 2 * pairs:2].set(receiver + moved)
    return lengths[jax.random.permutation(jax.random.fold_in(stream_key, 2), number_of)]


def gaussian(key, shape, scale, reach, shards=(), kind=jnp.bfloat16):
    values = jax.random.normal(key, shape, jnp.float32) * scale
    if len(shards) > 0:
        values = levels(key, shape, shards, -0.22, 0.18) * values
    return jnp.clip(values, min=-reach, max=reach).astype(kind)


def setup_inputs(seed: int = 0) -> dict:
    key_list = jax.random.split(jax.random.key(seed), 33)
    return {
        "tokens": gaussian(key_list[0], (SEQS, LEN, D), 1.0, 6.0, ((0, 2), (1, 16))),
        "segment_ids": jax.vmap(lambda own: jnp.searchsorted(jnp.cumsum(ragged_sizes(own, DOC_COUNT, LEN, DOC_MOST, 1)), jnp.arange(LEN), side="right"))(jax.random.split(key_list[1], SEQS)).reshape((SEQS, LEN)).astype(jnp.int32),
        "document_adapter": place_ends(jax.random.randint(key_list[2], (SEQS, DOC_COUNT), 0, NADAPT), jax.random.fold_in(key_list[2], 1), 0, NADAPT - 1).astype(jnp.int32),
        "out_cotangent": gaussian(key_list[3], (SEQS, LEN, D), 1.0, 6.0, ((0, 2), (1, 16))),
        "mixer_gain": jnp.clip(1.0 + 0.15 * jax.random.normal(key_list[4], (D,), jnp.float32), 0.25, 1.75),
        "feed_gain": jnp.clip(1.0 + 0.15 * jax.random.normal(key_list[5], (D,), jnp.float32), 0.25, 1.75),
        "filter_taps": gaussian(key_list[6], (TAPS, LRU), 0.5, 3.0, (), jnp.float32),
        "decay_param": draw_decay_param(jax.random.fold_in(key_list[32], 71), 0),
        "branch_weight": gaussian(key_list[8], (D, LRU), D ** -0.5, 0.15625, ((0, 2),)),
        "recur_weight": gaussian(key_list[9], (D, LRU), D ** -0.5, 0.15625, ((0, 2),)),
        "decay_blocks": gaussian(key_list[10], (NBLOCK, BLOCK, BLOCK), BLOCK ** -0.5, 0.5, ((0, 2),)),
        "inflow_blocks": gaussian(key_list[11], (NBLOCK, BLOCK, BLOCK), BLOCK ** -0.5, 0.5, ((0, 2),)),
        "output_weight": gaussian(key_list[12], (LRU, D), (LRU // 8) ** -0.5, 0.375, ((0, 2),)),
        "gating_weight": gaussian(key_list[13], (D, FF), D ** -0.5, 0.15625, ((0, 2),)),
        "upward_weight": gaussian(key_list[14], (D, FF), D ** -0.5, 0.15625, ((0, 2),)),
        "downward_weight": gaussian(key_list[15], (FF, D), (FF // 4) ** -0.5, 0.1875, ((0, 2),)),
        "branch_shrink": gaussian(key_list[16], (RANKALL, D), D ** -0.5, 0.15625, ((0, 2),)),
        "branch_expand": gaussian(key_list[17], (RANKALL, LRU), (RANK * 4) ** -0.5, 0.75, ((0, 2),)),
        "recur_shrink": gaussian(key_list[18], (RANKALL, D), D ** -0.5, 0.15625, ((0, 2),)),
        "recur_expand": gaussian(key_list[19], (RANKALL, LRU), (RANK * 4) ** -0.5, 0.75, ((0, 2),)),
        "decay_shrink": gaussian(key_list[20], (RANKALL, LRU), LRU ** -0.5, 0.125, ((0, 2),)),
        "decay_expand": gaussian(key_list[21], (RANKALL, LRU), (RANK * 4) ** -0.5, 0.75, ((0, 2),)),
        "inflow_shrink": gaussian(key_list[22], (RANKALL, LRU), LRU ** -0.5, 0.125, ((0, 2),)),
        "inflow_expand": gaussian(key_list[23], (RANKALL, LRU), (RANK * 4) ** -0.5, 0.75, ((0, 2),)),
        "output_shrink": gaussian(key_list[24], (RANKALL, LRU), LRU ** -0.5, 0.125, ((0, 2),)),
        "output_expand": gaussian(key_list[25], (RANKALL, D), (RANK * 4) ** -0.5, 0.75, ((0, 2),)),
        "gating_shrink": gaussian(key_list[26], (RANKALL, D), D ** -0.5, 0.15625, ((0, 2),)),
        "gating_expand": gaussian(key_list[27], (RANKALL, FF), (RANK * 4) ** -0.5, 0.75, ((0, 2),)),
        "upward_shrink": gaussian(key_list[28], (RANKALL, D), D ** -0.5, 0.15625, ((0, 2),)),
        "upward_expand": gaussian(key_list[29], (RANKALL, FF), (RANK * 4) ** -0.5, 0.75, ((0, 2),)),
        "downward_shrink": gaussian(key_list[30], (RANKALL, FF), FF ** -0.5, 0.09375, ((0, 2),)),
        "downward_expand": gaussian(key_list[31], (RANKALL, D), (RANK * 4) ** -0.5, 0.75, ((0, 2),)),
    }


@jax.custom_vjp
def low(v):
    return lax.optimization_barrier(v.astype(jnp.bfloat16)).astype(jnp.float32)

@jax.custom_vjp
def low_back(v):
    return v

def low_keep(v):
    return (low(v), None)

def low_pass(kept, grad):
    return (grad,)

def back_keep(v):
    return (v, None)

def back_low(kept, grad):
    return (low(grad),)
low.defvjp(low_keep, low_pass)
low_back.defvjp(back_keep, back_low)
EPSILON = 1e-06
RATE_SCALE = 8.0
ROOT_FLOOR = 0.001
HIGHEST = lax.Precision.HIGHEST

def product(left, right):
    return jnp.dot(left, right, precision=HIGHEST)

def blockwise(rows, blocks):
    length = rows.shape[0]
    split = rows.reshape(length, blocks.shape[0], blocks.shape[1])
    return jnp.einsum('tki,kio->tko', split, blocks, precision=HIGHEST).reshape(length, -1)

def adapted(rows, weight, shrink, expand, onehot, blocked):
    inner = low_back(product(rows, shrink.T))
    picked = low(inner * onehot)
    if blocked:
        main = blockwise(rows, weight)
    else:
        main = product(rows, weight)
    return low_back(main + product(picked, expand))

def normalize(values, gain):
    scale = lax.rsqrt(lax.optimization_barrier(jnp.mean(values * values, axis=-1, keepdims=True)) + EPSILON)
    return values * scale * gain

def combine(earlier, later):
    return (earlier[0] * later[0], later[0] * earlier[1] + later[1])

def smooth(values):
    return jax.nn.gelu(values, approximate=True)

def forward(tokens, factors, frozen, onehot, same):
    mixer_gain, feed_gain, filter_taps, decay_param, branch_weight, recur_weight, decay_blocks, inflow_blocks, output_weight, gating_weight, upward_weight, downward_weight = frozen
    normed = low(normalize(tokens, mixer_gain))
    branch = smooth(adapted(normed, branch_weight, factors[0], factors[1], onehot, False))
    recur = adapted(normed, recur_weight, factors[2], factors[3], onehot, False)
    mixed = filter_taps[0] * recur
    for lag in range(1, filter_taps.shape[0]):
        earlier = jnp.concatenate([jnp.zeros((lag, recur.shape[1]), jnp.float32), recur[:-lag]], axis=0)
        mixed = mixed + filter_taps[lag] * earlier * same[lag - 1][:, None]
    low_mixed = low(mixed)
    rate = jax.nn.sigmoid(adapted(low_mixed, decay_blocks, factors[4], factors[5], onehot, True))
    inflow = jax.nn.sigmoid(adapted(low_mixed, inflow_blocks, factors[6], factors[7], onehot, True))
    log_decay = -RATE_SCALE * rate * jax.nn.softplus(-decay_param)
    keep = same[0][:, None]
    decay = jnp.exp(log_decay) * keep
    root_raw = jnp.sqrt(jnp.maximum(-jnp.expm1(2.0 * log_decay), ROOT_FLOOR))
    root = keep * root_raw + (1.0 - keep)
    drive = root * inflow * mixed
    state = lax.associative_scan(combine, (decay, drive), axis=0)[1]
    merged = low(branch * state)
    residual = tokens + adapted(merged, output_weight, factors[8], factors[9], onehot, False)
    second = low(normalize(residual, feed_gain))
    gating = adapted(second, gating_weight, factors[10], factors[11], onehot, False)
    upward = adapted(second, upward_weight, factors[12], factors[13], onehot, False)
    hidden = low(smooth(gating) * upward)
    return residual + adapted(hidden, downward_weight, factors[14], factors[15], onehot, False)

def reference(tokens, segment_ids, document_adapter, out_cotangent, mixer_gain, feed_gain, filter_taps, decay_param, branch_weight, recur_weight, decay_blocks, inflow_blocks, output_weight, gating_weight, upward_weight, downward_weight, branch_shrink, branch_expand, recur_shrink, recur_expand, decay_shrink, decay_expand, inflow_shrink, inflow_expand, output_shrink, output_expand, gating_shrink, gating_expand, upward_shrink, upward_expand, downward_shrink, downward_expand):
    frozen = tuple((item.astype(jnp.float32) for item in (mixer_gain, feed_gain, filter_taps, decay_param, branch_weight, recur_weight, decay_blocks, inflow_blocks, output_weight, gating_weight, upward_weight, downward_weight)))
    factors = tuple((item.astype(jnp.float32) for item in (branch_shrink, branch_expand, recur_shrink, recur_expand, decay_shrink, decay_expand, inflow_shrink, inflow_expand, output_shrink, output_expand, gating_shrink, gating_expand, upward_shrink, upward_expand, downward_shrink, downward_expand)))
    owners = jnp.arange(RANKALL, dtype=jnp.int32) // RANK
    documents = jnp.arange(DOC_COUNT, dtype=jnp.int32)
    position = jnp.arange(LEN, dtype=jnp.int32)

    def one_sequence(totals, items):
        rows, segments, table, cotangent = items
        owner = lax.optimization_barrier(jnp.sum(jnp.where(segments[:, None] == documents[None, :], table[None, :], 0), axis=1))
        onehot = (owner[:, None] == owners[None, :]).astype(jnp.float32)
        same = []
        for lag in range(1, TAPS):
            prior = jnp.concatenate([jnp.zeros((lag,), segments.dtype), segments[:-lag]])
            same.append(((prior == segments) & (position >= lag)).astype(jnp.float32))

        def forward_rows(values, adapters):
            return forward(values, adapters, frozen, onehot, same)
        result, pullback = jax.vjp(forward_rows, rows.astype(jnp.float32), factors)
        grad_rows, grad_factors = pullback(cotangent.astype(jnp.float32))
        totals = tuple((total + grad for total, grad in zip(totals, grad_factors)))
        return (totals, (result.astype(jnp.bfloat16), grad_rows))
    initial = tuple((jnp.zeros(item.shape, jnp.float32) for item in factors))
    totals, (outputs, grads) = lax.scan(one_sequence, initial, (tokens, segment_ids, document_adapter, out_cotangent))
    return (outputs, grads) + totals
```

```python
import functools

import jax
import jax.numpy as jnp
from jax import lax
from jax.experimental import pallas as pl
from jax.experimental.pallas import tpu as pltpu
from jax.sharding import PartitionSpec as P

RANK = 16
EPSILON = 1e-06
RATE_SCALE = 8.0
ROOT_FLOOR = 0.001
GELU_A = 0.7978845608028654
GELU_B = 0.044715

HALO = 8
SEGS = 8
TILE = 512
LANES = 128
F32 = jnp.float32
BF16 = jnp.bfloat16


def mm(left, right):
    return lax.dot_general(left, right, (((1,), (0,)), ((), ())), preferred_element_type=F32)


def mm_nt(left, right):
    return lax.dot_general(left, right, (((1,), (1,)), ((), ())), preferred_element_type=F32)


def gelu_parts(x):
    square = x * x
    t = jnp.tanh(GELU_A * x * (1.0 + GELU_B * square))
    half = 0.5 * (1.0 + t)
    slope = half + 0.5 * x * (1.0 - t * t) * (GELU_A * (1.0 + 3.0 * GELU_B * square))
    return x * half, slope


def gelu(x):
    t = jnp.tanh(GELU_A * x * (1.0 + GELU_B * x * x))
    return 0.5 * x * (1.0 + t)


def stack_ranks(core, own, other):
    first = core == 0
    return jnp.concatenate([jnp.where(first, own, other), jnp.where(first, other, own)], axis=0)


def flipped(values):
    return values.T.astype(BF16)


def halves(core, width):
    step = width // 2
    return (
        pl.ds(pl.multiple_of(core * step, 128), step),
        pl.ds(pl.multiple_of((1 - core) * step, 128), step),
    )


def mixer_kernel(
    core_ref, tokens_ref, halo_ref, onehot_ref, masks_ref, gain_ref, taps_ref, soft_ref,
    wr_own, wr_oth, sb_own, sb_oth, sr_own, sr_oth, er_own, er_oth,
    sd_own, sd_oth, si_own, si_oth, bd_own, bd_oth, bi_own, bi_oth, ed_own, ed_oth, ei_own, ei_oth,
    normed_out, picked_br_out, picked_di_out, mixed_out, rate_out, inflow_out, local_out, reach_out,
    ends_out, spans_out, summary_out,
    normed, picked_r, inner_gate, picked_gate, mixed_all, filt, decay_buf, drive_buf,
):
    core = core_ref[0]
    step = pl.program_id(0)
    rows, width = tokens_ref.shape
    ranks = onehot_ref.shape[1]
    seqs = halo_ref.shape[0] // HALO
    steps = rows // seqs
    lane_tiles = pl.num_programs(0) // 2
    tile = mixed_out.shape[1]

    @pl.when(step == 0)
    def _():
        gain = gain_ref[...]
        for src, at, count in ((tokens_ref, 0, rows), (halo_ref, rows, seqs * HALO)):
            values = src[...].astype(F32)
            scale = lax.rsqrt(jnp.mean(values * values, axis=1, keepdims=True) + EPSILON)
            normed[at : at + count, :] = (values * scale * gain).astype(BF16)
        normed_out[...] = normed[:rows, :]
        shrink = jnp.concatenate(
            [stack_ranks(core, sb_own[...], sb_oth[...]), stack_ranks(core, sr_own[...], sr_oth[...])], axis=0
        )
        inner = mm_nt(normed[...], shrink)
        onehot = onehot_ref[...]
        picked = (inner * jnp.concatenate([onehot, onehot], axis=1)).astype(BF16)
        picked_r[...] = picked[:, ranks:]
        picked_br_out[...] = picked[:rows, :]
        inner_gate[...] = jnp.zeros_like(inner_gate)

    @pl.when(step < lane_tiles)
    def _():
        own, oth = halves(core, width)
        recur = (
            mm(normed[:, own], wr_own[...])
            + mm(normed[:, oth], wr_oth[...])
            + mm(picked_r[...], stack_ranks(core, er_own[...], er_oth[...]))
        )
        at = pl.multiple_of(step * tile, 128)
        for s in range(seqs):
            filt[s, :HALO, :] = recur[rows + s * HALO : rows + (s + 1) * HALO, :]
            filt[s, HALO:, :] = recur[s * steps : (s + 1) * steps, :]
        for s in range(seqs):
            here = slice(s * steps, (s + 1) * steps)
            total = taps_ref[0:1, :] * filt[s, HALO:, :]
            for lag in range(1, taps_ref.shape[0]):
                earlier = filt[s, HALO - lag : HALO - lag + steps, :]
                total = total + taps_ref[lag : lag + 1, :] * earlier * masks_ref[here, lag - 1 : lag]
            mixed_out[here, :] = total
            mixed_all[here, pl.ds(at, tile)] = total
        low = mixed_out[...].astype(BF16)
        shrink = jnp.concatenate(
            [stack_ranks(core, sd_own[...], sd_oth[...]), stack_ranks(core, si_own[...], si_oth[...])], axis=0
        )
        inner_gate[...] += mm_nt(low, shrink)

    @pl.when(step == lane_tiles - 1)
    def _():
        onehot = onehot_ref[:rows, :]
        picked = (inner_gate[...] * jnp.concatenate([onehot, onehot], axis=1)).astype(BF16)
        picked_gate[...] = picked
        picked_di_out[...] = picked

    @pl.when(step >= lane_tiles)
    def _():
        at = pl.multiple_of((step - lane_tiles) * tile, 128)
        mixed = mixed_all[:, pl.ds(at, tile)]
        low = mixed.astype(BF16)
        blocks, block = bd_own.shape[0], bd_own.shape[1]
        mine = (step - lane_tiles) // (lane_tiles // 2) == core
        rates, inflows = [], []
        for b in range(blocks):
            both = jnp.concatenate(
                [jnp.where(mine, bd_own[b], bd_oth[b]), jnp.where(mine, bi_own[b], bi_oth[b])], axis=1
            )
            pair = mm(low[:, b * block : (b + 1) * block], both)
            rates.append(pair[:, :block])
            inflows.append(pair[:, block:])
        rate_pre = jnp.concatenate(rates, axis=1) + mm(
            picked_gate[:, :ranks], stack_ranks(core, ed_own[...], ed_oth[...])
        )
        inflow_pre = jnp.concatenate(inflows, axis=1) + mm(
            picked_gate[:, ranks:], stack_ranks(core, ei_own[...], ei_oth[...])
        )
        rate = jax.nn.sigmoid(rate_pre)
        inflow = jax.nn.sigmoid(inflow_pre)
        rate_out[...] = rate
        inflow_out[...] = inflow
        keep = masks_ref[:, 0:1]
        raw = jnp.exp(-RATE_SCALE * rate * soft_ref[...])
        root_raw = jnp.sqrt(jnp.maximum((1.0 - raw) * (1.0 + raw), ROOT_FLOOR))
        root = keep * root_raw + (1.0 - keep)
        decay = raw * keep
        drive = root * inflow * mixed
        for q in range(tile // LANES):
            decay_buf[q] = decay[:, q * LANES : (q + 1) * LANES]
            drive_buf[q] = drive[:, q * LANES : (q + 1) * LANES]
        seg = steps // SEGS
        for q in range(tile // LANES):
            lanes = slice(q * LANES, (q + 1) * LANES)
            for s in range(seqs):
                at = pl.ds(s * steps, SEGS, stride=seg)
                held, span = drive_buf[q, at, :], decay_buf[q, at, :]
                local_out[q, at, :] = held
                reach_out[q, at, :] = span
                for i in range(1, seg):
                    at = pl.ds(s * steps + i, SEGS, stride=seg)
                    a = decay_buf[q, at, :]
                    held = a * held + drive_buf[q, at, :]
                    span = a * span
                    local_out[q, at, :] = held
                    reach_out[q, at, :] = span
                ends_out[s * SEGS : (s + 1) * SEGS, lanes] = held
                spans_out[s * SEGS : (s + 1) * SEGS, lanes] = span
                total = held[0:1, :]
                product = span[0:1, :]
                for g in range(1, SEGS):
                    total = held[g : g + 1, :] + span[g : g + 1, :] * total
                    product = span[g : g + 1, :] * product
                summary_out[s : s + 1, lanes] = product
                summary_out[seqs + s : seqs + s + 1, lanes] = total


def branch_kernel(core_ref, normed_ref, picked_ref, wb_own, wb_oth, eb_own, eb_oth, out_ref):
    core = core_ref[0]
    own, oth = halves(core, normed_ref.shape[1])
    out_ref[...] = (
        mm(normed_ref[:, own], wb_own[...])
        + mm(normed_ref[:, oth], wb_oth[...])
        + mm(picked_ref[...], stack_ranks(core, eb_own[...], eb_oth[...]))
    )


def arrived(messages, seqs):
    value = messages[-1][seqs : 2 * seqs, :]
    for message in reversed(messages[:-1]):
        value = message[seqs : 2 * seqs, :] + message[:seqs, :] * value
    return value


def output_kernel(
    core_ref, *refs, reach
):
    (local_ref, reach_ref, ends_ref, spans_ref) = refs[:4]
    messages = refs[4 : 4 + reach]
    (
        pre_ref, tokens_ref, onehot_ref, gain_ref, wo_own, wo_oth, so_own, so_oth, eo_own, eo_oth,
        state_out, merged_out, carry_out, residual_out, second_out, picked_out, acc, inner,
    ) = refs[4 + reach :]
    core = core_ref[0]
    step = pl.program_id(0)
    count = pl.num_programs(0)
    groups, rows, _ = local_ref.shape
    seqs = ends_ref.shape[0] // SEGS
    seg = rows // (seqs * SEGS)

    @pl.when(step == 0)
    def _():
        acc[...] = jnp.zeros_like(acc)
        inner[...] = jnp.zeros_like(inner)

    start = arrived([m[...] for m in messages], seqs)
    carry_out[...] = jnp.concatenate([start, jnp.zeros_like(start)], axis=0)
    for s in range(seqs):
        carry = start[s : s + 1, :]
        for g in range(SEGS):
            at = s * SEGS + g
            here = slice(at * seg, (at + 1) * seg)
            state = jnp.concatenate([local_ref[q, here, :] for q in range(groups)], axis=1) + (
                jnp.concatenate([reach_ref[q, here, :] for q in range(groups)], axis=1) * carry
            )
            state_out[here, :] = state
            merged_out[here, :] = (gelu(pre_ref[here, :]) * state).astype(BF16)
            carry = ends_ref[at : at + 1, :] + spans_ref[at : at + 1, :] * carry
    merged = merged_out[...]

    @pl.when(step < count // 2)
    def _():
        acc[...] += mm(merged, wo_own[...])

    @pl.when(step >= count // 2)
    def _():
        acc[...] += mm(merged, wo_oth[...])

    inner[...] += mm_nt(merged, stack_ranks(core, so_own[...], so_oth[...]))

    @pl.when(step == count - 1)
    def _():
        picked = (inner[...] * onehot_ref[...]).astype(BF16)
        picked_out[...] = picked
        residual = (
            tokens_ref[...].astype(F32)
            + acc[...]
            + mm(picked, stack_ranks(core, eo_own[...], eo_oth[...]))
        )
        residual_out[...] = residual
        scale = lax.rsqrt(jnp.mean(residual * residual, axis=1, keepdims=True) + EPSILON)
        second_out[...] = (residual * scale * gain_ref[...]).astype(BF16)


def feed_kernel(
    core_ref, second_ref, cot_ref, residual_ref, onehot_ref, gain_ref,
    g_own_a, g_own_b, g_oth_a, g_oth_b, u_own_a, u_own_b, u_oth_a, u_oth_b, d_own, d_oth,
    sg_own, sg_oth, su_own, su_oth, eg_own_a, eg_own_b, eg_oth_a, eg_oth_b,
    eu_own_a, eu_own_b, eu_oth_a, eu_oth_b, sd_own_a, sd_own_b, sd_oth_a, sd_oth_b, ed_own, ed_oth,
    out_ref, grad_residual_out, grad_low_out, deg_out, deu_out, dsd_out, dsgu_out, ded_out,
    picked, picked_t, gi_down, gi_down_t, down_acc, inner_down, grad_second, gi_gate,
):
    core = core_ref[0]
    step = pl.program_id(0)
    ranks = onehot_ref.shape[1]
    width = second_ref.shape[1]
    part = d_own.shape[0]
    own, oth = halves(core, width)

    @pl.when(step == 0)
    def _():
        onehot = onehot_ref[...]
        shrink = jnp.concatenate(
            [stack_ranks(core, sg_own[...], sg_oth[...]), stack_ranks(core, su_own[...], su_oth[...])], axis=0
        )
        both = mm_nt(second_ref[...], shrink) * jnp.concatenate([onehot, onehot], axis=1)
        picked[...] = both.astype(BF16)
        picked_t[...] = flipped(both)
        inner = mm_nt(cot_ref[...], stack_ranks(core, ed_own[...], ed_oth[...])) * onehot
        gi_down[...] = inner.astype(BF16)
        gi_down_t[...] = flipped(inner)
        down_acc[...] = jnp.zeros_like(down_acc)
        inner_down[...] = jnp.zeros_like(inner_down)
        grad_second[...] = jnp.zeros_like(grad_second)
        gi_gate[...] = jnp.zeros_like(gi_gate)

    join = lambda a, b: jnp.concatenate([a[...], b[...]], axis=1)
    g_own, g_oth = join(g_own_a, g_own_b), join(g_oth_a, g_oth_b)
    u_own, u_oth = join(u_own_a, u_own_b), join(u_oth_a, u_oth_b)
    down = jnp.concatenate([d_own[...], d_oth[...]], axis=0)
    eg = stack_ranks(core, join(eg_own_a, eg_own_b), join(eg_oth_a, eg_oth_b))
    eu = stack_ranks(core, join(eu_own_a, eu_own_b), join(eu_oth_a, eu_oth_b))
    sd = stack_ranks(core, join(sd_own_a, sd_own_b), join(sd_oth_a, sd_oth_b))

    x_own, x_oth = second_ref[:, own], second_ref[:, oth]
    gating = mm(x_own, g_own) + mm(x_oth, g_oth) + mm(picked[:, :ranks], eg)
    upward = mm(x_own, u_own) + mm(x_oth, u_oth) + mm(picked[:, ranks:], eu)
    grad_hidden = mm_nt(cot_ref[...], down) + mm(gi_down[...], sd)
    smooth, slope = gelu_parts(gating)
    hidden = (smooth * upward).astype(BF16)
    grad_gating = (grad_hidden * upward * slope).astype(BF16)
    grad_upward = (grad_hidden * smooth).astype(BF16)
    down_acc[...] += mm(hidden, down)
    inner_down[...] += mm_nt(hidden, sd)
    grad_second[:, own] += mm_nt(grad_gating, g_own) + mm_nt(grad_upward, u_own)
    grad_second[:, oth] += mm_nt(grad_gating, g_oth) + mm_nt(grad_upward, u_oth)
    gi_gate[:, :ranks] += mm_nt(grad_gating, eg)
    gi_gate[:, ranks:] += mm_nt(grad_upward, eu)
    for out, grad in (
        (deg_out, mm(picked_t[:ranks, :], grad_gating)),
        (deu_out, mm(picked_t[ranks:, :], grad_upward)),
        (dsd_out, mm(gi_down_t[...], hidden)),
    ):
        low, high = grad[:, :part], grad[:, part:]
        out[0] = jnp.where(core == 0, low, high)
        out[1] = jnp.where(core == 0, high, low)

    @pl.when(step == pl.num_programs(0) - 1)
    def _():
        onehot = onehot_ref[...]
        chosen = inner_down[...] * onehot
        residual = residual_ref[...]
        out_ref[...] = (
            residual + down_acc[...] + mm(chosen.astype(BF16), stack_ranks(core, ed_own[...], ed_oth[...]))
        ).astype(BF16)
        ded_out[...] = mm(flipped(chosen), cot_ref[...])
        inner = gi_gate[...] * jnp.concatenate([onehot, onehot], axis=1)
        shrink = jnp.concatenate(
            [stack_ranks(core, sg_own[...], sg_oth[...]), stack_ranks(core, su_own[...], su_oth[...])], axis=0
        )
        dsgu_out[...] = mm(flipped(inner), second_ref[...])
        weighted = (grad_second[...] + mm(inner.astype(BF16), shrink)) * gain_ref[...]
        scale = lax.rsqrt(jnp.mean(residual * residual, axis=1, keepdims=True) + EPSILON)
        grad = (
            cot_ref[...].astype(F32)
            + scale * weighted
            - residual * (scale * scale * scale * jnp.mean(weighted * residual, axis=1, keepdims=True))
        )
        grad_residual_out[...] = grad
        grad_low_out[...] = grad.astype(BF16)


def output_back_kernel(
    core_ref, low_ref, onehot_ref, masks_ref, soft_ref, picked_ref, pre_ref, state_ref, merged_ref, rate_ref,
    wo_own, wo_oth, so_own, so_oth, eo_own, eo_oth,
    pre_grad_out, local_out, reach_out, ends_out, spans_out, summary_out, dso_out, deo_out,
    gi, gi_t, decay_buf, drive_buf, grad_buf,
):
    core = core_ref[0]
    step = pl.program_id(0)
    rows, tile = pre_ref.shape
    seqs = ends_out.shape[0] // SEGS
    steps = rows // seqs
    seg = steps // SEGS

    @pl.when(step == 0)
    def _():
        inner = mm_nt(low_ref[...], stack_ranks(core, eo_own[...], eo_oth[...])) * onehot_ref[...]
        gi[...] = inner.astype(BF16)
        gi_t[...] = flipped(inner)
        deo_out[...] = mm(flipped(picked_ref[...].astype(F32)), low_ref[...])

    mine = step // (pl.num_programs(0) // 2) == core

    @pl.when(mine)
    def _():
        grad_buf[...] = mm_nt(low_ref[...], wo_own[...])

    @pl.when(jnp.logical_not(mine))
    def _():
        grad_buf[...] = mm_nt(low_ref[...], wo_oth[...])

    grad_merged = grad_buf[...] + mm(gi[...], stack_ranks(core, so_own[...], so_oth[...]))
    smooth, slope = gelu_parts(pre_ref[...])
    pre_grad_out[...] = (grad_merged * state_ref[...] * slope).astype(BF16)
    grad_state = grad_merged * smooth
    decay = jnp.exp(-RATE_SCALE * rate_ref[...] * soft_ref[...]) * masks_ref[:, 0:1]
    dso_out[...] = mm(gi_t[...], merged_ref[...])
    for q in range(tile // LANES):
        drive_buf[q] = grad_state[:, q * LANES : (q + 1) * LANES]
        decay_buf[q] = decay[:, q * LANES : (q + 1) * LANES]
    for q in range(tile // LANES):
        lanes = slice(q * LANES, (q + 1) * LANES)
        for s in range(seqs):
            at = pl.ds(s * steps + seg - 1, SEGS, stride=seg)
            held = drive_buf[q, at, :]
            span = jnp.ones_like(held)
            local_out[q, at, :] = held
            reach_out[q, at, :] = span
            for i in range(seg - 2, -1, -1):
                a = decay_buf[q, pl.ds(s * steps + i + 1, SEGS, stride=seg), :]
                at = pl.ds(s * steps + i, SEGS, stride=seg)
                held = a * held + drive_buf[q, at, :]
                span = a * span
                local_out[q, at, :] = held
                reach_out[q, at, :] = span
            a = decay_buf[q, pl.ds(s * steps, SEGS, stride=seg), :]
            held = a * held
            span = a * span
            ends_out[s * SEGS : (s + 1) * SEGS, lanes] = held
            spans_out[s * SEGS : (s + 1) * SEGS, lanes] = span
            total = held[SEGS - 1 : SEGS, :]
            product = span[SEGS - 1 : SEGS, :]
            for g in range(SEGS - 2, -1, -1):
                total = held[g : g + 1, :] + span[g : g + 1, :] * total
                product = span[g : g + 1, :] * product
            summary_out[s : s + 1, lanes] = product
            summary_out[seqs + s : seqs + s + 1, lanes] = total


def branch_back_kernel(
    core_ref, grad_ref, normed_ref, onehot_ref, picked_ref, wb_own, wb_oth, sb_own, sb_oth, eb_own, eb_oth,
    out_ref, dsb_out, deb_out, acc, inner, picked_t,
):
    core = core_ref[0]
    step = pl.program_id(0)
    own, oth = halves(core, out_ref.shape[1])

    @pl.when(step == 0)
    def _():
        acc[...] = jnp.zeros_like(acc)
        inner[...] = jnp.zeros_like(inner)
        picked_t[...] = flipped(picked_ref[...].astype(F32))

    grad = grad_ref[...]
    acc[:, own] += mm_nt(grad, wb_own[...])
    acc[:, oth] += mm_nt(grad, wb_oth[...])
    inner[...] += mm_nt(grad, stack_ranks(core, eb_own[...], eb_oth[...]))
    deb_out[...] = mm(picked_t[...], grad)

    @pl.when(step == pl.num_programs(0) - 1)
    def _():
        gi = inner[...] * onehot_ref[...]
        dsb_out[...] = mm(flipped(gi), normed_ref[...])
        out_ref[...] = acc[...] + mm(gi.astype(BF16), stack_ranks(core, sb_own[...], sb_oth[...]))


def gates_back_kernel(
    core_ref, *refs, reach
):
    (local_ref, reach_ref, ends_ref, spans_ref) = refs[:4]
    messages = refs[4 : 4 + reach]
    (
        carry_ref, state_ref, mixed_ref, mixed_late_ref, rate_ref, inflow_ref, masks_ref, onehot_ref, soft_ref, picked_ref,
        bd_own, bd_oth, bi_own, bi_oth, ed_own, ed_oth, ei_own, ei_oth, sd_own, sd_oth, si_own, si_oth,
        grad_out, ded_out, dei_out, dsd_out, dsi_out, head_out,
        flow, partial, inner, gi, gi_t, picked_t,
    ) = refs[4 + reach :]
    core = core_ref[0]
    step = pl.program_id(0)
    lane_tiles = pl.num_programs(0) // 2
    groups = local_ref.shape[0]
    rows, tile = state_ref.shape
    ranks = onehot_ref.shape[1]
    seqs = ends_ref.shape[0] // SEGS
    steps = rows // seqs
    seg = steps // SEGS

    @pl.when(step == 0)
    def _():
        inner[...] = jnp.zeros_like(inner)
        picked_t[...] = flipped(picked_ref[...].astype(F32))

    @pl.when(step < lane_tiles)
    def _():
        start = arrived([m[...] for m in messages], seqs)
        for s in range(seqs):
            carry = start[s : s + 1, :]
            for g in range(SEGS - 1, -1, -1):
                at = s * SEGS + g
                here = slice(at * seg, (at + 1) * seg)
                flow[here, :] = jnp.concatenate([local_ref[q, here, :] for q in range(groups)], axis=1) + (
                    jnp.concatenate([reach_ref[q, here, :] for q in range(groups)], axis=1) * carry
                )
                carry = ends_ref[at : at + 1, :] + spans_ref[at : at + 1, :] * carry
        priors = []
        first = lax.broadcasted_iota(jnp.int32, (steps, tile), 0) == 0
        for s in range(seqs):
            rolled = pltpu.roll(state_ref[s * steps : (s + 1) * steps, :], 1, 0)
            priors.append(jnp.where(first, carry_ref[s : s + 1, :], rolled))
        prior = jnp.concatenate(priors, axis=0)
        backflow = flow[...]
        mixed = mixed_ref[...]
        rate = rate_ref[...]
        inflow = inflow_ref[...]
        keep = masks_ref[:, 0:1]
        soft = soft_ref[...]
        raw = jnp.exp(-RATE_SCALE * rate * soft)
        square = raw * raw
        spread = (1.0 - raw) * (1.0 + raw)
        root_raw = jnp.sqrt(jnp.maximum(spread, ROOT_FLOOR))
        root = keep * root_raw + (1.0 - keep)
        pulled = backflow * inflow
        grad_spread = jnp.where(spread > ROOT_FLOOR, pulled * mixed * keep * 0.5 / root_raw, 0.0)
        grad_log = backflow * prior * raw * keep - 2.0 * square * grad_spread
        grad_rate = (grad_log * (-RATE_SCALE * soft) * rate * (1.0 - rate)).astype(BF16)
        grad_inflow = (backflow * root * mixed * inflow * (1.0 - inflow)).astype(BF16)
        blocks, block = bd_own.shape[0], bd_own.shape[1]
        mine = step // (lane_tiles // 2) == core
        pieces = []
        for b in range(blocks):
            lanes = slice(b * block, (b + 1) * block)
            both = jnp.concatenate(
                [jnp.where(mine, bd_own[b], bd_oth[b]), jnp.where(mine, bi_own[b], bi_oth[b])], axis=1
            )
            pieces.append(mm_nt(jnp.concatenate([grad_rate[:, lanes], grad_inflow[:, lanes]], axis=1), both))
        at = pl.multiple_of(step * tile, 128)
        partial[:, pl.ds(at, tile)] = pulled * root + jnp.concatenate(pieces, axis=1)
        inner[:, :ranks] += mm_nt(grad_rate, stack_ranks(core, ed_own[...], ed_oth[...]))
        inner[:, ranks:] += mm_nt(grad_inflow, stack_ranks(core, ei_own[...], ei_oth[...]))
        ded_out[...] = mm(picked_t[:ranks, :], grad_rate)
        dei_out[...] = mm(picked_t[ranks:, :], grad_inflow)

    @pl.when(step == lane_tiles - 1)
    def _():
        onehot = onehot_ref[...]
        chosen = inner[...] * jnp.concatenate([onehot, onehot], axis=1)
        gi[...] = chosen.astype(BF16)
        gi_t[...] = flipped(chosen)

    @pl.when(step >= lane_tiles)
    def _():
        at = pl.multiple_of((step - lane_tiles) * tile, 128)
        shrink = jnp.concatenate(
            [stack_ranks(core, sd_own[...], sd_oth[...]), stack_ranks(core, si_own[...], si_oth[...])], axis=0
        )
        grad = partial[:, pl.ds(at, tile)] + mm(gi[...], shrink)
        grad_out[...] = grad
        for s in range(seqs):
            head_out[s * HALO : (s + 1) * HALO, :] = grad[s * steps : s * steps + HALO, :]
        both = mm(gi_t[...], mixed_late_ref[...].astype(BF16))
        dsd_out[...] = both[:ranks, :]
        dsi_out[...] = both[ranks:, :]


def recur_back_kernel(
    core_ref, grad_ref, head_ref, masks_ref, taps_ref, normed_ref, onehot_ref, picked_ref, branch_ref, residual_ref,
    tokens_ref, gain_ref, wr_own, wr_oth, sr_own, sr_oth, er_own, er_oth,
    out_ref, dsr_out, der_out, acc, inner, picked_t, filt, low,
):
    core = core_ref[0]
    step = pl.program_id(0)
    own, oth = halves(core, out_ref.shape[1])
    rows, tile = grad_ref.shape
    seqs = head_ref.shape[0] // HALO
    steps = rows // seqs
    lags = taps_ref.shape[0] - 1

    @pl.when(step == 0)
    def _():
        acc[...] = branch_ref[...]
        inner[...] = jnp.zeros_like(inner)
        picked_t[...] = flipped(picked_ref[...].astype(F32))

    for s in range(seqs):
        filt[s, :steps, :] = grad_ref[s * steps : (s + 1) * steps, :]
        filt[s, steps:, :] = head_ref[s * HALO : (s + 1) * HALO, :]
    for s in range(seqs):
        here = slice(s * steps, (s + 1) * steps)
        total = taps_ref[0:1, :] * filt[s, :steps, :]
        for lag in range(1, lags + 1):
            later = filt[s, lag : lag + steps, :]
            total = total + taps_ref[lag : lag + 1, :] * later * masks_ref[here, lags + lag - 1 : lags + lag]
        low[here, :] = total.astype(BF16)
    grad = low[...]
    acc[:, own] += mm_nt(grad, wr_own[...])
    acc[:, oth] += mm_nt(grad, wr_oth[...])
    inner[...] += mm_nt(grad, stack_ranks(core, er_own[...], er_oth[...]))
    der_out[...] = mm(picked_t[...], grad)

    @pl.when(step == pl.num_programs(0) - 1)
    def _():
        gi = inner[...] * onehot_ref[...]
        dsr_out[...] = mm(flipped(gi), normed_ref[...])
        weighted = (acc[...] + mm(gi.astype(BF16), stack_ranks(core, sr_own[...], sr_oth[...]))) * gain_ref[...]
        values = tokens_ref[...].astype(F32)
        scale = lax.rsqrt(jnp.mean(values * values, axis=1, keepdims=True) + EPSILON)
        out_ref[...] = (
            residual_ref[...]
            + scale * weighted
            - values * (scale * scale * scale * jnp.mean(weighted * values, axis=1, keepdims=True))
        )


def whole_spec(shape):
    zeros = (0,) * len(shape)
    return pl.BlockSpec(shape, lambda j, c: zeros)


def call(kernel, name, grid, core, ins, outs, scratch, flops, nbytes):
    in_specs, arrays = [], []
    for item in ins:
        if isinstance(item, tuple):
            arrays.append(item[0])
            in_specs.append(pl.BlockSpec(item[1], item[2]))
        else:
            arrays.append(item)
            in_specs.append(whole_spec(item.shape))
    out_specs, shapes = [], []
    for item in outs:
        shapes.append(jax.ShapeDtypeStruct(item[0], item[1]))
        out_specs.append(pl.BlockSpec(item[2], item[3]) if len(item) == 4 else whole_spec(item[0]))
    return pl.pallas_call(
        kernel,
        grid_spec=pltpu.PrefetchScalarGridSpec(
            num_scalar_prefetch=1, grid=(grid,), in_specs=in_specs, out_specs=out_specs, scratch_shapes=scratch
        ),
        out_shape=shapes,
        name=name,
        compiler_params=pltpu.CompilerParams(
            dimension_semantics=("arbitrary",), vmem_limit_bytes=60 * 1024 * 1024
        ),
        cost_estimate=pl.CostEstimate(flops=flops, bytes_accessed=nbytes, transcendentals=0),
    )(core, *arrays)


def shifted(shard, by):
    peers = lax.axis_size("seq")
    pairs = [(i, i + by) for i in range(peers) if 0 <= i + by < peers]
    return lax.ppermute(shard, "seq", pairs)


def local(
    tokens, segment_ids, document_adapter, out_cotangent, mixer_gain, feed_gain, filter_taps, decay_param, *weights
):
    core = lax.axis_index("wshard").astype(jnp.int32).reshape(1)
    other = [lax.ppermute(item, "wshard", [(0, 1), (1, 0)]) for item in weights]
    (wb, wr, bd, bi, wo, wg, wu, wd) = [(a, b) for a, b in zip(weights[:8], other[:8])]
    (sb, eb, sr, er, sdec, edec, sinf, einf, so, eo, sg, eg, su, eu, sdn, edn) = [
        (a, b) for a, b in zip(weights[8:], other[8:])
    ]
    seqs, steps, width = tokens.shape
    rows = seqs * steps
    lru = filter_taps.shape[1]
    lags = filter_taps.shape[0] - 1
    ranks = 2 * sb[0].shape[0]
    feed = wg[0].shape[1]
    peers = lax.axis_size("seq")
    reach = peers // 4

    before = shifted(segment_ids, 1)
    after = shifted(segment_ids, -1)
    halo = shifted(tokens[:, steps - HALO :, :], 1).reshape(seqs * HALO, width)
    position = lax.axis_index("seq") * steps + jnp.arange(steps, dtype=jnp.int32)
    wide = jnp.concatenate([before[:, steps - HALO :], segment_ids, after[:, :HALO]], axis=1)
    columns = []
    for lag in range(1, lags + 1):
        prior = wide[:, HALO - lag : HALO - lag + steps]
        columns.append((prior == segment_ids) & (position >= lag)[None, :])
    for lag in range(1, lags + 1):
        later = wide[:, HALO + lag : HALO + lag + steps]
        columns.append((later == segment_ids) & (position + lag < peers * steps)[None, :])
    columns += [columns[0]] * (8 - len(columns))
    masks = jnp.stack([c.reshape(rows) for c in columns], axis=1).astype(F32)
    documents = jnp.arange(document_adapter.shape[1], dtype=jnp.int32)

    def owners_of(ids):
        owner = jnp.sum(
            jnp.where(ids[:, :, None] == documents[None, None, :], document_adapter[:, None, :], 0), axis=2
        )
        return owner.reshape(-1)

    owner = jnp.concatenate([owners_of(segment_ids), owners_of(before[:, steps - HALO :])])
    onehot = (owner[:, None] == (jnp.arange(ranks, dtype=jnp.int32) // RANK)[None, :]).astype(F32)
    onehot_own = onehot[:rows]
    soft = jax.nn.softplus(-decay_param)[None, :]
    gain_first = mixer_gain[None, :]
    gain_second = feed_gain[None, :]
    tokens2 = tokens.reshape(rows, width)
    cot = out_cotangent.reshape(rows, width)

    tile = TILE
    count = lru // tile
    half = width // 2
    blocks = tile // bd[0].shape[1]
    block = bd[0].shape[1]
    early = lambda j: jnp.minimum(j, count - 1)
    late = lambda j: jnp.maximum(j - count, 0)
    flat = lambda r, at: ((r, tile), lambda j, c: (0, at(j)))

    def tiled(array, r, at):
        block_shape, index = flat(r, at)
        return (array, block_shape, index)

    def tiled_out(r, dtype, at, total=None):
        block_shape, index = flat(r, at)
        return ((r, total or lru), dtype, block_shape, index)

    lane_groups = tile // LANES

    def grouped(array, index):
        return (array, (lane_groups, rows, LANES), index)

    def grouped_out(at):
        return ((lru // LANES, rows, LANES), F32, (lane_groups, rows, LANES), lambda j, c: (at(j), 0, 0))

    def both(pair, r, at):
        return [tiled(pair[0], r, at), tiled(pair[1], r, at)]

    def gate_blocks(pair, at):
        index = lambda j, c: (at(j) % (count // 2), 0, 0)
        return [(pair[0], (blocks, block, block), index), (pair[1], (blocks, block, block), index)]

    half_ranks = ranks // 2
    ident = lambda j: j
    groups = seqs * SEGS
    with jax.named_scope("mixer_forward"):
        (normed, picked_br, picked_di, mixed, rate, inflow, held, span, ends, spans, summary) = call(
            mixer_kernel, "mixer_forward", 2 * count, core,
            [tokens2, halo, onehot, masks, gain_first, tiled(filter_taps, lags + 1, early), tiled(soft, 1, late)]
            + both(wr, half, early) + list(sb) + list(sr) + both(er, half_ranks, early)
            + both(sdec, half_ranks, early) + both(sinf, half_ranks, early)
            + gate_blocks(bd, late) + gate_blocks(bi, late)
            + both(edec, half_ranks, late) + both(einf, half_ranks, late),
            [((rows, width), BF16), ((rows, 2 * ranks), BF16), ((rows, 2 * ranks), BF16),
             tiled_out(rows, F32, early), tiled_out(rows, F32, late), tiled_out(rows, F32, late),
             grouped_out(late), grouped_out(late),
             tiled_out(groups, F32, late), tiled_out(groups, F32, late), tiled_out(2 * seqs, F32, late)],
            [pltpu.VMEM((rows + seqs * HALO, width), BF16), pltpu.VMEM((rows + seqs * HALO, ranks), BF16),
             pltpu.VMEM((rows, 2 * ranks), F32), pltpu.VMEM((rows, 2 * ranks), BF16),
             pltpu.VMEM((rows, lru), F32), pltpu.VMEM((seqs, steps + HALO, tile), F32),
             pltpu.VMEM((lane_groups, rows, LANES), F32), pltpu.VMEM((lane_groups, rows, LANES), F32)],
            int(6e9), int(30e6),
        )
    messages = [shifted(summary, d) for d in range(1, reach + 1)]
    with jax.named_scope("branch_forward"):
        (branch_pre,) = call(
            branch_kernel, "branch_forward", count, core,
            [normed, (picked_br, (rows, ranks), lambda j, c: (0, 0))] + both(wb, half, ident) + both(eb, half_ranks, ident),
            [tiled_out(rows, F32, ident)], [], int(4e9), int(15e6),
        )

    def placed(j, c):
        return jnp.where(j < count // 2, c[0] * (count // 2) + j, (1 - c[0]) * (count // 2) + j - count // 2)

    def placed_in(array, r):
        return (array, (r, tile), lambda j, c: (0, placed(j, c)))

    def placed_out(r, dtype):
        return ((r, lru), dtype, (r, tile), lambda j, c: (0, placed(j, c)))

    with jax.named_scope("output_forward"):
        state, merged, carry, residual, second, picked_o = call(
            functools.partial(output_kernel, reach=reach), "output_forward", count, core,
            [grouped(held, lambda j, c: (placed(j, c), 0, 0)), grouped(span, lambda j, c: (placed(j, c), 0, 0)), placed_in(ends, groups), placed_in(spans, groups)]
            + [placed_in(m, 2 * seqs) for m in messages]
            + [placed_in(branch_pre, rows), tokens2, onehot_own, gain_second,
               (wo[0], (tile, width), lambda j, c: (jnp.minimum(j, count // 2 - 1), 0)),
               (wo[1], (tile, width), lambda j, c: (jnp.maximum(j - count // 2, 0), 0)),
               placed_in(so[0], half_ranks), placed_in(so[1], half_ranks)] + list(eo),
            [placed_out(rows, F32), placed_out(rows, BF16), placed_out(2 * seqs, F32),
             ((rows, width), F32), ((rows, width), BF16), ((rows, ranks), BF16)],
            [pltpu.VMEM((rows, width), F32), pltpu.VMEM((rows, ranks), F32)],
            int(4e9), int(30e6),
        )

    part = 256
    pieces = feed // (2 * part)

    def feed_cols(pair_item, r):
        return [
            (pair_item, (r, part), lambda j, c: (0, c[0] * pieces + j)),
            (pair_item, (r, part), lambda j, c: (0, (1 - c[0]) * pieces + j)),
        ]

    def feed_pair(pair, r):
        return feed_cols(pair[0], r) + feed_cols(pair[1], r)

    grad_cols = ((2, ranks, feed // 2), F32, (2, ranks, part), lambda j, c: (0, 0, j))
    with jax.named_scope("feed_forward_both_ways"):
        result, grad_residual, grad_low, deg, deu, dsdn, dsgu, dedn = call(
            feed_kernel, "feed_both_ways", pieces, core,
            [second, cot, residual, onehot_own, gain_second] + feed_pair(wg, half) + feed_pair(wu, half)
            + [(wd[0], (part, width), lambda j, c: (j, 0)), (wd[1], (part, width), lambda j, c: (j, 0))]
            + list(sg) + list(su) + feed_pair(eg, half_ranks) + feed_pair(eu, half_ranks)
            + feed_pair(sdn, half_ranks) + list(edn),
            [((rows, width), BF16), ((rows, width), F32), ((rows, width), BF16),
             grad_cols, grad_cols, grad_cols, ((2 * ranks, width), F32), ((ranks, width), F32)],
            [pltpu.VMEM((rows, 2 * ranks), BF16), pltpu.VMEM((2 * ranks, rows), BF16),
             pltpu.VMEM((rows, ranks), BF16), pltpu.VMEM((ranks, rows), BF16),
             pltpu.VMEM((rows, width), F32), pltpu.VMEM((rows, ranks), F32), pltpu.VMEM((rows, width), F32),
             pltpu.VMEM((rows, 2 * ranks), F32)],
            int(50e9), int(60e6),
        )

    own_rows = lambda pair: [
        (pair[0], (tile, width), lambda j, c: (j % (count // 2), 0)),
        (pair[1], (tile, width), lambda j, c: (j % (count // 2), 0)),
    ]
    with jax.named_scope("output_backward"):
        pre_grad, bheld, bspan, bends, bspans, bsummary, dso, deo = call(
            output_back_kernel, "output_backward", count, core,
            [grad_low, onehot_own, masks, tiled(soft, 1, ident), picked_o, tiled(branch_pre, rows, ident),
             tiled(state, rows, ident), tiled(merged, rows, ident), tiled(rate, rows, ident)]
            + own_rows(wo) + both(so, half_ranks, ident) + list(eo),
            [tiled_out(rows, BF16, ident), grouped_out(ident), grouped_out(ident),
             tiled_out(groups, F32, ident), tiled_out(groups, F32, ident), tiled_out(2 * seqs, F32, ident),
             tiled_out(ranks, F32, ident), ((ranks, width), F32)],
            [pltpu.VMEM((rows, ranks), BF16), pltpu.VMEM((ranks, rows), BF16),
             pltpu.VMEM((lane_groups, rows, LANES), F32), pltpu.VMEM((lane_groups, rows, LANES), F32),
             pltpu.VMEM((rows, tile), F32)],
            int(5e9), int(30e6),
        )
    back_messages = [shifted(bsummary, -d) for d in range(1, reach + 1)]
    with jax.named_scope("branch_backward"):
        grad_branch, dsb, deb = call(
            branch_back_kernel, "branch_backward", count, core,
            [tiled(pre_grad, rows, ident), normed, onehot_own, (picked_br, (rows, ranks), lambda j, c: (0, 0))]
            + both(wb, half, ident) + list(sb) + both(eb, half_ranks, ident),
            [((rows, width), F32), ((ranks, width), F32), tiled_out(ranks, F32, ident)],
            [pltpu.VMEM((rows, width), F32), pltpu.VMEM((rows, ranks), F32), pltpu.VMEM((ranks, rows), BF16)],
            int(5e9), int(15e6),
        )
    with jax.named_scope("gates_backward"):
        grad_mixed, dedec, deinf, dsdec, dsinf, heads = call(
            functools.partial(gates_back_kernel, reach=reach), "gates_backward", 2 * count, core,
            [grouped(bheld, lambda j, c: (early(j), 0, 0)), grouped(bspan, lambda j, c: (early(j), 0, 0)), tiled(bends, groups, early), tiled(bspans, groups, early)]
            + [tiled(m, 2 * seqs, early) for m in back_messages]
            + [tiled(carry, 2 * seqs, early), tiled(state, rows, early), tiled(mixed, rows, early),
               tiled(mixed, rows, late), tiled(rate, rows, early), tiled(inflow, rows, early),
               masks, onehot_own, tiled(soft, 1, early), picked_di]
            + gate_blocks(bd, early) + gate_blocks(bi, early)
            + both(edec, half_ranks, early) + both(einf, half_ranks, early)
            + both(sdec, half_ranks, late) + both(sinf, half_ranks, late),
            [tiled_out(rows, F32, late), tiled_out(ranks, F32, early), tiled_out(ranks, F32, early),
             tiled_out(ranks, F32, late), tiled_out(ranks, F32, late), tiled_out(seqs * HALO, F32, late)],
            [pltpu.VMEM((rows, tile), F32), pltpu.VMEM((rows, lru), F32), pltpu.VMEM((rows, 2 * ranks), F32),
             pltpu.VMEM((rows, 2 * ranks), BF16), pltpu.VMEM((2 * ranks, rows), BF16), pltpu.VMEM((2 * ranks, rows), BF16)],
            int(4e9), int(40e6),
        )
    next_heads = shifted(heads, -1)
    with jax.named_scope("recur_backward"):
        grad_tokens, dsr, der = call(
            recur_back_kernel, "recur_backward", count, core,
            [tiled(grad_mixed, rows, ident), tiled(next_heads, seqs * HALO, ident), masks,
             tiled(filter_taps, lags + 1, ident), normed, onehot_own,
             (picked_br, (rows, ranks), lambda j, c: (0, 1)), grad_branch, grad_residual, tokens2, gain_first]
            + both(wr, half, ident) + list(sr) + both(er, half_ranks, ident),
            [((rows, width), F32), ((ranks, width), F32), tiled_out(ranks, F32, ident)],
            [pltpu.VMEM((rows, width), F32), pltpu.VMEM((rows, ranks), F32), pltpu.VMEM((ranks, rows), BF16),
             pltpu.VMEM((seqs, steps + HALO, tile), F32), pltpu.VMEM((rows, tile), BF16)],
            int(5e9), int(30e6),
        )

    def unfold(grad):
        return jnp.concatenate([grad[0], grad[1]], axis=1)

    factors = [
        dsb, deb, dsr, der, dsdec, dedec, dsinf, deinf, dso, deo,
        dsgu[:ranks], unfold(deg), dsgu[ranks:], unfold(deu), unfold(dsdn), dedn,
    ]
    summed = tuple(lax.psum_scatter(g, ("seq", "wshard"), scatter_dimension=0, tiled=True) for g in factors)
    return (result.reshape(seqs, steps, width), grad_tokens.reshape(seqs, steps, width)) + summed


def solution(mesh):
    split = P("wshard", None)
    in_specs = (
        (P("wshard", "seq", None), P("wshard", "seq"), split, P("wshard", "seq", None))
        + (P(),) * 4
        + (split, split, P("wshard", None, None), P("wshard", None, None))
        + (split,) * 20
    )
    out_specs = (P("wshard", "seq", None),) * 2 + (P(("seq", "wshard"), None),) * 16
    return jax.shard_map(local, mesh=mesh, in_specs=in_specs, out_specs=out_specs, check_vma=False)
```

```python
import functools

import jax
import jax.numpy as jnp
from jax import lax
from jax.experimental import pallas as pl
from jax.experimental.pallas import tpu as pltpu
from jax.sharding import PartitionSpec as P

RANK = 16
EPSILON = 1e-06
RATE_SCALE = 8.0
ROOT_FLOOR = 0.001
GELU_A = 0.7978845608028654
GELU_B = 0.044715

HALO = 8
SEGS = 8
TILE = 512
LANES = 128
F32 = jnp.float32
BF16 = jnp.bfloat16


def mm(left, right):
    return lax.dot_general(left, right, (((1,), (0,)), ((), ())), preferred_element_type=F32)


def mm_nt(left, right):
    return lax.dot_general(left, right, (((1,), (1,)), ((), ())), preferred_element_type=F32)


def gelu_parts(x):
    square = x * x
    t = jnp.tanh(GELU_A * x * (1.0 + GELU_B * square))
    half = 0.5 * (1.0 + t)
    slope = half + 0.5 * x * (1.0 - t * t) * (GELU_A * (1.0 + 3.0 * GELU_B * square))
    return x * half, slope


def gelu(x):
    t = jnp.tanh(GELU_A * x * (1.0 + GELU_B * x * x))
    return 0.5 * x * (1.0 + t)


def stack_ranks(core, own, other):
    first = core == 0
    return jnp.concatenate([jnp.where(first, own, other), jnp.where(first, other, own)], axis=0)


def flipped(values):
    return values.T.astype(BF16)


def fold(grad):
    ranks, wide = grad.shape
    half = wide // 2
    left, right = grad[:, :half], grad[:, half:]
    upper = lax.broadcasted_iota(jnp.int32, (ranks, half), 0) % 8 < 4
    blocks = []
    for pair in (
        jnp.where(upper, left, pltpu.roll(right, 4, 0)),
        jnp.where(upper, pltpu.roll(left, ranks - 4, 0), right),
    ):
        eights = pair.reshape(ranks // 8, 8, half)
        blocks.append(
            jnp.concatenate([eights[:, :, : half // 2], eights[:, :, half // 2 :]], axis=1).astype(BF16)
        )
    return blocks


def put_folded(out, grad):
    first, second = fold(grad)
    out[0] = first
    out[1] = second


def unfold(rows4, wide):
    quarter = wide // 4
    pieces = []
    for at in range(0, rows4.shape[1], quarter):
        here = rows4[:, at : at + quarter]
        pieces += [here[0:4], here[8:12], here[4:8], here[12:16]]
    return pieces


def halves(core, width):
    step = width // 2
    return (
        pl.ds(pl.multiple_of(core * step, 128), step),
        pl.ds(pl.multiple_of((1 - core) * step, 128), step),
    )


def mixer_kernel(
    core_ref, tokens_ref, halo_ref, onehot_ref, masks_ref, gain_ref, taps_ref, soft_ref,
    wr_own, wr_oth, sb_own, sb_oth, sr_own, sr_oth, er_own, er_oth,
    sd_own, sd_oth, si_own, si_oth, bd_own, bd_oth, bi_own, bi_oth, ed_own, ed_oth, ei_own, ei_oth,
    normed_out, picked_br_out, picked_di_out, mixed_out, rate_out, inflow_out, local_out, reach_out,
    ends_out, spans_out, summary_out,
    normed, picked_r, inner_gate, picked_gate, mixed_all, filt, decay_buf, drive_buf,
):
    core = core_ref[0]
    step = pl.program_id(0)
    rows, width = tokens_ref.shape
    ranks = onehot_ref.shape[1]
    seqs = halo_ref.shape[0] // HALO
    steps = rows // seqs
    lane_tiles = pl.num_programs(0) // 2
    tile = mixed_out.shape[1]

    @pl.when(step == 0)
    def _():
        gain = gain_ref[...]
        for src, at, count in ((tokens_ref, 0, rows), (halo_ref, rows, seqs * HALO)):
            values = src[...].astype(F32)
            scale = lax.rsqrt(jnp.mean(values * values, axis=1, keepdims=True) + EPSILON)
            normed[at : at + count, :] = (values * scale * gain).astype(BF16)
        normed_out[...] = normed[:rows, :]
        shrink = jnp.concatenate(
            [stack_ranks(core, sb_own[...], sb_oth[...]), stack_ranks(core, sr_own[...], sr_oth[...])], axis=0
        )
        inner = mm_nt(normed[...], shrink)
        onehot = onehot_ref[...]
        picked = (inner * jnp.concatenate([onehot, onehot], axis=1)).astype(BF16)
        picked_r[...] = picked[:, ranks:]
        picked_br_out[...] = picked[:rows, :]
        inner_gate[...] = jnp.zeros_like(inner_gate)

    @pl.when(step < lane_tiles)
    def _():
        own, oth = halves(core, width)
        recur = (
            mm(normed[:, own], wr_own[...])
            + mm(normed[:, oth], wr_oth[...])
            + mm(picked_r[...], stack_ranks(core, er_own[...], er_oth[...]))
        )
        at = pl.multiple_of(step * tile, 128)
        for s in range(seqs):
            filt[s, :HALO, :] = recur[rows + s * HALO : rows + (s + 1) * HALO, :]
            filt[s, HALO:, :] = recur[s * steps : (s + 1) * steps, :]
        for s in range(seqs):
            here = slice(s * steps, (s + 1) * steps)
            total = taps_ref[0:1, :] * filt[s, HALO:, :]
            for lag in range(1, taps_ref.shape[0]):
                earlier = filt[s, HALO - lag : HALO - lag + steps, :]
                total = total + taps_ref[lag : lag + 1, :] * earlier * masks_ref[here, lag - 1 : lag]
            mixed_out[here, :] = total
            mixed_all[here, pl.ds(at, tile)] = total
        low = mixed_out[...].astype(BF16)
        shrink = jnp.concatenate(
            [stack_ranks(core, sd_own[...], sd_oth[...]), stack_ranks(core, si_own[...], si_oth[...])], axis=0
        )
        inner_gate[...] += mm_nt(low, shrink)

    @pl.when(step == lane_tiles - 1)
    def _():
        onehot = onehot_ref[:rows, :]
        picked = (inner_gate[...] * jnp.concatenate([onehot, onehot], axis=1)).astype(BF16)
        picked_gate[...] = picked
        picked_di_out[...] = picked

    @pl.when(step >= lane_tiles)
    def _():
        at = pl.multiple_of((step - lane_tiles) * tile, 128)
        mixed = mixed_all[:, pl.ds(at, tile)]
        low = mixed.astype(BF16)
        blocks, block = bd_own.shape[0], bd_own.shape[1]
        mine = (step - lane_tiles) // (lane_tiles // 2) == core
        rates, inflows = [], []
        for b in range(blocks):
            both = jnp.concatenate(
                [jnp.where(mine, bd_own[b], bd_oth[b]), jnp.where(mine, bi_own[b], bi_oth[b])], axis=1
            )
            pair = mm(low[:, b * block : (b + 1) * block], both)
            rates.append(pair[:, :block])
            inflows.append(pair[:, block:])
        rate_pre = jnp.concatenate(rates, axis=1) + mm(
            picked_gate[:, :ranks], stack_ranks(core, ed_own[...], ed_oth[...])
        )
        inflow_pre = jnp.concatenate(inflows, axis=1) + mm(
            picked_gate[:, ranks:], stack_ranks(core, ei_own[...], ei_oth[...])
        )
        rate = jax.nn.sigmoid(rate_pre)
        inflow = jax.nn.sigmoid(inflow_pre)
        rate_out[...] = rate
        inflow_out[...] = inflow
        keep = masks_ref[:, 0:1]
        raw = jnp.exp(-RATE_SCALE * rate * soft_ref[...])
        root_raw = jnp.sqrt(jnp.maximum((1.0 - raw) * (1.0 + raw), ROOT_FLOOR))
        root = keep * root_raw + (1.0 - keep)
        decay = raw * keep
        drive = root * inflow * mixed
        for q in range(tile // LANES):
            decay_buf[q] = decay[:, q * LANES : (q + 1) * LANES]
            drive_buf[q] = drive[:, q * LANES : (q + 1) * LANES]
        seg = steps // SEGS
        for q in range(tile // LANES):
            lanes = slice(q * LANES, (q + 1) * LANES)
            for s in range(seqs):
                at = pl.ds(s * steps, SEGS, stride=seg)
                held, span = drive_buf[q, at, :], decay_buf[q, at, :]
                local_out[q, at, :] = held
                reach_out[q, at, :] = span
                for i in range(1, seg):
                    at = pl.ds(s * steps + i, SEGS, stride=seg)
                    a = decay_buf[q, at, :]
                    held = a * held + drive_buf[q, at, :]
                    span = a * span
                    local_out[q, at, :] = held
                    reach_out[q, at, :] = span
                ends_out[s * SEGS : (s + 1) * SEGS, lanes] = held
                spans_out[s * SEGS : (s + 1) * SEGS, lanes] = span
                total = held[0:1, :]
                product = span[0:1, :]
                for g in range(1, SEGS):
                    total = held[g : g + 1, :] + span[g : g + 1, :] * total
                    product = span[g : g + 1, :] * product
                summary_out[s : s + 1, lanes] = product
                summary_out[seqs + s : seqs + s + 1, lanes] = total


def branch_kernel(core_ref, normed_ref, picked_ref, wb_own, wb_oth, eb_own, eb_oth, out_ref):
    core = core_ref[0]
    own, oth = halves(core, normed_ref.shape[1])
    out_ref[...] = (
        mm(normed_ref[:, own], wb_own[...])
        + mm(normed_ref[:, oth], wb_oth[...])
        + mm(picked_ref[...], stack_ranks(core, eb_own[...], eb_oth[...]))
    )


def arrived(messages, seqs):
    value = messages[-1][seqs : 2 * seqs, :]
    for message in reversed(messages[:-1]):
        value = message[seqs : 2 * seqs, :] + message[:seqs, :] * value
    return value


def output_kernel(
    core_ref, *refs, reach
):
    (local_ref, reach_ref, ends_ref, spans_ref) = refs[:4]
    messages = refs[4 : 4 + reach]
    (
        pre_ref, tokens_ref, onehot_ref, gain_ref, wo_own, wo_oth, so_own, so_oth, eo_own, eo_oth,
        state_out, merged_out, carry_out, residual_out, second_out, picked_out, acc, inner,
    ) = refs[4 + reach :]
    core = core_ref[0]
    step = pl.program_id(0)
    count = pl.num_programs(0)
    groups, rows, _ = local_ref.shape
    seqs = ends_ref.shape[0] // SEGS
    seg = rows // (seqs * SEGS)

    @pl.when(step == 0)
    def _():
        acc[...] = jnp.zeros_like(acc)
        inner[...] = jnp.zeros_like(inner)

    start = arrived([m[...] for m in messages], seqs)
    carry_out[...] = jnp.concatenate([start, jnp.zeros_like(start)], axis=0)
    for s in range(seqs):
        carry = start[s : s + 1, :]
        for g in range(SEGS):
            at = s * SEGS + g
            here = slice(at * seg, (at + 1) * seg)
            state = jnp.concatenate([local_ref[q, here, :] for q in range(groups)], axis=1) + (
                jnp.concatenate([reach_ref[q, here, :] for q in range(groups)], axis=1) * carry
            )
            state_out[here, :] = state
            merged_out[here, :] = (gelu(pre_ref[here, :]) * state).astype(BF16)
            carry = ends_ref[at : at + 1, :] + spans_ref[at : at + 1, :] * carry
    merged = merged_out[...]

    @pl.when(step < count // 2)
    def _():
        acc[...] += mm(merged, wo_own[...])

    @pl.when(step >= count // 2)
    def _():
        acc[...] += mm(merged, wo_oth[...])

    inner[...] += mm_nt(merged, stack_ranks(core, so_own[...], so_oth[...]))

    @pl.when(step == count - 1)
    def _():
        picked = (inner[...] * onehot_ref[...]).astype(BF16)
        picked_out[...] = picked
        residual = (
            tokens_ref[...].astype(F32)
            + acc[...]
            + mm(picked, stack_ranks(core, eo_own[...], eo_oth[...]))
        )
        residual_out[...] = residual
        scale = lax.rsqrt(jnp.mean(residual * residual, axis=1, keepdims=True) + EPSILON)
        second_out[...] = (residual * scale * gain_ref[...]).astype(BF16)


def feed_kernel(
    core_ref, second_ref, cot_ref, residual_ref, onehot_ref, gain_ref,
    g_own_a, g_own_b, g_oth_a, g_oth_b, u_own_a, u_own_b, u_oth_a, u_oth_b, d_own, d_oth,
    sg_own, sg_oth, su_own, su_oth, eg_own_a, eg_own_b, eg_oth_a, eg_oth_b,
    eu_own_a, eu_own_b, eu_oth_a, eu_oth_b, sd_own_a, sd_own_b, sd_oth_a, sd_oth_b, ed_own, ed_oth,
    out_ref, grad_residual_out, grad_low_out, deg_out, deu_out, dsd_out, dsg_out, dsu_out, ded_out,
    picked, picked_t, gi_down, gi_down_t, down_acc, inner_down, grad_second, gi_gate,
):
    core = core_ref[0]
    step = pl.program_id(0)
    ranks = onehot_ref.shape[1]
    width = second_ref.shape[1]
    part = d_own.shape[0]
    own, oth = halves(core, width)

    @pl.when(step == 0)
    def _():
        onehot = onehot_ref[...]
        shrink = jnp.concatenate(
            [stack_ranks(core, sg_own[...], sg_oth[...]), stack_ranks(core, su_own[...], su_oth[...])], axis=0
        )
        both = mm_nt(second_ref[...], shrink) * jnp.concatenate([onehot, onehot], axis=1)
        picked[...] = both.astype(BF16)
        picked_t[...] = flipped(both)
        inner = mm_nt(cot_ref[...], stack_ranks(core, ed_own[...], ed_oth[...])) * onehot
        gi_down[...] = inner.astype(BF16)
        gi_down_t[...] = flipped(inner)
        down_acc[...] = jnp.zeros_like(down_acc)
        inner_down[...] = jnp.zeros_like(inner_down)
        grad_second[...] = jnp.zeros_like(grad_second)
        gi_gate[...] = jnp.zeros_like(gi_gate)

    join = lambda a, b: jnp.concatenate([a[...], b[...]], axis=1)
    g_own, g_oth = join(g_own_a, g_own_b), join(g_oth_a, g_oth_b)
    u_own, u_oth = join(u_own_a, u_own_b), join(u_oth_a, u_oth_b)
    down = jnp.concatenate([d_own[...], d_oth[...]], axis=0)
    eg = stack_ranks(core, join(eg_own_a, eg_own_b), join(eg_oth_a, eg_oth_b))
    eu = stack_ranks(core, join(eu_own_a, eu_own_b), join(eu_oth_a, eu_oth_b))
    sd = stack_ranks(core, join(sd_own_a, sd_own_b), join(sd_oth_a, sd_oth_b))

    x_own, x_oth = second_ref[:, own], second_ref[:, oth]
    gating = mm(x_own, g_own) + mm(x_oth, g_oth) + mm(picked[:, :ranks], eg)
    upward = mm(x_own, u_own) + mm(x_oth, u_oth) + mm(picked[:, ranks:], eu)
    grad_hidden = mm_nt(cot_ref[...], down) + mm(gi_down[...], sd)
    smooth, slope = gelu_parts(gating)
    hidden = (smooth * upward).astype(BF16)
    grad_gating = (grad_hidden * upward * slope).astype(BF16)
    grad_upward = (grad_hidden * smooth).astype(BF16)
    down_acc[...] += mm(hidden, down)
    inner_down[...] += mm_nt(hidden, sd)
    grad_second[:, own] += mm_nt(grad_gating, g_own) + mm_nt(grad_upward, u_own)
    grad_second[:, oth] += mm_nt(grad_gating, g_oth) + mm_nt(grad_upward, u_oth)
    gi_gate[:, :ranks] += mm_nt(grad_gating, eg)
    gi_gate[:, ranks:] += mm_nt(grad_upward, eu)
    for out, grad in (
        (deg_out, mm(picked_t[:ranks, :], grad_gating)),
        (deu_out, mm(picked_t[ranks:, :], grad_upward)),
        (dsd_out, mm(gi_down_t[...], hidden)),
    ):
        low, high = grad[:, :part], grad[:, part:]
        first = core == 0
        put_folded(
            out, jnp.concatenate([jnp.where(first, low, high), jnp.where(first, high, low)], axis=1)
        )

    @pl.when(step == pl.num_programs(0) - 1)
    def _():
        onehot = onehot_ref[...]
        chosen = inner_down[...] * onehot
        residual = residual_ref[...]
        out_ref[...] = (
            residual + down_acc[...] + mm(chosen.astype(BF16), stack_ranks(core, ed_own[...], ed_oth[...]))
        ).astype(BF16)
        put_folded(ded_out, mm(flipped(chosen), cot_ref[...]))
        inner = gi_gate[...] * jnp.concatenate([onehot, onehot], axis=1)
        shrink = jnp.concatenate(
            [stack_ranks(core, sg_own[...], sg_oth[...]), stack_ranks(core, su_own[...], su_oth[...])], axis=0
        )
        grads = mm(flipped(inner), second_ref[...])
        put_folded(dsg_out, grads[:ranks, :])
        put_folded(dsu_out, grads[ranks:, :])
        weighted = (grad_second[...] + mm(inner.astype(BF16), shrink)) * gain_ref[...]
        scale = lax.rsqrt(jnp.mean(residual * residual, axis=1, keepdims=True) + EPSILON)
        grad = (
            cot_ref[...].astype(F32)
            + scale * weighted
            - residual * (scale * scale * scale * jnp.mean(weighted * residual, axis=1, keepdims=True))
        )
        grad_residual_out[...] = grad
        grad_low_out[...] = grad.astype(BF16)


def output_back_kernel(
    core_ref, low_ref, onehot_ref, masks_ref, soft_ref, picked_ref, pre_ref, state_ref, merged_ref, rate_ref,
    wo_own, wo_oth, so_own, so_oth, eo_own, eo_oth,
    pre_grad_out, local_out, reach_out, ends_out, spans_out, summary_out, dso_out, deo_out,
    gi, gi_t, decay_buf, drive_buf, grad_buf,
):
    core = core_ref[0]
    step = pl.program_id(0)
    rows, tile = pre_ref.shape
    seqs = ends_out.shape[0] // SEGS
    steps = rows // seqs
    seg = steps // SEGS

    @pl.when(step == 0)
    def _():
        inner = mm_nt(low_ref[...], stack_ranks(core, eo_own[...], eo_oth[...])) * onehot_ref[...]
        gi[...] = inner.astype(BF16)
        gi_t[...] = flipped(inner)
        put_folded(deo_out, mm(flipped(picked_ref[...].astype(F32)), low_ref[...]))

    mine = step // (pl.num_programs(0) // 2) == core

    @pl.when(mine)
    def _():
        grad_buf[...] = mm_nt(low_ref[...], wo_own[...])

    @pl.when(jnp.logical_not(mine))
    def _():
        grad_buf[...] = mm_nt(low_ref[...], wo_oth[...])

    grad_merged = grad_buf[...] + mm(gi[...], stack_ranks(core, so_own[...], so_oth[...]))
    smooth, slope = gelu_parts(pre_ref[...])
    pre_grad_out[...] = (grad_merged * state_ref[...] * slope).astype(BF16)
    grad_state = grad_merged * smooth
    decay = jnp.exp(-RATE_SCALE * rate_ref[...] * soft_ref[...]) * masks_ref[:, 0:1]
    put_folded(dso_out, mm(gi_t[...], merged_ref[...]))
    for q in range(tile // LANES):
        drive_buf[q] = grad_state[:, q * LANES : (q + 1) * LANES]
        decay_buf[q] = decay[:, q * LANES : (q + 1) * LANES]
    for q in range(tile // LANES):
        lanes = slice(q * LANES, (q + 1) * LANES)
        for s in range(seqs):
            at = pl.ds(s * steps + seg - 1, SEGS, stride=seg)
            held = drive_buf[q, at, :]
            span = jnp.ones_like(held)
            local_out[q, at, :] = held
            reach_out[q, at, :] = span
            for i in range(seg - 2, -1, -1):
                a = decay_buf[q, pl.ds(s * steps + i + 1, SEGS, stride=seg), :]
                at = pl.ds(s * steps + i, SEGS, stride=seg)
                held = a * held + drive_buf[q, at, :]
                span = a * span
                local_out[q, at, :] = held
                reach_out[q, at, :] = span
            a = decay_buf[q, pl.ds(s * steps, SEGS, stride=seg), :]
            held = a * held
            span = a * span
            ends_out[s * SEGS : (s + 1) * SEGS, lanes] = held
            spans_out[s * SEGS : (s + 1) * SEGS, lanes] = span
            total = held[SEGS - 1 : SEGS, :]
            product = span[SEGS - 1 : SEGS, :]
            for g in range(SEGS - 2, -1, -1):
                total = held[g : g + 1, :] + span[g : g + 1, :] * total
                product = span[g : g + 1, :] * product
            summary_out[s : s + 1, lanes] = product
            summary_out[seqs + s : seqs + s + 1, lanes] = total


def branch_back_kernel(
    core_ref, grad_ref, normed_ref, onehot_ref, picked_ref, wb_own, wb_oth, sb_own, sb_oth, eb_own, eb_oth,
    out_ref, dsb_out, deb_out, acc, inner, picked_t,
):
    core = core_ref[0]
    step = pl.program_id(0)
    own, oth = halves(core, out_ref.shape[1])

    @pl.when(step == 0)
    def _():
        acc[...] = jnp.zeros_like(acc)
        inner[...] = jnp.zeros_like(inner)
        picked_t[...] = flipped(picked_ref[...].astype(F32))

    grad = grad_ref[...]
    acc[:, own] += mm_nt(grad, wb_own[...])
    acc[:, oth] += mm_nt(grad, wb_oth[...])
    inner[...] += mm_nt(grad, stack_ranks(core, eb_own[...], eb_oth[...]))
    put_folded(deb_out, mm(picked_t[...], grad))

    @pl.when(step == pl.num_programs(0) - 1)
    def _():
        gi = inner[...] * onehot_ref[...]
        put_folded(dsb_out, mm(flipped(gi), normed_ref[...]))
        out_ref[...] = acc[...] + mm(gi.astype(BF16), stack_ranks(core, sb_own[...], sb_oth[...]))


def gates_back_kernel(
    core_ref, *refs, reach
):
    (local_ref, reach_ref, ends_ref, spans_ref) = refs[:4]
    messages = refs[4 : 4 + reach]
    (
        carry_ref, state_ref, mixed_ref, mixed_late_ref, rate_ref, inflow_ref, masks_ref, onehot_ref, soft_ref, picked_ref,
        bd_own, bd_oth, bi_own, bi_oth, ed_own, ed_oth, ei_own, ei_oth, sd_own, sd_oth, si_own, si_oth,
        grad_out, ded_out, dei_out, dsd_out, dsi_out, head_out,
        flow, partial, inner, gi, gi_t, picked_t,
    ) = refs[4 + reach :]
    core = core_ref[0]
    step = pl.program_id(0)
    lane_tiles = pl.num_programs(0) // 2
    groups = local_ref.shape[0]
    rows, tile = state_ref.shape
    ranks = onehot_ref.shape[1]
    seqs = ends_ref.shape[0] // SEGS
    steps = rows // seqs
    seg = steps // SEGS

    @pl.when(step == 0)
    def _():
        inner[...] = jnp.zeros_like(inner)
        picked_t[...] = flipped(picked_ref[...].astype(F32))

    @pl.when(step < lane_tiles)
    def _():
        start = arrived([m[...] for m in messages], seqs)
        for s in range(seqs):
            carry = start[s : s + 1, :]
            for g in range(SEGS - 1, -1, -1):
                at = s * SEGS + g
                here = slice(at * seg, (at + 1) * seg)
                flow[here, :] = jnp.concatenate([local_ref[q, here, :] for q in range(groups)], axis=1) + (
                    jnp.concatenate([reach_ref[q, here, :] for q in range(groups)], axis=1) * carry
                )
                carry = ends_ref[at : at + 1, :] + spans_ref[at : at + 1, :] * carry
        priors = []
        first = lax.broadcasted_iota(jnp.int32, (steps, tile), 0) == 0
        for s in range(seqs):
            rolled = pltpu.roll(state_ref[s * steps : (s + 1) * steps, :], 1, 0)
            priors.append(jnp.where(first, carry_ref[s : s + 1, :], rolled))
        prior = jnp.concatenate(priors, axis=0)
        backflow = flow[...]
        mixed = mixed_ref[...]
        rate = rate_ref[...]
        inflow = inflow_ref[...]
        keep = masks_ref[:, 0:1]
        soft = soft_ref[...]
        raw = jnp.exp(-RATE_SCALE * rate * soft)
        square = raw * raw
        spread = (1.0 - raw) * (1.0 + raw)
        root_raw = jnp.sqrt(jnp.maximum(spread, ROOT_FLOOR))
        root = keep * root_raw + (1.0 - keep)
        pulled = backflow * inflow
        grad_spread = jnp.where(spread > ROOT_FLOOR, pulled * mixed * keep * 0.5 / root_raw, 0.0)
        grad_log = backflow * prior * raw * keep - 2.0 * square * grad_spread
        grad_rate = (grad_log * (-RATE_SCALE * soft) * rate * (1.0 - rate)).astype(BF16)
        grad_inflow = (backflow * root * mixed * inflow * (1.0 - inflow)).astype(BF16)
        blocks, block = bd_own.shape[0], bd_own.shape[1]
        mine = step // (lane_tiles // 2) == core
        pieces = []
        for b in range(blocks):
            lanes = slice(b * block, (b + 1) * block)
            both = jnp.concatenate(
                [jnp.where(mine, bd_own[b], bd_oth[b]), jnp.where(mine, bi_own[b], bi_oth[b])], axis=1
            )
            pieces.append(mm_nt(jnp.concatenate([grad_rate[:, lanes], grad_inflow[:, lanes]], axis=1), both))
        at = pl.multiple_of(step * tile, 128)
        partial[:, pl.ds(at, tile)] = pulled * root + jnp.concatenate(pieces, axis=1)
        inner[:, :ranks] += mm_nt(grad_rate, stack_ranks(core, ed_own[...], ed_oth[...]))
        inner[:, ranks:] += mm_nt(grad_inflow, stack_ranks(core, ei_own[...], ei_oth[...]))
        put_folded(ded_out, mm(picked_t[:ranks, :], grad_rate))
        put_folded(dei_out, mm(picked_t[ranks:, :], grad_inflow))

    @pl.when(step == lane_tiles - 1)
    def _():
        onehot = onehot_ref[...]
        chosen = inner[...] * jnp.concatenate([onehot, onehot], axis=1)
        gi[...] = chosen.astype(BF16)
        gi_t[...] = flipped(chosen)

    @pl.when(step >= lane_tiles)
    def _():
        at = pl.multiple_of((step - lane_tiles) * tile, 128)
        shrink = jnp.concatenate(
            [stack_ranks(core, sd_own[...], sd_oth[...]), stack_ranks(core, si_own[...], si_oth[...])], axis=0
        )
        grad = partial[:, pl.ds(at, tile)] + mm(gi[...], shrink)
        grad_out[...] = grad
        for s in range(seqs):
            head_out[s * HALO : (s + 1) * HALO, :] = grad[s * steps : s * steps + HALO, :]
        both = mm(gi_t[...], mixed_late_ref[...].astype(BF16))
        put_folded(dsd_out, both[:ranks, :])
        put_folded(dsi_out, both[ranks:, :])


def recur_back_kernel(
    core_ref, grad_ref, head_ref, masks_ref, taps_ref, normed_ref, onehot_ref, picked_ref, branch_ref, residual_ref,
    tokens_ref, gain_ref, wr_own, wr_oth, sr_own, sr_oth, er_own, er_oth,
    out_ref, dsr_out, der_out, acc, inner, picked_t, filt, low,
):
    core = core_ref[0]
    step = pl.program_id(0)
    own, oth = halves(core, out_ref.shape[1])
    rows, tile = grad_ref.shape
    seqs = head_ref.shape[0] // HALO
    steps = rows // seqs
    lags = taps_ref.shape[0] - 1

    @pl.when(step == 0)
    def _():
        acc[...] = branch_ref[...]
        inner[...] = jnp.zeros_like(inner)
        picked_t[...] = flipped(picked_ref[...].astype(F32))

    for s in range(seqs):
        filt[s, :steps, :] = grad_ref[s * steps : (s + 1) * steps, :]
        filt[s, steps:, :] = head_ref[s * HALO : (s + 1) * HALO, :]
    for s in range(seqs):
        here = slice(s * steps, (s + 1) * steps)
        total = taps_ref[0:1, :] * filt[s, :steps, :]
        for lag in range(1, lags + 1):
            later = filt[s, lag : lag + steps, :]
            total = total + taps_ref[lag : lag + 1, :] * later * masks_ref[here, lags + lag - 1 : lags + lag]
        low[here, :] = total.astype(BF16)
    grad = low[...]
    acc[:, own] += mm_nt(grad, wr_own[...])
    acc[:, oth] += mm_nt(grad, wr_oth[...])
    inner[...] += mm_nt(grad, stack_ranks(core, er_own[...], er_oth[...]))
    put_folded(der_out, mm(picked_t[...], grad))

    @pl.when(step == pl.num_programs(0) - 1)
    def _():
        gi = inner[...] * onehot_ref[...]
        put_folded(dsr_out, mm(flipped(gi), normed_ref[...]))
        weighted = (acc[...] + mm(gi.astype(BF16), stack_ranks(core, sr_own[...], sr_oth[...]))) * gain_ref[...]
        values = tokens_ref[...].astype(F32)
        scale = lax.rsqrt(jnp.mean(values * values, axis=1, keepdims=True) + EPSILON)
        out_ref[...] = (
            residual_ref[...]
            + scale * weighted
            - values * (scale * scale * scale * jnp.mean(weighted * values, axis=1, keepdims=True))
        )


ORDER = (
    ("eg", 0), ("eu", 1), ("sdn", 0), ("sg", 1), ("su", 1), ("edn", 1), ("eo", 0), ("so", 1), ("eb", 0), ("sb", 1),
    ("edec", 0), ("einf", 1), ("sdec", 0), ("sinf", 1), ("er", 0), ("sr", 1),
)


def reduce_kernel(*refs, offsets, sizes):
    count = len(sizes)
    ins = refs[:count]
    out = refs[count]
    (own, core_in, kept1, send1, recv1, kept2, send2, recv2, send3, recv3,
     local_sem, core_s, core_r, s1_s, s1_r, s2_s, s2_r, s3_s, s3_r) = refs[count + 1 :]
    mesh_ids = pl.DeviceIdType.MESH
    core = lax.axis_index("wshard")
    chip = lax.axis_index("seq")
    x, y, z = chip % 2, (chip // 2) % 2, chip // 4
    x_peer = chip + 1 - 2 * x
    y_peer = chip + 2 - 4 * y
    z_peers = [((z + d) % 4) * 4 + chip % 4 for d in (1, 2, 3)]

    barrier = pltpu.get_barrier_semaphore()
    pl.semaphore_signal(barrier, inc=1, device_id={"wshard": 1 - core}, device_id_type=mesh_ids)
    for peer in [x_peer, y_peer] + z_peers:
        pl.semaphore_signal(barrier, inc=1, device_id={"seq": peer}, device_id_type=mesh_ids)
    pl.semaphore_wait(barrier, 6)

    cols = [pl.ds(o, n) for o, n in zip(offsets, sizes)]
    locals_, cores = [], []
    for a in range(count):
        copy = pltpu.make_async_remote_copy(
            ins[a].at[1 - core], core_in.at[:, :, cols[a]], core_s.at[a], core_r.at[a],
            device_id={"wshard": 1 - core}, device_id_type=mesh_ids,
        )
        copy.start()
        cores.append(copy)
        copy = pltpu.make_async_copy(ins[a].at[core], own.at[:, :, cols[a]], local_sem.at[a])
        copy.start()
        locals_.append(copy)

    firsts, seconds, thirds = [], [], []
    for a in range(count):
        locals_[a].wait()
        cores[a].wait_recv()
        along_x = ORDER[a][1] == 0
        for p in range(4):
            for o in range(2):
                keep = p * 4 + (o * 2 + x if along_x else y * 2 + o)
                give = p * 4 + (o * 2 + 1 - x if along_x else (1 - y) * 2 + o)
                at = p * 2 + o
                kept1[at, :, cols[a]] = own[keep, :, cols[a]].astype(F32) + core_in[keep, :, cols[a]].astype(F32)
                send1[at, :, cols[a]] = (
                    own[give, :, cols[a]].astype(F32) + core_in[give, :, cols[a]].astype(F32)
                ).astype(BF16)
        copy = pltpu.make_async_remote_copy(
            send1.at[:, :, cols[a]], recv1.at[:, :, cols[a]], s1_s.at[a], s1_r.at[a],
            device_id={"seq": x_peer if along_x else y_peer}, device_id_type=mesh_ids,
        )
        copy.start()
        firsts.append(copy)
    for a in range(count):
        firsts[a].wait_recv()
        along_x = ORDER[a][1] == 0
        mine = y if along_x else x
        for p in range(4):
            keep, give = p * 2 + mine, p * 2 + 1 - mine
            kept2[p, :, cols[a]] = kept1[keep, :, cols[a]] + recv1[keep, :, cols[a]].astype(F32)
            send2[p, :, cols[a]] = (kept1[give, :, cols[a]] + recv1[give, :, cols[a]].astype(F32)).astype(BF16)
        copy = pltpu.make_async_remote_copy(
            send2.at[:, :, cols[a]], recv2.at[:, :, cols[a]], s2_s.at[a], s2_r.at[a],
            device_id={"seq": y_peer if along_x else x_peer}, device_id_type=mesh_ids,
        )
        copy.start()
        seconds.append(copy)
    for a in range(count):
        seconds[a].wait_recv()
        out[:, cols[a]] = kept2[z, :, cols[a]] + recv2[z, :, cols[a]].astype(F32)
        for d in (1, 2, 3):
            to = (z + d) % 4
            send3[d - 1, :, cols[a]] = (kept2[to, :, cols[a]] + recv2[to, :, cols[a]].astype(F32)).astype(BF16)
        sent = []
        for d in (1, 2, 3):
            copy = pltpu.make_async_remote_copy(
                send3.at[d - 1, :, cols[a]], recv3.at[d - 1, :, cols[a]], s3_s.at[a, d - 1], s3_r.at[a, d - 1],
                device_id={"seq": z_peers[d - 1]}, device_id_type=mesh_ids,
            )
            copy.start()
            sent.append(copy)
        thirds.append(sent)
    for a in range(count):
        for copy in thirds[a]:
            copy.wait_recv()
        out[:, cols[a]] += (
            recv3[0, :, cols[a]].astype(F32) + recv3[1, :, cols[a]].astype(F32) + recv3[2, :, cols[a]].astype(F32)
        )
    for a in range(count):
        cores[a].wait_send()
        firsts[a].wait_send()
        seconds[a].wait_send()
        for copy in thirds[a]:
            copy.wait_send()


def unfold_kernel(in_ref, *outs, offsets, sizes, runs, split):
    for out, offset, size, run, two in zip(outs, offsets, sizes, runs, split):
        pieces = unfold(in_ref[:, offset : offset + size], run)
        if two:
            pieces = [p for i, p in enumerate(pieces) if i % 4 < 2] + [p for i, p in enumerate(pieces) if i % 4 >= 2]
        out[...] = jnp.concatenate(pieces, axis=1)


def sum_factors(grads, runs, feed):
    peers = lax.axis_size("seq")
    split = {k: k in ("eg", "eu", "sdn") for k in grads}
    if peers != 16:
        summed = {}
        for k, g in grads.items():
            quarter = runs[k] // 4
            g = g.astype(F32).reshape(2, g.shape[1], 4, 4, g.shape[3] // quarter, quarter)
            g = g[:, :, jnp.array([0, 2, 1, 3])]
            if split[k]:
                g = g.reshape(g.shape[:2] + (2, 2) + g.shape[3:]).transpose(1, 0, 4, 2, 5, 3, 6)
            else:
                g = g.transpose(1, 0, 3, 4, 2, 5)
            g = g.reshape(g.shape[0] * 8, -1)
            summed[k] = lax.psum_scatter(g, ("seq", "wshard"), scatter_dimension=0, tiled=True)
        return summed
    names = [k for k, _ in ORDER]
    sizes = [grads[k].shape[3] for k in names]
    offsets = [sum(sizes[:i]) for i in range(len(sizes))]
    total, count = sum(sizes), len(sizes)
    dma = pltpu.SemaphoreType.DMA
    folded = pl.pallas_call(
        functools.partial(reduce_kernel, offsets=offsets, sizes=sizes),
        out_shape=jax.ShapeDtypeStruct((16, total), F32),
        in_specs=[pl.BlockSpec(memory_space=pl.ANY)] * count,
        out_specs=pl.BlockSpec(memory_space=pltpu.VMEM),
        scratch_shapes=[
            pltpu.VMEM((16, 16, total), BF16), pltpu.VMEM((16, 16, total), BF16),
            pltpu.VMEM((8, 16, total), F32), pltpu.VMEM((8, 16, total), BF16), pltpu.VMEM((8, 16, total), BF16),
            pltpu.VMEM((4, 16, total), F32), pltpu.VMEM((4, 16, total), BF16), pltpu.VMEM((4, 16, total), BF16),
            pltpu.VMEM((3, 16, total), BF16), pltpu.VMEM((3, 16, total), BF16),
            dma((count,)), dma((count,)), dma((count,)), dma((count,)), dma((count,)), dma((count,)), dma((count,)),
            dma((count, 3)), dma((count, 3)),
        ],
        name="reduce_factors",
        compiler_params=pltpu.CompilerParams(collective_id=0, has_side_effects=True, vmem_limit_bytes=60 * 1024 * 1024),
    )(*[grads[k] for k in names])
    rows = 4
    outs = pl.pallas_call(
        functools.partial(
            unfold_kernel, offsets=offsets, sizes=sizes, runs=[runs[k] for k in names], split=[split[k] for k in names]
        ),
        out_shape=[jax.ShapeDtypeStruct((rows, n * 4), F32) for n in sizes],
        name="unfold_factors",
    )(folded)
    return dict(zip(names, outs))


def whole_spec(shape):
    zeros = (0,) * len(shape)
    return pl.BlockSpec(shape, lambda j, c: zeros)


def call(kernel, name, grid, core, ins, outs, scratch, flops, nbytes):
    in_specs, arrays = [], []
    for item in ins:
        if isinstance(item, tuple):
            arrays.append(item[0])
            in_specs.append(pl.BlockSpec(item[1], item[2]))
        else:
            arrays.append(item)
            in_specs.append(whole_spec(item.shape))
    out_specs, shapes = [], []
    for item in outs:
        shapes.append(jax.ShapeDtypeStruct(item[0], item[1]))
        out_specs.append(pl.BlockSpec(item[2], item[3]) if len(item) == 4 else whole_spec(item[0]))
    return pl.pallas_call(
        kernel,
        grid_spec=pltpu.PrefetchScalarGridSpec(
            num_scalar_prefetch=1, grid=(grid,), in_specs=in_specs, out_specs=out_specs, scratch_shapes=scratch
        ),
        out_shape=shapes,
        name=name,
        compiler_params=pltpu.CompilerParams(
            dimension_semantics=("arbitrary",), vmem_limit_bytes=60 * 1024 * 1024
        ),
        cost_estimate=pl.CostEstimate(flops=flops, bytes_accessed=nbytes, transcendentals=0),
    )(core, *arrays)


def shifted(shard, by):
    peers = lax.axis_size("seq")
    pairs = [(i, i + by) for i in range(peers) if 0 <= i + by < peers]
    return lax.ppermute(shard, "seq", pairs)


def local(
    tokens, segment_ids, document_adapter, out_cotangent, mixer_gain, feed_gain, filter_taps, decay_param, *weights
):
    core = lax.axis_index("wshard").astype(jnp.int32).reshape(1)
    swap = lambda item: lax.ppermute(item, "wshard", [(0, 1), (1, 0)])
    soon = (1, 2, 3, 8, 10, 11, 12, 13, 14, 15)
    early_other = {i: swap(weights[i]) for i in soon}
    rest = [i for i in range(len(weights)) if i not in soon]
    held_back = lax.optimization_barrier(tuple(weights[i] for i in rest) + tuple(early_other.values()))
    late_other = {i: swap(w) for i, w in zip(rest, held_back)}
    other = [early_other[i] if i in early_other else late_other[i] for i in range(len(weights))]
    (wb, wr, bd, bi, wo, wg, wu, wd) = [(a, b) for a, b in zip(weights[:8], other[:8])]
    (sb, eb, sr, er, sdec, edec, sinf, einf, so, eo, sg, eg, su, eu, sdn, edn) = [
        (a, b) for a, b in zip(weights[8:], other[8:])
    ]
    seqs, steps, width = tokens.shape
    rows = seqs * steps
    lru = filter_taps.shape[1]
    lags = filter_taps.shape[0] - 1
    ranks = 2 * sb[0].shape[0]
    feed = wg[0].shape[1]
    peers = lax.axis_size("seq")
    reach = peers // 4

    before = shifted(segment_ids, 1)
    after = shifted(segment_ids, -1)
    halo = shifted(tokens[:, steps - HALO :, :], 1).reshape(seqs * HALO, width)
    position = lax.axis_index("seq") * steps + jnp.arange(steps, dtype=jnp.int32)
    wide = jnp.concatenate([before[:, steps - HALO :], segment_ids, after[:, :HALO]], axis=1)
    columns = []
    for lag in range(1, lags + 1):
        prior = wide[:, HALO - lag : HALO - lag + steps]
        columns.append((prior == segment_ids) & (position >= lag)[None, :])
    for lag in range(1, lags + 1):
        later = wide[:, HALO + lag : HALO + lag + steps]
        columns.append((later == segment_ids) & (position + lag < peers * steps)[None, :])
    columns += [columns[0]] * (8 - len(columns))
    masks = jnp.stack([c.reshape(rows) for c in columns], axis=1).astype(F32)
    documents = jnp.arange(document_adapter.shape[1], dtype=jnp.int32)

    def owners_of(ids):
        owner = jnp.sum(
            jnp.where(ids[:, :, None] == documents[None, None, :], document_adapter[:, None, :], 0), axis=2
        )
        return owner.reshape(-1)

    owner = jnp.concatenate([owners_of(segment_ids), owners_of(before[:, steps - HALO :])])
    onehot = (owner[:, None] == (jnp.arange(ranks, dtype=jnp.int32) // RANK)[None, :]).astype(F32)
    onehot_own = onehot[:rows]
    soft = jax.nn.softplus(-decay_param)[None, :]
    gain_first = mixer_gain[None, :]
    gain_second = feed_gain[None, :]
    tokens2 = tokens.reshape(rows, width)
    cot = out_cotangent.reshape(rows, width)

    tile = TILE
    count = lru // tile
    half = width // 2
    blocks = tile // bd[0].shape[1]
    block = bd[0].shape[1]
    early = lambda j: jnp.minimum(j, count - 1)
    late = lambda j: jnp.maximum(j - count, 0)
    flat = lambda r, at: ((r, tile), lambda j, c: (0, at(j)))

    def tiled(array, r, at):
        block_shape, index = flat(r, at)
        return (array, block_shape, index)

    def tiled_out(r, dtype, at, total=None):
        block_shape, index = flat(r, at)
        return ((r, total or lru), dtype, block_shape, index)

    lane_groups = tile // LANES

    def grouped(array, index):
        return (array, (lane_groups, rows, LANES), index)

    def grouped_out(at):
        return ((lru // LANES, rows, LANES), F32, (lane_groups, rows, LANES), lambda j, c: (at(j), 0, 0))

    def both(pair, r, at):
        return [tiled(pair[0], r, at), tiled(pair[1], r, at)]

    def gate_blocks(pair, at):
        index = lambda j, c: (at(j) % (count // 2), 0, 0)
        return [(pair[0], (blocks, block, block), index), (pair[1], (blocks, block, block), index)]

    half_ranks = ranks // 2
    ident = lambda j: j
    groups = seqs * SEGS
    with jax.named_scope("mixer_forward"):
        (normed, picked_br, picked_di, mixed, rate, inflow, held, span, ends, spans, summary) = call(
            mixer_kernel, "mixer_forward", 2 * count, core,
            [tokens2, halo, onehot, masks, gain_first, tiled(filter_taps, lags + 1, early), tiled(soft, 1, late)]
            + both(wr, half, early) + list(sb) + list(sr) + both(er, half_ranks, early)
            + both(sdec, half_ranks, early) + both(sinf, half_ranks, early)
            + gate_blocks(bd, late) + gate_blocks(bi, late)
            + both(edec, half_ranks, late) + both(einf, half_ranks, late),
            [((rows, width), BF16), ((rows, 2 * ranks), BF16), ((rows, 2 * ranks), BF16),
             tiled_out(rows, F32, early), tiled_out(rows, F32, late), tiled_out(rows, F32, late),
             grouped_out(late), grouped_out(late),
             tiled_out(groups, F32, late), tiled_out(groups, F32, late), tiled_out(2 * seqs, F32, late)],
            [pltpu.VMEM((rows + seqs * HALO, width), BF16), pltpu.VMEM((rows + seqs * HALO, ranks), BF16),
             pltpu.VMEM((rows, 2 * ranks), F32), pltpu.VMEM((rows, 2 * ranks), BF16),
             pltpu.VMEM((rows, lru), F32), pltpu.VMEM((seqs, steps + HALO, tile), F32),
             pltpu.VMEM((lane_groups, rows, LANES), F32), pltpu.VMEM((lane_groups, rows, LANES), F32)],
            int(6e9), int(30e6),
        )
    messages = [shifted(summary, d) for d in range(1, reach + 1)]
    with jax.named_scope("branch_forward"):
        (branch_pre,) = call(
            branch_kernel, "branch_forward", count, core,
            [normed, (picked_br, (rows, ranks), lambda j, c: (0, 0))] + both(wb, half, ident) + both(eb, half_ranks, ident),
            [tiled_out(rows, F32, ident)], [], int(4e9), int(15e6),
        )

    def placed(j, c):
        return jnp.where(j < count // 2, c[0] * (count // 2) + j, (1 - c[0]) * (count // 2) + j - count // 2)

    def placed_in(array, r):
        return (array, (r, tile), lambda j, c: (0, placed(j, c)))

    def placed_out(r, dtype):
        return ((r, lru), dtype, (r, tile), lambda j, c: (0, placed(j, c)))

    with jax.named_scope("output_forward"):
        state, merged, carry, residual, second, picked_o = call(
            functools.partial(output_kernel, reach=reach), "output_forward", count, core,
            [grouped(held, lambda j, c: (placed(j, c), 0, 0)), grouped(span, lambda j, c: (placed(j, c), 0, 0)), placed_in(ends, groups), placed_in(spans, groups)]
            + [placed_in(m, 2 * seqs) for m in messages]
            + [placed_in(branch_pre, rows), tokens2, onehot_own, gain_second,
               (wo[0], (tile, width), lambda j, c: (jnp.minimum(j, count // 2 - 1), 0)),
               (wo[1], (tile, width), lambda j, c: (jnp.maximum(j - count // 2, 0), 0)),
               placed_in(so[0], half_ranks), placed_in(so[1], half_ranks)] + list(eo),
            [placed_out(rows, F32), placed_out(rows, BF16), placed_out(2 * seqs, F32),
             ((rows, width), F32), ((rows, width), BF16), ((rows, ranks), BF16)],
            [pltpu.VMEM((rows, width), F32), pltpu.VMEM((rows, ranks), F32)],
            int(4e9), int(30e6),
        )

    part = 256
    pieces = feed // (2 * part)

    def feed_cols(pair_item, r):
        return [
            (pair_item, (r, part), lambda j, c: (0, c[0] * pieces + j)),
            (pair_item, (r, part), lambda j, c: (0, (1 - c[0]) * pieces + j)),
        ]

    def feed_pair(pair, r):
        return feed_cols(pair[0], r) + feed_cols(pair[1], r)

    chips = ranks // 8
    grad_cols = ((2, chips, 16, feed // 4), BF16, (2, chips, 16, part // 2), lambda j, c: (0, 0, 0, j))
    grad_whole = ((2, chips, 16, width // 4), BF16)

    def grad_tile(at):
        return ((2, chips, 16, lru // 4), BF16, (2, chips, 16, tile // 4), lambda j, c: (0, 0, 0, at(j)))

    with jax.named_scope("feed_forward_both_ways"):
        result, grad_residual, grad_low, deg, deu, dsdn, dsg, dsu, dedn = call(
            feed_kernel, "feed_both_ways", pieces, core,
            [second, cot, residual, onehot_own, gain_second] + feed_pair(wg, half) + feed_pair(wu, half)
            + [(wd[0], (part, width), lambda j, c: (j, 0)), (wd[1], (part, width), lambda j, c: (j, 0))]
            + list(sg) + list(su) + feed_pair(eg, half_ranks) + feed_pair(eu, half_ranks)
            + feed_pair(sdn, half_ranks) + list(edn),
            [((rows, width), BF16), ((rows, width), F32), ((rows, width), BF16),
             grad_cols, grad_cols, grad_cols, grad_whole, grad_whole, grad_whole],
            [pltpu.VMEM((rows, 2 * ranks), BF16), pltpu.VMEM((2 * ranks, rows), BF16),
             pltpu.VMEM((rows, ranks), BF16), pltpu.VMEM((ranks, rows), BF16),
             pltpu.VMEM((rows, width), F32), pltpu.VMEM((rows, ranks), F32), pltpu.VMEM((rows, width), F32),
             pltpu.VMEM((rows, 2 * ranks), F32)],
            int(50e9), int(60e6),
        )

    own_rows = lambda pair: [
        (pair[0], (tile, width), lambda j, c: (j % (count // 2), 0)),
        (pair[1], (tile, width), lambda j, c: (j % (count // 2), 0)),
    ]
    with jax.named_scope("output_backward"):
        pre_grad, bheld, bspan, bends, bspans, bsummary, dso, deo = call(
            output_back_kernel, "output_backward", count, core,
            [grad_low, onehot_own, masks, tiled(soft, 1, ident), picked_o, tiled(branch_pre, rows, ident),
             tiled(state, rows, ident), tiled(merged, rows, ident), tiled(rate, rows, ident)]
            + own_rows(wo) + both(so, half_ranks, ident) + list(eo),
            [tiled_out(rows, BF16, ident), grouped_out(ident), grouped_out(ident),
             tiled_out(groups, F32, ident), tiled_out(groups, F32, ident), tiled_out(2 * seqs, F32, ident),
             grad_tile(ident), grad_whole],
            [pltpu.VMEM((rows, ranks), BF16), pltpu.VMEM((ranks, rows), BF16),
             pltpu.VMEM((lane_groups, rows, LANES), F32), pltpu.VMEM((lane_groups, rows, LANES), F32),
             pltpu.VMEM((rows, tile), F32)],
            int(5e9), int(30e6),
        )
    back_messages = [shifted(bsummary, -d) for d in range(1, reach + 1)]
    with jax.named_scope("branch_backward"):
        grad_branch, dsb, deb = call(
            branch_back_kernel, "branch_backward", count, core,
            [tiled(pre_grad, rows, ident), normed, onehot_own, (picked_br, (rows, ranks), lambda j, c: (0, 0))]
            + both(wb, half, ident) + list(sb) + both(eb, half_ranks, ident),
            [((rows, width), F32), grad_whole, grad_tile(ident)],
            [pltpu.VMEM((rows, width), F32), pltpu.VMEM((rows, ranks), F32), pltpu.VMEM((ranks, rows), BF16)],
            int(5e9), int(15e6),
        )
    with jax.named_scope("gates_backward"):
        grad_mixed, dedec, deinf, dsdec, dsinf, heads = call(
            functools.partial(gates_back_kernel, reach=reach), "gates_backward", 2 * count, core,
            [grouped(bheld, lambda j, c: (early(j), 0, 0)), grouped(bspan, lambda j, c: (early(j), 0, 0)), tiled(bends, groups, early), tiled(bspans, groups, early)]
            + [tiled(m, 2 * seqs, early) for m in back_messages]
            + [tiled(carry, 2 * seqs, early), tiled(state, rows, early), tiled(mixed, rows, early),
               tiled(mixed, rows, late), tiled(rate, rows, early), tiled(inflow, rows, early),
               masks, onehot_own, tiled(soft, 1, early), picked_di]
            + gate_blocks(bd, early) + gate_blocks(bi, early)
            + both(edec, half_ranks, early) + both(einf, half_ranks, early)
            + both(sdec, half_ranks, late) + both(sinf, half_ranks, late),
            [tiled_out(rows, F32, late), grad_tile(early), grad_tile(early), grad_tile(late), grad_tile(late), tiled_out(seqs * HALO, F32, late)],
            [pltpu.VMEM((rows, tile), F32), pltpu.VMEM((rows, lru), F32), pltpu.VMEM((rows, 2 * ranks), F32),
             pltpu.VMEM((rows, 2 * ranks), BF16), pltpu.VMEM((2 * ranks, rows), BF16), pltpu.VMEM((2 * ranks, rows), BF16)],
            int(4e9), int(40e6),
        )
    next_heads = shifted(heads, -1)
    with jax.named_scope("recur_backward"):
        grad_tokens, dsr, der = call(
            recur_back_kernel, "recur_backward", count, core,
            [tiled(grad_mixed, rows, ident), tiled(next_heads, seqs * HALO, ident), masks,
             tiled(filter_taps, lags + 1, ident), normed, onehot_own,
             (picked_br, (rows, ranks), lambda j, c: (0, 1)), grad_branch, grad_residual, tokens2, gain_first]
            + both(wr, half, ident) + list(sr) + both(er, half_ranks, ident),
            [((rows, width), F32), grad_whole, grad_tile(ident)],
            [pltpu.VMEM((rows, width), F32), pltpu.VMEM((rows, ranks), F32), pltpu.VMEM((ranks, rows), BF16),
             pltpu.VMEM((seqs, steps + HALO, tile), F32), pltpu.VMEM((rows, tile), BF16)],
            int(5e9), int(30e6),
        )

    grads = dict(
        sb=dsb, eb=deb, sr=dsr, er=der, sdec=dsdec, edec=dedec, sinf=dsinf, einf=deinf, so=dso, eo=deo,
        sg=dsg, eg=deg, su=dsu, eu=deu, sdn=dsdn, edn=dedn,
    )
    runs = {k: width if k in ("sb", "sr", "sg", "su", "eo", "edn") else (2 * part if k in ("eg", "eu", "sdn") else tile) for k in grads}
    with jax.named_scope("factor_gradients"):
        summed = sum_factors(grads, runs, feed)
    return (result.reshape(seqs, steps, width), grad_tokens.reshape(seqs, steps, width)) + tuple(
        summed[k] for k in grads
    )


def solution(mesh):
    split = P("wshard", None)
    in_specs = (
        (P("wshard", "seq", None), P("wshard", "seq"), split, P("wshard", "seq", None))
        + (P(),) * 4
        + (split, split, P("wshard", None, None), P("wshard", None, None))
        + (split,) * 20
    )
    out_specs = (P("wshard", "seq", None),) * 2 + (P(("seq", "wshard"), None),) * 16
    return jax.shard_map(local, mesh=mesh, in_specs=in_specs, out_specs=out_specs, check_vma=False)
```

```python
import functools

import jax
import jax.numpy as jnp
from jax import lax
from jax.experimental import pallas as pl
from jax.experimental.pallas import tpu as pltpu
from jax.sharding import PartitionSpec as P

RANK = 16
EPSILON = 1e-06
RATE_SCALE = 8.0
ROOT_FLOOR = 0.001
GELU_A = 0.7978845608028654
GELU_B = 0.044715

HALO = 8
SEGS = 8
TILE = 512
LANES = 128
F32 = jnp.float32
BF16 = jnp.bfloat16


def mm(left, right):
    return lax.dot_general(left, right, (((1,), (0,)), ((), ())), preferred_element_type=F32)


def mm_nt(left, right):
    return lax.dot_general(left, right, (((1,), (1,)), ((), ())), preferred_element_type=F32)


def gelu_parts(x):
    square = x * x
    t = jnp.tanh(GELU_A * x * (1.0 + GELU_B * square))
    half = 0.5 * (1.0 + t)
    slope = half + 0.5 * x * (1.0 - t * t) * (GELU_A * (1.0 + 3.0 * GELU_B * square))
    return x * half, slope


def gelu(x):
    t = jnp.tanh(GELU_A * x * (1.0 + GELU_B * x * x))
    return 0.5 * x * (1.0 + t)


def stack_ranks(core, own, other):
    first = core == 0
    return jnp.concatenate([jnp.where(first, own, other), jnp.where(first, other, own)], axis=0)


def flipped(values):
    return values.T.astype(BF16)


def fold(grad):
    ranks, wide = grad.shape
    half = wide // 2
    left, right = grad[:, :half], grad[:, half:]
    upper = lax.broadcasted_iota(jnp.int32, (ranks, half), 0) % 8 < 4
    blocks = []
    for pair in (
        jnp.where(upper, left, pltpu.roll(right, 4, 0)),
        jnp.where(upper, pltpu.roll(left, ranks - 4, 0), right),
    ):
        eights = pair.reshape(ranks // 8, 8, half)
        blocks.append(
            jnp.concatenate([eights[:, :, : half // 2], eights[:, :, half // 2 :]], axis=1).astype(BF16)
        )
    return blocks


def put_folded(out, grad):
    first, second = fold(grad)
    out[0] = first
    out[1] = second


def unfold(rows4, wide):
    quarter = wide // 4
    pieces = []
    for at in range(0, rows4.shape[1], quarter):
        here = rows4[:, at : at + quarter]
        pieces += [here[0:4], here[8:12], here[4:8], here[12:16]]
    return pieces


def halves(core, width):
    step = width // 2
    return (
        pl.ds(pl.multiple_of(core * step, 128), step),
        pl.ds(pl.multiple_of((1 - core) * step, 128), step),
    )


def greet_core():
    barrier = pltpu.get_barrier_semaphore()
    pl.semaphore_signal(
        barrier, inc=1, device_id={"wshard": 1 - lax.axis_index("wshard")}, device_id_type=pl.DeviceIdType.MESH
    )
    pl.semaphore_wait(barrier, 1)


def to_core(sources, targets, send_sem, recv_sem):
    return [
        pltpu.make_async_remote_copy(
            src, dst, send_sem.at[i], recv_sem.at[i],
            device_id={"wshard": 1 - lax.axis_index("wshard")}, device_id_type=pl.DeviceIdType.MESH,
        )
        for i, (src, dst) in enumerate(zip(sources, targets))
    ]


def mixer_kernel(
    tokens_ref, halo_ref, onehot_ref, masks_ref, gain_ref, taps_ref, soft_ref,
    wr_own, wr_oth, sb_own, sb_oth, sr_own, sr_oth, er_own, er_oth,
    sd_own, sd_oth, si_own, si_oth, bd_own, bd_oth, bi_own, bi_oth, ed_own, ed_oth, ei_own, ei_oth,
    *refs, carried,
):
    sources, refs = refs[:carried], refs[carried:]
    (normed_out, picked_br_out, picked_di_out, mixed_out, rate_out, inflow_out, local_out, reach_out,
     ends_out, spans_out, summary_out), refs = refs[:11], refs[11:]
    targets, refs = refs[:carried], refs[carried:]
    (normed, picked_r, inner_gate, picked_gate, mixed_all, filt, decay_buf, drive_buf, send_sem, recv_sem) = refs
    core = lax.axis_index("wshard")
    step = pl.program_id(0)

    @pl.when(step == 0)
    def _():
        greet_core()
        for copy in to_core(sources, targets, send_sem, recv_sem):
            copy.start()

    rows, width = tokens_ref.shape
    ranks = onehot_ref.shape[1]
    seqs = halo_ref.shape[0] // HALO
    steps = rows // seqs
    lane_tiles = pl.num_programs(0) // 2
    tile = mixed_out.shape[1]

    @pl.when(step == 0)
    def _():
        gain = gain_ref[...]
        for src, at, count in ((tokens_ref, 0, rows), (halo_ref, rows, seqs * HALO)):
            values = src[...].astype(F32)
            scale = lax.rsqrt(jnp.mean(values * values, axis=1, keepdims=True) + EPSILON)
            normed[at : at + count, :] = (values * scale * gain).astype(BF16)
        normed_out[...] = normed[:rows, :]
        shrink = jnp.concatenate(
            [stack_ranks(core, sb_own[...], sb_oth[...]), stack_ranks(core, sr_own[...], sr_oth[...])], axis=0
        )
        inner = mm_nt(normed[...], shrink)
        onehot = onehot_ref[...]
        picked = (inner * jnp.concatenate([onehot, onehot], axis=1)).astype(BF16)
        picked_r[...] = picked[:, ranks:]
        picked_br_out[...] = picked[:rows, :]
        inner_gate[...] = jnp.zeros_like(inner_gate)

    @pl.when(step < lane_tiles)
    def _():
        own, oth = halves(core, width)
        recur = (
            mm(normed[:, own], wr_own[...])
            + mm(normed[:, oth], wr_oth[...])
            + mm(picked_r[...], stack_ranks(core, er_own[...], er_oth[...]))
        )
        at = pl.multiple_of(step * tile, 128)
        for s in range(seqs):
            filt[s, :HALO, :] = recur[rows + s * HALO : rows + (s + 1) * HALO, :]
            filt[s, HALO:, :] = recur[s * steps : (s + 1) * steps, :]
        for s in range(seqs):
            here = slice(s * steps, (s + 1) * steps)
            total = taps_ref[0:1, :] * filt[s, HALO:, :]
            for lag in range(1, taps_ref.shape[0]):
                earlier = filt[s, HALO - lag : HALO - lag + steps, :]
                total = total + taps_ref[lag : lag + 1, :] * earlier * masks_ref[here, lag - 1 : lag]
            mixed_out[here, :] = total
            mixed_all[here, pl.ds(at, tile)] = total
        low = mixed_out[...].astype(BF16)
        shrink = jnp.concatenate(
            [stack_ranks(core, sd_own[...], sd_oth[...]), stack_ranks(core, si_own[...], si_oth[...])], axis=0
        )
        inner_gate[...] += mm_nt(low, shrink)

    @pl.when(step == lane_tiles - 1)
    def _():
        onehot = onehot_ref[:rows, :]
        picked = (inner_gate[...] * jnp.concatenate([onehot, onehot], axis=1)).astype(BF16)
        picked_gate[...] = picked
        picked_di_out[...] = picked

    @pl.when(step >= lane_tiles)
    def _():
        at = pl.multiple_of((step - lane_tiles) * tile, 128)
        mixed = mixed_all[:, pl.ds(at, tile)]
        low = mixed.astype(BF16)
        blocks, block = bd_own.shape[0], bd_own.shape[1]
        mine = (step - lane_tiles) // (lane_tiles // 2) == core
        rates, inflows = [], []
        for b in range(blocks):
            both = jnp.concatenate(
                [jnp.where(mine, bd_own[b], bd_oth[b]), jnp.where(mine, bi_own[b], bi_oth[b])], axis=1
            )
            pair = mm(low[:, b * block : (b + 1) * block], both)
            rates.append(pair[:, :block])
            inflows.append(pair[:, block:])
        rate_pre = jnp.concatenate(rates, axis=1) + mm(
            picked_gate[:, :ranks], stack_ranks(core, ed_own[...], ed_oth[...])
        )
        inflow_pre = jnp.concatenate(inflows, axis=1) + mm(
            picked_gate[:, ranks:], stack_ranks(core, ei_own[...], ei_oth[...])
        )
        rate = jax.nn.sigmoid(rate_pre)
        inflow = jax.nn.sigmoid(inflow_pre)
        rate_out[...] = rate
        inflow_out[...] = inflow
        keep = masks_ref[:, 0:1]
        raw = jnp.exp(-RATE_SCALE * rate * soft_ref[...])
        root_raw = jnp.sqrt(jnp.maximum((1.0 - raw) * (1.0 + raw), ROOT_FLOOR))
        root = keep * root_raw + (1.0 - keep)
        decay = raw * keep
        drive = root * inflow * mixed
        for q in range(tile // LANES):
            decay_buf[q] = decay[:, q * LANES : (q + 1) * LANES]
            drive_buf[q] = drive[:, q * LANES : (q + 1) * LANES]
        seg = steps // SEGS
        for q in range(tile // LANES):
            lanes = slice(q * LANES, (q + 1) * LANES)
            for s in range(seqs):
                at = pl.ds(s * steps, SEGS, stride=seg)
                held, span = drive_buf[q, at, :], decay_buf[q, at, :]
                local_out[q, at, :] = held
                reach_out[q, at, :] = span
                for i in range(1, seg):
                    at = pl.ds(s * steps + i, SEGS, stride=seg)
                    a = decay_buf[q, at, :]
                    held = a * held + drive_buf[q, at, :]
                    span = a * span
                    local_out[q, at, :] = held
                    reach_out[q, at, :] = span
                ends_out[s * SEGS : (s + 1) * SEGS, lanes] = held
                spans_out[s * SEGS : (s + 1) * SEGS, lanes] = span
                total = held[0:1, :]
                product = span[0:1, :]
                for g in range(1, SEGS):
                    total = held[g : g + 1, :] + span[g : g + 1, :] * total
                    product = span[g : g + 1, :] * product
                summary_out[s : s + 1, lanes] = product
                summary_out[seqs + s : seqs + s + 1, lanes] = total

    @pl.when(step == 2 * lane_tiles - 1)
    def _():
        for copy in to_core(sources, targets, send_sem, recv_sem):
            copy.wait()


def ring_peer(by):
    peers = lax.axis_size("seq")
    return {"seq": (lax.axis_index("seq") + by + peers) % peers}


def greet(shifts, with_core, chips=()):
    barrier = pltpu.get_barrier_semaphore()
    peers = [ring_peer(by) for by in shifts] + [{"seq": chip} for chip in chips]
    if with_core:
        peers.append({"wshard": 1 - lax.axis_index("wshard")})
    for peer in peers:
        pl.semaphore_signal(barrier, inc=1, device_id=peer, device_id_type=pl.DeviceIdType.MESH)
    pl.semaphore_wait(barrier, len(peers))


def message(src, inbox, send_sem, recv_sem, slot, by):
    return pltpu.make_async_remote_copy(
        src, inbox.at[slot], send_sem.at[slot], recv_sem.at[slot],
        device_id=ring_peer(by), device_id_type=pl.DeviceIdType.MESH,
    )


def arrived(inbox, seqs, lanes, valid):
    value = None
    for d in range(inbox.shape[0], 0, -1):
        total = jnp.where(valid(d), inbox[d - 1, seqs : 2 * seqs, lanes], 0.0)
        if value is not None:
            total = total + jnp.where(valid(d), inbox[d - 1, :seqs, lanes], 0.0) * value
        value = total
    return value


def branch_output_kernel(
    summary_ref, normed_ref, picked_ref, wb_own, wb_oth, eb_own, eb_oth,
    local_ref, reach_ref, ends_ref, spans_ref, tokens_ref, onehot_ref, gain_ref,
    wo_own, wo_oth, so_own, so_oth, eo_own, eo_oth,
    *refs, carried,
):
    sources, refs = refs[:carried], refs[carried:]
    (pre_out, state_out, merged_out, carry_out, residual_out, second_out, picked_out), refs = refs[:7], refs[7:]
    targets, refs = refs[:carried], refs[carried:]
    branch_all, acc, inner, inbox, send_sem, recv_sem, core_s, core_r = refs
    core = lax.axis_index("wshard")
    step = pl.program_id(0)
    count = pl.num_programs(0) // 2
    hops = inbox.shape[0]
    groups, rows, _ = local_ref.shape
    tile = pre_out.shape[1]
    seqs = ends_ref.shape[0] // SEGS
    seg = rows // (seqs * SEGS)

    @pl.when(step == 0)
    def _():
        greet([d for d in range(1, hops + 1)] + [-d for d in range(1, hops + 1)], True)
        for copy in to_core(sources, targets, core_s, core_r):
            copy.start()
        for d in range(1, hops + 1):
            message(summary_ref, inbox, send_sem, recv_sem, d - 1, d).start()
        acc[...] = jnp.zeros_like(acc)
        inner[...] = jnp.zeros_like(inner)

    @pl.when(step < count)
    def _():
        own, oth = halves(core, normed_ref.shape[1])
        pre = (
            mm(normed_ref[:, own], wb_own[...])
            + mm(normed_ref[:, oth], wb_oth[...])
            + mm(picked_ref[...], stack_ranks(core, eb_own[...], eb_oth[...]))
        )
        pre_out[...] = pre
        branch_all[:, pl.ds(pl.multiple_of(step * tile, 128), tile)] = gelu(pre)

    @pl.when(step == count)
    def _():
        for d in range(1, hops + 1):
            copy = message(summary_ref, inbox, send_sem, recv_sem, d - 1, d)
            copy.wait_send()
            copy.wait_recv()

    @pl.when(step >= count)
    def _():
        at = pl.multiple_of((step - count) * tile, 128)
        start = arrived(inbox, seqs, pl.ds(at, tile), lambda d: lax.axis_index("seq") >= d)
        carry_out[...] = jnp.concatenate([start, jnp.zeros_like(start)], axis=0)
        for s in range(seqs):
            carry = start[s : s + 1, :]
            for g in range(SEGS):
                row = s * SEGS + g
                here = slice(row * seg, (row + 1) * seg)
                state = jnp.concatenate([local_ref[q, here, :] for q in range(groups)], axis=1) + (
                    jnp.concatenate([reach_ref[q, here, :] for q in range(groups)], axis=1) * carry
                )
                state_out[here, :] = state
                merged_out[here, :] = (branch_all[here, pl.ds(at, tile)] * state).astype(BF16)
                carry = ends_ref[row : row + 1, :] + spans_ref[row : row + 1, :] * carry
        merged = merged_out[...]
        mine = (step - count) // (count // 2) == core

        @pl.when(mine)
        def _():
            acc[...] += mm(merged, wo_own[...])

        @pl.when(jnp.logical_not(mine))
        def _():
            acc[...] += mm(merged, wo_oth[...])

        inner[...] += mm_nt(merged, stack_ranks(core, so_own[...], so_oth[...]))

    @pl.when(step == 2 * count - 1)
    def _():
        picked = (inner[...] * onehot_ref[...]).astype(BF16)
        picked_out[...] = picked
        residual = (
            tokens_ref[...].astype(F32)
            + acc[...]
            + mm(picked, stack_ranks(core, eo_own[...], eo_oth[...]))
        )
        residual_out[...] = residual
        scale = lax.rsqrt(jnp.mean(residual * residual, axis=1, keepdims=True) + EPSILON)
        second_out[...] = (residual * scale * gain_ref[...]).astype(BF16)
        for copy in to_core(sources, targets, core_s, core_r):
            copy.wait()


def feed_kernel(
    core_ref, second_ref, cot_ref, residual_ref, onehot_ref, gain_ref,
    g_own_a, g_own_b, g_oth_a, g_oth_b, u_own_a, u_own_b, u_oth_a, u_oth_b, d_own, d_oth,
    sg_own, sg_oth, su_own, su_oth, eg_own_a, eg_own_b, eg_oth_a, eg_oth_b,
    eu_own_a, eu_own_b, eu_oth_a, eu_oth_b, sd_own_a, sd_own_b, sd_oth_a, sd_oth_b, ed_own, ed_oth,
    out_ref, grad_residual_out, grad_low_out, deg_out, deu_out, dsd_out, dsg_out, dsu_out, ded_out,
    picked, picked_t, gi_down, gi_down_t, down_acc, inner_down, grad_second, gi_gate,
):
    core = core_ref[0]
    step = pl.program_id(0)
    ranks = onehot_ref.shape[1]
    width = second_ref.shape[1]
    part = d_own.shape[0]
    own, oth = halves(core, width)

    @pl.when(step == 0)
    def _():
        onehot = onehot_ref[...]
        shrink = jnp.concatenate(
            [stack_ranks(core, sg_own[...], sg_oth[...]), stack_ranks(core, su_own[...], su_oth[...])], axis=0
        )
        both = mm_nt(second_ref[...], shrink) * jnp.concatenate([onehot, onehot], axis=1)
        picked[...] = both.astype(BF16)
        picked_t[...] = flipped(both)
        inner = mm_nt(cot_ref[...], stack_ranks(core, ed_own[...], ed_oth[...])) * onehot
        gi_down[...] = inner.astype(BF16)
        gi_down_t[...] = flipped(inner)
        down_acc[...] = jnp.zeros_like(down_acc)
        inner_down[...] = jnp.zeros_like(inner_down)
        grad_second[...] = jnp.zeros_like(grad_second)
        gi_gate[...] = jnp.zeros_like(gi_gate)

    join = lambda a, b: jnp.concatenate([a[...], b[...]], axis=1)
    g_own, g_oth = join(g_own_a, g_own_b), join(g_oth_a, g_oth_b)
    u_own, u_oth = join(u_own_a, u_own_b), join(u_oth_a, u_oth_b)
    down = jnp.concatenate([d_own[...], d_oth[...]], axis=0)
    eg = stack_ranks(core, join(eg_own_a, eg_own_b), join(eg_oth_a, eg_oth_b))
    eu = stack_ranks(core, join(eu_own_a, eu_own_b), join(eu_oth_a, eu_oth_b))
    sd = stack_ranks(core, join(sd_own_a, sd_own_b), join(sd_oth_a, sd_oth_b))

    x_own, x_oth = second_ref[:, own], second_ref[:, oth]
    gating = mm(x_own, g_own) + mm(x_oth, g_oth) + mm(picked[:, :ranks], eg)
    upward = mm(x_own, u_own) + mm(x_oth, u_oth) + mm(picked[:, ranks:], eu)
    grad_hidden = mm_nt(cot_ref[...], down) + mm(gi_down[...], sd)
    smooth, slope = gelu_parts(gating)
    hidden = (smooth * upward).astype(BF16)
    grad_gating = (grad_hidden * upward * slope).astype(BF16)
    grad_upward = (grad_hidden * smooth).astype(BF16)
    down_acc[...] += mm(hidden, down)
    inner_down[...] += mm_nt(hidden, sd)
    grad_second[:, own] += mm_nt(grad_gating, g_own) + mm_nt(grad_upward, u_own)
    grad_second[:, oth] += mm_nt(grad_gating, g_oth) + mm_nt(grad_upward, u_oth)
    gi_gate[:, :ranks] += mm_nt(grad_gating, eg)
    gi_gate[:, ranks:] += mm_nt(grad_upward, eu)
    for out, grad in (
        (deg_out, mm(picked_t[:ranks, :], grad_gating)),
        (deu_out, mm(picked_t[ranks:, :], grad_upward)),
        (dsd_out, mm(gi_down_t[...], hidden)),
    ):
        low, high = grad[:, :part], grad[:, part:]
        first = core == 0
        put_folded(
            out, jnp.concatenate([jnp.where(first, low, high), jnp.where(first, high, low)], axis=1)
        )

    @pl.when(step == pl.num_programs(0) - 1)
    def _():
        onehot = onehot_ref[...]
        chosen = inner_down[...] * onehot
        residual = residual_ref[...]
        out_ref[...] = (
            residual + down_acc[...] + mm(chosen.astype(BF16), stack_ranks(core, ed_own[...], ed_oth[...]))
        ).astype(BF16)
        put_folded(ded_out, mm(flipped(chosen), cot_ref[...]))
        inner = gi_gate[...] * jnp.concatenate([onehot, onehot], axis=1)
        shrink = jnp.concatenate(
            [stack_ranks(core, sg_own[...], sg_oth[...]), stack_ranks(core, su_own[...], su_oth[...])], axis=0
        )
        grads = mm(flipped(inner), second_ref[...])
        put_folded(dsg_out, grads[:ranks, :])
        put_folded(dsu_out, grads[ranks:, :])
        weighted = (grad_second[...] + mm(inner.astype(BF16), shrink)) * gain_ref[...]
        scale = lax.rsqrt(jnp.mean(residual * residual, axis=1, keepdims=True) + EPSILON)
        grad = (
            cot_ref[...].astype(F32)
            + scale * weighted
            - residual * (scale * scale * scale * jnp.mean(weighted * residual, axis=1, keepdims=True))
        )
        grad_residual_out[...] = grad
        grad_low_out[...] = grad.astype(BF16)


FEED_ORDER = (("eg", 0), ("eu", 1), ("sdn", 0), ("sg", 1), ("su", 1), ("edn", 1))
MIXER_ORDER = (
    ("eo", 0), ("so", 1), ("eb", 0), ("sb", 1),
    ("edec", 0), ("einf", 1), ("sdec", 0), ("sinf", 1), ("er", 0), ("sr", 1),
)


class Links:
    def __init__(self):
        self.core = lax.axis_index("wshard")
        chip = lax.axis_index("seq")
        self.x, self.y, self.z = chip % 2, (chip // 2) % 2, chip // 4
        self.x_peer = chip + 1 - 2 * self.x
        self.y_peer = chip + 2 - 4 * self.y
        self.z_peers = [((self.z + d) % 4) * 4 + chip % 4 for d in (1, 2, 3)]

    def chips(self):
        return [self.x_peer, self.y_peer] + self.z_peers

    def copy(self, src, dst, send, recv, device):
        return pltpu.make_async_remote_copy(
            src, dst, send, recv, device_id=device, device_id_type=pl.DeviceIdType.MESH
        )

    def across(self, src, core_in, cols, send, recv):
        return self.copy(src, core_in.at[:, :, cols], send, recv, {"wshard": 1 - self.core})

    def first(self, send1, recv1, cols, direction, send, recv):
        peer = self.x_peer if direction == 0 else self.y_peer
        return self.copy(send1.at[:, :, cols], recv1.at[:, :, cols], send, recv, {"seq": peer})

    def second(self, send2, recv2, cols, direction, send, recv):
        peer = self.y_peer if direction == 0 else self.x_peer
        return self.copy(send2.at[:, :, cols], recv2.at[:, :, cols], send, recv, {"seq": peer})

    def third(self, send3, recv3, cols, send, recv, index):
        return [
            self.copy(
                send3.at[d, :, cols], recv3.at[d, :, cols], send.at[index, d], recv.at[index, d], {"seq": self.z_peers[d]}
            )
            for d in range(3)
        ]

    def split_first(self, own, core_in, kept, send1, own_cols, cols, direction):
        for p in range(4):
            for o in range(2):
                keep = p * 4 + (o * 2 + self.x if direction == 0 else self.y * 2 + o)
                give = p * 4 + (o * 2 + 1 - self.x if direction == 0 else (1 - self.y) * 2 + o)
                at = p * 2 + o
                if kept is not None:
                    kept[at, :, cols] = own[keep, :, own_cols].astype(F32) + core_in[keep, :, cols].astype(F32)
                send1[at, :, cols] = (
                    own[give, :, own_cols].astype(F32) + core_in[give, :, cols].astype(F32)
                ).astype(BF16)

    def split_second(self, own, core_in, recv1, kept2, send2, cols, direction):
        for p in range(4):
            at = p * 2 + (self.y if direction == 0 else self.x)
            keep = p * 4 + self.y * 2 + self.x
            kept2[p, :, cols] = (
                own[keep, :, cols].astype(F32) + core_in[keep, :, cols].astype(F32) + recv1[at, :, cols].astype(F32)
            )
            at = p * 2 + 1 - (self.y if direction == 0 else self.x)
            give = p * 4 + ((1 - self.y) * 2 + self.x if direction == 0 else self.y * 2 + 1 - self.x)
            send2[p, :, cols] = (
                own[give, :, cols].astype(F32) + core_in[give, :, cols].astype(F32) + recv1[at, :, cols].astype(F32)
            ).astype(BF16)

    def split_third(self, kept2, recv2, send3, out, cols, out_cols):
        out[:, out_cols] = kept2[self.z, :, cols] + recv2[self.z, :, cols].astype(F32)
        for d in range(3):
            to = (self.z + d + 1) % 4
            send3[d, :, cols] = (kept2[to, :, cols] + recv2[to, :, cols].astype(F32)).astype(BF16)

    def finish(self, recv3, out, cols, out_cols):
        out[:, out_cols] += (
            recv3[0, :, cols].astype(F32) + recv3[1, :, cols].astype(F32) + recv3[2, :, cols].astype(F32)
        )


def columns_of(sizes):
    return [pl.ds(sum(sizes[:i]), n) for i, n in enumerate(sizes)]


def unfold_kernel(in_ref, *outs, offsets, sizes, runs, split):
    for out, offset, size, run, two in zip(outs, offsets, sizes, runs, split):
        pieces = unfold(in_ref[:, offset : offset + size], run)
        if two:
            pieces = [p for i, p in enumerate(pieces) if i % 4 < 2] + [p for i, p in enumerate(pieces) if i % 4 >= 2]
        out[...] = jnp.concatenate(pieces, axis=1)


def unfold_all(folded, names, sizes, runs, split):
    outs = pl.pallas_call(
        functools.partial(
            unfold_kernel, offsets=[sum(sizes[:i]) for i in range(len(sizes))], sizes=sizes,
            runs=[runs[k] for k in names], split=[k in split for k in names],
        ),
        out_shape=[jax.ShapeDtypeStruct((4, n * 4), F32) for n in sizes],
        name="unfold_factors",
    )(folded)
    return dict(zip(names, outs))


def scatter_plain(grads, runs, split):
    summed = {}
    for k, g in grads.items():
        quarter = runs[k] // 4
        g = g.astype(F32).reshape(2, g.shape[1], 4, 4, g.shape[3] // quarter, quarter)
        g = g[:, :, jnp.array([0, 2, 1, 3])]
        if k in split:
            g = g.reshape(g.shape[:2] + (2, 2) + g.shape[3:]).transpose(1, 0, 4, 2, 5, 3, 6)
        else:
            g = g.transpose(1, 0, 3, 4, 2, 5)
        g = g.reshape(g.shape[0] * 8, -1)
        summed[k] = lax.psum_scatter(g, ("seq", "wshard"), scatter_dimension=0, tiled=True)
    return summed


def branch_back_kernel(
    low_ref, onehot_ref, masks_ref, soft_ref, picked_ref, pre_ref, state_ref, merged_ref, rate_ref,
    wo_own, wo_oth, so_own, so_oth, eo_own, eo_oth,
    normed_ref, picked_b_ref, wb_own, wb_oth, sb_own, sb_oth, eb_own, eb_oth,
    *refs, feed_sizes, reduce,
):
    count_feed = len(feed_sizes)
    feed, refs = refs[:count_feed], refs[count_feed:]
    (grad_state_out, ends_out, spans_out, start_out, branch_out, dso_out, deo_out, dsb_out, deb_out), refs = refs[:9], refs[9:]
    if reduce:
        half_out, refs = refs[0], refs[1:]
    (gi, gi_t, decay_buf, drive_buf, grad_buf, pre_grad, inner, picked_t, summary, inbox, send_sem, recv_sem), refs = refs[:12], refs[12:]
    core = lax.axis_index("wshard")
    step = pl.program_id(0)
    count = pl.num_programs(0) // 2
    hops = inbox.shape[0]
    rows, tile = pre_ref.shape
    seqs = ends_out.shape[0] // SEGS
    steps = rows // seqs
    seg = steps // SEGS
    shifts = [d for d in range(1, hops + 1)] + [-d for d in range(1, hops + 1)]
    if reduce:
        own, core_in, send1, recv1, local_sem, core_s, core_r, s1_s, s1_r = refs
        cols = columns_of(feed_sizes)
        order = [d for _, d in FEED_ORDER]

    @pl.when(step == 0)
    def _():
        if reduce:
            links = Links()
            greet(shifts, True, links.chips())
            for a in range(count_feed):
                links.across(feed[a].at[1 - core], core_in, cols[a], core_s.at[a], core_r.at[a]).start()
                pltpu.make_async_copy(feed[a].at[core], own.at[:, :, cols[a]], local_sem.at[a]).start()
        else:
            greet(shifts, False)
        grad = mm_nt(low_ref[...], stack_ranks(core, eo_own[...], eo_oth[...])) * onehot_ref[...]
        gi[...] = grad.astype(BF16)
        gi_t[...] = flipped(grad)
        put_folded(deo_out, mm(flipped(picked_ref[...].astype(F32)), low_ref[...]))

    if reduce:

        @pl.when(step == 2)
        def _():
            links = Links()
            for a in range(count_feed):
                pltpu.make_async_copy(feed[a].at[core], own.at[:, :, cols[a]], local_sem.at[a]).wait()
                links.across(feed[a].at[1 - core], core_in, cols[a], core_s.at[a], core_r.at[a]).wait()
                links.split_first(own, core_in, half_out, send1, cols[a], cols[a], order[a])
                links.first(send1, recv1, cols[a], order[a], s1_s.at[a], s1_r.at[a]).start()

    @pl.when(step < count)
    def _():
        at = pl.multiple_of(step * tile, 128)
        mine = step // (count // 2) == core

        @pl.when(mine)
        def _():
            grad_buf[...] = mm_nt(low_ref[...], wo_own[...])

        @pl.when(jnp.logical_not(mine))
        def _():
            grad_buf[...] = mm_nt(low_ref[...], wo_oth[...])

        grad_merged = grad_buf[...] + mm(gi[...], stack_ranks(core, so_own[...], so_oth[...]))
        smooth, slope = gelu_parts(pre_ref[...])
        pre_grad[:, pl.ds(at, tile)] = (grad_merged * state_ref[...] * slope).astype(BF16)
        grad_state = grad_merged * smooth
        decay = jnp.exp(-RATE_SCALE * rate_ref[...] * soft_ref[...]) * masks_ref[:, 0:1]
        put_folded(dso_out, mm(gi_t[...], merged_ref[...]))
        for q in range(tile // LANES):
            grad_state_out[q] = grad_state[:, q * LANES : (q + 1) * LANES]
            decay_buf[q] = decay[:, q * LANES : (q + 1) * LANES]
        for q in range(tile // LANES):
            lanes = slice(q * LANES, (q + 1) * LANES)
            wide = pl.ds(pl.multiple_of(at + q * LANES, 128), LANES)
            for s in range(seqs):
                held = grad_state_out[q, pl.ds(s * steps + seg - 1, SEGS, stride=seg), :]
                span = None
                for i in range(seg - 2, -1, -1):
                    a = decay_buf[q, pl.ds(s * steps + i + 1, SEGS, stride=seg), :]
                    held = a * held + grad_state_out[q, pl.ds(s * steps + i, SEGS, stride=seg), :]
                    span = a if span is None else a * span
                a = decay_buf[q, pl.ds(s * steps, SEGS, stride=seg), :]
                held = a * held
                span = a * span
                ends_out[s * SEGS : (s + 1) * SEGS, lanes] = held
                spans_out[s * SEGS : (s + 1) * SEGS, lanes] = span
                total = held[SEGS - 1 : SEGS, :]
                product = span[SEGS - 1 : SEGS, :]
                for g in range(SEGS - 2, -1, -1):
                    total = held[g : g + 1, :] + span[g : g + 1, :] * total
                    product = span[g : g + 1, :] * product
                summary[s : s + 1, wide] = product
                summary[seqs + s : seqs + s + 1, wide] = total

    @pl.when(step == count)
    def _():
        for d in range(1, hops + 1):
            message(summary, inbox, send_sem, recv_sem, d - 1, -d).start()
        branch_out[...] = jnp.zeros_like(branch_out)
        inner[...] = jnp.zeros_like(inner)
        picked_t[...] = flipped(picked_b_ref[...].astype(F32))

    @pl.when(step >= count)
    def _():
        left, right = halves(core, branch_out.shape[1])
        grad = pre_grad[:, pl.ds(pl.multiple_of((step - count) * tile, 128), tile)]
        branch_out[:, left] += mm_nt(grad, wb_own[...])
        branch_out[:, right] += mm_nt(grad, wb_oth[...])
        inner[...] += mm_nt(grad, stack_ranks(core, eb_own[...], eb_oth[...]))
        put_folded(deb_out, mm(picked_t[...], grad))

    @pl.when(step == 2 * count - 1)
    def _():
        grad = inner[...] * onehot_ref[...]
        put_folded(dsb_out, mm(flipped(grad), normed_ref[...]))
        branch_out[...] += mm(grad.astype(BF16), stack_ranks(core, sb_own[...], sb_oth[...]))
        for d in range(1, hops + 1):
            copy = message(summary, inbox, send_sem, recv_sem, d - 1, -d)
            copy.wait_send()
            copy.wait_recv()
        peers = lax.axis_size("seq")
        start = arrived(inbox, seqs, slice(None), lambda d: lax.axis_index("seq") + d < peers)
        start_out[...] = jnp.concatenate([start, jnp.zeros_like(start)], axis=0)
        if reduce:
            links = Links()
            for a in range(count_feed):
                links.first(send1, recv1, cols[a], order[a], s1_s.at[a], s1_r.at[a]).wait()
                for at in range(half_out.shape[0]):
                    half_out[at, :, cols[a]] += recv1[at, :, cols[a]].astype(F32)


def recur_back_kernel(
    grad_state_ref, ends_ref, spans_ref, start_ref, carry_ref, state_ref, mixed_ref, rate_ref, inflow_ref,
    masks_ref, onehot_ref, soft_ref, picked_ref,
    bd_own, bd_oth, bi_own, bi_oth, ed_own, ed_oth, ei_own, ei_oth, sd_own, sd_oth, si_own, si_oth,
    taps_ref, normed_ref, picked_r_ref, branch_ref, residual_ref, tokens_ref, gain_ref,
    wr_own, wr_oth, sr_own, sr_oth, er_own, er_oth,
    *refs, feed_sizes, mixer_sizes, reduce,
):
    if reduce:
        half_ref, early_grads, refs = refs[0], refs[1:5], refs[5:]
        out_ref, sums_out, refs = refs[0], refs[1], refs[2:]
    else:
        out_ref, late_outs, refs = refs[0], refs[1:7], refs[7:]
    (decay_buf, flow_buf, partial, inner, gi, gi_t, picked_t, filt, low, inner_r, picked_rt, heads, inbox,
     head_s, head_r), refs = refs[:15], refs[15:]
    core = lax.axis_index("wshard")
    step = pl.program_id(0)
    count = pl.num_programs(0) // 3
    groups = grad_state_ref.shape[0]
    rows, tile = state_ref.shape
    ranks = onehot_ref.shape[1]
    seqs = ends_ref.shape[0] // SEGS
    steps = rows // seqs
    seg = steps // SEGS
    lags = taps_ref.shape[0] - 1
    order = [d for _, d in MIXER_ORDER]

    if reduce:
        (kept2_f, send2_f, recv2_f, send3_f, recv3_f, f2_s, f2_r, f3_s, f3_r,
         mine_g, core_in, send1, recv1, kept2, send2, recv2, send3, recv3,
         local_sem, core_s, core_r, s1_s, s1_r, s2_s, s2_r, s3_s, s3_r) = refs
        fcols = columns_of(feed_sizes)
        forder = [d for _, d in FEED_ORDER]
        mcols = columns_of(mixer_sizes)
        base = sum(feed_sizes)
        sums_cols = [pl.ds(base + sum(mixer_sizes[:i]), n) for i, n in enumerate(mixer_sizes)]

        def feed_second(links):
            for a in range(len(feed_sizes)):
                mine = links.y if forder[a] == 0 else links.x
                for p in range(4):
                    kept2_f[p, :, fcols[a]] = half_ref[p * 2 + mine, :, fcols[a]]
                    send2_f[p, :, fcols[a]] = half_ref[p * 2 + 1 - mine, :, fcols[a]].astype(BF16)
                links.second(send2_f, recv2_f, fcols[a], forder[a], f2_s.at[a], f2_r.at[a]).start()

        def feed_third(links):
            for a in range(len(feed_sizes)):
                links.second(send2_f, recv2_f, fcols[a], forder[a], f2_s.at[a], f2_r.at[a]).wait()
                links.split_third(kept2_f, recv2_f, send3_f, sums_out, fcols[a], fcols[a])
                for copy in links.third(send3_f, recv3_f, fcols[a], f3_s, f3_r, a):
                    copy.start()

        def feed_finish(links):
            for a in range(len(feed_sizes)):
                for copy in links.third(send3_f, recv3_f, fcols[a], f3_s, f3_r, a):
                    copy.wait()
                links.finish(recv3_f, sums_out, fcols[a], fcols[a])

        def cross(links, which):
            for a in which:
                if a < 4:
                    pltpu.make_async_copy(
                        early_grads[a].at[core], mine_g.at[core, :, :, mcols[a]], local_sem.at[a]
                    ).start()
                    src = early_grads[a].at[1 - core]
                else:
                    src = mine_g.at[1 - core, :, :, mcols[a]]
                links.across(src, core_in, mcols[a], core_s.at[a], core_r.at[a]).start()

        def first(links, which):
            for a in which:
                if a < 4:
                    pltpu.make_async_copy(
                        early_grads[a].at[core], mine_g.at[core, :, :, mcols[a]], local_sem.at[a]
                    ).wait()
                    src = early_grads[a].at[1 - core]
                else:
                    src = mine_g.at[1 - core, :, :, mcols[a]]
                links.across(src, core_in, mcols[a], core_s.at[a], core_r.at[a]).wait()
                links.split_first(mine_g.at[core], core_in, None, send1, mcols[a], mcols[a], order[a])
                links.first(send1, recv1, mcols[a], order[a], s1_s.at[a], s1_r.at[a]).start()

        def second(links, which):
            for a in which:
                links.first(send1, recv1, mcols[a], order[a], s1_s.at[a], s1_r.at[a]).wait()
                links.split_second(mine_g.at[core], core_in, recv1, kept2, send2, mcols[a], order[a])
                links.second(send2, recv2, mcols[a], order[a], s2_s.at[a], s2_r.at[a]).start()

        def third(links, which):
            for a in which:
                links.second(send2, recv2, mcols[a], order[a], s2_s.at[a], s2_r.at[a]).wait()
                links.split_third(kept2, recv2, send3, sums_out, mcols[a], sums_cols[a])
                for copy in links.third(send3, recv3, mcols[a], s3_s, s3_r, a):
                    copy.start()

        def finish(links, which):
            for a in which:
                for copy in links.third(send3, recv3, mcols[a], s3_s, s3_r, a):
                    copy.wait()
                links.finish(recv3, sums_out, mcols[a], sums_cols[a])

        A, B, C, D = (0, 1, 2, 3), (4, 5), (6, 7), (8, 9)
        plan = {
            0: [(feed_second, None), (cross, A)],
            2: [(first, A)],
            3: [(feed_third, None)],
            4: [(cross, B)],
            5: [(feed_finish, None), (first, B)],
            6: [(second, A)],
            8: [(cross, C), (second, B), (third, A)],
            9: [(first, C)],
            10: [(third, B), (finish, A)],
            11: [(second, C)],
        }
        tail = [(cross, D), (third, C), (finish, B), (first, D), (second, D), (finish, C), (third, D), (finish, D)]

        def run(links, what):
            for action, which in what:
                action(links) if which is None else action(links, which)

        def late_grad(index, grad, piece=None):
            width = grad.shape[1] // 4
            start = sum(mixer_sizes[:index])
            if piece is None:
                at = pl.ds(start, width)
            else:
                at = pl.ds(pl.multiple_of(start + piece * width, 128), width)
            for half, block in enumerate(fold(grad)):
                mine_g[half, :, :, at] = block

    else:

        def late_grad(index, grad, piece=None):
            put_folded(late_outs[index - 4], grad)

    @pl.when(step == 0)
    def _():
        if reduce:
            greet([1, -1], True, Links().chips())
        else:
            greet([1, -1], False)
        inner[...] = jnp.zeros_like(inner)
        inner_r[...] = jnp.zeros_like(inner_r)
        picked_t[...] = flipped(picked_ref[...].astype(F32))
        picked_rt[...] = flipped(picked_r_ref[...].astype(F32))

    if reduce:
        for at_step, what in plan.items():

            @pl.when(step == at_step)
            def _(what=what):
                run(Links(), what)

    def head_copy(slot):
        return pltpu.make_async_remote_copy(
            heads.at[slot], inbox.at[slot], head_s.at[slot], head_r.at[slot],
            device_id=ring_peer(-1), device_id_type=pl.DeviceIdType.MESH,
        )

    @pl.when(step < count)
    def _():
        keep = masks_ref[:, 0:1]
        soft = soft_ref[...]
        rate = rate_ref[...]
        raw = jnp.exp(-RATE_SCALE * rate * soft)
        decay = raw * keep
        for q in range(groups):
            decay_buf[q] = decay[:, q * LANES : (q + 1) * LANES]
        for s in range(seqs):
            carry = start_ref[s : s + 1, :]
            carries = [carry]
            for g in range(SEGS - 1, 0, -1):
                row = s * SEGS + g
                carry = ends_ref[row : row + 1, :] + spans_ref[row : row + 1, :] * carry
                carries.append(carry)
            entering = jnp.concatenate(carries[::-1], axis=0)
            for q in range(groups):
                at = pl.ds(s * steps + seg - 1, SEGS, stride=seg)
                flow = grad_state_ref[q, at, :] + entering[:, q * LANES : (q + 1) * LANES]
                flow_buf[q, at, :] = flow
                for i in range(seg - 2, -1, -1):
                    a = decay_buf[q, pl.ds(s * steps + i + 1, SEGS, stride=seg), :]
                    at = pl.ds(s * steps + i, SEGS, stride=seg)
                    flow = a * flow + grad_state_ref[q, at, :]
                    flow_buf[q, at, :] = flow
        priors = []
        top = lax.broadcasted_iota(jnp.int32, (steps, tile), 0) == 0
        for s in range(seqs):
            rolled = pltpu.roll(state_ref[s * steps : (s + 1) * steps, :], 1, 0)
            priors.append(jnp.where(top, carry_ref[s : s + 1, :], rolled))
        prior = jnp.concatenate(priors, axis=0)
        backflow = jnp.concatenate([flow_buf[q] for q in range(groups)], axis=1)
        mixed = mixed_ref[...]
        inflow = inflow_ref[...]
        spread = (1.0 - raw) * (1.0 + raw)
        root_raw = jnp.sqrt(jnp.maximum(spread, ROOT_FLOOR))
        root = keep * root_raw + (1.0 - keep)
        pulled = backflow * inflow
        grad_spread = jnp.where(spread > ROOT_FLOOR, pulled * mixed * (keep * 0.5) / root_raw, 0.0)
        grad_log = backflow * prior * decay - 2.0 * (raw * raw) * grad_spread
        grad_rate = (grad_log * (-RATE_SCALE * soft) * rate * (1.0 - rate)).astype(BF16)
        through = pulled * root
        grad_inflow = (through * mixed * (1.0 - inflow)).astype(BF16)
        blocks, block = bd_own.shape[0], bd_own.shape[1]
        mine = step // (count // 2) == core
        pieces = []
        for b in range(blocks):
            lanes = slice(b * block, (b + 1) * block)
            both = jnp.concatenate(
                [jnp.where(mine, bd_own[b], bd_oth[b]), jnp.where(mine, bi_own[b], bi_oth[b])], axis=1
            )
            pieces.append(mm_nt(jnp.concatenate([grad_rate[:, lanes], grad_inflow[:, lanes]], axis=1), both))
        partial[:, pl.ds(pl.multiple_of(step * tile, 128), tile)] = through + jnp.concatenate(pieces, axis=1)
        inner[:, :ranks] += mm_nt(grad_rate, stack_ranks(core, ed_own[...], ed_oth[...]))
        inner[:, ranks:] += mm_nt(grad_inflow, stack_ranks(core, ei_own[...], ei_oth[...]))
        late_grad(4, mm(picked_t[:ranks, :], grad_rate), step)
        late_grad(5, mm(picked_t[ranks:, :], grad_inflow), step)

    @pl.when(step == count - 1)
    def _():
        onehot = onehot_ref[...]
        chosen = inner[...] * jnp.concatenate([onehot, onehot], axis=1)
        gi[...] = chosen.astype(BF16)
        gi_t[...] = flipped(chosen)

    @pl.when(jnp.logical_and(step >= count, step < 2 * count))
    def _():
        piece = step - count
        at = pl.multiple_of(piece * tile, 128)
        shrink = jnp.concatenate(
            [stack_ranks(core, sd_own[...], sd_oth[...]), stack_ranks(core, si_own[...], si_oth[...])], axis=0
        )
        grad = partial[:, pl.ds(at, tile)] + mm(gi[...], shrink)
        partial[:, pl.ds(at, tile)] = grad
        for s in range(seqs):
            heads[piece, s * HALO : (s + 1) * HALO, :] = grad[s * steps : s * steps + HALO, :]
        both = mm(gi_t[...], mixed_ref[...].astype(BF16))
        late_grad(6, both[:ranks, :], piece)
        late_grad(7, both[ranks:, :], piece)
        head_copy(piece).start()

    @pl.when(step == 2 * count)
    def _():
        out_ref[...] = branch_ref[...]

    @pl.when(step >= 2 * count)
    def _():
        piece = step - 2 * count
        at = pl.multiple_of(piece * tile, 128)
        head_copy(piece).wait()
        for s in range(seqs):
            filt[s, :steps, :] = partial[s * steps : (s + 1) * steps, pl.ds(at, tile)]
            filt[s, steps:, :] = inbox[piece, s * HALO : (s + 1) * HALO, :]
        for s in range(seqs):
            here = slice(s * steps, (s + 1) * steps)
            total = taps_ref[0:1, :] * filt[s, :steps, :]
            for lag in range(1, lags + 1):
                later = filt[s, lag : lag + steps, :]
                total = total + taps_ref[lag : lag + 1, :] * later * masks_ref[here, lags + lag - 1 : lags + lag]
            low[here, :] = total.astype(BF16)
        grad = low[...]
        left, right = halves(core, out_ref.shape[1])
        out_ref[:, left] += mm_nt(grad, wr_own[...])
        out_ref[:, right] += mm_nt(grad, wr_oth[...])
        inner_r[...] += mm_nt(grad, stack_ranks(core, er_own[...], er_oth[...]))
        late_grad(8, mm(picked_rt[...], grad), piece)

    @pl.when(step == 3 * count - 1)
    def _():
        chosen = inner_r[...] * onehot_ref[...]
        late_grad(9, mm(flipped(chosen), normed_ref[...]))
        if reduce:
            run(Links(), tail[:1])
        weighted = (out_ref[...] + mm(chosen.astype(BF16), stack_ranks(core, sr_own[...], sr_oth[...]))) * gain_ref[...]
        values = tokens_ref[...].astype(F32)
        scale = lax.rsqrt(jnp.mean(values * values, axis=1, keepdims=True) + EPSILON)
        out_ref[...] = (
            residual_ref[...]
            + scale * weighted
            - values * (scale * scale * scale * jnp.mean(weighted * values, axis=1, keepdims=True))
        )
        if reduce:
            run(Links(), tail[1:])


def indexed(shape, index, scalars):
    if scalars:
        return pl.BlockSpec(shape, index)
    return pl.BlockSpec(shape, lambda j: index(j, None))


def call(kernel, name, grid, core, ins, outs, scratch, flops, nbytes, collective=None):
    scalars = core is not None

    def still(shape):
        zeros = (0,) * len(shape)
        if scalars:
            return pl.BlockSpec(shape, lambda j, c: zeros, pipeline_mode=pl.Buffered(1))
        return pl.BlockSpec(shape, lambda j: zeros, pipeline_mode=pl.Buffered(1))

    in_specs, arrays = [], []
    for item in ins:
        if isinstance(item, tuple) and len(item) == 1:
            arrays.append(item[0])
            in_specs.append(pl.BlockSpec(memory_space=pl.ANY))
        elif isinstance(item, tuple):
            arrays.append(item[0])
            in_specs.append(indexed(item[1], item[2], scalars))
        else:
            arrays.append(item)
            in_specs.append(still(item.shape))
    out_specs, shapes = [], []
    for item in outs:
        shapes.append(jax.ShapeDtypeStruct(item[0], item[1]))
        if len(item) == 3:
            out_specs.append(pl.BlockSpec(memory_space=pl.ANY))
        else:
            out_specs.append(indexed(item[2], item[3], scalars) if len(item) == 4 else still(item[0]))
    return pl.pallas_call(
        kernel,
        grid_spec=pltpu.PrefetchScalarGridSpec(
            num_scalar_prefetch=int(scalars), grid=(grid,), in_specs=in_specs, out_specs=out_specs, scratch_shapes=scratch
        ),
        out_shape=shapes,
        name=name,
        compiler_params=pltpu.CompilerParams(
            dimension_semantics=("arbitrary",), vmem_limit_bytes=67043328, collective_id=collective,
            has_side_effects=collective is not None,
        ),
        cost_estimate=pl.CostEstimate(flops=flops, bytes_accessed=nbytes, transcendentals=0),
    )(*([core] if scalars else []), *arrays)


def shifted(shard, by):
    peers = lax.axis_size("seq")
    pairs = [(i, i + by) for i in range(peers) if 0 <= i + by < peers]
    return lax.ppermute(shard, "seq", pairs)


def local(
    tokens, segment_ids, document_adapter, out_cotangent, mixer_gain, feed_gain, filter_taps, decay_param, *weights
):
    core = lax.axis_index("wshard").astype(jnp.int32).reshape(1)
    anywhere = pl.ANY
    swap = lambda item: lax.ppermute(item, "wshard", [(0, 1), (1, 0)])
    soon = (1, 2, 3, 8, 10, 11, 12, 13, 14, 15)
    with_mixer = (0, 9, 16, 17, 4, 5, 18, 19, 20, 21, 22, 23)
    with_branch = (6, 7)
    other = {i: swap(weights[i]) for i in soon}
    pair = lambda i: (weights[i], other[i])
    wr, bd, bi, sb, sr, er, sdec, edec, sinf, einf = [pair(i) for i in (1, 2, 3, 8, 10, 11, 12, 13, 14, 15)]
    seqs, steps, width = tokens.shape
    rows = seqs * steps
    lru = filter_taps.shape[1]
    lags = filter_taps.shape[0] - 1
    ranks = 2 * sb[0].shape[0]
    feed = weights[5].shape[1]
    peers = lax.axis_size("seq")
    reach = peers // 4

    before = shifted(segment_ids, 1)
    after = shifted(segment_ids, -1)
    halo = shifted(tokens[:, steps - HALO :, :], 1).reshape(seqs * HALO, width)
    position = lax.axis_index("seq") * steps + jnp.arange(steps, dtype=jnp.int32)
    wide = jnp.concatenate([before[:, steps - HALO :], segment_ids, after[:, :HALO]], axis=1)
    columns = []
    for lag in range(1, lags + 1):
        prior = wide[:, HALO - lag : HALO - lag + steps]
        columns.append((prior == segment_ids) & (position >= lag)[None, :])
    for lag in range(1, lags + 1):
        later = wide[:, HALO + lag : HALO + lag + steps]
        columns.append((later == segment_ids) & (position + lag < peers * steps)[None, :])
    columns += [columns[0]] * (8 - len(columns))
    masks = jnp.stack([c.reshape(rows) for c in columns], axis=1).astype(F32)
    documents = jnp.arange(document_adapter.shape[1], dtype=jnp.int32)

    def owners_of(ids):
        owner = jnp.sum(
            jnp.where(ids[:, :, None] == documents[None, None, :], document_adapter[:, None, :], 0), axis=2
        )
        return owner.reshape(-1)

    owner = jnp.concatenate([owners_of(segment_ids), owners_of(before[:, steps - HALO :])])
    onehot = (owner[:, None] == (jnp.arange(ranks, dtype=jnp.int32) // RANK)[None, :]).astype(F32)
    onehot_own = onehot[:rows]
    soft = jax.nn.softplus(-decay_param)[None, :]
    gain_first = mixer_gain[None, :]
    gain_second = feed_gain[None, :]
    tokens2 = tokens.reshape(rows, width)
    cot = out_cotangent.reshape(rows, width)

    tile = TILE
    count = lru // tile
    half = width // 2
    blocks = tile // bd[0].shape[1]
    block = bd[0].shape[1]
    early = lambda j: jnp.minimum(j, count - 1)
    late = lambda j: jnp.maximum(j - count, 0)
    flat = lambda r, at: ((r, tile), lambda j, c: (0, at(j)))

    def tiled(array, r, at):
        block_shape, index = flat(r, at)
        return (array, block_shape, index)

    def tiled_out(r, dtype, at, total=None):
        block_shape, index = flat(r, at)
        return ((r, total or lru), dtype, block_shape, index)

    lane_groups = tile // LANES

    def grouped(array, index):
        return (array, (lane_groups, rows, LANES), index)

    def grouped_out(at):
        return ((lru // LANES, rows, LANES), F32, (lane_groups, rows, LANES), lambda j, c: (at(j), 0, 0))

    def both(pair, r, at):
        return [tiled(pair[0], r, at), tiled(pair[1], r, at)]

    def gate_blocks(pair, at):
        index = lambda j, c: (at(j) % (count // 2), 0, 0)
        return [(pair[0], (blocks, block, block), index), (pair[1], (blocks, block, block), index)]

    half_ranks = ranks // 2
    ident = lambda j: j
    groups = seqs * SEGS
    with jax.named_scope("mixer_forward"):
        (normed, picked_br, picked_di, mixed, rate, inflow, held, span, ends, spans, summary, *moved) = call(
            functools.partial(mixer_kernel, carried=len(with_mixer)), "mixer_forward", 2 * count, None,
            [tokens2, halo, onehot, masks, gain_first, tiled(filter_taps, lags + 1, early), tiled(soft, 1, late)]
            + both(wr, half, early) + list(sb) + list(sr) + both(er, half_ranks, early)
            + both(sdec, half_ranks, early) + both(sinf, half_ranks, early)
            + gate_blocks(bd, late) + gate_blocks(bi, late)
            + both(edec, half_ranks, late) + both(einf, half_ranks, late)
            + [(weights[i],) for i in with_mixer],
            [((rows, width), BF16), ((rows, 2 * ranks), BF16), ((rows, 2 * ranks), BF16),
             tiled_out(rows, F32, early), tiled_out(rows, F32, late), tiled_out(rows, F32, late),
             grouped_out(late), grouped_out(late),
             tiled_out(groups, F32, late), tiled_out(groups, F32, late), tiled_out(2 * seqs, F32, late)]
            + [(weights[i].shape, BF16, anywhere) for i in with_mixer],
            [pltpu.VMEM((rows + seqs * HALO, width), BF16), pltpu.VMEM((rows + seqs * HALO, ranks), BF16),
             pltpu.VMEM((rows, 2 * ranks), F32), pltpu.VMEM((rows, 2 * ranks), BF16),
             pltpu.VMEM((rows, lru), F32), pltpu.VMEM((seqs, steps + HALO, tile), F32),
             pltpu.VMEM((lane_groups, rows, LANES), F32), pltpu.VMEM((lane_groups, rows, LANES), F32),
             pltpu.SemaphoreType.DMA((len(with_mixer),)), pltpu.SemaphoreType.DMA((len(with_mixer),))],
            int(6e9), int(30e6), collective=2,
        )
    other.update(zip(with_mixer, moved))
    wb, eb, so, eo, wo, wg = pair(0), pair(9), pair(16), pair(17), pair(4), pair(5)
    sg, eg, su, eu, sdn, edn = [pair(i) for i in (18, 19, 20, 21, 22, 23)]
    own_rows = lambda pair, at: [
        (pair[0], (tile, width), lambda j, c: (at(j) % (count // 2), 0)),
        (pair[1], (tile, width), lambda j, c: (at(j) % (count // 2), 0)),
    ]
    with jax.named_scope("branch_and_output_forward"):
        branch_pre, state, merged, carry, residual, second, picked_o, *moved = call(
            functools.partial(branch_output_kernel, carried=len(with_branch)), "branch_output_forward", 2 * count, None,
            [summary, normed, (picked_br, (rows, ranks), lambda j, c: (0, 0))] + both(wb, half, early)
            + both(eb, half_ranks, early)
            + [grouped(held, lambda j, c: (late(j), 0, 0)), grouped(span, lambda j, c: (late(j), 0, 0)),
               tiled(ends, groups, late), tiled(spans, groups, late), tokens2, onehot_own, gain_second]
            + own_rows(wo, late) + both(so, half_ranks, late) + list(eo) + [(weights[i],) for i in with_branch],
            [tiled_out(rows, F32, early), tiled_out(rows, F32, late), tiled_out(rows, BF16, late),
             tiled_out(2 * seqs, F32, late), ((rows, width), F32), ((rows, width), BF16), ((rows, ranks), BF16)]
            + [(weights[i].shape, BF16, anywhere) for i in with_branch],
            [pltpu.VMEM((rows, lru), F32), pltpu.VMEM((rows, width), F32), pltpu.VMEM((rows, ranks), F32),
             pltpu.VMEM((reach, 2 * seqs, lru), F32), pltpu.SemaphoreType.DMA((reach,)), pltpu.SemaphoreType.DMA((reach,)),
             pltpu.SemaphoreType.DMA((len(with_branch),)), pltpu.SemaphoreType.DMA((len(with_branch),))],
            int(8e9), int(45e6), collective=1,
        )
    other.update(zip(with_branch, moved))
    wu, wd = pair(6), pair(7)

    part = 256
    pieces = feed // (2 * part)

    def feed_cols(pair_item, r):
        return [
            (pair_item, (r, part), lambda j, c: (0, c[0] * pieces + j)),
            (pair_item, (r, part), lambda j, c: (0, (1 - c[0]) * pieces + j)),
        ]

    def feed_pair(pair, r):
        return feed_cols(pair[0], r) + feed_cols(pair[1], r)

    chips = ranks // 8
    grad_cols = ((2, chips, 16, feed // 4), BF16, (2, chips, 16, part // 2), lambda j, c: (0, 0, 0, j))
    grad_whole = ((2, chips, 16, width // 4), BF16)

    def grad_tile(at):
        return ((2, chips, 16, lru // 4), BF16, (2, chips, 16, tile // 4), lambda j, c: (0, 0, 0, at(j)))

    with jax.named_scope("feed_forward_both_ways"):
        result, grad_residual, grad_low, deg, deu, dsdn, dsg, dsu, dedn = call(
            feed_kernel, "feed_both_ways", pieces, core,
            [second, cot, residual, onehot_own, gain_second] + feed_pair(wg, half) + feed_pair(wu, half)
            + [(wd[0], (part, width), lambda j, c: (j, 0)), (wd[1], (part, width), lambda j, c: (j, 0))]
            + list(sg) + list(su) + feed_pair(eg, half_ranks) + feed_pair(eu, half_ranks)
            + feed_pair(sdn, half_ranks) + list(edn),
            [((rows, width), BF16), ((rows, width), F32), ((rows, width), BF16),
             grad_cols, grad_cols, grad_cols, grad_whole, grad_whole, grad_whole],
            [pltpu.VMEM((rows, 2 * ranks), BF16), pltpu.VMEM((2 * ranks, rows), BF16),
             pltpu.VMEM((rows, ranks), BF16), pltpu.VMEM((ranks, rows), BF16),
             pltpu.VMEM((rows, width), F32), pltpu.VMEM((rows, ranks), F32), pltpu.VMEM((rows, width), F32),
             pltpu.VMEM((rows, 2 * ranks), F32)],
            int(50e9), int(60e6),
        )

    split = ("eg", "eu", "sdn")
    runs = dict(sb=width, eb=tile, sr=width, er=tile, sdec=tile, edec=tile, sinf=tile, einf=tile, so=tile, eo=width,
                sg=width, eg=2 * part, su=width, eu=2 * part, sdn=2 * part, edn=width)
    reduce = peers == 16 and ranks == 128
    grads = dict(eg=deg, eu=deu, sdn=dsdn, sg=dsg, su=dsu, edn=dedn)
    size_of = lambda k: (width if k in ("eo", "sb", "sr", "sg", "su", "edn") else feed if k in split else lru) // 4
    feed_sizes = [size_of(k) for k, _ in FEED_ORDER]
    mixer_sizes = [size_of(k) for k, _ in MIXER_ORDER]
    feed_grads = [(grads[k],) for k, _ in FEED_ORDER] if reduce else []
    wide, narrow = sum(feed_sizes), sum(mixer_sizes)
    dma = pltpu.SemaphoreType.DMA
    vm = lambda *shape: pltpu.VMEM(shape, BF16)
    vf = lambda *shape: pltpu.VMEM(shape, F32)
    nf, nm = len(feed_sizes), len(mixer_sizes)

    with jax.named_scope("output_and_branch_backward"):
        (grad_state, bends, bspans, bstart, grad_branch, dso, deo, dsb, deb, *halved) = call(
            functools.partial(branch_back_kernel, feed_sizes=feed_sizes if reduce else [], reduce=reduce),
            "output_branch_backward", 2 * count, None,
            [grad_low, onehot_own, masks, tiled(soft, 1, early), picked_o, tiled(branch_pre, rows, early),
             tiled(state, rows, early), tiled(merged, rows, early), tiled(rate, rows, early)]
            + own_rows(wo, early) + both(so, half_ranks, early) + list(eo)
            + [normed, (picked_br, (rows, ranks), lambda j, c: (0, 0))]
            + both(wb, half, late) + list(sb) + both(eb, half_ranks, late) + feed_grads,
            [grouped_out(early), tiled_out(groups, F32, early), tiled_out(groups, F32, early),
             ((2 * seqs, lru), F32), ((rows, width), F32), grad_tile(early), grad_whole, grad_whole, grad_tile(late)]
            + ([((8, 16, wide), F32)] if reduce else []),
            [vm(rows, ranks), vm(ranks, rows), vf(lane_groups, rows, LANES), vf(lane_groups, rows, LANES), vf(rows, tile),
             vm(rows, lru), vf(rows, ranks), vm(ranks, rows), vf(2 * seqs, lru), vf(reach, 2 * seqs, lru),
             dma((reach,)), dma((reach,))]
            + ([vm(16, 16, wide), vm(16, 16, wide), vm(8, 16, wide), vm(8, 16, wide)] + [dma((nf,))] * 5 if reduce else []),
            int(10e9), int(50e6), collective=3,
        )
    early_grads = dict(eo=deo, so=dso, eb=deb, sb=dsb)
    grads.update(early_grads)
    third = 3
    first_of = lambda j: jnp.minimum(j, count - 1)
    middle = lambda j: jnp.clip(j - count, 0, count - 1)
    last = lambda j: jnp.clip(j - 2 * count, 0, count - 1)
    twice = lambda j: jnp.where(j < count, j, jnp.clip(j - count, 0, count - 1))
    with jax.named_scope("gates_and_recur_backward"):
        grad_tokens, *late = call(
            functools.partial(recur_back_kernel, feed_sizes=feed_sizes, mixer_sizes=mixer_sizes, reduce=reduce),
            "gates_recur_backward", 3 * count, None,
            [grouped(grad_state, lambda j, c: (first_of(j), 0, 0)), tiled(bends, groups, first_of), tiled(bspans, groups, first_of),
             tiled(bstart, 2 * seqs, first_of), tiled(carry, 2 * seqs, first_of), tiled(state, rows, first_of),
             tiled(mixed, rows, twice), tiled(rate, rows, first_of), tiled(inflow, rows, first_of),
             masks, onehot_own, tiled(soft, 1, first_of), picked_di]
            + gate_blocks(bd, first_of) + gate_blocks(bi, first_of)
            + both(edec, half_ranks, first_of) + both(einf, half_ranks, first_of)
            + both(sdec, half_ranks, middle) + both(sinf, half_ranks, middle)
            + [tiled(filter_taps, lags + 1, last), normed, (picked_br, (rows, ranks), lambda j, c: (0, 1)),
               grad_branch, grad_residual, tokens2, gain_first]
            + both(wr, half, last) + list(sr) + both(er, half_ranks, last)
            + ([halved[0]] + [(early_grads[k],) for k, _ in MIXER_ORDER[:4]] if reduce else []),
            [((rows, width), F32)]
            + ([((16, wide + narrow), F32)] if reduce else
               [grad_tile(first_of), grad_tile(first_of), grad_tile(middle), grad_tile(middle), grad_tile(last), grad_whole]),
            [vf(lane_groups, rows, LANES), vf(lane_groups, rows, LANES), vf(rows, lru), vf(rows, 2 * ranks),
             vm(rows, 2 * ranks), vm(2 * ranks, rows), vm(2 * ranks, rows), vf(seqs, steps + HALO, tile), vm(rows, tile),
             vf(rows, ranks), vm(ranks, rows), vf(count, seqs * HALO, tile), vf(count, seqs * HALO, tile),
             dma((count,)), dma((count,))]
            + ([vf(4, 16, wide), vm(4, 16, wide), vm(4, 16, wide), vm(3, 16, wide), vm(3, 16, wide),
                dma((nf,)), dma((nf,)), dma((nf, 3)), dma((nf, 3)),
                vm(2, 16, 16, narrow), vm(16, 16, narrow), vm(8, 16, narrow), vm(8, 16, narrow),
                vf(4, 16, narrow), vm(4, 16, narrow), vm(4, 16, narrow), vm(3, 16, narrow), vm(3, 16, narrow)]
               + [dma((nm,))] * 7 + [dma((nm, 3))] * 2 if reduce else []),
            int(10e9), int(50e6), collective=4,
        )

    names = ("sb", "eb", "sr", "er", "sdec", "edec", "sinf", "einf", "so", "eo", "sg", "eg", "su", "eu", "sdn", "edn")
    with jax.named_scope("factor_gradients"):
        if reduce:
            both_names = [k for k, _ in FEED_ORDER + MIXER_ORDER]
            summed = unfold_all(late[0], both_names, feed_sizes + mixer_sizes, runs, split)
        else:
            grads.update(zip([k for k, _ in MIXER_ORDER[4:]], late))
            summed = scatter_plain(grads, runs, split)
    return (result.reshape(seqs, steps, width), grad_tokens.reshape(seqs, steps, width)) + tuple(
        summed[k] for k in names
    )


def solution(mesh):
    split = P("wshard", None)
    in_specs = (
        (P("wshard", "seq", None), P("wshard", "seq"), split, P("wshard", "seq", None))
        + (P(),) * 4
        + (split, split, P("wshard", None, None), P("wshard", None, None))
        + (split,) * 20
    )
    out_specs = (P("wshard", "seq", None),) * 2 + (P(("seq", "wshard"), None),) * 16
    return jax.shard_map(local, mesh=mesh, in_specs=in_specs, out_specs=out_specs, check_vma=False)
```

```python
import functools

import jax
import jax.numpy as jnp
from jax import lax
from jax.experimental import pallas as pl
from jax.experimental.pallas import tpu as pltpu
from jax.sharding import PartitionSpec as P

RANK = 16
EPSILON = 1e-06
RATE_SCALE = 8.0
ROOT_FLOOR = 0.001
GELU_A = 0.7978845608028654
GELU_B = 0.044715
LOG2_E = 1.4426950408889634
CHUNK = (16, 256)

HALO = 8
SEGS = 8
TILE = 512
LANES = 128
F32 = jnp.float32
BF16 = jnp.bfloat16


def mm(left, right):
    return lax.dot_general(left, right, (((1,), (0,)), ((), ())), preferred_element_type=F32)


def mm_nt(left, right):
    return lax.dot_general(left, right, (((1,), (1,)), ((), ())), preferred_element_type=F32)


def gelu_parts(x):
    square = x * x
    t = jnp.tanh(GELU_A * x * (1.0 + GELU_B * square))
    half = 0.5 * (1.0 + t)
    slope = half + 0.5 * x * (1.0 - t * t) * (GELU_A * (1.0 + 3.0 * GELU_B * square))
    return x * half, slope


def gelu(x):
    t = jnp.tanh(GELU_A * x * (1.0 + GELU_B * x * x))
    return 0.5 * x * (1.0 + t)


def over_chunks(rows, lanes, body):
    def some(i, none):
        for r in range(4):
            first = pl.multiple_of(i * (4 * CHUNK[0]) + r * CHUNK[0], CHUNK[0])
            for q in range(0, lanes, CHUNK[1]):
                body(first, pl.ds(first, CHUNK[0]), slice(q, q + CHUNK[1]))
        return none

    lax.fori_loop(0, rows // (4 * CHUNK[0]), some, 0)


def by_group(lanes):
    return [(q, slice(q * LANES - lanes.start, (q + 1) * LANES - lanes.start)) for q in range(lanes.start // LANES, lanes.stop // LANES)]


def stack_ranks(core, own, other):
    first = core == 0
    return jnp.concatenate([jnp.where(first, own, other), jnp.where(first, other, own)], axis=0)


def flipped(values):
    return values.T.astype(BF16)


def fold(grad):
    ranks, wide = grad.shape
    half = wide // 2
    left, right = grad[:, :half], grad[:, half:]
    upper = lax.broadcasted_iota(jnp.int32, (ranks, half), 0) % 8 < 4
    blocks = []
    for pair in (
        jnp.where(upper, left, pltpu.roll(right, 4, 0)),
        jnp.where(upper, pltpu.roll(left, ranks - 4, 0), right),
    ):
        eights = pair.reshape(ranks // 8, 8, half)
        blocks.append(
            jnp.concatenate([eights[:, :, : half // 2], eights[:, :, half // 2 :]], axis=1).astype(BF16)
        )
    return blocks


def put_folded(out, grad):
    first, second = fold(grad)
    out[0] = first
    out[1] = second


def unfold(rows4, wide):
    quarter = wide // 4
    pieces = []
    for at in range(0, rows4.shape[1], quarter):
        here = rows4[:, at : at + quarter]
        pieces += [here[0:4], here[8:12], here[4:8], here[12:16]]
    return pieces


def halves(core, width):
    step = width // 2
    return (
        pl.ds(pl.multiple_of(core * step, 128), step),
        pl.ds(pl.multiple_of((1 - core) * step, 128), step),
    )


def to_core(sources, targets, send_sem, recv_sem):
    return [
        pltpu.make_async_remote_copy(
            src, dst, send_sem.at[i], recv_sem.at[i],
            device_id={"wshard": 1 - lax.axis_index("wshard")}, device_id_type=pl.DeviceIdType.MESH,
        )
        for i, (src, dst) in enumerate(zip(sources, targets))
    ]


def mixer_kernel(
    tokens_ref, ids_ref, table_ref, gain_ref, taps_ref, soft_ref,
    wr_own, sb_own, sr_own, er_own, sd_own, si_own, bd_own, bi_own, ed_own, ei_own,
    *refs, carried,
):
    needed = 10
    first_sources, sources, refs = refs[:needed], refs[needed : needed + carried], refs[needed + carried :]
    (normed_out, picked_br_out, picked_di_out, mixed_out, rate_out, inflow_out, local_out, reach_out,
     ends_out, spans_out, summary_out, onehot_ref, masks_ref), refs = refs[:13], refs[13:]
    first_targets, targets, refs = refs[:needed], refs[needed : needed + carried], refs[needed + carried :]
    arriving, refs = refs[:needed], refs[needed:]
    wr_oth, sb_oth, sr_oth, er_oth, sd_oth, si_oth, bd_oth, bi_oth, ed_oth, ei_oth = arriving
    (normed, picked_r, inner_gate, picked_gate, mixed_all, filt, decay_buf, drive_buf, halo, ids_in,
     first_s, first_r, wr_s, wr_r, keep_sem, halo_s, halo_r, ids_s, ids_r, send_sem, recv_sem) = refs
    core = lax.axis_index("wshard")
    chip = lax.axis_index("seq")
    step = pl.program_id(0)
    rows, width = tokens_ref.shape
    ranks = onehot_ref.shape[1]
    seqs = ids_ref.shape[0]
    steps = rows // seqs
    lane_tiles = pl.num_programs(0) // 2
    tile = mixed_out.shape[1]
    lags = taps_ref.shape[0] - 1

    def rim_copies():
        return [
            pltpu.make_async_remote_copy(
                tokens_ref.at[(s + 1) * steps - 2 * HALO : (s + 1) * steps, :], halo.at[s], halo_s.at[s], halo_r.at[s],
                device_id=ring_peer(1), device_id_type=pl.DeviceIdType.MESH,
            )
            for s in range(seqs)
        ] + [message(ids_ref, ids_in, ids_s, ids_r, slot, by) for slot, by in enumerate((1, -1))]

    def weight_copies(low, high):
        return [
            pltpu.make_async_remote_copy(
                first_sources[i], arriving[i], first_s.at[i - 1], first_r.at[i - 1],
                device_id={"wshard": 1 - core}, device_id_type=pl.DeviceIdType.MESH,
            )
            for i in range(low, high)
        ]

    def wr_copy(piece):
        cols = pl.ds(pl.multiple_of(piece * tile, 128), tile)
        return pltpu.make_async_remote_copy(
            first_sources[0].at[:, cols], wr_oth.at[:, cols], wr_s.at[piece], wr_r.at[piece],
            device_id={"wshard": 1 - core}, device_id_type=pl.DeviceIdType.MESH,
        )

    def kept_copies():
        return [
            pltpu.make_async_copy(src, dst, keep_sem.at[i]) for i, (src, dst) in enumerate(zip(arriving, first_targets))
        ]

    @pl.when(step == 0)
    def _():
        greet([1, -1], True)
        for copy in rim_copies():
            copy.start()
        for copy in weight_copies(1, 4):
            copy.start()
        for piece in range(wr_s.shape[0]):
            wr_copy(piece).start()
        for copy in weight_copies(4, needed):
            copy.start()
        for copy in to_core(sources, targets, send_sem, recv_sem):
            copy.start()
        gain = gain_ref[...]

        def norm(values):
            scale = lax.rsqrt(jnp.mean(values * values, axis=1, keepdims=True) + EPSILON)
            return (values * scale * gain).astype(BF16)

        def some(i, none):
            here = pl.ds(pl.multiple_of(i * 32, 32), 32)
            low = norm(tokens_ref[here, :].astype(F32))
            normed[here, :] = low
            normed_out[here, :] = low
            return none

        lax.fori_loop(0, rows // 32, some, 0)
        for copy in rim_copies():
            copy.wait()
        rim = jnp.concatenate([halo[s].astype(F32)[HALO:, :] for s in range(seqs)], axis=0)
        normed[rows:, :] = norm(jnp.where(chip > 0, rim, 0.0))
        blank = jnp.zeros((steps - seqs, steps), F32)
        upright = lambda ids: jnp.concatenate([ids.astype(F32), blank], axis=0).T
        mine, before, after = upright(ids_ref[...]), upright(ids_in[0]), upright(ids_in[1])
        row = lax.broadcasted_iota(jnp.int32, (steps, steps), 0)
        lane = lax.broadcasted_iota(jnp.int32, (steps, ranks), 1)
        columns = []
        for lag in range(1, lags + 1):
            prior = jnp.where(row < lag, pltpu.roll(before, lag, 0), pltpu.roll(mine, lag, 0))
            inside = jnp.logical_or(row >= lag, chip > 0)
            columns.append(jnp.where(jnp.logical_and(prior == mine, inside), 1.0, 0.0))
        for lag in range(1, lags + 1):
            later = jnp.where(row >= steps - lag, pltpu.roll(after, steps - lag, 0), pltpu.roll(mine, steps - lag, 0))
            inside = jnp.logical_or(row < steps - lag, chip < lax.axis_size("seq") - 1)
            columns.append(jnp.where(jnp.logical_and(later == mine, inside), 1.0, 0.0))

        def owned(ids, s):
            owner = jnp.zeros_like(ids)
            for d in range(table_ref.shape[1]):
                owner = jnp.where(ids == float(d), table_ref[s, d].astype(F32), owner)
            return jnp.where(owner == (lane[: ids.shape[0], :] // RANK).astype(F32), 1.0, 0.0)

        halo_owned = []
        for s in range(seqs):
            here = slice(s * steps, (s + 1) * steps)
            packed = jnp.zeros((steps, ranks), F32)
            for at, column in enumerate(columns):
                packed = jnp.where(lane == at, jnp.broadcast_to(column[:, s : s + 1], (steps, ranks)), packed)
            masks_ref[here, :] = packed
            onehot_ref[here, :] = owned(jnp.broadcast_to(mine[:, s : s + 1], (steps, ranks)), s)
            halo_owned.append(owned(jnp.broadcast_to(before[steps - HALO :, s : s + 1], (HALO, ranks)), s))
        for copy in weight_copies(1, 4):
            copy.wait()
        shrink = jnp.concatenate(
            [stack_ranks(core, sb_own[...], sb_oth[...]), stack_ranks(core, sr_own[...], sr_oth[...])], axis=0
        )
        inner = mm_nt(normed[...], shrink)
        onehot = jnp.concatenate([onehot_ref[...]] + halo_owned, axis=0)
        picked = (inner * jnp.concatenate([onehot, onehot], axis=1)).astype(BF16)
        picked_r[...] = picked[:, ranks:]
        picked_br_out[...] = picked[:rows, :]
        inner_gate[...] = jnp.zeros_like(inner_gate)

    @pl.when(step < lane_tiles)
    def _():
        own, oth = halves(core, width)
        at = pl.multiple_of(step * tile, 128)
        cols = pl.ds(at, tile)
        recur = mm(normed[:, own], wr_own[...]) + mm(
            picked_r[...], stack_ranks(core, er_own[...], er_oth[:, cols])
        )
        wr_copy(step).wait()
        recur = recur + mm(normed[:, oth], wr_oth[:, cols])
        for s in range(seqs):
            filt[s, :HALO, :] = recur[rows + s * HALO : rows + (s + 1) * HALO, :]
            filt[s, HALO:, :] = recur[s * steps : (s + 1) * steps, :]
        for s in range(seqs):
            here = slice(s * steps, (s + 1) * steps)
            total = taps_ref[0:1, :] * filt[s, HALO:, :]
            for lag in range(1, lags + 1):
                earlier = filt[s, HALO - lag : HALO - lag + steps, :]
                total = total + taps_ref[lag : lag + 1, :] * earlier * masks_ref[here, lag - 1 : lag]
            mixed_out[here, :] = total
            mixed_all[here, cols] = total

        @pl.when(step == 0)
        def _():
            for copy in weight_copies(4, needed):
                copy.wait()

        shrink = jnp.concatenate(
            [stack_ranks(core, sd_own[...], sd_oth[:, cols]), stack_ranks(core, si_own[...], si_oth[:, cols])], axis=0
        )
        inner_gate[...] += mm_nt(mixed_out[...].astype(BF16), shrink)

    @pl.when(step == lane_tiles - 1)
    def _():
        for copy in kept_copies():
            copy.start()
        onehot = onehot_ref[...]
        picked = (inner_gate[...] * jnp.concatenate([onehot, onehot], axis=1)).astype(BF16)
        picked_gate[...] = picked
        picked_di_out[...] = picked

    @pl.when(step >= lane_tiles)
    def _():
        at = pl.multiple_of((step - lane_tiles) * tile, 128)
        cols = pl.ds(at, tile)
        low = mixed_all[:, cols].astype(BF16)
        blocks, block = bd_own.shape[0], bd_own.shape[1]
        piece = step - lane_tiles
        mine = piece // (lane_tiles // 2) == core
        local_block = (piece % (lane_tiles // 2)) * blocks
        rates, inflows = [], []
        for b in range(blocks):
            both = jnp.concatenate(
                [jnp.where(mine, bd_own[b], bd_oth[local_block + b]), jnp.where(mine, bi_own[b], bi_oth[local_block + b])],
                axis=1,
            )
            pair = mm(low[:, b * block : (b + 1) * block], both)
            rates.append(pair[:, :block])
            inflows.append(pair[:, block:])
        rate_pre = jnp.concatenate(rates, axis=1) + mm(
            picked_gate[:, :ranks], stack_ranks(core, ed_own[...], ed_oth[:, cols])
        )
        inflow_pre = jnp.concatenate(inflows, axis=1) + mm(
            picked_gate[:, ranks:], stack_ranks(core, ei_own[...], ei_oth[:, cols])
        )
        rate_out[...] = rate_pre
        inflow_out[...] = inflow_pre
        def chain(start, here, lanes):
            rate = jax.nn.sigmoid(rate_out[here, lanes])
            inflow = jax.nn.sigmoid(inflow_out[here, lanes])
            rate_out[here, lanes] = rate
            inflow_out[here, lanes] = inflow
            keep = masks_ref[here, 0:1]
            raw = jnp.exp2(rate * soft_ref[:, lanes])
            bounded = jnp.maximum((1.0 - raw) * (1.0 + raw), ROOT_FLOOR)
            root = keep * (bounded * lax.rsqrt(bounded)) + (1.0 - keep)
            decay = raw * keep
            drive = root * inflow * mixed_all[here, pl.ds(pl.multiple_of(at + lanes.start, 128), CHUNK[1])]
            for q, part in by_group(lanes):
                decay_buf[q, here, :] = decay[:, part]
                drive_buf[q, here, :] = drive[:, part]

        over_chunks(rows, tile, chain)
        seg = steps // SEGS
        for q in range(tile // LANES):
            lanes = slice(q * LANES, (q + 1) * LANES)
            for s in range(seqs):
                at = pl.ds(s * steps, SEGS, stride=seg)
                held, span = drive_buf[q, at, :], decay_buf[q, at, :]
                local_out[q, at, :] = held
                reach_out[q, at, :] = span
                for i in range(1, seg):
                    at = pl.ds(s * steps + i, SEGS, stride=seg)
                    a = decay_buf[q, at, :]
                    held = a * held + drive_buf[q, at, :]
                    span = a * span
                    local_out[q, at, :] = held
                    reach_out[q, at, :] = span
                ends_out[s * SEGS : (s + 1) * SEGS, lanes] = held
                spans_out[s * SEGS : (s + 1) * SEGS, lanes] = span
                total = held[0:1, :]
                product = span[0:1, :]
                for g in range(1, SEGS):
                    total = held[g : g + 1, :] + span[g : g + 1, :] * total
                    product = span[g : g + 1, :] * product
                summary_out[s : s + 1, lanes] = product
                summary_out[seqs + s : seqs + s + 1, lanes] = total

    @pl.when(step == 2 * lane_tiles - 1)
    def _():
        for copy in kept_copies():
            copy.wait()
        for copy in to_core(sources, targets, send_sem, recv_sem):
            copy.wait()


def ring_peer(by):
    peers = lax.axis_size("seq")
    return {"seq": (lax.axis_index("seq") + by + peers) % peers}


def greet(shifts, with_core, chips=()):
    barrier = pltpu.get_barrier_semaphore()
    peers = [ring_peer(by) for by in shifts] + [{"seq": chip} for chip in chips]
    if with_core:
        peers.append({"wshard": 1 - lax.axis_index("wshard")})
    for peer in peers:
        pl.semaphore_signal(barrier, inc=1, device_id=peer, device_id_type=pl.DeviceIdType.MESH)
    pl.semaphore_wait(barrier, len(peers))


def message(src, inbox, send_sem, recv_sem, slot, by):
    return pltpu.make_async_remote_copy(
        src, inbox.at[slot], send_sem.at[slot], recv_sem.at[slot],
        device_id=ring_peer(by), device_id_type=pl.DeviceIdType.MESH,
    )


def arrived(inbox, seqs, lanes, valid):
    value = None
    for d in range(inbox.shape[0], 0, -1):
        total = jnp.where(valid(d), inbox[d - 1, seqs : 2 * seqs, lanes], 0.0)
        if value is not None:
            total = total + jnp.where(valid(d), inbox[d - 1, :seqs, lanes], 0.0) * value
        value = total
    return value


def branch_output_kernel(
    summary_ref, normed_ref, picked_ref, wb_own, wb_oth, eb_own, eb_oth,
    local_ref, reach_ref, ends_ref, spans_ref, tokens_ref, onehot_ref, gain_ref,
    wo_own, wo_oth, so_own, so_oth, eo_own, eo_oth,
    *refs, carried,
):
    sources, refs = refs[:carried], refs[carried:]
    (pre_out, state_out, merged_out, carry_out, residual_out, second_out, picked_out), refs = refs[:7], refs[7:]
    targets, refs = refs[:carried], refs[carried:]
    branch_all, acc, inner, inbox, send_sem, recv_sem, core_s, core_r = refs
    core = lax.axis_index("wshard")
    step = pl.program_id(0)
    count = pl.num_programs(0) // 2
    hops = inbox.shape[0]
    groups, rows, _ = local_ref.shape
    tile = pre_out.shape[1]
    seqs = ends_ref.shape[0] // SEGS
    seg = rows // (seqs * SEGS)

    @pl.when(step == 0)
    def _():
        greet([d for d in range(1, hops + 1)] + [-d for d in range(1, hops + 1)], True)
        for copy in to_core(sources, targets, core_s, core_r):
            copy.start()
        for d in range(1, hops + 1):
            message(summary_ref, inbox, send_sem, recv_sem, d - 1, d).start()
        acc[...] = jnp.zeros_like(acc)
        inner[...] = jnp.zeros_like(inner)

    @pl.when(step < count)
    def _():
        own, oth = halves(core, normed_ref.shape[1])
        pre = (
            mm(normed_ref[:, own], wb_own[...])
            + mm(normed_ref[:, oth], wb_oth[...])
            + mm(picked_ref[...], stack_ranks(core, eb_own[...], eb_oth[...]))
        )
        pre_out[...] = pre
        branch_all[:, pl.ds(pl.multiple_of(step * tile, 128), tile)] = gelu(pre)

    @pl.when(step == count)
    def _():
        for d in range(1, hops + 1):
            copy = message(summary_ref, inbox, send_sem, recv_sem, d - 1, d)
            copy.wait_send()
            copy.wait_recv()

    @pl.when(step >= count)
    def _():
        at = pl.multiple_of((step - count) * tile, 128)
        start = arrived(inbox, seqs, pl.ds(at, tile), lambda d: lax.axis_index("seq") >= d)
        carry_out[...] = jnp.concatenate([start, jnp.zeros_like(start)], axis=0)
        for s in range(seqs):
            carry = start[s : s + 1, :]
            for g in range(SEGS):
                row = s * SEGS + g
                here = slice(row * seg, (row + 1) * seg)
                state = jnp.concatenate([local_ref[q, here, :] for q in range(groups)], axis=1) + (
                    jnp.concatenate([reach_ref[q, here, :] for q in range(groups)], axis=1) * carry
                )
                state_out[here, :] = state
                merged_out[here, :] = (branch_all[here, pl.ds(at, tile)] * state).astype(BF16)
                carry = ends_ref[row : row + 1, :] + spans_ref[row : row + 1, :] * carry
        merged = merged_out[...]
        mine = (step - count) // (count // 2) == core

        @pl.when(mine)
        def _():
            acc[...] += mm(merged, wo_own[...])

        @pl.when(jnp.logical_not(mine))
        def _():
            acc[...] += mm(merged, wo_oth[...])

        inner[...] += mm_nt(merged, stack_ranks(core, so_own[...], so_oth[...]))

    @pl.when(step == 2 * count - 1)
    def _():
        picked = (inner[...] * onehot_ref[...]).astype(BF16)
        picked_out[...] = picked
        residual = (
            tokens_ref[...].astype(F32)
            + acc[...]
            + mm(picked, stack_ranks(core, eo_own[...], eo_oth[...]))
        )
        residual_out[...] = residual
        scale = lax.rsqrt(jnp.mean(residual * residual, axis=1, keepdims=True) + EPSILON)
        second_out[...] = (residual * scale * gain_ref[...]).astype(BF16)
        for copy in to_core(sources, targets, core_s, core_r):
            copy.wait()


def feed_kernel(
    core_ref, second_ref, cot_ref, residual_ref, onehot_ref, gain_ref,
    g_own_a, g_own_b, g_oth_a, g_oth_b, u_own_a, u_own_b, u_oth_a, u_oth_b, d_own, d_oth,
    sg_own, sg_oth, su_own, su_oth, eg_own_a, eg_own_b, eg_oth_a, eg_oth_b,
    eu_own_a, eu_own_b, eu_oth_a, eu_oth_b, sd_own_a, sd_own_b, sd_oth_a, sd_oth_b, ed_own, ed_oth,
    out_ref, grad_residual_out, grad_low_out, deg_out, deu_out, dsd_out, dsg_out, dsu_out, ded_out,
    picked, picked_t, gi_down, gi_down_t, down_acc, inner_down, grad_second, gi_gate,
):
    core = core_ref[0]
    step = pl.program_id(0)
    ranks = onehot_ref.shape[1]
    width = second_ref.shape[1]
    part = d_own.shape[0]
    own, oth = halves(core, width)

    @pl.when(step == 0)
    def _():
        onehot = onehot_ref[...]
        shrink = jnp.concatenate(
            [stack_ranks(core, sg_own[...], sg_oth[...]), stack_ranks(core, su_own[...], su_oth[...])], axis=0
        )
        both = mm_nt(second_ref[...], shrink) * jnp.concatenate([onehot, onehot], axis=1)
        picked[...] = both.astype(BF16)
        picked_t[...] = flipped(both)
        inner = mm_nt(cot_ref[...], stack_ranks(core, ed_own[...], ed_oth[...])) * onehot
        gi_down[...] = inner.astype(BF16)
        gi_down_t[...] = flipped(inner)
        down_acc[...] = jnp.zeros_like(down_acc)
        inner_down[...] = jnp.zeros_like(inner_down)
        grad_second[...] = jnp.zeros_like(grad_second)
        gi_gate[...] = jnp.zeros_like(gi_gate)

    join = lambda a, b: jnp.concatenate([a[...], b[...]], axis=1)
    g_own, g_oth = join(g_own_a, g_own_b), join(g_oth_a, g_oth_b)
    u_own, u_oth = join(u_own_a, u_own_b), join(u_oth_a, u_oth_b)
    down = jnp.concatenate([d_own[...], d_oth[...]], axis=0)
    eg = stack_ranks(core, join(eg_own_a, eg_own_b), join(eg_oth_a, eg_oth_b))
    eu = stack_ranks(core, join(eu_own_a, eu_own_b), join(eu_oth_a, eu_oth_b))
    sd = stack_ranks(core, join(sd_own_a, sd_own_b), join(sd_oth_a, sd_oth_b))

    x_own, x_oth = second_ref[:, own], second_ref[:, oth]
    gating = mm(x_own, g_own) + mm(x_oth, g_oth) + mm(picked[:, :ranks], eg)
    upward = mm(x_own, u_own) + mm(x_oth, u_oth) + mm(picked[:, ranks:], eu)
    grad_hidden = mm_nt(cot_ref[...], down) + mm(gi_down[...], sd)
    smooth, slope = gelu_parts(gating)
    hidden = (smooth * upward).astype(BF16)
    grad_gating = (grad_hidden * upward * slope).astype(BF16)
    grad_upward = (grad_hidden * smooth).astype(BF16)
    down_acc[...] += mm(hidden, down)
    inner_down[...] += mm_nt(hidden, sd)
    grad_second[:, own] += mm_nt(grad_gating, g_own) + mm_nt(grad_upward, u_own)
    grad_second[:, oth] += mm_nt(grad_gating, g_oth) + mm_nt(grad_upward, u_oth)
    gi_gate[:, :ranks] += mm_nt(grad_gating, eg)
    gi_gate[:, ranks:] += mm_nt(grad_upward, eu)
    for out, grad in (
        (deg_out, mm(picked_t[:ranks, :], grad_gating)),
        (deu_out, mm(picked_t[ranks:, :], grad_upward)),
        (dsd_out, mm(gi_down_t[...], hidden)),
    ):
        low, high = grad[:, :part], grad[:, part:]
        first = core == 0
        put_folded(
            out, jnp.concatenate([jnp.where(first, low, high), jnp.where(first, high, low)], axis=1)
        )

    @pl.when(step == pl.num_programs(0) - 1)
    def _():
        onehot = onehot_ref[...]
        chosen = inner_down[...] * onehot
        residual = residual_ref[...]
        out_ref[...] = (
            residual + down_acc[...] + mm(chosen.astype(BF16), stack_ranks(core, ed_own[...], ed_oth[...]))
        ).astype(BF16)
        put_folded(ded_out, mm(flipped(chosen), cot_ref[...]))
        inner = gi_gate[...] * jnp.concatenate([onehot, onehot], axis=1)
        shrink = jnp.concatenate(
            [stack_ranks(core, sg_own[...], sg_oth[...]), stack_ranks(core, su_own[...], su_oth[...])], axis=0
        )
        grads = mm(flipped(inner), second_ref[...])
        put_folded(dsg_out, grads[:ranks, :])
        put_folded(dsu_out, grads[ranks:, :])
        weighted = (grad_second[...] + mm(inner.astype(BF16), shrink)) * gain_ref[...]
        scale = lax.rsqrt(jnp.mean(residual * residual, axis=1, keepdims=True) + EPSILON)
        grad = (
            cot_ref[...].astype(F32)
            + scale * weighted
            - residual * (scale * scale * scale * jnp.mean(weighted * residual, axis=1, keepdims=True))
        )
        grad_residual_out[...] = grad
        grad_low_out[...] = grad.astype(BF16)


FEED_ORDER = (("eg", 0), ("eu", 1), ("sdn", 0), ("sg", 1), ("su", 1), ("edn", 1))
MIXER_ORDER = (
    ("eo", 0), ("so", 1), ("eb", 0), ("sb", 1),
    ("edec", 0), ("einf", 1), ("sdec", 0), ("sinf", 1), ("er", 0), ("sr", 1),
)


class Links:
    def __init__(self):
        self.core = lax.axis_index("wshard")
        chip = lax.axis_index("seq")
        self.x, self.y, self.z = chip % 2, (chip // 2) % 2, chip // 4
        self.x_peer = chip + 1 - 2 * self.x
        self.y_peer = chip + 2 - 4 * self.y
        self.z_peers = [((self.z + d) % 4) * 4 + chip % 4 for d in (1, 2, 3)]

    def chips(self):
        return [self.x_peer, self.y_peer] + self.z_peers

    def copy(self, src, dst, send, recv, device):
        return pltpu.make_async_remote_copy(
            src, dst, send, recv, device_id=device, device_id_type=pl.DeviceIdType.MESH
        )

    def across(self, src, core_in, cols, send, recv):
        return self.copy(src, core_in.at[:, :, cols], send, recv, {"wshard": 1 - self.core})

    def first(self, send1, recv1, cols, direction, send, recv):
        peer = self.x_peer if direction == 0 else self.y_peer
        return self.copy(send1.at[:, :, cols], recv1.at[:, :, cols], send, recv, {"seq": peer})

    def second(self, send2, recv2, cols, direction, send, recv):
        peer = self.y_peer if direction == 0 else self.x_peer
        return self.copy(send2.at[:, :, cols], recv2.at[:, :, cols], send, recv, {"seq": peer})

    def third(self, send3, recv3, cols, send, recv, index):
        return [
            self.copy(
                send3.at[d, :, cols], recv3.at[d, :, cols], send.at[index, d], recv.at[index, d], {"seq": self.z_peers[d]}
            )
            for d in range(3)
        ]

    def split_first(self, own, core_in, kept, send1, own_cols, cols, direction):
        for p in range(4):
            for o in range(2):
                keep = p * 4 + (o * 2 + self.x if direction == 0 else self.y * 2 + o)
                give = p * 4 + (o * 2 + 1 - self.x if direction == 0 else (1 - self.y) * 2 + o)
                at = p * 2 + o
                if kept is not None:
                    kept[at, :, cols] = own[keep, :, own_cols].astype(F32) + core_in[keep, :, cols].astype(F32)
                send1[at, :, cols] = (
                    own[give, :, own_cols].astype(F32) + core_in[give, :, cols].astype(F32)
                ).astype(BF16)

    def split_second(self, own, core_in, recv1, kept2, send2, cols, direction):
        for p in range(4):
            at = p * 2 + (self.y if direction == 0 else self.x)
            keep = p * 4 + self.y * 2 + self.x
            kept2[p, :, cols] = (
                own[keep, :, cols].astype(F32) + core_in[keep, :, cols].astype(F32) + recv1[at, :, cols].astype(F32)
            )
            at = p * 2 + 1 - (self.y if direction == 0 else self.x)
            give = p * 4 + ((1 - self.y) * 2 + self.x if direction == 0 else self.y * 2 + 1 - self.x)
            send2[p, :, cols] = (
                own[give, :, cols].astype(F32) + core_in[give, :, cols].astype(F32) + recv1[at, :, cols].astype(F32)
            ).astype(BF16)

    def split_third(self, kept2, recv2, send3, out, cols, out_cols):
        out[:, out_cols] = kept2[self.z, :, cols] + recv2[self.z, :, cols].astype(F32)
        for d in range(3):
            to = (self.z + d + 1) % 4
            send3[d, :, cols] = (kept2[to, :, cols] + recv2[to, :, cols].astype(F32)).astype(BF16)

    def finish(self, recv3, out, cols, out_cols):
        out[:, out_cols] += (
            recv3[0, :, cols].astype(F32) + recv3[1, :, cols].astype(F32) + recv3[2, :, cols].astype(F32)
        )


def columns_of(sizes):
    return [pl.ds(sum(sizes[:i]), n) for i, n in enumerate(sizes)]


def last_kernel(grad_ref, residual_ref, tokens_ref, gain_ref, *refs, sizes, runs, split):
    if sizes:
        sums_ref, refs = refs[0], refs[1:]
    out_ref, outs = refs[0], refs[1:]
    weighted = grad_ref[...] * gain_ref[...]
    values = tokens_ref[...].astype(F32)
    scale = lax.rsqrt(jnp.mean(values * values, axis=1, keepdims=True) + EPSILON)
    out_ref[...] = (
        residual_ref[...]
        + scale * weighted
        - values * (scale * scale * scale * jnp.mean(weighted * values, axis=1, keepdims=True))
    )

    @pl.when(pl.program_id(0) == 0)
    def _():
        offset = 0
        for out, size, run, two in zip(outs, sizes, runs, split):
            pieces = unfold(sums_ref[:, offset : offset + size], run)
            if two:
                pieces = [p for i, p in enumerate(pieces) if i % 4 < 2] + [p for i, p in enumerate(pieces) if i % 4 >= 2]
            out[...] = jnp.concatenate(pieces, axis=1)
            offset += size


def scatter_plain(grads, runs, split):
    summed = {}
    for k, g in grads.items():
        quarter = runs[k] // 4
        g = g.astype(F32).reshape(2, g.shape[1], 4, 4, g.shape[3] // quarter, quarter)
        g = g[:, :, jnp.array([0, 2, 1, 3])]
        if k in split:
            g = g.reshape(g.shape[:2] + (2, 2) + g.shape[3:]).transpose(1, 0, 4, 2, 5, 3, 6)
        else:
            g = g.transpose(1, 0, 3, 4, 2, 5)
        g = g.reshape(g.shape[0] * 8, -1)
        summed[k] = lax.psum_scatter(g, ("seq", "wshard"), scatter_dimension=0, tiled=True)
    return summed


def branch_back_kernel(
    low_ref, onehot_ref, masks_ref, soft_ref, picked_ref, pre_ref, state_ref, merged_ref, rate_ref,
    wo_own, wo_oth, so_own, so_oth, eo_own, eo_oth,
    normed_ref, picked_b_ref, eb_own, eb_oth,
    *refs, feed_sizes, reduce,
):
    count_feed = len(feed_sizes)
    feed, refs = refs[:count_feed], refs[count_feed:]
    (grad_state_out, ends_out, spans_out, start_out, pre_grad_out, gi_b_out, dso_out, deo_out, dsb_out, deb_out), refs = (
        refs[:10], refs[10:]
    )
    if reduce:
        half_out, refs = refs[0], refs[1:]
    (gi, gi_t, decay_buf, grad_buf, pre_grad, summary, inbox, send_sem, recv_sem), refs = refs[:9], refs[9:]
    core = lax.axis_index("wshard")
    step = pl.program_id(0)
    count = pl.num_programs(0) - 1
    hops = inbox.shape[0]
    rows, tile = pre_ref.shape
    seqs = ends_out.shape[0] // SEGS
    steps = rows // seqs
    seg = steps // SEGS
    shifts = [d for d in range(1, hops + 1)] + [-d for d in range(1, hops + 1)]
    if reduce:
        own, core_in, send1, recv1, local_sem, core_s, core_r, s1_s, s1_r = refs
        cols = columns_of(feed_sizes)
        order = [d for _, d in FEED_ORDER]

    @pl.when(step == 0)
    def _():
        if reduce:
            links = Links()
            greet(shifts, True, links.chips())
            for a in range(count_feed):
                links.across(feed[a].at[1 - core], core_in, cols[a], core_s.at[a], core_r.at[a]).start()
                pltpu.make_async_copy(feed[a].at[core], own.at[:, :, cols[a]], local_sem.at[a]).start()
        else:
            greet(shifts, False)
        grad = mm_nt(low_ref[...], stack_ranks(core, eo_own[...], eo_oth[...])) * onehot_ref[...]
        gi[...] = grad.astype(BF16)
        gi_t[...] = flipped(grad)
        put_folded(deo_out, mm(flipped(picked_ref[...].astype(F32)), low_ref[...]))

    if reduce:

        @pl.when(step == 1)
        def _():
            links = Links()
            for a in range(count_feed):
                pltpu.make_async_copy(feed[a].at[core], own.at[:, :, cols[a]], local_sem.at[a]).wait()
                links.across(feed[a].at[1 - core], core_in, cols[a], core_s.at[a], core_r.at[a]).wait()
                links.split_first(own, core_in, half_out, send1, cols[a], cols[a], order[a])
                links.first(send1, recv1, cols[a], order[a], s1_s.at[a], s1_r.at[a]).start()

    @pl.when(step < count)
    def _():
        at = pl.multiple_of(step * tile, 128)
        mine = step // (count // 2) == core

        @pl.when(mine)
        def _():
            grad_buf[...] = mm_nt(low_ref[...], wo_own[...])

        @pl.when(jnp.logical_not(mine))
        def _():
            grad_buf[...] = mm_nt(low_ref[...], wo_oth[...])

        grad_buf[...] += mm(gi[...], stack_ranks(core, so_own[...], so_oth[...]))
        put_folded(dso_out, mm(gi_t[...], merged_ref[...]))
        def chain(start, here, lanes):
            grad_merged = grad_buf[here, lanes]
            smooth, slope = gelu_parts(pre_ref[here, lanes])
            pre = (grad_merged * state_ref[here, lanes] * slope).astype(BF16)
            pre_grad[here, pl.ds(pl.multiple_of(at + lanes.start, 128), CHUNK[1])] = pre
            pre_grad_out[here, lanes] = pre
            grad_state = grad_merged * smooth
            decay = jnp.exp2(rate_ref[here, lanes] * soft_ref[:, lanes]) * masks_ref[here, 0:1]
            for q, part in by_group(lanes):
                grad_state_out[q, here, :] = grad_state[:, part]
                decay_buf[q, here, :] = decay[:, part]

        over_chunks(rows, tile, chain)
        for q in range(tile // LANES):
            lanes = slice(q * LANES, (q + 1) * LANES)
            wide = pl.ds(pl.multiple_of(at + q * LANES, 128), LANES)
            for s in range(seqs):
                held = grad_state_out[q, pl.ds(s * steps + seg - 1, SEGS, stride=seg), :]
                span = None
                for i in range(seg - 2, -1, -1):
                    a = decay_buf[q, pl.ds(s * steps + i + 1, SEGS, stride=seg), :]
                    held = a * held + grad_state_out[q, pl.ds(s * steps + i, SEGS, stride=seg), :]
                    span = a if span is None else a * span
                a = decay_buf[q, pl.ds(s * steps, SEGS, stride=seg), :]
                held = a * held
                span = a * span
                ends_out[s * SEGS : (s + 1) * SEGS, lanes] = held
                spans_out[s * SEGS : (s + 1) * SEGS, lanes] = span
                total = held[SEGS - 1 : SEGS, :]
                product = span[SEGS - 1 : SEGS, :]
                for g in range(SEGS - 2, -1, -1):
                    total = held[g : g + 1, :] + span[g : g + 1, :] * total
                    product = span[g : g + 1, :] * product
                summary[s : s + 1, wide] = product
                summary[seqs + s : seqs + s + 1, wide] = total

    @pl.when(step == count)
    def _():
        for d in range(1, hops + 1):
            message(summary, inbox, send_sem, recv_sem, d - 1, -d).start()
        picked_t = flipped(picked_b_ref[...].astype(F32))
        expand = stack_ranks(core, eb_own[...], eb_oth[...])
        grad = mm_nt(pre_grad[...], expand) * onehot_ref[...]
        gi_b_out[...] = grad.astype(BF16)
        put_folded(dsb_out, mm(flipped(grad), normed_ref[...]))
        for piece in range(pre_grad.shape[1] // tile):
            first, second = fold(mm(picked_t, pre_grad[:, piece * tile : (piece + 1) * tile]))
            lanes = slice(piece * tile // 4, (piece + 1) * tile // 4)
            deb_out[0, :, :, lanes] = first
            deb_out[1, :, :, lanes] = second
        for d in range(1, hops + 1):
            copy = message(summary, inbox, send_sem, recv_sem, d - 1, -d)
            copy.wait_send()
            copy.wait_recv()
        peers = lax.axis_size("seq")
        start = arrived(inbox, seqs, slice(None), lambda d: lax.axis_index("seq") + d < peers)
        start_out[...] = jnp.concatenate([start, jnp.zeros_like(start)], axis=0)
        if reduce:
            links = Links()
            for a in range(count_feed):
                links.first(send1, recv1, cols[a], order[a], s1_s.at[a], s1_r.at[a]).wait()
                for at in range(half_out.shape[0]):
                    half_out[at, :, cols[a]] += recv1[at, :, cols[a]].astype(F32)


def recur_back_kernel(
    grad_state_ref, ends_ref, spans_ref, start_ref, carry_ref, state_ref, mixed_ref, rate_ref, inflow_ref,
    masks_ref, onehot_ref, soft_ref, picked_ref,
    bd_own, bd_oth, bi_own, bi_oth, ed_own, ed_oth, ei_own, ei_oth, sd_own, sd_oth, si_own, si_oth,
    taps_ref, normed_ref, picked_r_ref, er_own, er_oth,
    wr_own, wr_oth, sr_own, sr_oth, pre_grad_ref, gi_b_ref, wb_own, wb_oth, sb_own, sb_oth,
    *refs, feed_sizes, mixer_sizes, reduce,
):
    if reduce:
        half_ref, early_grads, refs = refs[0], refs[1:5], refs[5:]
        out_ref, sums_out, refs = refs[0], refs[1], refs[2:]
    else:
        out_ref, late_outs, refs = refs[0], refs[1:7], refs[7:]
    (decay_buf, flow_buf, partial, inner, gi, gi_t, picked_t, filt, low, inner_r, picked_rt, heads, inbox,
     head_s, head_r, rate_grad, inflow_grad), refs = refs[:17], refs[17:]
    core = lax.axis_index("wshard")
    step = pl.program_id(0)
    count = pl.num_programs(0) // 4
    groups = grad_state_ref.shape[0]
    rows, tile = state_ref.shape
    ranks = onehot_ref.shape[1]
    seqs = ends_ref.shape[0] // SEGS
    steps = rows // seqs
    seg = steps // SEGS
    lags = taps_ref.shape[0] - 1
    order = [d for _, d in MIXER_ORDER]

    if reduce:
        (kept2_f, send2_f, recv2_f, send3_f, recv3_f, f2_s, f2_r, f3_s, f3_r,
         mine_g, core_in, send1, recv1, kept2, send2, recv2, send3, recv3,
         local_sem, core_s, core_r, s1_s, s1_r, s2_s, s2_r, s3_s, s3_r) = refs
        fcols = columns_of(feed_sizes)
        forder = [d for _, d in FEED_ORDER]
        mcols = columns_of(mixer_sizes)
        base = sum(feed_sizes)
        sums_cols = [pl.ds(base + sum(mixer_sizes[:i]), n) for i, n in enumerate(mixer_sizes)]

        def feed_second(links):
            for a in range(len(feed_sizes)):
                mine = links.y if forder[a] == 0 else links.x
                for p in range(4):
                    kept2_f[p, :, fcols[a]] = half_ref[p * 2 + mine, :, fcols[a]]
                    send2_f[p, :, fcols[a]] = half_ref[p * 2 + 1 - mine, :, fcols[a]].astype(BF16)
                links.second(send2_f, recv2_f, fcols[a], forder[a], f2_s.at[a], f2_r.at[a]).start()

        def feed_third(links):
            for a in range(len(feed_sizes)):
                links.second(send2_f, recv2_f, fcols[a], forder[a], f2_s.at[a], f2_r.at[a]).wait()
                links.split_third(kept2_f, recv2_f, send3_f, sums_out, fcols[a], fcols[a])
                for copy in links.third(send3_f, recv3_f, fcols[a], f3_s, f3_r, a):
                    copy.start()

        def feed_finish(links):
            for a in range(len(feed_sizes)):
                for copy in links.third(send3_f, recv3_f, fcols[a], f3_s, f3_r, a):
                    copy.wait()
                links.finish(recv3_f, sums_out, fcols[a], fcols[a])

        def cross(links, which):
            for a in which:
                if a < 4:
                    pltpu.make_async_copy(
                        early_grads[a].at[core], mine_g.at[core, :, :, mcols[a]], local_sem.at[a]
                    ).start()
                    src = early_grads[a].at[1 - core]
                else:
                    src = mine_g.at[1 - core, :, :, mcols[a]]
                links.across(src, core_in, mcols[a], core_s.at[a], core_r.at[a]).start()

        def first(links, which):
            for a in which:
                if a < 4:
                    pltpu.make_async_copy(
                        early_grads[a].at[core], mine_g.at[core, :, :, mcols[a]], local_sem.at[a]
                    ).wait()
                    src = early_grads[a].at[1 - core]
                else:
                    src = mine_g.at[1 - core, :, :, mcols[a]]
                links.across(src, core_in, mcols[a], core_s.at[a], core_r.at[a]).wait()
                links.split_first(mine_g.at[core], core_in, None, send1, mcols[a], mcols[a], order[a])
                links.first(send1, recv1, mcols[a], order[a], s1_s.at[a], s1_r.at[a]).start()

        def second(links, which):
            for a in which:
                links.first(send1, recv1, mcols[a], order[a], s1_s.at[a], s1_r.at[a]).wait()
                links.split_second(mine_g.at[core], core_in, recv1, kept2, send2, mcols[a], order[a])
                links.second(send2, recv2, mcols[a], order[a], s2_s.at[a], s2_r.at[a]).start()

        def third(links, which):
            for a in which:
                links.second(send2, recv2, mcols[a], order[a], s2_s.at[a], s2_r.at[a]).wait()
                links.split_third(kept2, recv2, send3, sums_out, mcols[a], sums_cols[a])
                for copy in links.third(send3, recv3, mcols[a], s3_s, s3_r, a):
                    copy.start()

        def finish(links, which):
            for a in which:
                for copy in links.third(send3, recv3, mcols[a], s3_s, s3_r, a):
                    copy.wait()
                links.finish(recv3, sums_out, mcols[a], sums_cols[a])

        A, B, C, D = (0, 1, 2, 3), (4, 5), (6, 7), (8, 9)
        plan = {
            0: [(feed_second, None), (cross, A)],
            1: [(first, A)],
            2: [(feed_third, None)],
            3: [(second, A)],
            4: [(cross, B), (third, A)],
            6: [(first, B)],
            8: [(cross, C)],
            10: [(first, C), (second, B)],
            12: [(cross, D), (third, B), (feed_finish, None)],
            13: [(first, D), (second, C), (finish, A)],
            15: [(third, C), (second, D), (finish, B)],
        }
        tail = [(third, D), (finish, C), (finish, D)]

        def run(links, what):
            for action, which in what:
                action(links) if which is None else action(links, which)

        def late_grad(index, grad, piece=None):
            width = grad.shape[1] // 4
            start = sum(mixer_sizes[:index])
            if piece is None:
                at = pl.ds(start, width)
            else:
                at = pl.ds(pl.multiple_of(start + piece * width, 128), width)
            for half, block in enumerate(fold(grad)):
                mine_g[half, :, :, at] = block

    else:

        def late_grad(index, grad, piece=None):
            put_folded(late_outs[index - 4], grad)

    @pl.when(step == 0)
    def _():
        if reduce:
            greet([1, -1], True, Links().chips())
        else:
            greet([1, -1], False)
        inner[...] = jnp.zeros_like(inner)
        inner_r[...] = jnp.zeros_like(inner_r)
        picked_t[...] = flipped(picked_ref[...].astype(F32))
        picked_rt[...] = flipped(picked_r_ref[...].astype(F32))

    if reduce:
        for at_step, what in plan.items():

            @pl.when(step == at_step)
            def _(what=what):
                run(Links(), what)

    def head_copy(slot):
        return pltpu.make_async_remote_copy(
            heads.at[slot], inbox.at[slot], head_s.at[slot], head_r.at[slot],
            device_id=ring_peer(-1), device_id_type=pl.DeviceIdType.MESH,
        )

    @pl.when(step < count)
    def _():
        def chain(start, here, lanes):
            decay = jnp.exp2(rate_ref[here, lanes] * soft_ref[:, lanes]) * masks_ref[here, 0:1]
            for q, part in by_group(lanes):
                decay_buf[q, here, :] = decay[:, part]

        over_chunks(rows, tile, chain)
        for s in range(seqs):
            carry = start_ref[s : s + 1, :]
            carries = [carry]
            for g in range(SEGS - 1, 0, -1):
                row = s * SEGS + g
                carry = ends_ref[row : row + 1, :] + spans_ref[row : row + 1, :] * carry
                carries.append(carry)
            entering = jnp.concatenate(carries[::-1], axis=0)
            for q in range(groups):
                at = pl.ds(s * steps + seg - 1, SEGS, stride=seg)
                flow = grad_state_ref[q, at, :] + entering[:, q * LANES : (q + 1) * LANES]
                flow_buf[q, at, :] = flow
                for i in range(seg - 2, -1, -1):
                    a = decay_buf[q, pl.ds(s * steps + i + 1, SEGS, stride=seg), :]
                    at = pl.ds(s * steps + i, SEGS, stride=seg)
                    flow = a * flow + grad_state_ref[q, at, :]
                    flow_buf[q, at, :] = flow
        top = lax.broadcasted_iota(jnp.int32, CHUNK, 0) == 0
        def chain(start, here, lanes):
            before = jnp.where(
                start % steps == 0,
                carry_ref[pl.ds(start // steps, 1), lanes],
                state_ref[pl.ds(jnp.maximum(start - 1, 0), 1), lanes],
            )
            prior = jnp.where(top, before, pltpu.roll(state_ref[here, lanes], 1, 0))
            backflow = jnp.concatenate([flow_buf[q, here, :] for q, _ in by_group(lanes)], axis=1)
            decay = jnp.concatenate([decay_buf[q, here, :] for q, _ in by_group(lanes)], axis=1)
            rate = rate_ref[here, lanes]
            inflow = inflow_ref[here, lanes]
            mixed = mixed_ref[here, lanes]
            soft = soft_ref[:, lanes]
            keep = masks_ref[here, 0:1]
            raw = jnp.exp2(rate * soft)
            spread = (1.0 - raw) * (1.0 + raw)
            bounded = jnp.maximum(spread, ROOT_FLOOR)
            inverse = lax.rsqrt(bounded)
            root = keep * (bounded * inverse) + (1.0 - keep)
            pulled = backflow * inflow
            through = pulled * root
            grad_spread = jnp.where(spread > ROOT_FLOOR, pulled * mixed * (inverse * keep), 0.0)
            grad_log = backflow * prior * decay - raw * raw * grad_spread
            rate_grad[here, lanes] = (grad_log * (soft * (1.0 / LOG2_E)) * rate * (1.0 - rate)).astype(BF16)
            inflow_grad[here, lanes] = (through * mixed * (1.0 - inflow)).astype(BF16)
            partial[here, pl.ds(pl.multiple_of(step * tile + lanes.start, 128), CHUNK[1])] = through

        over_chunks(rows, tile, chain)
        grad_rate, grad_inflow = rate_grad[...], inflow_grad[...]
        blocks, block = bd_own.shape[0], bd_own.shape[1]
        mine = step // (count // 2) == core
        pieces = []
        for b in range(blocks):
            lanes = slice(b * block, (b + 1) * block)
            both = jnp.concatenate(
                [jnp.where(mine, bd_own[b], bd_oth[b]), jnp.where(mine, bi_own[b], bi_oth[b])], axis=1
            )
            pieces.append(mm_nt(jnp.concatenate([grad_rate[:, lanes], grad_inflow[:, lanes]], axis=1), both))
        partial[:, pl.ds(pl.multiple_of(step * tile, 128), tile)] += jnp.concatenate(pieces, axis=1)
        inner[:, :ranks] += mm_nt(grad_rate, stack_ranks(core, ed_own[...], ed_oth[...]))
        inner[:, ranks:] += mm_nt(grad_inflow, stack_ranks(core, ei_own[...], ei_oth[...]))
        late_grad(4, mm(picked_t[:ranks, :], grad_rate), step)
        late_grad(5, mm(picked_t[ranks:, :], grad_inflow), step)

    @pl.when(step == count - 1)
    def _():
        onehot = onehot_ref[...]
        chosen = inner[...] * jnp.concatenate([onehot, onehot], axis=1)
        gi[...] = chosen.astype(BF16)
        gi_t[...] = flipped(chosen)

    @pl.when(jnp.logical_and(step >= count, step < 2 * count))
    def _():
        piece = step - count
        at = pl.multiple_of(piece * tile, 128)
        shrink = jnp.concatenate(
            [stack_ranks(core, sd_own[...], sd_oth[...]), stack_ranks(core, si_own[...], si_oth[...])], axis=0
        )
        grad = partial[:, pl.ds(at, tile)] + mm(gi[...], shrink)
        partial[:, pl.ds(at, tile)] = grad
        for s in range(seqs):
            heads[piece, s * HALO : (s + 1) * HALO, :] = grad[s * steps : s * steps + HALO, :]
        both = mm(gi_t[...], mixed_ref[...].astype(BF16))
        late_grad(6, both[:ranks, :], piece)
        late_grad(7, both[ranks:, :], piece)
        head_copy(piece).start()

    @pl.when(jnp.logical_and(step >= 2 * count, step < 3 * count))
    def _():
        piece = step - 2 * count
        at = pl.multiple_of(piece * tile, 128)
        head_copy(piece).wait()
        for s in range(seqs):
            filt[s, :steps, :] = partial[s * steps : (s + 1) * steps, pl.ds(at, tile)]
            filt[s, steps:, :] = inbox[piece, s * HALO : (s + 1) * HALO, :]
        for s in range(seqs):
            here = slice(s * steps, (s + 1) * steps)
            total = taps_ref[0:1, :] * filt[s, :steps, :]
            for lag in range(1, lags + 1):
                later = filt[s, lag : lag + steps, :]
                total = total + taps_ref[lag : lag + 1, :] * later * masks_ref[here, lags + lag - 1 : lags + lag]
            low[piece, here, :] = total.astype(BF16)
        grad = low[piece]
        inner_r[...] += mm_nt(grad, stack_ranks(core, er_own[...], er_oth[...]))
        late_grad(8, mm(picked_rt[...], grad), piece)

    @pl.when(step == 3 * count - 1)
    def _():
        chosen = inner_r[...] * onehot_ref[...]
        late_grad(9, mm(flipped(chosen), normed_ref[...]))
        out_ref[...] = mm(chosen.astype(BF16), stack_ranks(core, sr_own[...], sr_oth[...])) + mm(
            gi_b_ref[...], stack_ranks(core, sb_own[...], sb_oth[...])
        )

    @pl.when(step >= 3 * count)
    def _():
        left, right = halves(core, out_ref.shape[1])
        recur_grad, branch_grad = low[step - 3 * count], pre_grad_ref[...]
        out_ref[:, left] += mm_nt(recur_grad, wr_own[...]) + mm_nt(branch_grad, wb_own[...])
        out_ref[:, right] += mm_nt(recur_grad, wr_oth[...]) + mm_nt(branch_grad, wb_oth[...])

    if reduce:

        @pl.when(step == 4 * count - 1)
        def _():
            run(Links(), tail)


def indexed(shape, index, scalars):
    if scalars:
        return pl.BlockSpec(shape, index)
    return pl.BlockSpec(shape, lambda j: index(j, None))


def call(kernel, name, grid, core, ins, outs, scratch, flops, nbytes, collective=None):
    scalars = core is not None

    def still(shape):
        zeros = (0,) * len(shape)
        if scalars:
            return pl.BlockSpec(shape, lambda j, c: zeros, pipeline_mode=pl.Buffered(1))
        return pl.BlockSpec(shape, lambda j: zeros, pipeline_mode=pl.Buffered(1))

    in_specs, arrays = [], []
    for item in ins:
        if isinstance(item, tuple) and len(item) == 1:
            arrays.append(item[0])
            in_specs.append(pl.BlockSpec(memory_space=pl.ANY))
        elif isinstance(item, tuple) and len(item) == 2:
            arrays.append(item[0])
            in_specs.append(pl.BlockSpec(memory_space=item[1]))
        elif isinstance(item, tuple):
            arrays.append(item[0])
            in_specs.append(indexed(item[1], item[2], scalars))
        else:
            arrays.append(item)
            in_specs.append(still(item.shape))
    out_specs, shapes = [], []
    for item in outs:
        shapes.append(jax.ShapeDtypeStruct(item[0], item[1]))
        if len(item) == 3:
            out_specs.append(pl.BlockSpec(memory_space=pl.ANY))
        else:
            out_specs.append(indexed(item[2], item[3], scalars) if len(item) == 4 else still(item[0]))
    return pl.pallas_call(
        kernel,
        grid_spec=pltpu.PrefetchScalarGridSpec(
            num_scalar_prefetch=int(scalars), grid=(grid,), in_specs=in_specs, out_specs=out_specs, scratch_shapes=scratch
        ),
        out_shape=shapes,
        name=name,
        compiler_params=pltpu.CompilerParams(
            dimension_semantics=("arbitrary",), vmem_limit_bytes=67043328, collective_id=collective,
            has_side_effects=collective is not None,
        ),
        cost_estimate=pl.CostEstimate(flops=flops, bytes_accessed=nbytes, transcendentals=0),
    )(*([core] if scalars else []), *arrays)


def local(
    tokens, segment_ids, document_adapter, out_cotangent, mixer_gain, feed_gain, filter_taps, decay_param, *weights
):
    core = lax.axis_index("wshard").astype(jnp.int32).reshape(1)
    anywhere = pl.ANY
    at_once = (1, 8, 10, 11, 12, 14, 2, 3, 13, 15)
    with_mixer = (0, 9, 16, 17, 4, 5, 18, 19, 20, 21, 22, 23)
    with_branch = (6, 7)
    other = {}
    pair = lambda i: (weights[i], other[i])
    wr, sb, sr, er, sdec, sinf, bd, bi, edec, einf = [weights[i] for i in at_once]
    seqs, steps, width = tokens.shape
    rows = seqs * steps
    lru = filter_taps.shape[1]
    lags = filter_taps.shape[0] - 1
    ranks = 2 * sb.shape[0]
    feed = weights[5].shape[1]
    peers = lax.axis_size("seq")
    reach = peers // 4

    soft = (jax.nn.softplus(-decay_param) * (-RATE_SCALE * LOG2_E))[None, :]
    gain_first = mixer_gain[None, :]
    gain_second = feed_gain[None, :]
    tokens2 = tokens.reshape(rows, width)
    cot = out_cotangent.reshape(rows, width)

    tile = TILE
    count = lru // tile
    half = width // 2
    blocks = tile // bd.shape[1]
    block = bd.shape[1]
    early = lambda j: jnp.minimum(j, count - 1)
    late = lambda j: jnp.maximum(j - count, 0)
    flat = lambda r, at: ((r, tile), lambda j, c: (0, at(j)))

    def tiled(array, r, at):
        block_shape, index = flat(r, at)
        return (array, block_shape, index)

    def tiled_out(r, dtype, at, total=None):
        block_shape, index = flat(r, at)
        return ((r, total or lru), dtype, block_shape, index)

    lane_groups = tile // LANES

    def grouped(array, index):
        return (array, (lane_groups, rows, LANES), index)

    def grouped_out(at):
        return ((lru // LANES, rows, LANES), F32, (lane_groups, rows, LANES), lambda j, c: (at(j), 0, 0))

    def both(pair, r, at):
        return [tiled(pair[0], r, at), tiled(pair[1], r, at)]

    def gate_blocks(pair, at):
        index = lambda j, c: (at(j) % (count // 2), 0, 0)
        return [(pair[0], (blocks, block, block), index), (pair[1], (blocks, block, block), index)]

    half_ranks = ranks // 2
    ident = lambda j: j
    groups = seqs * SEGS
    def gate_half(array, at):
        return (array, (blocks, block, block), lambda j, c: (at(j) % (count // 2), 0, 0))

    dma = pltpu.SemaphoreType.DMA
    vm = lambda *shape: pltpu.VMEM(shape, BF16)
    vf = lambda *shape: pltpu.VMEM(shape, F32)
    with jax.named_scope("mixer_forward"):
        (normed, picked_br, picked_di, mixed, rate, inflow, held, span, ends, spans, summary, onehot_own, masks, *moved) = call(
            functools.partial(mixer_kernel, carried=len(with_mixer)), "mixer_forward", 2 * count, None,
            [tokens2, segment_ids, (document_adapter, pltpu.SMEM), gain_first, tiled(filter_taps, lags + 1, early), tiled(soft, 1, late),
             tiled(wr, half, early), sb, sr, tiled(er, half_ranks, early),
             tiled(sdec, half_ranks, early), tiled(sinf, half_ranks, early), gate_half(bd, late), gate_half(bi, late),
             tiled(edec, half_ranks, late), tiled(einf, half_ranks, late)]
            + [(weights[i],) for i in at_once + with_mixer],
            [((rows, width), BF16), ((rows, 2 * ranks), BF16), ((rows, 2 * ranks), BF16),
             tiled_out(rows, F32, early), tiled_out(rows, F32, late), tiled_out(rows, F32, late),
             grouped_out(late), grouped_out(late),
             tiled_out(groups, F32, late), tiled_out(groups, F32, late), tiled_out(2 * seqs, F32, late),
             ((rows, ranks), F32), ((rows, ranks), F32)]
            + [(weights[i].shape, BF16, anywhere) for i in at_once + with_mixer],
            [vm(*weights[i].shape) for i in at_once]
            + [vm(rows + seqs * HALO, width), vm(rows + seqs * HALO, ranks), vf(rows, 2 * ranks), vm(rows, 2 * ranks),
               vf(rows, lru), vf(seqs, steps + HALO, tile), vf(lane_groups, rows, LANES), vf(lane_groups, rows, LANES),
               vm(seqs, 2 * HALO, width), pltpu.VMEM((2, seqs, steps), jnp.int32),
               dma((len(at_once) - 1,)), dma((len(at_once) - 1,)), dma((count,)), dma((count,)), dma((len(at_once),)),
               dma((seqs,)), dma((seqs,)), dma((2,)), dma((2,)), dma((len(with_mixer),)), dma((len(with_mixer),))],
            int(6e9), int(30e6), collective=2,
        )
    other.update(zip(at_once + with_mixer, moved))
    wr, bd, bi, sb, sr, er, sdec, edec, sinf, einf = [pair(i) for i in (1, 2, 3, 8, 10, 11, 12, 13, 14, 15)]
    wb, eb, so, eo, wo, wg = pair(0), pair(9), pair(16), pair(17), pair(4), pair(5)
    sg, eg, su, eu, sdn, edn = [pair(i) for i in (18, 19, 20, 21, 22, 23)]
    own_rows = lambda pair, at: [
        (pair[0], (tile, width), lambda j, c: (at(j) % (count // 2), 0)),
        (pair[1], (tile, width), lambda j, c: (at(j) % (count // 2), 0)),
    ]
    with jax.named_scope("branch_and_output_forward"):
        branch_pre, state, merged, carry, residual, second, picked_o, *moved = call(
            functools.partial(branch_output_kernel, carried=len(with_branch)), "branch_output_forward", 2 * count, None,
            [summary, normed, (picked_br, (rows, ranks), lambda j, c: (0, 0))] + both(wb, half, early)
            + both(eb, half_ranks, early)
            + [grouped(held, lambda j, c: (late(j), 0, 0)), grouped(span, lambda j, c: (late(j), 0, 0)),
               tiled(ends, groups, late), tiled(spans, groups, late), tokens2, onehot_own, gain_second]
            + own_rows(wo, late) + both(so, half_ranks, late) + list(eo) + [(weights[i],) for i in with_branch],
            [tiled_out(rows, F32, early), tiled_out(rows, F32, late), tiled_out(rows, BF16, late),
             tiled_out(2 * seqs, F32, late), ((rows, width), F32), ((rows, width), BF16), ((rows, ranks), BF16)]
            + [(weights[i].shape, BF16, anywhere) for i in with_branch],
            [pltpu.VMEM((rows, lru), F32), pltpu.VMEM((rows, width), F32), pltpu.VMEM((rows, ranks), F32),
             pltpu.VMEM((reach, 2 * seqs, lru), F32), pltpu.SemaphoreType.DMA((reach,)), pltpu.SemaphoreType.DMA((reach,)),
             pltpu.SemaphoreType.DMA((len(with_branch),)), pltpu.SemaphoreType.DMA((len(with_branch),))],
            int(8e9), int(45e6), collective=1,
        )
    other.update(zip(with_branch, moved))
    wu, wd = pair(6), pair(7)

    part = 256
    pieces = feed // (2 * part)

    def feed_cols(pair_item, r):
        return [
            (pair_item, (r, part), lambda j, c: (0, c[0] * pieces + j)),
            (pair_item, (r, part), lambda j, c: (0, (1 - c[0]) * pieces + j)),
        ]

    def feed_pair(pair, r):
        return feed_cols(pair[0], r) + feed_cols(pair[1], r)

    chips = ranks // 8
    grad_cols = ((2, chips, 16, feed // 4), BF16, (2, chips, 16, part // 2), lambda j, c: (0, 0, 0, j))
    grad_whole = ((2, chips, 16, width // 4), BF16)

    def grad_tile(at):
        return ((2, chips, 16, lru // 4), BF16, (2, chips, 16, tile // 4), lambda j, c: (0, 0, 0, at(j)))

    with jax.named_scope("feed_forward_both_ways"):
        result, grad_residual, grad_low, deg, deu, dsdn, dsg, dsu, dedn = call(
            feed_kernel, "feed_both_ways", pieces, core,
            [second, cot, residual, onehot_own, gain_second] + feed_pair(wg, half) + feed_pair(wu, half)
            + [(wd[0], (part, width), lambda j, c: (j, 0)), (wd[1], (part, width), lambda j, c: (j, 0))]
            + list(sg) + list(su) + feed_pair(eg, half_ranks) + feed_pair(eu, half_ranks)
            + feed_pair(sdn, half_ranks) + list(edn),
            [((rows, width), BF16), ((rows, width), F32), ((rows, width), BF16),
             grad_cols, grad_cols, grad_cols, grad_whole, grad_whole, grad_whole],
            [pltpu.VMEM((rows, 2 * ranks), BF16), pltpu.VMEM((2 * ranks, rows), BF16),
             pltpu.VMEM((rows, ranks), BF16), pltpu.VMEM((ranks, rows), BF16),
             pltpu.VMEM((rows, width), F32), pltpu.VMEM((rows, ranks), F32), pltpu.VMEM((rows, width), F32),
             pltpu.VMEM((rows, 2 * ranks), F32)],
            int(50e9), int(60e6),
        )

    split = ("eg", "eu", "sdn")
    runs = dict(sb=width, eb=tile, sr=width, er=tile, sdec=tile, edec=tile, sinf=tile, einf=tile, so=tile, eo=width,
                sg=width, eg=2 * part, su=width, eu=2 * part, sdn=2 * part, edn=width)
    reduce = peers == 16 and ranks == 128
    grads = dict(eg=deg, eu=deu, sdn=dsdn, sg=dsg, su=dsu, edn=dedn)
    size_of = lambda k: (width if k in ("eo", "sb", "sr", "sg", "su", "edn") else feed if k in split else lru) // 4
    feed_sizes = [size_of(k) for k, _ in FEED_ORDER]
    mixer_sizes = [size_of(k) for k, _ in MIXER_ORDER]
    feed_grads = [(grads[k],) for k, _ in FEED_ORDER] if reduce else []
    wide, narrow = sum(feed_sizes), sum(mixer_sizes)
    dma = pltpu.SemaphoreType.DMA
    vm = lambda *shape: pltpu.VMEM(shape, BF16)
    vf = lambda *shape: pltpu.VMEM(shape, F32)
    nf, nm = len(feed_sizes), len(mixer_sizes)

    with jax.named_scope("output_and_branch_backward"):
        (grad_state, bends, bspans, bstart, pre_grad, gi_b, dso, deo, dsb, deb, *halved) = call(
            functools.partial(branch_back_kernel, feed_sizes=feed_sizes if reduce else [], reduce=reduce),
            "output_branch_backward", count + 1, None,
            [grad_low, onehot_own, masks, tiled(soft, 1, early), picked_o, tiled(branch_pre, rows, early),
             tiled(state, rows, early), tiled(merged, rows, early), tiled(rate, rows, early)]
            + own_rows(wo, early) + both(so, half_ranks, early) + list(eo)
            + [normed, (picked_br, (rows, ranks), lambda j, c: (0, 0))]
            + list(eb) + feed_grads,
            [grouped_out(early), tiled_out(groups, F32, early), tiled_out(groups, F32, early),
             ((2 * seqs, lru), F32), tiled_out(rows, BF16, early), ((rows, ranks), BF16),
             grad_tile(early), grad_whole, grad_whole, ((2, chips, 16, lru // 4), BF16)]
            + ([((8, 16, wide), F32)] if reduce else []),
            [vm(rows, ranks), vm(ranks, rows), vf(lane_groups, rows, LANES), vf(rows, tile),
             vm(rows, lru), vf(2 * seqs, lru), vf(reach, 2 * seqs, lru), dma((reach,)), dma((reach,))]
            + ([vm(16, 16, wide), vm(16, 16, wide), vm(8, 16, wide), vm(8, 16, wide)] + [dma((nf,))] * 5 if reduce else []),
            int(10e9), int(50e6), collective=3,
        )
    early_grads = dict(eo=deo, so=dso, eb=deb, sb=dsb)
    grads.update(early_grads)
    third = 3
    first_of = lambda j: jnp.minimum(j, count - 1)
    middle = lambda j: jnp.clip(j - count, 0, count - 1)
    last = lambda j: jnp.clip(j - 2 * count, 0, count - 1)
    dense = lambda j: jnp.clip(j - 3 * count, 0, count - 1)
    twice = lambda j: jnp.where(j < count, j, jnp.clip(j - count, 0, count - 1))
    with jax.named_scope("gates_and_recur_backward"):
        grad_normed, *late = call(
            functools.partial(recur_back_kernel, feed_sizes=feed_sizes, mixer_sizes=mixer_sizes, reduce=reduce),
            "gates_recur_backward", 4 * count, None,
            [grouped(grad_state, lambda j, c: (first_of(j), 0, 0)), tiled(bends, groups, first_of), tiled(bspans, groups, first_of),
             tiled(bstart, 2 * seqs, first_of), tiled(carry, 2 * seqs, first_of), tiled(state, rows, first_of),
             tiled(mixed, rows, twice), tiled(rate, rows, first_of), tiled(inflow, rows, first_of),
             masks, onehot_own, tiled(soft, 1, first_of), picked_di]
            + gate_blocks(bd, first_of) + gate_blocks(bi, first_of)
            + both(edec, half_ranks, first_of) + both(einf, half_ranks, first_of)
            + both(sdec, half_ranks, middle) + both(sinf, half_ranks, middle)
            + [tiled(filter_taps, lags + 1, last), normed, (picked_br, (rows, ranks), lambda j, c: (0, 1)),
               *both(er, half_ranks, last)]
            + both(wr, half, dense) + list(sr) + [tiled(pre_grad, rows, dense), gi_b] + both(wb, half, dense) + list(sb)
            + ([halved[0]] + [(early_grads[k],) for k, _ in MIXER_ORDER[:4]] if reduce else []),
            [((rows, width), F32)]
            + ([((16, wide + narrow), F32)] if reduce else
               [grad_tile(first_of), grad_tile(first_of), grad_tile(middle), grad_tile(middle), grad_tile(last), grad_whole]),
            [vf(lane_groups, rows, LANES), vf(lane_groups, rows, LANES), vf(rows, lru), vf(rows, 2 * ranks),
             vm(rows, 2 * ranks), vm(2 * ranks, rows), vm(2 * ranks, rows), vf(seqs, steps + HALO, tile), vm(count, rows, tile),
             vf(rows, ranks), vm(ranks, rows), vf(count, seqs * HALO, tile), vf(count, seqs * HALO, tile),
             dma((count,)), dma((count,)), vm(rows, tile), vm(rows, tile)]
            + ([vf(4, 16, wide), vm(4, 16, wide), vm(4, 16, wide), vm(3, 16, wide), vm(3, 16, wide),
                dma((nf,)), dma((nf,)), dma((nf, 3)), dma((nf, 3)),
                vm(2, 16, 16, narrow), vm(16, 16, narrow), vm(8, 16, narrow), vm(8, 16, narrow),
                vf(4, 16, narrow), vm(4, 16, narrow), vm(4, 16, narrow), vm(3, 16, narrow), vm(3, 16, narrow)]
               + [dma((nm,))] * 7 + [dma((nm, 3))] * 2 if reduce else []),
            int(10e9), int(50e6), collective=4,
        )

    names = ("sb", "eb", "sr", "er", "sdec", "edec", "sinf", "einf", "so", "eo", "sg", "eg", "su", "eu", "sdn", "edn")
    all_names = [k for k, _ in FEED_ORDER + MIXER_ORDER] if reduce else []
    all_sizes = feed_sizes + mixer_sizes if reduce else []
    by_rows = lambda array: (array, (steps, width), lambda j, c: (j, 0))
    with jax.named_scope("first_norm_backward"):
        grad_tokens, *sums = call(
            functools.partial(
                last_kernel, sizes=all_sizes, runs=[runs[k] for k in all_names], split=[k in split for k in all_names]
            ),
            "first_norm_backward", seqs, None,
            [by_rows(grad_normed), by_rows(grad_residual), by_rows(tokens2), gain_first] + late[: int(reduce)],
            [((rows, width), F32, (steps, width), lambda j, c: (j, 0))] + [((4, 4 * n), F32) for n in all_sizes],
            [], int(1e7), int(11e6),
        )
    with jax.named_scope("factor_gradients"):
        if reduce:
            summed = dict(zip(all_names, sums))
        else:
            grads.update(zip([k for k, _ in MIXER_ORDER[4:]], late))
            summed = scatter_plain(grads, runs, split)
    return (result.reshape(seqs, steps, width), grad_tokens.reshape(seqs, steps, width)) + tuple(
        summed[k] for k in names
    )


def solution(mesh):
    split = P("wshard", None)
    in_specs = (
        (P("wshard", "seq", None), P("wshard", "seq"), split, P("wshard", "seq", None))
        + (P(),) * 4
        + (split, split, P("wshard", None, None), P("wshard", None, None))
        + (split,) * 20
    )
    out_specs = (P("wshard", "seq", None),) * 2 + (P(("seq", "wshard"), None),) * 16
    return jax.shard_map(local, mesh=mesh, in_specs=in_specs, out_specs=out_specs, check_vma=False)
```

```python
import functools

import jax
import jax.numpy as jnp
from jax import lax
from jax.experimental import pallas as pl
from jax.experimental.pallas import tpu as pltpu
from jax.sharding import PartitionSpec as P

RANK = 16
EPSILON = 1e-06
RATE_SCALE = 8.0
ROOT_FLOOR = 0.001
GELU_A = 0.7978845608028654
GELU_B = 0.044715
LOG2_E = 1.4426950408889634
CHUNK = (16, 256)

HALO = 8
SEGS = 8
TILE = 512
LANES = 128
F32 = jnp.float32
BF16 = jnp.bfloat16


def mm(left, right):
    return lax.dot_general(left, right, (((1,), (0,)), ((), ())), preferred_element_type=F32)


def mm_nt(left, right):
    return lax.dot_general(left, right, (((1,), (1,)), ((), ())), preferred_element_type=F32)


def gelu_parts(x):
    square = x * x
    t = jnp.tanh(GELU_A * x * (1.0 + GELU_B * square))
    half = 0.5 * (1.0 + t)
    slope = half + 0.5 * x * (1.0 - t * t) * (GELU_A * (1.0 + 3.0 * GELU_B * square))
    return x * half, slope


def gelu(x):
    t = jnp.tanh(GELU_A * x * (1.0 + GELU_B * x * x))
    return 0.5 * x * (1.0 + t)


def interleave(steps, back=False):
    a = lax.broadcasted_iota(jnp.int32, (steps, steps), 0)
    b = lax.broadcasted_iota(jnp.int32, (steps, steps), 1)
    if back:
        a, b = b, a
    return jnp.where(b == (a % SEGS) * (steps // SEGS) + a // SEGS, 1.0, 0.0).astype(BF16)


def per_sequence(seqs, body):
    def one(s, none):
        body(s)
        return none

    lax.fori_loop(0, seqs, one, 0)


def row_at(start, offset, size):
    return pl.ds(pl.multiple_of(start + offset, size), size)


def shift_in(rows8, edge, down):
    row = lax.broadcasted_iota(jnp.int32, rows8.shape, 0)
    if down:
        return jnp.where(row == 0, edge, pltpu.roll(rows8, 1, 0))
    return jnp.where(row == SEGS - 1, edge, pltpu.roll(rows8, SEGS - 1, 0))


def stack_ranks(core, own, other):
    first = core == 0
    return jnp.concatenate([jnp.where(first, own, other), jnp.where(first, other, own)], axis=0)


def flipped(values):
    return values.T.astype(BF16)


def fold(grad):
    ranks, wide = grad.shape
    half = wide // 2
    left, right = grad[:, :half], grad[:, half:]
    upper = lax.broadcasted_iota(jnp.int32, (ranks, half), 0) % 8 < 4
    blocks = []
    for pair in (
        jnp.where(upper, left, pltpu.roll(right, 4, 0)),
        jnp.where(upper, pltpu.roll(left, ranks - 4, 0), right),
    ):
        eights = pair.reshape(ranks // 8, 8, half)
        blocks.append(
            jnp.concatenate([eights[:, :, : half // 2], eights[:, :, half // 2 :]], axis=1).astype(BF16)
        )
    return blocks


def put_folded(out, grad):
    first, second = fold(grad)
    out[0] = first
    out[1] = second


def unfold(rows4, wide):
    quarter = wide // 4
    pieces = []
    for at in range(0, rows4.shape[1], quarter):
        here = rows4[:, at : at + quarter]
        pieces += [here[0:4], here[8:12], here[4:8], here[12:16]]
    return pieces


def halves(core, width):
    step = width // 2
    return (
        pl.ds(pl.multiple_of(core * step, 128), step),
        pl.ds(pl.multiple_of((1 - core) * step, 128), step),
    )


def to_core(sources, targets, send_sem, recv_sem):
    return [
        pltpu.make_async_remote_copy(
            src, dst, send_sem.at[i], recv_sem.at[i],
            device_id={"wshard": 1 - lax.axis_index("wshard")}, device_id_type=pl.DeviceIdType.MESH,
        )
        for i, (src, dst) in enumerate(zip(sources, targets))
    ]


def mixer_kernel(
    tokens_ref, ids_ref, table_ref, gain_ref, taps_ref, soft_ref,
    wr_own, sb_own, sr_own, er_own, sd_own, si_own, bd_own, bi_own, ed_own, ei_own,
    *refs, carried,
):
    needed = 10
    first_sources, sources, refs = refs[:needed], refs[needed : needed + carried], refs[needed + carried :]
    (normed_out, picked_br_out, picked_di_out, mixed_out, rate_out, inflow_out, local_out, reach_out,
     ends_out, spans_out, summary_out, onehot_ref, masks_ref, tokens_out), refs = refs[:14], refs[14:]
    first_targets, targets, refs = refs[:needed], refs[needed : needed + carried], refs[needed + carried :]
    arriving, refs = refs[:needed], refs[needed:]
    wr_oth, sb_oth, sr_oth, er_oth, sd_oth, si_oth, bd_oth, bi_oth, ed_oth, ei_oth = arriving
    (normed, picked_r, inner_gate, picked_gate, mixed_all, filt, halo, ids_in,
     first_s, first_r, wr_s, wr_r, keep_sem, halo_s, halo_r, ids_s, ids_r, send_sem, recv_sem) = refs
    core = lax.axis_index("wshard")
    chip = lax.axis_index("seq")
    step = pl.program_id(0)
    rows, width = tokens_ref.shape
    ranks = onehot_ref.shape[1]
    seqs = ids_ref.shape[0]
    steps = rows // seqs
    lane_tiles = pl.num_programs(0) // 2
    tile = mixed_out.shape[1]
    lags = taps_ref.shape[0] - 1

    def rim_copies():
        return [
            pltpu.make_async_remote_copy(
                tokens_ref.at[(s + 1) * steps - 2 * HALO : (s + 1) * steps, :], halo.at[s], halo_s.at[s], halo_r.at[s],
                device_id=ring_peer(1), device_id_type=pl.DeviceIdType.MESH,
            )
            for s in range(seqs)
        ] + [message(ids_ref, ids_in, ids_s, ids_r, slot, by) for slot, by in enumerate((1, -1))]

    def weight_copies(low, high):
        return [
            pltpu.make_async_remote_copy(
                first_sources[i], arriving[i], first_s.at[i - 1], first_r.at[i - 1],
                device_id={"wshard": 1 - core}, device_id_type=pl.DeviceIdType.MESH,
            )
            for i in range(low, high)
        ]

    def wr_copy(piece):
        cols = pl.ds(pl.multiple_of(piece * tile, 128), tile)
        return pltpu.make_async_remote_copy(
            first_sources[0].at[:, cols], wr_oth.at[:, cols], wr_s.at[piece], wr_r.at[piece],
            device_id={"wshard": 1 - core}, device_id_type=pl.DeviceIdType.MESH,
        )

    def kept_copies():
        return [
            pltpu.make_async_copy(src, dst, keep_sem.at[i]) for i, (src, dst) in enumerate(zip(arriving, first_targets))
        ]

    @pl.when(step == 0)
    def _():
        greet([1, -1], True)
        for copy in rim_copies():
            copy.start()
        for copy in weight_copies(1, 4):
            copy.start()
        for piece in range(wr_s.shape[0]):
            wr_copy(piece).start()
        for copy in weight_copies(4, needed):
            copy.start()
        for copy in to_core(sources, targets, send_sem, recv_sem):
            copy.start()
        gain = gain_ref[0:1, :width]

        def norm(values):
            scale = lax.rsqrt(jnp.mean(values * values, axis=1, keepdims=True) + EPSILON)
            return (values * scale * gain).astype(BF16)

        order = interleave(steps)
        for s in range(seqs):
            here = slice(s * steps, (s + 1) * steps)
            tokens_out[here, :] = mm(order, tokens_ref[here, :]).astype(BF16)

        def some(i, none):
            here = pl.ds(pl.multiple_of(i * 32, 32), 32)
            low = norm(tokens_out[here, :].astype(F32))
            normed[here, :] = low
            normed_out[here, :] = low
            return none

        lax.fori_loop(0, rows // 32, some, 0)
        for copy in rim_copies():
            copy.wait()
        rim = jnp.concatenate([halo[s].astype(F32)[HALO:, :] for s in range(seqs)], axis=0)
        normed[rows:, :] = norm(jnp.where(chip > 0, rim, 0.0))
        blank = jnp.zeros((steps - seqs, steps), F32)
        upright = lambda ids: jnp.concatenate([ids.astype(F32), blank], axis=0).T
        mine, before, after = upright(ids_ref[...]), upright(ids_in[0]), upright(ids_in[1])
        row = lax.broadcasted_iota(jnp.int32, (steps, steps), 0)
        lane = lax.broadcasted_iota(jnp.int32, (steps, ranks), 1)
        columns = []
        for lag in range(1, lags + 1):
            prior = jnp.where(row < lag, pltpu.roll(before, lag, 0), pltpu.roll(mine, lag, 0))
            inside = jnp.logical_or(row >= lag, chip > 0)
            columns.append(jnp.where(jnp.logical_and(prior == mine, inside), 1.0, 0.0))
        for lag in range(1, lags + 1):
            later = jnp.where(row >= steps - lag, pltpu.roll(after, steps - lag, 0), pltpu.roll(mine, steps - lag, 0))
            inside = jnp.logical_or(row < steps - lag, chip < lax.axis_size("seq") - 1)
            columns.append(jnp.where(jnp.logical_and(later == mine, inside), 1.0, 0.0))

        def owned(ids, s):
            owner = jnp.zeros_like(ids)
            for d in range(table_ref.shape[1]):
                owner = jnp.where(ids == float(d), table_ref[s, d].astype(F32), owner)
            return jnp.where(owner == (lane[: ids.shape[0], :] // RANK).astype(F32), 1.0, 0.0)

        halo_owned = []
        for s in range(seqs):
            here = slice(s * steps, (s + 1) * steps)
            packed = jnp.zeros((steps, ranks), F32)
            for at, column in enumerate(columns):
                packed = jnp.where(lane == at, jnp.broadcast_to(column[:, s : s + 1], (steps, ranks)), packed)
            masks_ref[here, :] = mm(order, packed.astype(BF16))
            onehot_ref[here, :] = mm(order, owned(jnp.broadcast_to(mine[:, s : s + 1], (steps, ranks)), s).astype(BF16))
            halo_owned.append(owned(jnp.broadcast_to(before[steps - HALO :, s : s + 1], (HALO, ranks)), s))
        for copy in weight_copies(1, 4):
            copy.wait()
        shrink = jnp.concatenate(
            [stack_ranks(core, sb_own[...], sb_oth[...]), stack_ranks(core, sr_own[...], sr_oth[...])], axis=0
        )
        inner = mm_nt(normed[...], shrink)
        onehot = jnp.concatenate([onehot_ref[...]] + halo_owned, axis=0)
        picked = (inner * jnp.concatenate([onehot, onehot], axis=1)).astype(BF16)
        picked_r[...] = picked[:, ranks:]
        picked_br_out[...] = picked[:rows, :]
        inner_gate[...] = jnp.zeros_like(inner_gate)

    @pl.when(step < lane_tiles)
    def _():
        own, oth = halves(core, width)
        at = pl.multiple_of(step * tile, 128)
        cols = pl.ds(at, tile)
        recur = mm(normed[:, own], wr_own[...]) + mm(
            picked_r[...], stack_ranks(core, er_own[...], er_oth[:, cols])
        )
        wr_copy(step).wait()
        recur = recur + mm(normed[:, oth], wr_oth[:, cols])
        filt[...] = recur
        seg = steps // SEGS

        def filtered(s):
            start = s * steps
            at_run = lambda i: filt[row_at(start, i * SEGS, SEGS), :]
            rim = filt[row_at(rows + s * HALO, 0, HALO), :]
            runs = {-lag: shift_in(at_run(seg - lag), rim[HALO - lag : HALO - lag + 1, :], True) for lag in range(1, lags + 1)}
            for i in range(seg):
                here = row_at(start, i * SEGS, SEGS)
                runs[i] = at_run(i)
                total = taps_ref[0:1, :] * runs[i]
                for lag in range(1, lags + 1):
                    total = total + taps_ref[lag : lag + 1, :] * runs[i - lag] * masks_ref[here, lag - 1 : lag]
                mixed_out[here, :] = total
                mixed_all[here, cols] = total

        per_sequence(seqs, filtered)

        @pl.when(step == 0)
        def _():
            for copy in weight_copies(4, needed):
                copy.wait()

        shrink = jnp.concatenate(
            [stack_ranks(core, sd_own[...], sd_oth[:, cols]), stack_ranks(core, si_own[...], si_oth[:, cols])], axis=0
        )
        inner_gate[...] += mm_nt(mixed_out[...].astype(BF16), shrink)

    @pl.when(step == lane_tiles - 1)
    def _():
        for copy in kept_copies():
            copy.start()
        onehot = onehot_ref[...]
        picked = (inner_gate[...] * jnp.concatenate([onehot, onehot], axis=1)).astype(BF16)
        picked_gate[...] = picked
        picked_di_out[...] = picked

    @pl.when(step >= lane_tiles)
    def _():
        at = pl.multiple_of((step - lane_tiles) * tile, 128)
        cols = pl.ds(at, tile)
        low = mixed_all[:, cols].astype(BF16)
        blocks, block = bd_own.shape[0], bd_own.shape[1]
        piece = step - lane_tiles
        mine = piece // (lane_tiles // 2) == core
        local_block = (piece % (lane_tiles // 2)) * blocks
        rates, inflows = [], []
        for b in range(blocks):
            both = jnp.concatenate(
                [jnp.where(mine, bd_own[b], bd_oth[local_block + b]), jnp.where(mine, bi_own[b], bi_oth[local_block + b])],
                axis=1,
            )
            pair = mm(low[:, b * block : (b + 1) * block], both)
            rates.append(pair[:, :block])
            inflows.append(pair[:, block:])
        rate_pre = jnp.concatenate(rates, axis=1) + mm(
            picked_gate[:, :ranks], stack_ranks(core, ed_own[...], ed_oth[:, cols])
        )
        inflow_pre = jnp.concatenate(inflows, axis=1) + mm(
            picked_gate[:, ranks:], stack_ranks(core, ei_own[...], ei_oth[:, cols])
        )
        rate_out[...] = rate_pre
        inflow_out[...] = inflow_pre
        seg = steps // SEGS

        def scanned(s):
            held = span = None
            for i in range(seg):
                here = row_at(s * steps, i * SEGS, SEGS)
                rate = jax.nn.sigmoid(rate_out[here, :])
                inflow = jax.nn.sigmoid(inflow_out[here, :])
                rate_out[here, :] = rate
                inflow_out[here, :] = inflow
                keep = masks_ref[here, 0:1]
                raw = jnp.exp2(rate * soft_ref[2:3, :])
                bounded = jnp.maximum((1.0 - raw) * (1.0 + raw), ROOT_FLOOR)
                root = keep * (bounded * lax.rsqrt(bounded)) + (1.0 - keep)
                decay = raw * keep
                drive = root * inflow * mixed_all[here, cols]
                held = drive if held is None else decay * held + drive
                span = decay if span is None else decay * span
                local_out[here, :] = held
                reach_out[here, :] = span
            ends_out[row_at(s * SEGS, 0, SEGS), :] = held
            spans_out[row_at(s * SEGS, 0, SEGS), :] = span
            total, product = held[0:1, :], span[0:1, :]
            for g in range(1, SEGS):
                total = held[g : g + 1, :] + span[g : g + 1, :] * total
                product = span[g : g + 1, :] * product
            summary_out[pl.ds(s, 1), :] = product
            summary_out[pl.ds(seqs + s, 1), :] = total

        per_sequence(seqs, scanned)

    @pl.when(step == 2 * lane_tiles - 1)
    def _():
        for copy in kept_copies():
            copy.wait()
        for copy in to_core(sources, targets, send_sem, recv_sem):
            copy.wait()


def ring_peer(by):
    peers = lax.axis_size("seq")
    return {"seq": (lax.axis_index("seq") + by + peers) % peers}


def greet(shifts, with_core, chips=()):
    barrier = pltpu.get_barrier_semaphore()
    peers = [ring_peer(by) for by in shifts] + [{"seq": chip} for chip in chips]
    if with_core:
        peers.append({"wshard": 1 - lax.axis_index("wshard")})
    for peer in peers:
        pl.semaphore_signal(barrier, inc=1, device_id=peer, device_id_type=pl.DeviceIdType.MESH)
    pl.semaphore_wait(barrier, len(peers))


def message(src, inbox, send_sem, recv_sem, slot, by):
    return pltpu.make_async_remote_copy(
        src, inbox.at[slot], send_sem.at[slot], recv_sem.at[slot],
        device_id=ring_peer(by), device_id_type=pl.DeviceIdType.MESH,
    )


def arrived(inbox, seqs, lanes, valid):
    value = None
    for d in range(inbox.shape[0], 0, -1):
        total = jnp.where(valid(d), inbox[d - 1, seqs : 2 * seqs, lanes], 0.0)
        if value is not None:
            total = total + jnp.where(valid(d), inbox[d - 1, :seqs, lanes], 0.0) * value
        value = total
    return value


def branch_output_kernel(
    summary_ref, normed_ref, picked_ref, wb_own, wb_oth, eb_own, eb_oth,
    local_ref, reach_ref, ends_ref, spans_ref, tokens_ref, onehot_ref, gain_ref,
    wo_own, wo_oth, so_own, so_oth, eo_own, eo_oth,
    *refs, carried,
):
    sources, refs = refs[:carried], refs[carried:]
    (pre_out, state_out, merged_out, carry_out, residual_out, second_out, picked_out), refs = refs[:7], refs[7:]
    targets, refs = refs[:carried], refs[carried:]
    branch_all, acc, inner, inbox, send_sem, recv_sem, core_s, core_r = refs
    core = lax.axis_index("wshard")
    step = pl.program_id(0)
    count = pl.num_programs(0) // 2
    hops = inbox.shape[0]
    rows, tile = local_ref.shape
    seqs = ends_ref.shape[0] // SEGS
    steps = rows // seqs
    seg = steps // SEGS

    @pl.when(step == 0)
    def _():
        greet([d for d in range(1, hops + 1)] + [-d for d in range(1, hops + 1)], True)
        for copy in to_core(sources, targets, core_s, core_r):
            copy.start()
        for d in range(1, hops + 1):
            message(summary_ref, inbox, send_sem, recv_sem, d - 1, d).start()
        acc[...] = jnp.zeros_like(acc)
        inner[...] = jnp.zeros_like(inner)

    @pl.when(step < count)
    def _():
        own, oth = halves(core, normed_ref.shape[1])
        pre = (
            mm(normed_ref[:, own], wb_own[...])
            + mm(normed_ref[:, oth], wb_oth[...])
            + mm(picked_ref[...], stack_ranks(core, eb_own[...], eb_oth[...]))
        )
        pre_out[...] = pre
        branch_all[:, pl.ds(pl.multiple_of(step * tile, 128), tile)] = gelu(pre)

    @pl.when(step == count)
    def _():
        for d in range(1, hops + 1):
            copy = message(summary_ref, inbox, send_sem, recv_sem, d - 1, d)
            copy.wait_send()
            copy.wait_recv()

    @pl.when(step >= count)
    def _():
        at = pl.multiple_of((step - count) * tile, 128)
        start = arrived(inbox, seqs, pl.ds(at, tile), lambda d: lax.axis_index("seq") >= d)
        carry_out[...] = jnp.concatenate([start, jnp.zeros_like(start)], axis=0)
        for s in range(seqs):
            carries = [start[s : s + 1, :]]
            for g in range(SEGS - 1):
                row = s * SEGS + g
                carries.append(ends_ref[row : row + 1, :] + spans_ref[row : row + 1, :] * carries[-1])
            carry = jnp.concatenate(carries, axis=0)
            for i in range(0, seg, 2):
                states = []
                for k in (i, i + 1):
                    here = slice(s * steps + k * SEGS, s * steps + (k + 1) * SEGS)
                    state = local_ref[here, :] + reach_ref[here, :] * carry
                    state_out[here, :] = state
                    states.append(branch_all[here, pl.ds(at, tile)] * state)
                merged_out[s * steps + i * SEGS : s * steps + (i + 2) * SEGS, :] = jnp.concatenate(states, axis=0).astype(BF16)
        merged = merged_out[...]
        mine = (step - count) // (count // 2) == core

        @pl.when(mine)
        def _():
            acc[...] += mm(merged, wo_own[...])

        @pl.when(jnp.logical_not(mine))
        def _():
            acc[...] += mm(merged, wo_oth[...])

        inner[...] += mm_nt(merged, stack_ranks(core, so_own[...], so_oth[...]))

    @pl.when(step == 2 * count - 1)
    def _():
        picked = (inner[...] * onehot_ref[...]).astype(BF16)
        picked_out[...] = picked
        residual = (
            tokens_ref[...].astype(F32)
            + acc[...]
            + mm(picked, stack_ranks(core, eo_own[...], eo_oth[...]))
        )
        residual_out[...] = residual
        scale = lax.rsqrt(jnp.mean(residual * residual, axis=1, keepdims=True) + EPSILON)
        second_out[...] = (residual * scale * gain_ref[1:2, : residual.shape[1]]).astype(BF16)
        for copy in to_core(sources, targets, core_s, core_r):
            copy.wait()


def feed_kernel(
    core_ref, second_ref, cot_ref, residual_ref, onehot_ref, gain_ref,
    g_own_a, g_own_b, g_oth_a, g_oth_b, u_own_a, u_own_b, u_oth_a, u_oth_b, d_own, d_oth,
    sg_own, sg_oth, su_own, su_oth, eg_own_a, eg_own_b, eg_oth_a, eg_oth_b,
    eu_own_a, eu_own_b, eu_oth_a, eu_oth_b, sd_own_a, sd_own_b, sd_oth_a, sd_oth_b, ed_own, ed_oth,
    out_ref, grad_residual_out, grad_low_out, deg_out, deu_out, dsd_out, dsg_out, dsu_out, ded_out,
    picked, picked_t, gi_down, gi_down_t, down_acc, inner_down, grad_second, gi_gate, cot, *, seqs,
):
    core = core_ref[0]
    step = pl.program_id(0)
    ranks = onehot_ref.shape[1]
    width = second_ref.shape[1]
    part = d_own.shape[0]
    own, oth = halves(core, width)
    steps = second_ref.shape[0] // seqs

    @pl.when(step == 0)
    def _():
        onehot = onehot_ref[...]
        shrink = jnp.concatenate(
            [stack_ranks(core, sg_own[...], sg_oth[...]), stack_ranks(core, su_own[...], su_oth[...])], axis=0
        )
        both = mm_nt(second_ref[...], shrink) * jnp.concatenate([onehot, onehot], axis=1)
        picked[...] = both.astype(BF16)
        picked_t[...] = flipped(both)
        order = interleave(steps)
        for s in range(seqs):
            here = slice(s * steps, (s + 1) * steps)
            cot[here, :] = mm(order, cot_ref[here, :]).astype(BF16)
        inner = mm_nt(cot[...], stack_ranks(core, ed_own[...], ed_oth[...])) * onehot
        gi_down[...] = inner.astype(BF16)
        gi_down_t[...] = flipped(inner)
        down_acc[...] = jnp.zeros_like(down_acc)
        inner_down[...] = jnp.zeros_like(inner_down)
        grad_second[...] = jnp.zeros_like(grad_second)
        gi_gate[...] = jnp.zeros_like(gi_gate)

    join = lambda a, b: jnp.concatenate([a[...], b[...]], axis=1)
    g_own, g_oth = join(g_own_a, g_own_b), join(g_oth_a, g_oth_b)
    u_own, u_oth = join(u_own_a, u_own_b), join(u_oth_a, u_oth_b)
    down = jnp.concatenate([d_own[...], d_oth[...]], axis=0)
    eg = stack_ranks(core, join(eg_own_a, eg_own_b), join(eg_oth_a, eg_oth_b))
    eu = stack_ranks(core, join(eu_own_a, eu_own_b), join(eu_oth_a, eu_oth_b))
    sd = stack_ranks(core, join(sd_own_a, sd_own_b), join(sd_oth_a, sd_oth_b))

    x_own, x_oth = second_ref[:, own], second_ref[:, oth]
    gating = mm(x_own, g_own) + mm(x_oth, g_oth) + mm(picked[:, :ranks], eg)
    upward = mm(x_own, u_own) + mm(x_oth, u_oth) + mm(picked[:, ranks:], eu)
    grad_hidden = mm_nt(cot[...], down) + mm(gi_down[...], sd)
    smooth, slope = gelu_parts(gating)
    hidden = (smooth * upward).astype(BF16)
    grad_gating = (grad_hidden * upward * slope).astype(BF16)
    grad_upward = (grad_hidden * smooth).astype(BF16)
    down_acc[...] += mm(hidden, down)
    inner_down[...] += mm_nt(hidden, sd)
    grad_second[:, own] += mm_nt(grad_gating, g_own) + mm_nt(grad_upward, u_own)
    grad_second[:, oth] += mm_nt(grad_gating, g_oth) + mm_nt(grad_upward, u_oth)
    gi_gate[:, :ranks] += mm_nt(grad_gating, eg)
    gi_gate[:, ranks:] += mm_nt(grad_upward, eu)
    for out, grad in (
        (deg_out, mm(picked_t[:ranks, :], grad_gating)),
        (deu_out, mm(picked_t[ranks:, :], grad_upward)),
        (dsd_out, mm(gi_down_t[...], hidden)),
    ):
        low, high = grad[:, :part], grad[:, part:]
        first = core == 0
        put_folded(
            out, jnp.concatenate([jnp.where(first, low, high), jnp.where(first, high, low)], axis=1)
        )

    @pl.when(step == pl.num_programs(0) - 1)
    def _():
        onehot = onehot_ref[...]
        chosen = inner_down[...] * onehot
        residual = residual_ref[...]
        result = (
            residual + down_acc[...] + mm(chosen.astype(BF16), stack_ranks(core, ed_own[...], ed_oth[...]))
        ).astype(BF16)
        order = interleave(steps, True)
        for s in range(seqs):
            here = slice(s * steps, (s + 1) * steps)
            out_ref[here, :] = mm(order, result[here, :]).astype(BF16)
        put_folded(ded_out, mm(flipped(chosen), cot[...]))
        inner = gi_gate[...] * jnp.concatenate([onehot, onehot], axis=1)
        shrink = jnp.concatenate(
            [stack_ranks(core, sg_own[...], sg_oth[...]), stack_ranks(core, su_own[...], su_oth[...])], axis=0
        )
        grads = mm(flipped(inner), second_ref[...])
        put_folded(dsg_out, grads[:ranks, :])
        put_folded(dsu_out, grads[ranks:, :])
        weighted = (grad_second[...] + mm(inner.astype(BF16), shrink)) * gain_ref[1:2, : residual.shape[1]]
        scale = lax.rsqrt(jnp.mean(residual * residual, axis=1, keepdims=True) + EPSILON)
        grad = (
            cot[...].astype(F32)
            + scale * weighted
            - residual * (scale * scale * scale * jnp.mean(weighted * residual, axis=1, keepdims=True))
        )
        grad_residual_out[...] = grad
        grad_low_out[...] = grad.astype(BF16)


FEED_ORDER = ("eg", "sdn", "eu", "sg", "su", "edn")
MIXER_ORDER = ("eo", "eb", "so", "sb", "edec", "sdec", "einf", "sinf", "er", "sr")
FEED_PIECES = ((0, 2, 0), (2, 4, 1))
MIXER_PIECES = ((0, 2, 0), (2, 2, 1), (4, 2, 0), (6, 2, 1), (8, 1, 0), (9, 1, 1))


class Links:
    def __init__(self):
        self.core = lax.axis_index("wshard")
        chip = lax.axis_index("seq")
        self.x, self.y, self.z = chip % 2, (chip // 2) % 2, chip // 4
        self.x_peer = chip + 1 - 2 * self.x
        self.y_peer = chip + 2 - 4 * self.y
        self.z_peers = [((self.z + d) % 4) * 4 + chip % 4 for d in (1, 2, 3)]

    def chips(self):
        return [self.x_peer, self.y_peer] + self.z_peers

    def copy(self, src, dst, send, recv, device):
        return pltpu.make_async_remote_copy(
            src, dst, send, recv, device_id=device, device_id_type=pl.DeviceIdType.MESH
        )

    def across(self, src, core_in, cols, send, recv):
        return self.copy(src, core_in.at[:, :, cols], send, recv, {"wshard": 1 - self.core})

    def first(self, send1, recv1, cols, direction, send, recv):
        peer = self.x_peer if direction == 0 else self.y_peer
        return self.copy(send1.at[:, :, cols], recv1.at[:, :, cols], send, recv, {"seq": peer})

    def second(self, send2, recv2, cols, direction, send, recv):
        peer = self.y_peer if direction == 0 else self.x_peer
        return self.copy(send2.at[:, :, cols], recv2.at[:, :, cols], send, recv, {"seq": peer})

    def third(self, send3, recv3, cols, send, recv, index):
        return [
            self.copy(
                send3.at[d, :, cols], recv3.at[d, :, cols], send.at[index, d], recv.at[index, d], {"seq": self.z_peers[d]}
            )
            for d in range(3)
        ]

    def split_first(self, own, core_in, kept, send1, own_cols, cols, direction):
        for p in range(4):
            for o in range(2):
                keep = p * 4 + (o * 2 + self.x if direction == 0 else self.y * 2 + o)
                give = p * 4 + (o * 2 + 1 - self.x if direction == 0 else (1 - self.y) * 2 + o)
                at = p * 2 + o
                if kept is not None:
                    kept[at, :, cols] = own[keep, :, own_cols].astype(F32) + core_in[keep, :, cols].astype(F32)
                send1[at, :, cols] = (
                    own[give, :, own_cols].astype(F32) + core_in[give, :, cols].astype(F32)
                ).astype(BF16)

    def split_second(self, own, core_in, recv1, kept2, send2, cols, direction):
        for p in range(4):
            at = p * 2 + (self.y if direction == 0 else self.x)
            keep = p * 4 + self.y * 2 + self.x
            kept2[p, :, cols] = (
                own[keep, :, cols].astype(F32) + core_in[keep, :, cols].astype(F32) + recv1[at, :, cols].astype(F32)
            )
            at = p * 2 + 1 - (self.y if direction == 0 else self.x)
            give = p * 4 + ((1 - self.y) * 2 + self.x if direction == 0 else self.y * 2 + 1 - self.x)
            send2[p, :, cols] = (
                own[give, :, cols].astype(F32) + core_in[give, :, cols].astype(F32) + recv1[at, :, cols].astype(F32)
            ).astype(BF16)

    def split_third(self, kept2, recv2, send3, out, cols, out_cols):
        out[:, out_cols] = kept2[self.z, :, cols] + recv2[self.z, :, cols].astype(F32)
        for d in range(3):
            to = (self.z + d + 1) % 4
            send3[d, :, cols] = (kept2[to, :, cols] + recv2[to, :, cols].astype(F32)).astype(BF16)

    def finish(self, recv3, out, cols, out_cols):
        out[:, out_cols] += (
            recv3[0, :, cols].astype(F32) + recv3[1, :, cols].astype(F32) + recv3[2, :, cols].astype(F32)
        )


def columns_of(sizes):
    return [pl.ds(sum(sizes[:i]), n) for i, n in enumerate(sizes)]


def pieces_of(sizes, pieces):
    return [pl.ds(sum(sizes[:i]), sum(sizes[i : i + n])) for i, n, _ in pieces]


def last_kernel(grad_ref, residual_ref, tokens_ref, gain_ref, *refs, sizes, runs, split):
    if sizes:
        sums_ref, refs = refs[0], refs[1:]
    out_ref, outs, kept = refs[0], refs[1:-1], refs[-1]
    weighted = grad_ref[...] * gain_ref[0:1, : grad_ref.shape[1]]
    values = tokens_ref[...].astype(F32)
    scale = lax.rsqrt(jnp.mean(values * values, axis=1, keepdims=True) + EPSILON)
    grad = (
        residual_ref[...]
        + scale * weighted
        - values * (scale * scale * scale * jnp.mean(weighted * values, axis=1, keepdims=True))
    )
    steps = grad.shape[0]
    for q in range(kept.shape[0]):
        kept[q, :steps, :] = grad[:, q * LANES : (q + 1) * LANES]
    for t in range(0, steps, SEGS):
        first = t % (steps // SEGS) * SEGS + t // (steps // SEGS)
        out_ref[t : t + SEGS, :] = jnp.concatenate(
            [kept[q, pl.ds(first, SEGS, stride=SEGS), :] for q in range(kept.shape[0])], axis=1
        )

    @pl.when(pl.program_id(0) == 0)
    def _():
        offset = 0
        for out, size, run, two in zip(outs, sizes, runs, split):
            pieces = unfold(sums_ref[:, offset : offset + size], run)
            if two:
                pieces = [p for i, p in enumerate(pieces) if i % 4 < 2] + [p for i, p in enumerate(pieces) if i % 4 >= 2]
            out[...] = jnp.concatenate(pieces, axis=1)
            offset += size


def scatter_plain(grads, runs, split):
    summed = {}
    for k, g in grads.items():
        quarter = runs[k] // 4
        g = g.astype(F32).reshape(2, g.shape[1], 4, 4, g.shape[3] // quarter, quarter)
        g = g[:, :, jnp.array([0, 2, 1, 3])]
        if k in split:
            g = g.reshape(g.shape[:2] + (2, 2) + g.shape[3:]).transpose(1, 0, 4, 2, 5, 3, 6)
        else:
            g = g.transpose(1, 0, 3, 4, 2, 5)
        g = g.reshape(g.shape[0] * 8, -1)
        summed[k] = lax.psum_scatter(g, ("seq", "wshard"), scatter_dimension=0, tiled=True)
    return summed


def branch_back_kernel(
    low_ref, onehot_ref, masks_ref, soft_ref, picked_ref, pre_ref, state_ref, merged_ref, rate_ref,
    wo_own, wo_oth, so_own, so_oth, eo_own, eo_oth,
    normed_ref, picked_b_ref, eb_own, eb_oth,
    *refs, feed_sizes, reduce,
):
    count_feed = len(feed_sizes)
    feed, refs = refs[:count_feed], refs[count_feed:]
    (grad_state_out, ends_out, spans_out, start_out, pre_grad_out, gi_b_out, dso_out, deo_out, dsb_out, deb_out), refs = (
        refs[:10], refs[10:]
    )
    if reduce:
        half_out, refs = refs[0], refs[1:]
    (gi, gi_t, grad_buf, pre_grad, summary, inbox, send_sem, recv_sem), refs = refs[:8], refs[8:]
    core = lax.axis_index("wshard")
    step = pl.program_id(0)
    count = pl.num_programs(0) - 1
    hops = inbox.shape[0]
    rows, tile = pre_ref.shape
    seqs = ends_out.shape[0] // SEGS
    steps = rows // seqs
    seg = steps // SEGS
    shifts = [d for d in range(1, hops + 1)] + [-d for d in range(1, hops + 1)]
    if reduce:
        own, core_in, send1, recv1, local_sem, core_s, core_r, s1_s, s1_r = refs
        cols = columns_of(feed_sizes)
        pieces = pieces_of(feed_sizes, FEED_PIECES)
        order = [d for _, _, d in FEED_PIECES]

    @pl.when(step == 0)
    def _():
        if reduce:
            links = Links()
            greet(shifts, True, links.chips())
            for a in range(count_feed):
                links.across(feed[a].at[1 - core], core_in, cols[a], core_s.at[a], core_r.at[a]).start()
                pltpu.make_async_copy(feed[a].at[core], own.at[:, :, cols[a]], local_sem.at[a]).start()
        else:
            greet(shifts, False)
        grad = mm_nt(low_ref[...], stack_ranks(core, eo_own[...], eo_oth[...])) * onehot_ref[...]
        gi[...] = grad.astype(BF16)
        gi_t[...] = flipped(grad)
        put_folded(deo_out, mm(flipped(picked_ref[...].astype(F32)), low_ref[...]))

    if reduce:

        @pl.when(step == 1)
        def _():
            links = Links()
            for a in range(count_feed):
                pltpu.make_async_copy(feed[a].at[core], own.at[:, :, cols[a]], local_sem.at[a]).wait()
                links.across(feed[a].at[1 - core], core_in, cols[a], core_s.at[a], core_r.at[a]).wait()
            for p, piece in enumerate(pieces):
                links.split_first(own, core_in, half_out, send1, piece, piece, order[p])
                links.first(send1, recv1, piece, order[p], s1_s.at[p], s1_r.at[p]).start()

    @pl.when(step < count)
    def _():
        at = pl.multiple_of(step * tile, 128)
        mine = step // (count // 2) == core

        @pl.when(mine)
        def _():
            grad_buf[...] = mm_nt(low_ref[...], wo_own[...])

        @pl.when(jnp.logical_not(mine))
        def _():
            grad_buf[...] = mm_nt(low_ref[...], wo_oth[...])

        grad_buf[...] += mm(gi[...], stack_ranks(core, so_own[...], so_oth[...]))
        put_folded(dso_out, mm(gi_t[...], merged_ref[...]))
        cols = pl.ds(at, tile)

        def scanned(s):
            held = span = above = None
            for i in range(seg - 2, -1, -2):
                pres = []
                for k in (i + 1, i):
                    here = row_at(s * steps, k * SEGS, SEGS)
                    grad_merged = grad_buf[here, :]
                    smooth, slope = gelu_parts(pre_ref[here, :])
                    pres.append(grad_merged * state_ref[here, :] * slope)
                    grad_state = grad_merged * smooth
                    grad_state_out[here, :] = grad_state
                    held = grad_state if held is None else above * held + grad_state
                    if above is not None:
                        span = above if span is None else above * span
                    above = jnp.exp2(rate_ref[here, :] * soft_ref[2:3, :]) * masks_ref[here, 0:1]
                pre = jnp.concatenate(pres[::-1], axis=0).astype(BF16)
                here = row_at(s * steps, i * SEGS, 2 * SEGS)
                pre_grad[here, cols] = pre
                pre_grad_out[here, :] = pre
            held = above * held
            span = above * span
            ends_out[row_at(s * SEGS, 0, SEGS), :] = held
            spans_out[row_at(s * SEGS, 0, SEGS), :] = span
            total, product = held[SEGS - 1 : SEGS, :], span[SEGS - 1 : SEGS, :]
            for g in range(SEGS - 2, -1, -1):
                total = held[g : g + 1, :] + span[g : g + 1, :] * total
                product = span[g : g + 1, :] * product
            summary[pl.ds(s, 1), cols] = product
            summary[pl.ds(seqs + s, 1), cols] = total

        per_sequence(seqs, scanned)

    @pl.when(step == count)
    def _():
        for d in range(1, hops + 1):
            message(summary, inbox, send_sem, recv_sem, d - 1, -d).start()
        picked_t = flipped(picked_b_ref[...].astype(F32))
        expand = stack_ranks(core, eb_own[...], eb_oth[...])
        grad = mm_nt(pre_grad[...], expand) * onehot_ref[...]
        gi_b_out[...] = grad.astype(BF16)
        put_folded(dsb_out, mm(flipped(grad), normed_ref[...]))
        for piece in range(pre_grad.shape[1] // tile):
            first, second = fold(mm(picked_t, pre_grad[:, piece * tile : (piece + 1) * tile]))
            lanes = slice(piece * tile // 4, (piece + 1) * tile // 4)
            deb_out[0, :, :, lanes] = first
            deb_out[1, :, :, lanes] = second
        for d in range(1, hops + 1):
            copy = message(summary, inbox, send_sem, recv_sem, d - 1, -d)
            copy.wait_send()
            copy.wait_recv()
        peers = lax.axis_size("seq")
        start = arrived(inbox, seqs, slice(None), lambda d: lax.axis_index("seq") + d < peers)
        start_out[...] = jnp.concatenate([start, jnp.zeros_like(start)], axis=0)
        if reduce:
            links = Links()
            for p, piece in enumerate(pieces):
                links.first(send1, recv1, piece, order[p], s1_s.at[p], s1_r.at[p]).wait()
            for at in range(half_out.shape[0]):
                half_out[at] += recv1[at].astype(F32)


def recur_back_kernel(
    grad_state_ref, ends_ref, spans_ref, start_ref, carry_ref, state_ref, mixed_ref, rate_ref, inflow_ref,
    masks_ref, onehot_ref, soft_ref, picked_ref,
    bd_own, bd_oth, bi_own, bi_oth, ed_own, ed_oth, ei_own, ei_oth, sd_own, sd_oth, si_own, si_oth,
    taps_ref, normed_ref, picked_r_ref, er_own, er_oth,
    wr_own, wr_oth, sr_own, sr_oth, pre_grad_ref, gi_b_ref, wb_own, wb_oth, sb_own, sb_oth,
    *refs, feed_sizes, mixer_sizes, reduce,
):
    if reduce:
        half_ref, early_grads, refs = refs[0], refs[1:5], refs[5:]
        out_ref, sums_out, refs = refs[0], refs[1], refs[2:]
    else:
        out_ref, late_outs, refs = refs[0], refs[1:7], refs[7:]
    (partial, inner, gi, gi_t, picked_t, low, inner_r, picked_rt, heads, inbox,
     head_s, head_r, rate_grad, inflow_grad), refs = refs[:14], refs[14:]
    core = lax.axis_index("wshard")
    step = pl.program_id(0)
    count = pl.num_programs(0) // 4
    rows, tile = state_ref.shape
    ranks = onehot_ref.shape[1]
    seqs = ends_ref.shape[0] // SEGS
    steps = rows // seqs
    seg = steps // SEGS
    lags = taps_ref.shape[0] - 1
    order = [d for _, _, d in MIXER_PIECES]

    if reduce:
        (kept2_f, send2_f, recv2_f, send3_f, recv3_f, f2_s, f2_r, f3_s, f3_r,
         mine_g, core_in, send1, recv1, kept2, send2, recv2, send3, recv3,
         local_sem, core_s, core_r, s1_s, s1_r, s2_s, s2_r, s3_s, s3_r) = refs
        fcols = pieces_of(feed_sizes, FEED_PIECES)
        forder = [d for _, _, d in FEED_PIECES]
        mcols = columns_of(mixer_sizes)
        pcols = pieces_of(mixer_sizes, MIXER_PIECES)
        base = sum(feed_sizes)
        sums_cols = [pl.ds(base + c.start, c.size) for c in pcols]

        def feed_second(links):
            for a in range(len(fcols)):
                mine = links.y if forder[a] == 0 else links.x
                for p in range(4):
                    kept2_f[p, :, fcols[a]] = half_ref[p * 2 + mine, :, fcols[a]]
                    send2_f[p, :, fcols[a]] = half_ref[p * 2 + 1 - mine, :, fcols[a]].astype(BF16)
                links.second(send2_f, recv2_f, fcols[a], forder[a], f2_s.at[a], f2_r.at[a]).start()

        def feed_third(links):
            for a in range(len(fcols)):
                links.second(send2_f, recv2_f, fcols[a], forder[a], f2_s.at[a], f2_r.at[a]).wait()
                links.split_third(kept2_f, recv2_f, send3_f, sums_out, fcols[a], fcols[a])
                for copy in links.third(send3_f, recv3_f, fcols[a], f3_s, f3_r, a):
                    copy.start()

        def feed_finish(links):
            for a in range(len(fcols)):
                for copy in links.third(send3_f, recv3_f, fcols[a], f3_s, f3_r, a):
                    copy.wait()
                links.finish(recv3_f, sums_out, fcols[a], fcols[a])

        def source(a):
            return early_grads[a].at[1 - core] if a < 4 else mine_g.at[1 - core, :, :, mcols[a]]

        def cross(links, which):
            for a in which:
                if a < 4:
                    pltpu.make_async_copy(
                        early_grads[a].at[core], mine_g.at[core, :, :, mcols[a]], local_sem.at[a]
                    ).start()
                links.across(source(a), core_in, mcols[a], core_s.at[a], core_r.at[a]).start()

        def first(links, which):
            for p in which:
                for a in range(MIXER_PIECES[p][0], MIXER_PIECES[p][0] + MIXER_PIECES[p][1]):
                    if a < 4:
                        pltpu.make_async_copy(
                            early_grads[a].at[core], mine_g.at[core, :, :, mcols[a]], local_sem.at[a]
                        ).wait()
                    links.across(source(a), core_in, mcols[a], core_s.at[a], core_r.at[a]).wait()
                links.split_first(mine_g.at[core], core_in, None, send1, pcols[p], pcols[p], order[p])
                links.first(send1, recv1, pcols[p], order[p], s1_s.at[p], s1_r.at[p]).start()

        def second(links, which):
            for p in which:
                links.first(send1, recv1, pcols[p], order[p], s1_s.at[p], s1_r.at[p]).wait()
                links.split_second(mine_g.at[core], core_in, recv1, kept2, send2, pcols[p], order[p])
                links.second(send2, recv2, pcols[p], order[p], s2_s.at[p], s2_r.at[p]).start()

        def third(links, which):
            for p in which:
                links.second(send2, recv2, pcols[p], order[p], s2_s.at[p], s2_r.at[p]).wait()
                links.split_third(kept2, recv2, send3, sums_out, pcols[p], sums_cols[p])
                for copy in links.third(send3, recv3, pcols[p], s3_s, s3_r, p):
                    copy.start()

        def finish(links, which):
            for p in which:
                for copy in links.third(send3, recv3, pcols[p], s3_s, s3_r, p):
                    copy.wait()
                links.finish(recv3, sums_out, pcols[p], sums_cols[p])

        A, B, D = (0, 1), (2, 3), (4, 5)
        plan = {
            0: [(cross, (0, 1, 2, 3)), (feed_second, None)],
            1: [(first, A)],
            2: [(feed_third, None)],
            3: [(second, A)],
            5: [(third, A), (cross, (4, 6))],
            8: [(cross, (5, 7))],
            9: [(first, B)],
            12: [(cross, (8, 9)), (second, B)],
            13: [(first, D)],
            14: [(third, B)],
            15: [(second, D)],
        }
        tail = [(third, D), (finish, B), (feed_finish, None), (finish, A), (finish, D)]

        def run(links, what):
            for action, which in what:
                action(links) if which is None else action(links, which)

        def late_grad(index, grad, piece=None):
            width = grad.shape[1] // 4
            start = sum(mixer_sizes[:index])
            if piece is None:
                at = pl.ds(start, width)
            else:
                at = pl.ds(pl.multiple_of(start + piece * width, 128), width)
            for half, block in enumerate(fold(grad)):
                mine_g[half, :, :, at] = block

    else:

        def late_grad(index, grad, piece=None):
            put_folded(late_outs[index - 4], grad)

    @pl.when(step == 0)
    def _():
        if reduce:
            greet([1, -1], True, Links().chips())
        else:
            greet([1, -1], False)
        inner[...] = jnp.zeros_like(inner)
        inner_r[...] = jnp.zeros_like(inner_r)
        picked_t[...] = flipped(picked_ref[...].astype(F32))
        picked_rt[...] = flipped(picked_r_ref[...].astype(F32))

    if reduce:
        for at_step, what in plan.items():

            @pl.when(step == at_step)
            def _(what=what):
                run(Links(), what)

    def head_copy(slot):
        return pltpu.make_async_remote_copy(
            heads.at[slot], inbox.at[slot], head_s.at[slot], head_r.at[slot],
            device_id=ring_peer(-1), device_id_type=pl.DeviceIdType.MESH,
        )

    @pl.when(step < count)
    def _():
        cols = pl.ds(pl.multiple_of(step * tile, 128), tile)

        def scanned(s):
            carries = [start_ref[pl.ds(s, 1), :]]
            ends, spans = ends_ref[row_at(s * SEGS, 0, SEGS), :], spans_ref[row_at(s * SEGS, 0, SEGS), :]
            for g in range(SEGS - 1, 0, -1):
                carries.append(ends[g : g + 1, :] + spans[g : g + 1, :] * carries[-1])
            flow = jnp.concatenate(carries[::-1], axis=0)
            above = None
            soft = soft_ref[2:3, :]
            for i in range(seg - 2, -1, -2):
                rate_parts, inflow_parts, mixed_parts = [], [], []
                for k in (i + 1, i):
                    here = row_at(s * steps, k * SEGS, SEGS)
                    backflow = grad_state_ref[here, :] + (flow if above is None else above * flow)
                    flow = backflow
                    if k > 0:
                        prior = state_ref[row_at(s * steps, (k - 1) * SEGS, SEGS), :]
                    else:
                        prior = shift_in(
                            state_ref[row_at(s * steps, (seg - 1) * SEGS, SEGS), :], carry_ref[pl.ds(s, 1), :], True
                        )
                    rate = rate_ref[here, :]
                    inflow = inflow_ref[here, :]
                    mixed = mixed_ref[here, :]
                    keep = masks_ref[here, 0:1]
                    raw = jnp.exp2(rate * soft)
                    above = raw * keep
                    spread = (1.0 - raw) * (1.0 + raw)
                    bounded = jnp.maximum(spread, ROOT_FLOOR)
                    inverse = lax.rsqrt(bounded)
                    root = keep * (bounded * inverse) + (1.0 - keep)
                    pulled = backflow * inflow
                    through = pulled * root
                    grad_spread = jnp.where(spread > ROOT_FLOOR, pulled * mixed * (inverse * keep), 0.0)
                    grad_log = backflow * prior * above - raw * raw * grad_spread
                    rate_parts.append(grad_log * (soft * (1.0 / LOG2_E)) * rate * (1.0 - rate))
                    inflow_parts.append(through * mixed * (1.0 - inflow))
                    mixed_parts.append(mixed)
                    partial[here, cols] = through
                both = row_at(s * steps, i * SEGS, 2 * SEGS)
                rate_grad[both, :] = jnp.concatenate(rate_parts[::-1], axis=0).astype(BF16)
                inflow_grad[both, :] = jnp.concatenate(inflow_parts[::-1], axis=0).astype(BF16)
                low[step, both, :] = jnp.concatenate(mixed_parts[::-1], axis=0).astype(BF16)

        per_sequence(seqs, scanned)
        grad_rate, grad_inflow = rate_grad[...], inflow_grad[...]
        blocks, block = bd_own.shape[0], bd_own.shape[1]
        mine = step // (count // 2) == core
        pieces = []
        for b in range(blocks):
            lanes = slice(b * block, (b + 1) * block)
            both = jnp.concatenate(
                [jnp.where(mine, bd_own[b], bd_oth[b]), jnp.where(mine, bi_own[b], bi_oth[b])], axis=1
            )
            pieces.append(mm_nt(jnp.concatenate([grad_rate[:, lanes], grad_inflow[:, lanes]], axis=1), both))
        partial[:, pl.ds(pl.multiple_of(step * tile, 128), tile)] += jnp.concatenate(pieces, axis=1)
        inner[:, :ranks] += mm_nt(grad_rate, stack_ranks(core, ed_own[...], ed_oth[...]))
        inner[:, ranks:] += mm_nt(grad_inflow, stack_ranks(core, ei_own[...], ei_oth[...]))
        late_grad(4, mm(picked_t[:ranks, :], grad_rate), step)
        late_grad(6, mm(picked_t[ranks:, :], grad_inflow), step)

    @pl.when(step == count - 1)
    def _():
        onehot = onehot_ref[...]
        chosen = inner[...] * jnp.concatenate([onehot, onehot], axis=1)
        gi[...] = chosen.astype(BF16)
        gi_t[...] = flipped(chosen)

    @pl.when(jnp.logical_and(step >= count, step < 2 * count))
    def _():
        piece = step - count
        at = pl.multiple_of(piece * tile, 128)
        shrink = jnp.concatenate(
            [stack_ranks(core, sd_own[...], sd_oth[...]), stack_ranks(core, si_own[...], si_oth[...])], axis=0
        )
        grad = partial[:, pl.ds(at, tile)] + mm(gi[...], shrink)
        partial[:, pl.ds(at, tile)] = grad
        for s in range(seqs):
            firsts = [grad[s * steps + i * SEGS : s * steps + i * SEGS + 1, :] for i in range(HALO)]
            heads[piece, s * HALO : (s + 1) * HALO, :] = jnp.concatenate(firsts, axis=0)
        both = mm(gi_t[...], low[piece])
        late_grad(5, both[:ranks, :], piece)
        late_grad(7, both[ranks:, :], piece)
        head_copy(piece).start()

    @pl.when(jnp.logical_and(step >= 2 * count, step < 3 * count))
    def _():
        piece = step - 2 * count
        at = pl.multiple_of(piece * tile, 128)
        head_copy(piece).wait()
        cols = pl.ds(at, tile)

        def filtered(s):
            at_run = lambda i: partial[row_at(s * steps, i * SEGS, SEGS), cols]
            rim = inbox[piece, row_at(s * HALO, 0, HALO), :]
            runs = {seg + k: shift_in(at_run(k), rim[k : k + 1, :], False) for k in range(lags)}
            for i in range(lags):
                runs[i] = at_run(i)
            for i in range(0, seg, 2):
                totals = []
                for k in (i, i + 1):
                    here = row_at(s * steps, k * SEGS, SEGS)
                    if k + lags < seg:
                        runs[k + lags] = at_run(k + lags)
                    total = taps_ref[0:1, :] * runs[k]
                    for lag in range(1, lags + 1):
                        total = total + taps_ref[lag : lag + 1, :] * runs[k + lag] * masks_ref[here, lags + lag - 1 : lags + lag]
                    totals.append(total)
                low[piece, row_at(s * steps, i * SEGS, 2 * SEGS), :] = jnp.concatenate(totals, axis=0).astype(BF16)

        per_sequence(seqs, filtered)
        grad = low[piece]
        inner_r[...] += mm_nt(grad, stack_ranks(core, er_own[...], er_oth[...]))
        late_grad(8, mm(picked_rt[...], grad), piece)

    @pl.when(step == 3 * count - 1)
    def _():
        chosen = inner_r[...] * onehot_ref[...]
        late_grad(9, mm(flipped(chosen), normed_ref[...]))
        out_ref[...] = mm(chosen.astype(BF16), stack_ranks(core, sr_own[...], sr_oth[...])) + mm(
            gi_b_ref[...], stack_ranks(core, sb_own[...], sb_oth[...])
        )

    @pl.when(step >= 3 * count)
    def _():
        left, right = halves(core, out_ref.shape[1])
        recur_grad, branch_grad = low[step - 3 * count], pre_grad_ref[...]
        out_ref[:, left] += mm_nt(recur_grad, wr_own[...]) + mm_nt(branch_grad, wb_own[...])
        out_ref[:, right] += mm_nt(recur_grad, wr_oth[...]) + mm_nt(branch_grad, wb_oth[...])

    if reduce:

        @pl.when(step == 4 * count - 1)
        def _():
            run(Links(), tail)


def indexed(shape, index, scalars):
    if scalars:
        return pl.BlockSpec(shape, index)
    return pl.BlockSpec(shape, lambda j: index(j, None))


def call(kernel, name, grid, core, ins, outs, scratch, flops, nbytes, collective=None):
    scalars = core is not None

    def still(shape):
        zeros = (0,) * len(shape)
        if scalars:
            return pl.BlockSpec(shape, lambda j, c: zeros, pipeline_mode=pl.Buffered(1))
        return pl.BlockSpec(shape, lambda j: zeros, pipeline_mode=pl.Buffered(1))

    in_specs, arrays = [], []
    for item in ins:
        if isinstance(item, tuple) and len(item) == 1:
            arrays.append(item[0])
            in_specs.append(pl.BlockSpec(memory_space=pl.ANY))
        elif isinstance(item, tuple) and len(item) == 2:
            arrays.append(item[0])
            in_specs.append(pl.BlockSpec(memory_space=item[1]))
        elif isinstance(item, tuple):
            arrays.append(item[0])
            in_specs.append(indexed(item[1], item[2], scalars))
        else:
            arrays.append(item)
            in_specs.append(still(item.shape))
    out_specs, shapes = [], []
    for item in outs:
        shapes.append(jax.ShapeDtypeStruct(item[0], item[1]))
        if len(item) == 3:
            out_specs.append(pl.BlockSpec(memory_space=pl.ANY))
        else:
            out_specs.append(indexed(item[2], item[3], scalars) if len(item) == 4 else still(item[0]))
    return pl.pallas_call(
        kernel,
        grid_spec=pltpu.PrefetchScalarGridSpec(
            num_scalar_prefetch=int(scalars), grid=(grid,), in_specs=in_specs, out_specs=out_specs, scratch_shapes=scratch
        ),
        out_shape=shapes,
        name=name,
        compiler_params=pltpu.CompilerParams(
            dimension_semantics=("arbitrary",), vmem_limit_bytes=67043328, collective_id=collective,
            has_side_effects=collective is not None,
        ),
        cost_estimate=pl.CostEstimate(flops=flops, bytes_accessed=nbytes, transcendentals=0),
    )(*([core] if scalars else []), *arrays)


def local(
    tokens, segment_ids, document_adapter, out_cotangent, mixer_gain, feed_gain, filter_taps, decay_param, *weights
):
    core = lax.axis_index("wshard").astype(jnp.int32).reshape(1)
    anywhere = pl.ANY
    at_once = (1, 8, 10, 11, 12, 14, 2, 3, 13, 15)
    with_mixer = (0, 9, 16, 17, 4, 5, 18, 19, 20, 21, 22, 23)
    with_branch = (6, 7)
    other = {}
    pair = lambda i: (weights[i], other[i])
    wr, sb, sr, er, sdec, sinf, bd, bi, edec, einf = [weights[i] for i in at_once]
    seqs, steps, width = tokens.shape
    rows = seqs * steps
    lru = filter_taps.shape[1]
    lags = filter_taps.shape[0] - 1
    ranks = 2 * sb.shape[0]
    feed = weights[5].shape[1]
    peers = lax.axis_size("seq")
    reach = peers // 4

    soft = jax.nn.softplus(-decay_param) * (-RATE_SCALE * LOG2_E)
    wider = lambda gain: jnp.pad(gain, (0, lru - width))
    params = jnp.stack([wider(mixer_gain), wider(feed_gain), soft, soft, soft, soft, soft, soft])
    tokens2 = tokens.reshape(rows, width)
    cot = out_cotangent.reshape(rows, width)

    tile = TILE
    count = lru // tile
    half = width // 2
    blocks = tile // bd.shape[1]
    block = bd.shape[1]
    early = lambda j: jnp.minimum(j, count - 1)
    late = lambda j: jnp.maximum(j - count, 0)
    flat = lambda r, at: ((r, tile), lambda j, c: (0, at(j)))

    def tiled(array, r, at):
        block_shape, index = flat(r, at)
        return (array, block_shape, index)

    def tiled_out(r, dtype, at, total=None):
        block_shape, index = flat(r, at)
        return ((r, total or lru), dtype, block_shape, index)

    def both(pair, r, at):
        return [tiled(pair[0], r, at), tiled(pair[1], r, at)]

    def gate_blocks(pair, at):
        index = lambda j, c: (at(j) % (count // 2), 0, 0)
        return [(pair[0], (blocks, block, block), index), (pair[1], (blocks, block, block), index)]

    half_ranks = ranks // 2
    ident = lambda j: j
    groups = seqs * SEGS
    def gate_half(array, at):
        return (array, (blocks, block, block), lambda j, c: (at(j) % (count // 2), 0, 0))

    dma = pltpu.SemaphoreType.DMA
    vm = lambda *shape: pltpu.VMEM(shape, BF16)
    vf = lambda *shape: pltpu.VMEM(shape, F32)
    with jax.named_scope("mixer_forward"):
        (normed, picked_br, picked_di, mixed, rate, inflow, held, span, ends, spans, summary, onehot_own, masks, tokens_in, *moved) = call(
            functools.partial(mixer_kernel, carried=len(with_mixer)), "mixer_forward", 2 * count, None,
            [tokens2, segment_ids, (document_adapter, pltpu.SMEM), params, tiled(filter_taps, lags + 1, early), tiled(params, 8, late),
             tiled(wr, half, early), sb, sr, tiled(er, half_ranks, early),
             tiled(sdec, half_ranks, early), tiled(sinf, half_ranks, early), gate_half(bd, late), gate_half(bi, late),
             tiled(edec, half_ranks, late), tiled(einf, half_ranks, late)]
            + [(weights[i],) for i in at_once + with_mixer],
            [((rows, width), BF16), ((rows, 2 * ranks), BF16), ((rows, 2 * ranks), BF16),
             tiled_out(rows, F32, early), tiled_out(rows, F32, late), tiled_out(rows, F32, late),
             tiled_out(rows, F32, late), tiled_out(rows, F32, late),
             tiled_out(groups, F32, late), tiled_out(groups, F32, late), tiled_out(2 * seqs, F32, late),
             ((rows, ranks), F32), ((rows, ranks), F32), ((rows, width), BF16)]
            + [(weights[i].shape, BF16, anywhere) for i in at_once + with_mixer],
            [vm(*weights[i].shape) for i in at_once]
            + [vm(rows + seqs * HALO, width), vm(rows + seqs * HALO, ranks), vf(rows, 2 * ranks), vm(rows, 2 * ranks),
               vf(rows, lru), vf(rows + seqs * HALO, tile),
               vm(seqs, 2 * HALO, width), pltpu.VMEM((2, seqs, steps), jnp.int32),
               dma((len(at_once) - 1,)), dma((len(at_once) - 1,)), dma((count,)), dma((count,)), dma((len(at_once),)),
               dma((seqs,)), dma((seqs,)), dma((2,)), dma((2,)), dma((len(with_mixer),)), dma((len(with_mixer),))],
            int(6e9), int(30e6), collective=2,
        )
    other.update(zip(at_once + with_mixer, moved))
    wr, bd, bi, sb, sr, er, sdec, edec, sinf, einf = [pair(i) for i in (1, 2, 3, 8, 10, 11, 12, 13, 14, 15)]
    wb, eb, so, eo, wo, wg = pair(0), pair(9), pair(16), pair(17), pair(4), pair(5)
    sg, eg, su, eu, sdn, edn = [pair(i) for i in (18, 19, 20, 21, 22, 23)]
    def own_rows(pair, at):
        part_of = lambda j, which: jnp.clip(at(j) - (count // 2) * which, 0, count // 2 - 1)
        return [
            (pair[0], (tile, width), lambda j, c: (part_of(j, lax.axis_index("wshard")), 0)),
            (pair[1], (tile, width), lambda j, c: (part_of(j, 1 - lax.axis_index("wshard")), 0)),
        ]

    with jax.named_scope("branch_and_output_forward"):
        branch_pre, state, merged, carry, residual, second, picked_o, *moved = call(
            functools.partial(branch_output_kernel, carried=len(with_branch)), "branch_output_forward", 2 * count, None,
            [summary, normed, (picked_br, (rows, ranks), lambda j, c: (0, 0))] + both(wb, half, early)
            + both(eb, half_ranks, early)
            + [tiled(held, rows, late), tiled(span, rows, late),
               tiled(ends, groups, late), tiled(spans, groups, late), tokens_in, onehot_own, params]
            + own_rows(wo, late) + both(so, half_ranks, late) + list(eo) + [(weights[i],) for i in with_branch],
            [tiled_out(rows, F32, early), tiled_out(rows, F32, late), tiled_out(rows, BF16, late),
             tiled_out(2 * seqs, F32, late), ((rows, width), F32), ((rows, width), BF16), ((rows, ranks), BF16)]
            + [(weights[i].shape, BF16, anywhere) for i in with_branch],
            [pltpu.VMEM((rows, lru), F32), pltpu.VMEM((rows, width), F32), pltpu.VMEM((rows, ranks), F32),
             pltpu.VMEM((reach, 2 * seqs, lru), F32), pltpu.SemaphoreType.DMA((reach,)), pltpu.SemaphoreType.DMA((reach,)),
             pltpu.SemaphoreType.DMA((len(with_branch),)), pltpu.SemaphoreType.DMA((len(with_branch),))],
            int(8e9), int(45e6), collective=1,
        )
    other.update(zip(with_branch, moved))
    wu, wd = pair(6), pair(7)

    part = 256
    pieces = feed // (2 * part)

    def feed_cols(pair_item, r):
        return [
            (pair_item, (r, part), lambda j, c: (0, c[0] * pieces + j)),
            (pair_item, (r, part), lambda j, c: (0, (1 - c[0]) * pieces + j)),
        ]

    def feed_pair(pair, r):
        return feed_cols(pair[0], r) + feed_cols(pair[1], r)

    chips = ranks // 8
    grad_cols = ((2, chips, 16, feed // 4), BF16, (2, chips, 16, part // 2), lambda j, c: (0, 0, 0, j))
    grad_whole = ((2, chips, 16, width // 4), BF16)

    def grad_tile(at):
        return ((2, chips, 16, lru // 4), BF16, (2, chips, 16, tile // 4), lambda j, c: (0, 0, 0, at(j)))

    with jax.named_scope("feed_forward_both_ways"):
        result, grad_residual, grad_low, deg, deu, dsdn, dsg, dsu, dedn = call(
            functools.partial(feed_kernel, seqs=seqs), "feed_both_ways", pieces, core,
            [second, cot, residual, onehot_own, params] + feed_pair(wg, half) + feed_pair(wu, half)
            + [(wd[0], (part, width), lambda j, c: (j, 0)), (wd[1], (part, width), lambda j, c: (j, 0))]
            + list(sg) + list(su) + feed_pair(eg, half_ranks) + feed_pair(eu, half_ranks)
            + feed_pair(sdn, half_ranks) + list(edn),
            [((rows, width), BF16), ((rows, width), F32), ((rows, width), BF16),
             grad_cols, grad_cols, grad_cols, grad_whole, grad_whole, grad_whole],
            [pltpu.VMEM((rows, 2 * ranks), BF16), pltpu.VMEM((2 * ranks, rows), BF16),
             pltpu.VMEM((rows, ranks), BF16), pltpu.VMEM((ranks, rows), BF16),
             pltpu.VMEM((rows, width), F32), pltpu.VMEM((rows, ranks), F32), pltpu.VMEM((rows, width), F32),
             pltpu.VMEM((rows, 2 * ranks), F32), vm(rows, width)],
            int(50e9), int(60e6),
        )

    split = ("eg", "eu", "sdn")
    runs = dict(sb=width, eb=tile, sr=width, er=tile, sdec=tile, edec=tile, sinf=tile, einf=tile, so=tile, eo=width,
                sg=width, eg=2 * part, su=width, eu=2 * part, sdn=2 * part, edn=width)
    reduce = peers == 16 and ranks == 128
    grads = dict(eg=deg, eu=deu, sdn=dsdn, sg=dsg, su=dsu, edn=dedn)
    size_of = lambda k: (width if k in ("eo", "sb", "sr", "sg", "su", "edn") else feed if k in split else lru) // 4
    feed_sizes = [size_of(k) for k in FEED_ORDER]
    mixer_sizes = [size_of(k) for k in MIXER_ORDER]
    feed_grads = [(grads[k],) for k in FEED_ORDER] if reduce else []
    wide, narrow = sum(feed_sizes), sum(mixer_sizes)
    dma = pltpu.SemaphoreType.DMA
    vm = lambda *shape: pltpu.VMEM(shape, BF16)
    vf = lambda *shape: pltpu.VMEM(shape, F32)
    nf, nm = len(feed_sizes), len(mixer_sizes)

    with jax.named_scope("output_and_branch_backward"):
        (grad_state, bends, bspans, bstart, pre_grad, gi_b, dso, deo, dsb, deb, *halved) = call(
            functools.partial(branch_back_kernel, feed_sizes=feed_sizes if reduce else [], reduce=reduce),
            "output_branch_backward", count + 1, None,
            [grad_low, onehot_own, masks, tiled(params, 8, early), picked_o, tiled(branch_pre, rows, early),
             tiled(state, rows, early), tiled(merged, rows, early), tiled(rate, rows, early)]
            + own_rows(wo, early) + both(so, half_ranks, early) + list(eo)
            + [normed, (picked_br, (rows, ranks), lambda j, c: (0, 0))]
            + list(eb) + feed_grads,
            [tiled_out(rows, F32, early), tiled_out(groups, F32, early), tiled_out(groups, F32, early),
             ((2 * seqs, lru), F32), tiled_out(rows, BF16, early), ((rows, ranks), BF16),
             grad_tile(early), grad_whole, grad_whole, ((2, chips, 16, lru // 4), BF16)]
            + ([((8, 16, wide), F32)] if reduce else []),
            [vm(rows, ranks), vm(ranks, rows), vf(rows, tile),
             vm(rows, lru), vf(2 * seqs, lru), vf(reach, 2 * seqs, lru), dma((reach,)), dma((reach,))]
            + ([vm(16, 16, wide), vm(16, 16, wide), vm(8, 16, wide), vm(8, 16, wide)] + [dma((nf,))] * 5 if reduce else []),
            int(10e9), int(50e6), collective=3,
        )
    early_grads = dict(eo=deo, so=dso, eb=deb, sb=dsb)
    grads.update(early_grads)
    third = 3
    first_of = lambda j: jnp.minimum(j, count - 1)
    middle = lambda j: jnp.clip(j - count, 0, count - 1)
    last = lambda j: jnp.clip(j - 2 * count, 0, count - 1)
    dense = lambda j: jnp.clip(j - 3 * count, 0, count - 1)
    with jax.named_scope("gates_and_recur_backward"):
        grad_normed, *late = call(
            functools.partial(recur_back_kernel, feed_sizes=feed_sizes, mixer_sizes=mixer_sizes, reduce=reduce),
            "gates_recur_backward", 4 * count, None,
            [tiled(grad_state, rows, first_of), tiled(bends, groups, first_of), tiled(bspans, groups, first_of),
             tiled(bstart, 2 * seqs, first_of), tiled(carry, 2 * seqs, first_of), tiled(state, rows, first_of),
             tiled(mixed, rows, first_of), tiled(rate, rows, first_of), tiled(inflow, rows, first_of),
             masks, onehot_own, tiled(params, 8, first_of), picked_di]
            + gate_blocks(bd, first_of) + gate_blocks(bi, first_of)
            + both(edec, half_ranks, first_of) + both(einf, half_ranks, first_of)
            + both(sdec, half_ranks, middle) + both(sinf, half_ranks, middle)
            + [tiled(filter_taps, lags + 1, last), normed, (picked_br, (rows, ranks), lambda j, c: (0, 1)),
               *both(er, half_ranks, last)]
            + both(wr, half, dense) + list(sr) + [tiled(pre_grad, rows, dense), gi_b] + both(wb, half, dense) + list(sb)
            + ([halved[0]] + [(early_grads[k],) for k in MIXER_ORDER[:4]] if reduce else []),
            [((rows, width), F32)]
            + ([((16, wide + narrow), F32)] if reduce else
               [grad_tile(first_of), grad_tile(middle), grad_tile(first_of), grad_tile(middle), grad_tile(last), grad_whole]),
            [vf(rows, lru), vf(rows, 2 * ranks),
             vm(rows, 2 * ranks), vm(2 * ranks, rows), vm(2 * ranks, rows), vm(count, rows, tile),
             vf(rows, ranks), vm(ranks, rows), vf(count, seqs * HALO, tile), vf(count, seqs * HALO, tile),
             dma((count,)), dma((count,)), vm(rows, tile), vm(rows, tile)]
            + ([vf(4, 16, wide), vm(4, 16, wide), vm(4, 16, wide), vm(3, 16, wide), vm(3, 16, wide),
                dma((nf,)), dma((nf,)), dma((nf, 3)), dma((nf, 3)),
                vm(2, 16, 16, narrow), vm(16, 16, narrow), vm(8, 16, narrow), vm(8, 16, narrow),
                vf(4, 16, narrow), vm(4, 16, narrow), vm(4, 16, narrow), vm(3, 16, narrow), vm(3, 16, narrow)]
               + [dma((nm,))] * 7 + [dma((nm, 3))] * 2 if reduce else []),
            int(10e9), int(50e6), collective=4,
        )

    names = ("sb", "eb", "sr", "er", "sdec", "edec", "sinf", "einf", "so", "eo", "sg", "eg", "su", "eu", "sdn", "edn")
    all_names = [k for k in FEED_ORDER + MIXER_ORDER] if reduce else []
    all_sizes = feed_sizes + mixer_sizes if reduce else []
    by_rows = lambda array: (array, (steps, width), lambda j, c: (j, 0))
    with jax.named_scope("first_norm_backward"):
        grad_tokens, *sums = call(
            functools.partial(
                last_kernel, sizes=all_sizes, runs=[runs[k] for k in all_names], split=[k in split for k in all_names]
            ),
            "first_norm_backward", seqs, None,
            [by_rows(grad_normed), by_rows(grad_residual), by_rows(tokens_in), params] + late[: int(reduce)],
            [((rows, width), F32, (steps, width), lambda j, c: (j, 0))] + [((4, 4 * n), F32) for n in all_sizes],
            [vf(width // LANES, steps + SEGS * SEGS, LANES)], int(1e7), int(11e6),
        )
    with jax.named_scope("factor_gradients"):
        if reduce:
            summed = dict(zip(all_names, sums))
        else:
            grads.update(zip([k for k in MIXER_ORDER[4:]], late))
            summed = scatter_plain(grads, runs, split)
    return (result.reshape(seqs, steps, width), grad_tokens.reshape(seqs, steps, width)) + tuple(
        summed[k] for k in names
    )


def solution(mesh):
    split = P("wshard", None)
    in_specs = (
        (P("wshard", "seq", None), P("wshard", "seq"), split, P("wshard", "seq", None))
        + (P(),) * 4
        + (split, split, P("wshard", None, None), P("wshard", None, None))
        + (split,) * 20
    )
    out_specs = (P("wshard", "seq", None),) * 2 + (P(("seq", "wshard"), None),) * 16
    return jax.shard_map(local, mesh=mesh, in_specs=in_specs, out_specs=out_specs, check_vma=False)
```

```python
import functools

import jax
import jax.numpy as jnp
from jax import lax
from jax.experimental import pallas as pl
from jax.experimental.pallas import tpu as pltpu
from jax.sharding import PartitionSpec as P

RANK = 16
EPSILON = 1e-06
RATE_SCALE = 8.0
ROOT_FLOOR = 0.001
GELU_A = 0.7978845608028654
GELU_B = 0.044715
LOG2_E = 1.4426950408889634
CHUNK = (16, 256)

HALO = 8
SEGS = 8
TILE = 512
LANES = 128
F32 = jnp.float32
BF16 = jnp.bfloat16


def mm(left, right):
    return lax.dot_general(left, right, (((1,), (0,)), ((), ())), preferred_element_type=F32)


def mm_nt(left, right):
    return lax.dot_general(left, right, (((1,), (1,)), ((), ())), preferred_element_type=F32)


def gelu_parts(x):
    square = x * x
    t = jnp.tanh(GELU_A * x * (1.0 + GELU_B * square))
    half = 0.5 * (1.0 + t)
    slope = half + 0.5 * x * (1.0 - t * t) * (GELU_A * (1.0 + 3.0 * GELU_B * square))
    return x * half, slope


def gelu(x):
    t = jnp.tanh(GELU_A * x * (1.0 + GELU_B * x * x))
    return 0.5 * x * (1.0 + t)


def interleave(steps, back=False):
    a = lax.broadcasted_iota(jnp.int32, (steps, steps), 0)
    b = lax.broadcasted_iota(jnp.int32, (steps, steps), 1)
    if back:
        a, b = b, a
    return jnp.where(b == (a % SEGS) * (steps // SEGS) + a // SEGS, 1.0, 0.0).astype(BF16)


def per_sequence(seqs, body):
    def one(s, none):
        body(s)
        return none

    lax.fori_loop(0, seqs, one, 0)


def row_at(start, offset, size):
    return pl.ds(pl.multiple_of(start + offset, size), size)


def shift_in(rows8, edge, down):
    row = lax.broadcasted_iota(jnp.int32, rows8.shape, 0)
    if down:
        return jnp.where(row == 0, edge, pltpu.roll(rows8, 1, 0))
    return jnp.where(row == SEGS - 1, edge, pltpu.roll(rows8, SEGS - 1, 0))


def stack_ranks(core, own, other):
    first = core == 0
    return jnp.concatenate([jnp.where(first, own, other), jnp.where(first, other, own)], axis=0)


def flipped(values):
    return values.T.astype(BF16)


def fold(grad):
    ranks, wide = grad.shape
    half = wide // 2
    left, right = grad[:, :half], grad[:, half:]
    upper = lax.broadcasted_iota(jnp.int32, (ranks, half), 0) % 8 < 4
    blocks = []
    for pair in (
        jnp.where(upper, left, pltpu.roll(right, 4, 0)),
        jnp.where(upper, pltpu.roll(left, ranks - 4, 0), right),
    ):
        eights = pair.reshape(ranks // 8, 8, half)
        blocks.append(
            jnp.concatenate([eights[:, :, : half // 2], eights[:, :, half // 2 :]], axis=1).astype(BF16)
        )
    return blocks


def put_folded(out, grad):
    first, second = fold(grad)
    out[0] = first
    out[1] = second


def unfold(rows4, wide):
    quarter = wide // 4
    pieces = []
    for at in range(0, rows4.shape[1], quarter):
        here = rows4[:, at : at + quarter]
        pieces += [here[0:4], here[8:12], here[4:8], here[12:16]]
    return pieces


def halves(core, width):
    step = width // 2
    return (
        pl.ds(pl.multiple_of(core * step, 128), step),
        pl.ds(pl.multiple_of((1 - core) * step, 128), step),
    )


def to_core(sources, targets, send_sem, recv_sem):
    return [
        pltpu.make_async_remote_copy(
            src, dst, send_sem.at[i], recv_sem.at[i],
            device_id={"wshard": 1 - lax.axis_index("wshard")}, device_id_type=pl.DeviceIdType.MESH,
        )
        for i, (src, dst) in enumerate(zip(sources, targets))
    ]


def mixer_kernel(
    tokens_ref, ids_ref, table_ref, gain_ref, taps_ref, soft_ref,
    wr_own, sb_own, sr_own, er_own, sd_own, si_own, bd_own, bi_own, ed_own, ei_own,
    *refs, carried,
):
    needed = 10
    first_sources, sources, refs = refs[:needed], refs[needed : needed + carried], refs[needed + carried :]
    (normed_out, picked_br_out, picked_di_out, mixed_out, rate_out, inflow_out, local_out, reach_out,
     ends_out, spans_out, summary_out, onehot_ref, masks_ref, tokens_out), refs = refs[:14], refs[14:]
    first_targets, targets, refs = refs[:needed], refs[needed : needed + carried], refs[needed + carried :]
    arriving, refs = refs[:needed], refs[needed:]
    wr_oth, sb_oth, sr_oth, er_oth, sd_oth, si_oth, bd_oth, bi_oth, ed_oth, ei_oth = arriving
    (normed, picked_r, inner_gate, picked_gate, mixed_all, filt, halo, ids_in,
     first_s, first_r, wr_s, wr_r, keep_sem, halo_s, halo_r, ids_s, ids_r, send_sem, recv_sem) = refs
    core = lax.axis_index("wshard")
    chip = lax.axis_index("seq")
    step = pl.program_id(0)
    rows, width = tokens_ref.shape
    ranks = onehot_ref.shape[1]
    seqs = ids_ref.shape[0]
    steps = rows // seqs
    lane_tiles = pl.num_programs(0) // 2
    tile = mixed_out.shape[1]
    lags = taps_ref.shape[0] - 1

    def rim_copies():
        return [
            pltpu.make_async_remote_copy(
                tokens_ref.at[(s + 1) * steps - 2 * HALO : (s + 1) * steps, :], halo.at[s], halo_s.at[s], halo_r.at[s],
                device_id=ring_peer(1), device_id_type=pl.DeviceIdType.MESH,
            )
            for s in range(seqs)
        ] + [message(ids_ref, ids_in, ids_s, ids_r, slot, by) for slot, by in enumerate((1, -1))]

    def weight_copies(low, high):
        return [
            pltpu.make_async_remote_copy(
                first_sources[i], arriving[i], first_s.at[i - 1], first_r.at[i - 1],
                device_id={"wshard": 1 - core}, device_id_type=pl.DeviceIdType.MESH,
            )
            for i in range(low, high)
        ]

    def wr_copy(piece):
        cols = pl.ds(pl.multiple_of(piece * tile, 128), tile)
        return pltpu.make_async_remote_copy(
            first_sources[0].at[:, cols], wr_oth.at[:, cols], wr_s.at[piece], wr_r.at[piece],
            device_id={"wshard": 1 - core}, device_id_type=pl.DeviceIdType.MESH,
        )

    def kept_copies():
        return [
            pltpu.make_async_copy(src, dst, keep_sem.at[i]) for i, (src, dst) in enumerate(zip(arriving, first_targets))
        ]

    @pl.when(step == 0)
    def _():
        greet([1, -1], True)
        for copy in rim_copies():
            copy.start()
        for copy in weight_copies(1, 4):
            copy.start()
        for piece in range(wr_s.shape[0]):
            wr_copy(piece).start()
        for copy in weight_copies(4, needed):
            copy.start()
        for copy in to_core(sources, targets, send_sem, recv_sem):
            copy.start()
        gain = gain_ref[0:1, :width]

        def norm(values):
            scale = lax.rsqrt(jnp.mean(values * values, axis=1, keepdims=True) + EPSILON)
            return (values * scale * gain).astype(BF16)

        order = interleave(steps)
        for s in range(seqs):
            here = slice(s * steps, (s + 1) * steps)
            tokens_out[here, :] = mm(order, tokens_ref[here, :]).astype(BF16)

        def some(i, none):
            here = pl.ds(pl.multiple_of(i * 32, 32), 32)
            low = norm(tokens_out[here, :].astype(F32))
            normed[here, :] = low
            normed_out[here, :] = low
            return none

        lax.fori_loop(0, rows // 32, some, 0)
        for copy in rim_copies():
            copy.wait()
        rim = jnp.concatenate([halo[s].astype(F32)[HALO:, :] for s in range(seqs)], axis=0)
        normed[rows:, :] = norm(jnp.where(chip > 0, rim, 0.0))
        blank = jnp.zeros((steps - seqs, steps), F32)
        upright = lambda ids: jnp.concatenate([ids.astype(F32), blank], axis=0).T
        mine, before, after = upright(ids_ref[...]), upright(ids_in[0]), upright(ids_in[1])
        row = lax.broadcasted_iota(jnp.int32, (steps, steps), 0)
        lane = lax.broadcasted_iota(jnp.int32, (steps, ranks), 1)
        columns = []
        for lag in range(1, lags + 1):
            prior = jnp.where(row < lag, pltpu.roll(before, lag, 0), pltpu.roll(mine, lag, 0))
            inside = jnp.logical_or(row >= lag, chip > 0)
            columns.append(jnp.where(jnp.logical_and(prior == mine, inside), 1.0, 0.0))
        for lag in range(1, lags + 1):
            later = jnp.where(row >= steps - lag, pltpu.roll(after, steps - lag, 0), pltpu.roll(mine, steps - lag, 0))
            inside = jnp.logical_or(row < steps - lag, chip < lax.axis_size("seq") - 1)
            columns.append(jnp.where(jnp.logical_and(later == mine, inside), 1.0, 0.0))

        def owned(ids, s):
            owner = jnp.zeros_like(ids)
            for d in range(table_ref.shape[1]):
                owner = jnp.where(ids == float(d), table_ref[s, d].astype(F32), owner)
            return jnp.where(owner == (lane[: ids.shape[0], :] // RANK).astype(F32), 1.0, 0.0)

        halo_owned = []
        for s in range(seqs):
            here = slice(s * steps, (s + 1) * steps)
            packed = jnp.zeros((steps, ranks), F32)
            for at, column in enumerate(columns):
                packed = jnp.where(lane == at, jnp.broadcast_to(column[:, s : s + 1], (steps, ranks)), packed)
            masks_ref[here, :] = mm(order, packed.astype(BF16))
            onehot_ref[here, :] = mm(order, owned(jnp.broadcast_to(mine[:, s : s + 1], (steps, ranks)), s).astype(BF16))
            halo_owned.append(owned(jnp.broadcast_to(before[steps - HALO :, s : s + 1], (HALO, ranks)), s))
        for copy in weight_copies(1, 4):
            copy.wait()
        shrink = jnp.concatenate(
            [stack_ranks(core, sb_own[...], sb_oth[...]), stack_ranks(core, sr_own[...], sr_oth[...])], axis=0
        )
        inner = mm_nt(normed[...], shrink)
        onehot = jnp.concatenate([onehot_ref[...]] + halo_owned, axis=0)
        picked = (inner * jnp.concatenate([onehot, onehot], axis=1)).astype(BF16)
        picked_r[...] = picked[:, ranks:]
        picked_br_out[...] = picked[:rows, :]
        inner_gate[...] = jnp.zeros_like(inner_gate)

    @pl.when(step < lane_tiles)
    def _():
        own, oth = halves(core, width)
        at = pl.multiple_of(step * tile, 128)
        cols = pl.ds(at, tile)
        recur = mm(normed[:, own], wr_own[...]) + mm(
            picked_r[...], stack_ranks(core, er_own[...], er_oth[:, cols])
        )
        wr_copy(step).wait()
        recur = recur + mm(normed[:, oth], wr_oth[:, cols])
        filt[...] = recur
        seg = steps // SEGS

        def filtered(s):
            start = s * steps
            at_run = lambda i: filt[row_at(start, i * SEGS, SEGS), :]
            rim = filt[row_at(rows + s * HALO, 0, HALO), :]
            runs = {-lag: shift_in(at_run(seg - lag), rim[HALO - lag : HALO - lag + 1, :], True) for lag in range(1, lags + 1)}
            for i in range(seg):
                here = row_at(start, i * SEGS, SEGS)
                runs[i] = at_run(i)
                total = taps_ref[0:1, :] * runs[i]
                for lag in range(1, lags + 1):
                    total = total + taps_ref[lag : lag + 1, :] * runs[i - lag] * masks_ref[here, lag - 1 : lag]
                mixed_out[here, :] = total
                mixed_all[here, cols] = total

        per_sequence(seqs, filtered)

        @pl.when(step == 0)
        def _():
            for copy in weight_copies(4, needed):
                copy.wait()

        shrink = jnp.concatenate(
            [stack_ranks(core, sd_own[...], sd_oth[:, cols]), stack_ranks(core, si_own[...], si_oth[:, cols])], axis=0
        )
        inner_gate[...] += mm_nt(mixed_out[...].astype(BF16), shrink)

    @pl.when(step == lane_tiles - 1)
    def _():
        for copy in kept_copies():
            copy.start()
        onehot = onehot_ref[...]
        picked = (inner_gate[...] * jnp.concatenate([onehot, onehot], axis=1)).astype(BF16)
        picked_gate[...] = picked
        picked_di_out[...] = picked

    @pl.when(step >= lane_tiles)
    def _():
        at = pl.multiple_of((step - lane_tiles) * tile, 128)
        cols = pl.ds(at, tile)
        low = mixed_all[:, cols].astype(BF16)
        blocks, block = bd_own.shape[0], bd_own.shape[1]
        piece = step - lane_tiles
        mine = piece // (lane_tiles // 2) == core
        local_block = (piece % (lane_tiles // 2)) * blocks
        rates, inflows = [], []
        for b in range(blocks):
            both = jnp.concatenate(
                [jnp.where(mine, bd_own[b], bd_oth[local_block + b]), jnp.where(mine, bi_own[b], bi_oth[local_block + b])],
                axis=1,
            )
            pair = mm(low[:, b * block : (b + 1) * block], both)
            rates.append(pair[:, :block])
            inflows.append(pair[:, block:])
        rate_pre = jnp.concatenate(rates, axis=1) + mm(
            picked_gate[:, :ranks], stack_ranks(core, ed_own[...], ed_oth[:, cols])
        )
        inflow_pre = jnp.concatenate(inflows, axis=1) + mm(
            picked_gate[:, ranks:], stack_ranks(core, ei_own[...], ei_oth[:, cols])
        )
        rate_out[...] = rate_pre
        inflow_out[...] = inflow_pre
        seg = steps // SEGS

        def scanned(s):
            held = span = None
            for i in range(seg):
                here = row_at(s * steps, i * SEGS, SEGS)
                rate = jax.nn.sigmoid(rate_out[here, :])
                inflow = jax.nn.sigmoid(inflow_out[here, :])
                rate_out[here, :] = rate
                inflow_out[here, :] = inflow
                keep = masks_ref[here, 0:1]
                raw = jnp.exp2(rate * soft_ref[2:3, :])
                bounded = jnp.maximum((1.0 - raw) * (1.0 + raw), ROOT_FLOOR)
                root = keep * (bounded * lax.rsqrt(bounded)) + (1.0 - keep)
                decay = raw * keep
                drive = root * inflow * mixed_all[here, cols]
                held = drive if held is None else decay * held + drive
                span = decay if span is None else decay * span
                local_out[here, :] = held
                reach_out[here, :] = span
            ends_out[row_at(s * SEGS, 0, SEGS), :] = held
            spans_out[row_at(s * SEGS, 0, SEGS), :] = span
            total, product = held[0:1, :], span[0:1, :]
            for g in range(1, SEGS):
                total = held[g : g + 1, :] + span[g : g + 1, :] * total
                product = span[g : g + 1, :] * product
            summary_out[pl.ds(s, 1), :] = product
            summary_out[pl.ds(seqs + s, 1), :] = total

        per_sequence(seqs, scanned)

    @pl.when(step == 2 * lane_tiles - 1)
    def _():
        for copy in kept_copies():
            copy.wait()
        for copy in to_core(sources, targets, send_sem, recv_sem):
            copy.wait()


def ring_peer(by):
    peers = lax.axis_size("seq")
    return {"seq": (lax.axis_index("seq") + by + peers) % peers}


def greet(shifts, with_core, chips=()):
    barrier = pltpu.get_barrier_semaphore()
    peers = [ring_peer(by) for by in shifts] + [{"seq": chip} for chip in chips]
    if with_core:
        peers.append({"wshard": 1 - lax.axis_index("wshard")})
    for peer in peers:
        pl.semaphore_signal(barrier, inc=1, device_id=peer, device_id_type=pl.DeviceIdType.MESH)
    pl.semaphore_wait(barrier, len(peers))


def message(src, inbox, send_sem, recv_sem, slot, by):
    return pltpu.make_async_remote_copy(
        src, inbox.at[slot], send_sem.at[slot], recv_sem.at[slot],
        device_id=ring_peer(by), device_id_type=pl.DeviceIdType.MESH,
    )


def arrived(inbox, seqs, lanes, valid):
    value = None
    for d in range(inbox.shape[0], 0, -1):
        total = jnp.where(valid(d), inbox[d - 1, seqs : 2 * seqs, lanes], 0.0)
        if value is not None:
            total = total + jnp.where(valid(d), inbox[d - 1, :seqs, lanes], 0.0) * value
        value = total
    return value


def branch_output_kernel(
    summary_ref, normed_ref, picked_ref, wb_own, wb_oth, eb_own, eb_oth,
    local_ref, reach_ref, ends_ref, spans_ref, tokens_ref, onehot_ref, gain_ref,
    wo_own, wo_oth, so_own, so_oth, eo_own, eo_oth,
    *refs, carried,
):
    sources, refs = refs[:carried], refs[carried:]
    (pre_out, state_out, merged_out, carry_out, residual_out, second_out, picked_out), refs = refs[:7], refs[7:]
    targets, refs = refs[:carried], refs[carried:]
    branch_all, acc, inner, inbox, send_sem, recv_sem, core_s, core_r = refs
    core = lax.axis_index("wshard")
    step = pl.program_id(0)
    count = pl.num_programs(0) // 2
    hops = inbox.shape[0]
    rows, tile = local_ref.shape
    seqs = ends_ref.shape[0] // SEGS
    steps = rows // seqs
    seg = steps // SEGS

    @pl.when(step == 0)
    def _():
        greet([d for d in range(1, hops + 1)] + [-d for d in range(1, hops + 1)], True)
        for copy in to_core(sources, targets, core_s, core_r):
            copy.start()
        for d in range(1, hops + 1):
            message(summary_ref, inbox, send_sem, recv_sem, d - 1, d).start()
        acc[...] = jnp.zeros_like(acc)
        inner[...] = jnp.zeros_like(inner)

    @pl.when(step < count)
    def _():
        own, oth = halves(core, normed_ref.shape[1])
        pre = (
            mm(normed_ref[:, own], wb_own[...])
            + mm(normed_ref[:, oth], wb_oth[...])
            + mm(picked_ref[...], stack_ranks(core, eb_own[...], eb_oth[...]))
        )
        pre_out[...] = pre
        branch_all[:, pl.ds(pl.multiple_of(step * tile, 128), tile)] = gelu(pre)

    @pl.when(step == count)
    def _():
        for d in range(1, hops + 1):
            copy = message(summary_ref, inbox, send_sem, recv_sem, d - 1, d)
            copy.wait_send()
            copy.wait_recv()

    @pl.when(step >= count)
    def _():
        at = pl.multiple_of((step - count) * tile, 128)
        start = arrived(inbox, seqs, pl.ds(at, tile), lambda d: lax.axis_index("seq") >= d)
        carry_out[...] = jnp.concatenate([start, jnp.zeros_like(start)], axis=0)
        for s in range(seqs):
            carries = [start[s : s + 1, :]]
            for g in range(SEGS - 1):
                row = s * SEGS + g
                carries.append(ends_ref[row : row + 1, :] + spans_ref[row : row + 1, :] * carries[-1])
            carry = jnp.concatenate(carries, axis=0)
            for i in range(0, seg, 2):
                states = []
                for k in (i, i + 1):
                    here = slice(s * steps + k * SEGS, s * steps + (k + 1) * SEGS)
                    state = local_ref[here, :] + reach_ref[here, :] * carry
                    state_out[here, :] = state
                    states.append(branch_all[here, pl.ds(at, tile)] * state)
                merged_out[s * steps + i * SEGS : s * steps + (i + 2) * SEGS, :] = jnp.concatenate(states, axis=0).astype(BF16)
        merged = merged_out[...]
        mine = (step - count) // (count // 2) == core

        @pl.when(mine)
        def _():
            acc[...] += mm(merged, wo_own[...])

        @pl.when(jnp.logical_not(mine))
        def _():
            acc[...] += mm(merged, wo_oth[...])

        inner[...] += mm_nt(merged, stack_ranks(core, so_own[...], so_oth[...]))

    @pl.when(step == 2 * count - 1)
    def _():
        picked = (inner[...] * onehot_ref[...]).astype(BF16)
        picked_out[...] = picked
        residual = (
            tokens_ref[...].astype(F32)
            + acc[...]
            + mm(picked, stack_ranks(core, eo_own[...], eo_oth[...]))
        )
        residual_out[...] = residual
        scale = lax.rsqrt(jnp.mean(residual * residual, axis=1, keepdims=True) + EPSILON)
        second_out[...] = (residual * scale * gain_ref[1:2, : residual.shape[1]]).astype(BF16)
        for copy in to_core(sources, targets, core_s, core_r):
            copy.wait()


def feed_kernel(
    core_ref, second_ref, cot_ref, residual_ref, onehot_ref, gain_ref,
    g_own_a, g_own_b, g_oth_a, g_oth_b, u_own_a, u_own_b, u_oth_a, u_oth_b, d_own, d_oth,
    sg_own, sg_oth, su_own, su_oth, eg_own_a, eg_own_b, eg_oth_a, eg_oth_b,
    eu_own_a, eu_own_b, eu_oth_a, eu_oth_b, sd_own_a, sd_own_b, sd_oth_a, sd_oth_b, ed_own, ed_oth,
    out_ref, grad_residual_out, grad_low_out, deg_out, deu_out, dsd_out, dsg_out, dsu_out, ded_out,
    picked, picked_t, gi_down, gi_down_t, down_acc, inner_down, grad_second, gi_gate, cot, *, seqs,
):
    core = core_ref[0]
    step = pl.program_id(0)
    ranks = onehot_ref.shape[1]
    width = second_ref.shape[1]
    part = d_own.shape[0]
    own, oth = halves(core, width)
    steps = second_ref.shape[0] // seqs

    @pl.when(step == 0)
    def _():
        onehot = onehot_ref[...]
        shrink = jnp.concatenate(
            [stack_ranks(core, sg_own[...], sg_oth[...]), stack_ranks(core, su_own[...], su_oth[...])], axis=0
        )
        both = mm_nt(second_ref[...], shrink) * jnp.concatenate([onehot, onehot], axis=1)
        picked[...] = both.astype(BF16)
        picked_t[...] = flipped(both)
        order = interleave(steps)
        for s in range(seqs):
            here = slice(s * steps, (s + 1) * steps)
            cot[here, :] = mm(order, cot_ref[here, :]).astype(BF16)
        inner = mm_nt(cot[...], stack_ranks(core, ed_own[...], ed_oth[...])) * onehot
        gi_down[...] = inner.astype(BF16)
        gi_down_t[...] = flipped(inner)
        down_acc[...] = jnp.zeros_like(down_acc)
        inner_down[...] = jnp.zeros_like(inner_down)
        grad_second[...] = jnp.zeros_like(grad_second)
        gi_gate[...] = jnp.zeros_like(gi_gate)

    join = lambda a, b: jnp.concatenate([a[...], b[...]], axis=1)
    g_own, g_oth = join(g_own_a, g_own_b), join(g_oth_a, g_oth_b)
    u_own, u_oth = join(u_own_a, u_own_b), join(u_oth_a, u_oth_b)
    down = jnp.concatenate([d_own[...], d_oth[...]], axis=0)
    eg = stack_ranks(core, join(eg_own_a, eg_own_b), join(eg_oth_a, eg_oth_b))
    eu = stack_ranks(core, join(eu_own_a, eu_own_b), join(eu_oth_a, eu_oth_b))
    sd = stack_ranks(core, join(sd_own_a, sd_own_b), join(sd_oth_a, sd_oth_b))

    x_own, x_oth = second_ref[:, own], second_ref[:, oth]
    def first_products(side, g_up, g_low, u_up, u_low, rows_down):
        lanes = slice(side * part, (side + 1) * part)
        gating = mm(x_own, g_up[...]) + mm(x_oth, g_low[...]) + mm(picked[:, :ranks], eg[:, lanes])
        upward = mm(x_own, u_up[...]) + mm(x_oth, u_low[...]) + mm(picked[:, ranks:], eu[:, lanes])
        grad_hidden = mm_nt(cot[...], rows_down[...]) + mm(gi_down[...], sd[:, lanes])
        return gating, upward, grad_hidden

    def chain(gating, upward, grad_hidden):
        smooth, slope = gelu_parts(gating)
        return (
            (smooth * upward).astype(BF16),
            (grad_hidden * upward * slope).astype(BF16),
            (grad_hidden * smooth).astype(BF16),
        )

    mine = first_products(0, g_own_a, g_oth_a, u_own_a, u_oth_a, d_own)
    hidden_a, grad_gating_a, grad_upward_a = chain(*mine)
    other = first_products(1, g_own_b, g_oth_b, u_own_b, u_oth_b, d_oth)
    hidden_b, grad_gating_b, grad_upward_b = chain(*other)
    hidden = jnp.concatenate([hidden_a, hidden_b], axis=1)
    grad_gating = jnp.concatenate([grad_gating_a, grad_gating_b], axis=1)
    grad_upward = jnp.concatenate([grad_upward_a, grad_upward_b], axis=1)
    down_acc[...] += mm(hidden, down)
    inner_down[...] += mm_nt(hidden, sd)
    grad_second[:, own] += mm_nt(grad_gating, g_own) + mm_nt(grad_upward, u_own)
    grad_second[:, oth] += mm_nt(grad_gating, g_oth) + mm_nt(grad_upward, u_oth)
    gi_gate[:, :ranks] += mm_nt(grad_gating, eg)
    gi_gate[:, ranks:] += mm_nt(grad_upward, eu)
    for out, grad in (
        (deg_out, mm(picked_t[:ranks, :], grad_gating)),
        (deu_out, mm(picked_t[ranks:, :], grad_upward)),
        (dsd_out, mm(gi_down_t[...], hidden)),
    ):
        low, high = grad[:, :part], grad[:, part:]
        first = core == 0
        put_folded(
            out, jnp.concatenate([jnp.where(first, low, high), jnp.where(first, high, low)], axis=1)
        )

    @pl.when(step == pl.num_programs(0) - 1)
    def _():
        onehot = onehot_ref[...]
        chosen = inner_down[...] * onehot
        residual = residual_ref[...]
        result = (
            residual + down_acc[...] + mm(chosen.astype(BF16), stack_ranks(core, ed_own[...], ed_oth[...]))
        ).astype(BF16)
        order = interleave(steps, True)
        for s in range(seqs):
            here = slice(s * steps, (s + 1) * steps)
            out_ref[here, :] = mm(order, result[here, :]).astype(BF16)
        put_folded(ded_out, mm(flipped(chosen), cot[...]))
        inner = gi_gate[...] * jnp.concatenate([onehot, onehot], axis=1)
        shrink = jnp.concatenate(
            [stack_ranks(core, sg_own[...], sg_oth[...]), stack_ranks(core, su_own[...], su_oth[...])], axis=0
        )
        grads = mm(flipped(inner), second_ref[...])
        put_folded(dsg_out, grads[:ranks, :])
        put_folded(dsu_out, grads[ranks:, :])
        weighted = (grad_second[...] + mm(inner.astype(BF16), shrink)) * gain_ref[1:2, : residual.shape[1]]
        scale = lax.rsqrt(jnp.mean(residual * residual, axis=1, keepdims=True) + EPSILON)
        grad = (
            cot[...].astype(F32)
            + scale * weighted
            - residual * (scale * scale * scale * jnp.mean(weighted * residual, axis=1, keepdims=True))
        )
        grad_residual_out[...] = grad
        grad_low_out[...] = grad.astype(BF16)


FEED_ORDER = ("eg", "sdn", "eu", "sg", "su", "edn")
MIXER_ORDER = ("eo", "eb", "so", "sb", "edec", "sdec", "einf", "sinf", "er", "sr")
FEED_PIECES = ((0, 2, 0), (2, 4, 1))
MIXER_PIECES = ((0, 2, 0), (2, 2, 1), (4, 2, 0), (6, 2, 1), (8, 1, 0), (9, 1, 1))


class Links:
    def __init__(self):
        self.core = lax.axis_index("wshard")
        chip = lax.axis_index("seq")
        self.x, self.y, self.z = chip % 2, (chip // 2) % 2, chip // 4
        self.x_peer = chip + 1 - 2 * self.x
        self.y_peer = chip + 2 - 4 * self.y
        self.z_peers = [((self.z + d) % 4) * 4 + chip % 4 for d in (1, 2, 3)]

    def chips(self):
        return [self.x_peer, self.y_peer] + self.z_peers

    def copy(self, src, dst, send, recv, device):
        return pltpu.make_async_remote_copy(
            src, dst, send, recv, device_id=device, device_id_type=pl.DeviceIdType.MESH
        )

    def across(self, src, core_in, cols, send, recv):
        return self.copy(src, core_in.at[:, :, cols], send, recv, {"wshard": 1 - self.core})

    def first(self, send1, recv1, cols, direction, send, recv):
        peer = self.x_peer if direction == 0 else self.y_peer
        return self.copy(send1.at[:, :, cols], recv1.at[:, :, cols], send, recv, {"seq": peer})

    def second(self, send2, recv2, cols, direction, send, recv):
        peer = self.y_peer if direction == 0 else self.x_peer
        return self.copy(send2.at[:, :, cols], recv2.at[:, :, cols], send, recv, {"seq": peer})

    def third(self, send3, recv3, cols, send, recv, index):
        return [
            self.copy(
                send3.at[d, :, cols], recv3.at[d, :, cols], send.at[index, d], recv.at[index, d], {"seq": self.z_peers[d]}
            )
            for d in range(3)
        ]

    def split_first(self, own, core_in, kept, send1, own_cols, cols, direction):
        for p in range(4):
            for o in range(2):
                keep = p * 4 + (o * 2 + self.x if direction == 0 else self.y * 2 + o)
                give = p * 4 + (o * 2 + 1 - self.x if direction == 0 else (1 - self.y) * 2 + o)
                at = p * 2 + o
                if kept is not None:
                    kept[at, :, cols] = own[keep, :, own_cols].astype(F32) + core_in[keep, :, cols].astype(F32)
                send1[at, :, cols] = (
                    own[give, :, own_cols].astype(F32) + core_in[give, :, cols].astype(F32)
                ).astype(BF16)

    def split_second(self, own, core_in, recv1, kept2, send2, cols, direction):
        for p in range(4):
            at = p * 2 + (self.y if direction == 0 else self.x)
            keep = p * 4 + self.y * 2 + self.x
            kept2[p, :, cols] = (
                own[keep, :, cols].astype(F32) + core_in[keep, :, cols].astype(F32) + recv1[at, :, cols].astype(F32)
            )
            at = p * 2 + 1 - (self.y if direction == 0 else self.x)
            give = p * 4 + ((1 - self.y) * 2 + self.x if direction == 0 else self.y * 2 + 1 - self.x)
            send2[p, :, cols] = (
                own[give, :, cols].astype(F32) + core_in[give, :, cols].astype(F32) + recv1[at, :, cols].astype(F32)
            ).astype(BF16)

    def split_third(self, kept2, recv2, send3, out, cols, out_cols):
        out[:, out_cols] = kept2[self.z, :, cols] + recv2[self.z, :, cols].astype(F32)
        for d in range(3):
            to = (self.z + d + 1) % 4
            send3[d, :, cols] = (kept2[to, :, cols] + recv2[to, :, cols].astype(F32)).astype(BF16)

    def finish(self, recv3, out, cols, out_cols):
        out[:, out_cols] += (
            recv3[0, :, cols].astype(F32) + recv3[1, :, cols].astype(F32) + recv3[2, :, cols].astype(F32)
        )


def columns_of(sizes):
    return [pl.ds(sum(sizes[:i]), n) for i, n in enumerate(sizes)]


def pieces_of(sizes, pieces):
    return [pl.ds(sum(sizes[:i]), sum(sizes[i : i + n])) for i, n, _ in pieces]


def last_kernel(grad_ref, residual_ref, tokens_ref, gain_ref, *refs, sizes, runs, split):
    if sizes:
        sums_ref, refs = refs[0], refs[1:]
    out_ref, outs, kept = refs[0], refs[1:-1], refs[-1]
    weighted = grad_ref[...] * gain_ref[0:1, : grad_ref.shape[1]]
    values = tokens_ref[...].astype(F32)
    scale = lax.rsqrt(jnp.mean(values * values, axis=1, keepdims=True) + EPSILON)
    grad = (
        residual_ref[...]
        + scale * weighted
        - values * (scale * scale * scale * jnp.mean(weighted * values, axis=1, keepdims=True))
    )
    steps = grad.shape[0]
    for q in range(kept.shape[0]):
        kept[q, :steps, :] = grad[:, q * LANES : (q + 1) * LANES]
    for t in range(0, steps, SEGS):
        first = t % (steps // SEGS) * SEGS + t // (steps // SEGS)
        out_ref[t : t + SEGS, :] = jnp.concatenate(
            [kept[q, pl.ds(first, SEGS, stride=SEGS), :] for q in range(kept.shape[0])], axis=1
        )

    @pl.when(pl.program_id(0) == 0)
    def _():
        offset = 0
        for out, size, run, two in zip(outs, sizes, runs, split):
            pieces = unfold(sums_ref[:, offset : offset + size], run)
            if two:
                pieces = [p for i, p in enumerate(pieces) if i % 4 < 2] + [p for i, p in enumerate(pieces) if i % 4 >= 2]
            out[...] = jnp.concatenate(pieces, axis=1)
            offset += size


def scatter_plain(grads, runs, split):
    summed = {}
    for k, g in grads.items():
        quarter = runs[k] // 4
        g = g.astype(F32).reshape(2, g.shape[1], 4, 4, g.shape[3] // quarter, quarter)
        g = g[:, :, jnp.array([0, 2, 1, 3])]
        if k in split:
            g = g.reshape(g.shape[:2] + (2, 2) + g.shape[3:]).transpose(1, 0, 4, 2, 5, 3, 6)
        else:
            g = g.transpose(1, 0, 3, 4, 2, 5)
        g = g.reshape(g.shape[0] * 8, -1)
        summed[k] = lax.psum_scatter(g, ("seq", "wshard"), scatter_dimension=0, tiled=True)
    return summed


def branch_back_kernel(
    low_ref, onehot_ref, masks_ref, soft_ref, picked_ref, pre_ref, state_ref, merged_ref, rate_ref,
    wo_own, wo_oth, so_own, so_oth, eo_own, eo_oth,
    normed_ref, picked_b_ref, eb_own, eb_oth,
    *refs, feed_sizes, reduce,
):
    count_feed = len(feed_sizes)
    feed, refs = refs[:count_feed], refs[count_feed:]
    (grad_state_out, ends_out, spans_out, start_out, pre_grad_out, gi_b_out, dso_out, deo_out, dsb_out, deb_out), refs = (
        refs[:10], refs[10:]
    )
    if reduce:
        half_out, refs = refs[0], refs[1:]
    (gi, gi_t, grad_buf, pre_grad, summary, inbox, send_sem, recv_sem), refs = refs[:8], refs[8:]
    core = lax.axis_index("wshard")
    step = pl.program_id(0)
    count = pl.num_programs(0) - 1
    hops = inbox.shape[0]
    rows, tile = pre_ref.shape
    seqs = ends_out.shape[0] // SEGS
    steps = rows // seqs
    seg = steps // SEGS
    shifts = [d for d in range(1, hops + 1)] + [-d for d in range(1, hops + 1)]
    if reduce:
        own, core_in, send1, recv1, local_sem, core_s, core_r, s1_s, s1_r = refs
        cols = columns_of(feed_sizes)
        pieces = pieces_of(feed_sizes, FEED_PIECES)
        order = [d for _, _, d in FEED_PIECES]

    @pl.when(step == 0)
    def _():
        if reduce:
            links = Links()
            greet(shifts, True, links.chips())
            for a in range(count_feed):
                links.across(feed[a].at[1 - core], core_in, cols[a], core_s.at[a], core_r.at[a]).start()
                pltpu.make_async_copy(feed[a].at[core], own.at[:, :, cols[a]], local_sem.at[a]).start()
        else:
            greet(shifts, False)
        grad = mm_nt(low_ref[...], stack_ranks(core, eo_own[...], eo_oth[...])) * onehot_ref[...]
        gi[...] = grad.astype(BF16)
        gi_t[...] = flipped(grad)
        put_folded(deo_out, mm(flipped(picked_ref[...].astype(F32)), low_ref[...]))

    if reduce:

        @pl.when(step == 1)
        def _():
            links = Links()
            for a in range(count_feed):
                pltpu.make_async_copy(feed[a].at[core], own.at[:, :, cols[a]], local_sem.at[a]).wait()
                links.across(feed[a].at[1 - core], core_in, cols[a], core_s.at[a], core_r.at[a]).wait()
            for p, piece in enumerate(pieces):
                links.split_first(own, core_in, half_out, send1, piece, piece, order[p])
                links.first(send1, recv1, piece, order[p], s1_s.at[p], s1_r.at[p]).start()

    @pl.when(step < count)
    def _():
        at = pl.multiple_of(step * tile, 128)
        mine = step // (count // 2) == core

        @pl.when(mine)
        def _():
            grad_buf[...] = mm_nt(low_ref[...], wo_own[...])

        @pl.when(jnp.logical_not(mine))
        def _():
            grad_buf[...] = mm_nt(low_ref[...], wo_oth[...])

        grad_buf[...] += mm(gi[...], stack_ranks(core, so_own[...], so_oth[...]))
        put_folded(dso_out, mm(gi_t[...], merged_ref[...]))
        cols = pl.ds(at, tile)

        def scanned(s):
            held = span = above = None
            for i in range(seg - 2, -1, -2):
                pres = []
                for k in (i + 1, i):
                    here = row_at(s * steps, k * SEGS, SEGS)
                    grad_merged = grad_buf[here, :]
                    smooth, slope = gelu_parts(pre_ref[here, :])
                    pres.append(grad_merged * state_ref[here, :] * slope)
                    grad_state = grad_merged * smooth
                    grad_state_out[here, :] = grad_state
                    held = grad_state if held is None else above * held + grad_state
                    if above is not None:
                        span = above if span is None else above * span
                    above = jnp.exp2(rate_ref[here, :] * soft_ref[2:3, :]) * masks_ref[here, 0:1]
                pre = jnp.concatenate(pres[::-1], axis=0).astype(BF16)
                here = row_at(s * steps, i * SEGS, 2 * SEGS)
                pre_grad[here, cols] = pre
                pre_grad_out[here, :] = pre
            held = above * held
            span = above * span
            ends_out[row_at(s * SEGS, 0, SEGS), :] = held
            spans_out[row_at(s * SEGS, 0, SEGS), :] = span
            total, product = held[SEGS - 1 : SEGS, :], span[SEGS - 1 : SEGS, :]
            for g in range(SEGS - 2, -1, -1):
                total = held[g : g + 1, :] + span[g : g + 1, :] * total
                product = span[g : g + 1, :] * product
            summary[pl.ds(s, 1), cols] = product
            summary[pl.ds(seqs + s, 1), cols] = total

        per_sequence(seqs, scanned)

    @pl.when(step == count)
    def _():
        for d in range(1, hops + 1):
            message(summary, inbox, send_sem, recv_sem, d - 1, -d).start()
        picked_t = flipped(picked_b_ref[...].astype(F32))
        expand = stack_ranks(core, eb_own[...], eb_oth[...])
        grad = mm_nt(pre_grad[...], expand) * onehot_ref[...]
        gi_b_out[...] = grad.astype(BF16)
        put_folded(dsb_out, mm(flipped(grad), normed_ref[...]))
        for piece in range(pre_grad.shape[1] // tile):
            first, second = fold(mm(picked_t, pre_grad[:, piece * tile : (piece + 1) * tile]))
            lanes = slice(piece * tile // 4, (piece + 1) * tile // 4)
            deb_out[0, :, :, lanes] = first
            deb_out[1, :, :, lanes] = second
        for d in range(1, hops + 1):
            copy = message(summary, inbox, send_sem, recv_sem, d - 1, -d)
            copy.wait_send()
            copy.wait_recv()
        peers = lax.axis_size("seq")
        start = arrived(inbox, seqs, slice(None), lambda d: lax.axis_index("seq") + d < peers)
        start_out[...] = jnp.concatenate([start, jnp.zeros_like(start)], axis=0)
        if reduce:
            links = Links()
            for p, piece in enumerate(pieces):
                links.first(send1, recv1, piece, order[p], s1_s.at[p], s1_r.at[p]).wait()
            for at in range(half_out.shape[0]):
                half_out[at] += recv1[at].astype(F32)


def recur_back_kernel(
    grad_state_ref, ends_ref, spans_ref, start_ref, carry_ref, state_ref, mixed_ref, rate_ref, inflow_ref,
    masks_ref, onehot_ref, soft_ref, picked_ref,
    bd_own, bd_oth, bi_own, bi_oth, ed_own, ed_oth, ei_own, ei_oth, sd_own, sd_oth, si_own, si_oth,
    taps_ref, normed_ref, picked_r_ref, er_own, er_oth,
    wr_own, wr_oth, sr_own, sr_oth, pre_grad_ref, gi_b_ref, wb_own, wb_oth, sb_own, sb_oth,
    *refs, feed_sizes, mixer_sizes, reduce,
):
    if reduce:
        half_ref, early_grads, refs = refs[0], refs[1:5], refs[5:]
        out_ref, sums_out, refs = refs[0], refs[1], refs[2:]
    else:
        out_ref, late_outs, refs = refs[0], refs[1:7], refs[7:]
    (partial, inner, gi, gi_t, picked_t, low, inner_r, picked_rt, heads, inbox,
     head_s, head_r, rate_grad, inflow_grad), refs = refs[:14], refs[14:]
    core = lax.axis_index("wshard")
    step = pl.program_id(0)
    count = (pl.num_programs(0) - 1) // 3
    rows, tile = state_ref.shape
    ranks = onehot_ref.shape[1]
    seqs = ends_ref.shape[0] // SEGS
    steps = rows // seqs
    seg = steps // SEGS
    lags = taps_ref.shape[0] - 1
    order = [d for _, _, d in MIXER_PIECES]

    if reduce:
        (kept2_f, send2_f, recv2_f, send3_f, recv3_f, f2_s, f2_r, f3_s, f3_r,
         mine_g, core_in, send1, recv1, kept2, send2, recv2, send3, recv3,
         local_sem, core_s, core_r, s1_s, s1_r, s2_s, s2_r, s3_s, s3_r) = refs
        fcols = pieces_of(feed_sizes, FEED_PIECES)
        forder = [d for _, _, d in FEED_PIECES]
        mcols = columns_of(mixer_sizes)
        pcols = pieces_of(mixer_sizes, MIXER_PIECES)
        base = sum(feed_sizes)
        sums_cols = [pl.ds(base + c.start, c.size) for c in pcols]

        def feed_second(links):
            for a in range(len(fcols)):
                mine = links.y if forder[a] == 0 else links.x
                for p in range(4):
                    kept2_f[p, :, fcols[a]] = half_ref[p * 2 + mine, :, fcols[a]]
                    send2_f[p, :, fcols[a]] = half_ref[p * 2 + 1 - mine, :, fcols[a]].astype(BF16)
                links.second(send2_f, recv2_f, fcols[a], forder[a], f2_s.at[a], f2_r.at[a]).start()

        def feed_third(links):
            for a in range(len(fcols)):
                links.second(send2_f, recv2_f, fcols[a], forder[a], f2_s.at[a], f2_r.at[a]).wait()
                links.split_third(kept2_f, recv2_f, send3_f, sums_out, fcols[a], fcols[a])
                for copy in links.third(send3_f, recv3_f, fcols[a], f3_s, f3_r, a):
                    copy.start()

        def feed_finish(links):
            for a in range(len(fcols)):
                for copy in links.third(send3_f, recv3_f, fcols[a], f3_s, f3_r, a):
                    copy.wait()
                links.finish(recv3_f, sums_out, fcols[a], fcols[a])

        def source(a):
            return early_grads[a].at[1 - core] if a < 4 else mine_g.at[1 - core, :, :, mcols[a]]

        def cross(links, which):
            for a in which:
                if a < 4:
                    pltpu.make_async_copy(
                        early_grads[a].at[core], mine_g.at[core, :, :, mcols[a]], local_sem.at[a]
                    ).start()
                links.across(source(a), core_in, mcols[a], core_s.at[a], core_r.at[a]).start()

        def first(links, which):
            for p in which:
                for a in range(MIXER_PIECES[p][0], MIXER_PIECES[p][0] + MIXER_PIECES[p][1]):
                    if a < 4:
                        pltpu.make_async_copy(
                            early_grads[a].at[core], mine_g.at[core, :, :, mcols[a]], local_sem.at[a]
                        ).wait()
                    links.across(source(a), core_in, mcols[a], core_s.at[a], core_r.at[a]).wait()
                links.split_first(mine_g.at[core], core_in, None, send1, pcols[p], pcols[p], order[p])
                links.first(send1, recv1, pcols[p], order[p], s1_s.at[p], s1_r.at[p]).start()

        def second(links, which):
            for p in which:
                links.first(send1, recv1, pcols[p], order[p], s1_s.at[p], s1_r.at[p]).wait()
                links.split_second(mine_g.at[core], core_in, recv1, kept2, send2, pcols[p], order[p])
                links.second(send2, recv2, pcols[p], order[p], s2_s.at[p], s2_r.at[p]).start()

        def third(links, which):
            for p in which:
                links.second(send2, recv2, pcols[p], order[p], s2_s.at[p], s2_r.at[p]).wait()
                links.split_third(kept2, recv2, send3, sums_out, pcols[p], sums_cols[p])
                for copy in links.third(send3, recv3, pcols[p], s3_s, s3_r, p):
                    copy.start()

        def finish(links, which):
            for p in which:
                for copy in links.third(send3, recv3, pcols[p], s3_s, s3_r, p):
                    copy.wait()
                links.finish(recv3, sums_out, pcols[p], sums_cols[p])

        A, B, D = (0, 1), (2, 3), (4, 5)
        plan = {
            0: [(cross, (0, 1, 2, 3)), (feed_second, None)],
            1: [(first, A)],
            2: [(feed_third, None)],
            3: [(second, A)],
            4: [(cross, (4, 6)), (third, A)],
            5: [(cross, (5, 7))],
            6: [(first, B)],
            8: [(second, B)],
            9: [(cross, (8, 9))],
            10: [(first, D), (third, B)],
            12: [(second, D), (feed_finish, None), (finish, A)],
        }
        tail = [(third, D), (finish, B), (finish, D)]

        def run(links, what):
            for action, which in what:
                action(links) if which is None else action(links, which)

        def late_grad(index, grad, piece=None):
            width = grad.shape[1] // 4
            start = sum(mixer_sizes[:index])
            if piece is None or isinstance(piece, int):
                at = pl.ds(start + (piece or 0) * width, width)
            else:
                at = pl.ds(pl.multiple_of(start + piece * width, 128), width)
            for half, block in enumerate(fold(grad)):
                mine_g[half, :, :, at] = block

    else:

        def late_grad(index, grad, piece=None):
            if isinstance(piece, int):
                lanes = slice(piece * grad.shape[1] // 4, (piece + 1) * grad.shape[1] // 4)
                for half, block in enumerate(fold(grad)):
                    late_outs[index - 4][half, :, :, lanes] = block
            else:
                put_folded(late_outs[index - 4], grad)

    @pl.when(step == 0)
    def _():
        if reduce:
            greet([1, -1], True, Links().chips())
        else:
            greet([1, -1], False)
        inner[...] = jnp.zeros_like(inner)
        inner_r[...] = jnp.zeros_like(inner_r)
        picked_t[...] = flipped(picked_ref[...].astype(F32))
        picked_rt[...] = flipped(picked_r_ref[...].astype(F32))

    if reduce:
        for at_step, what in plan.items():

            @pl.when(step == at_step)
            def _(what=what):
                run(Links(), what)

    def head_copy(slot):
        return pltpu.make_async_remote_copy(
            heads.at[slot], inbox.at[slot], head_s.at[slot], head_r.at[slot],
            device_id=ring_peer(-1), device_id_type=pl.DeviceIdType.MESH,
        )

    @pl.when(step < count)
    def _():
        cols = pl.ds(pl.multiple_of(step * tile, 128), tile)

        def scanned(s):
            carries = [start_ref[pl.ds(s, 1), :]]
            ends, spans = ends_ref[row_at(s * SEGS, 0, SEGS), :], spans_ref[row_at(s * SEGS, 0, SEGS), :]
            for g in range(SEGS - 1, 0, -1):
                carries.append(ends[g : g + 1, :] + spans[g : g + 1, :] * carries[-1])
            flow = jnp.concatenate(carries[::-1], axis=0)
            above = None
            soft = soft_ref[2:3, :]
            for i in range(seg - 2, -1, -2):
                rate_parts, inflow_parts, mixed_parts = [], [], []
                for k in (i + 1, i):
                    here = row_at(s * steps, k * SEGS, SEGS)
                    backflow = grad_state_ref[here, :] + (flow if above is None else above * flow)
                    flow = backflow
                    if k > 0:
                        prior = state_ref[row_at(s * steps, (k - 1) * SEGS, SEGS), :]
                    else:
                        prior = shift_in(
                            state_ref[row_at(s * steps, (seg - 1) * SEGS, SEGS), :], carry_ref[pl.ds(s, 1), :], True
                        )
                    rate = rate_ref[here, :]
                    inflow = inflow_ref[here, :]
                    mixed = mixed_ref[here, :]
                    keep = masks_ref[here, 0:1]
                    raw = jnp.exp2(rate * soft)
                    above = raw * keep
                    spread = (1.0 - raw) * (1.0 + raw)
                    bounded = jnp.maximum(spread, ROOT_FLOOR)
                    inverse = lax.rsqrt(bounded)
                    root = keep * (bounded * inverse) + (1.0 - keep)
                    pulled = backflow * inflow
                    through = pulled * root
                    grad_spread = jnp.where(spread > ROOT_FLOOR, pulled * mixed * (inverse * keep), 0.0)
                    grad_log = backflow * prior * above - raw * raw * grad_spread
                    rate_parts.append(grad_log * (soft * (1.0 / LOG2_E)) * rate * (1.0 - rate))
                    inflow_parts.append(through * mixed * (1.0 - inflow))
                    mixed_parts.append(mixed)
                    partial[here, cols] = through
                both = row_at(s * steps, i * SEGS, 2 * SEGS)
                rate_grad[both, :] = jnp.concatenate(rate_parts[::-1], axis=0).astype(BF16)
                inflow_grad[both, :] = jnp.concatenate(inflow_parts[::-1], axis=0).astype(BF16)
                low[step, both, :] = jnp.concatenate(mixed_parts[::-1], axis=0).astype(BF16)

        per_sequence(seqs, scanned)
        grad_rate, grad_inflow = rate_grad[...], inflow_grad[...]
        blocks, block = bd_own.shape[0], bd_own.shape[1]
        mine = step // (count // 2) == core
        pieces = []
        for b in range(blocks):
            lanes = slice(b * block, (b + 1) * block)
            both = jnp.concatenate(
                [jnp.where(mine, bd_own[b], bd_oth[b]), jnp.where(mine, bi_own[b], bi_oth[b])], axis=1
            )
            pieces.append(mm_nt(jnp.concatenate([grad_rate[:, lanes], grad_inflow[:, lanes]], axis=1), both))
        partial[:, pl.ds(pl.multiple_of(step * tile, 128), tile)] += jnp.concatenate(pieces, axis=1)
        inner[:, :ranks] += mm_nt(grad_rate, stack_ranks(core, ed_own[...], ed_oth[...]))
        inner[:, ranks:] += mm_nt(grad_inflow, stack_ranks(core, ei_own[...], ei_oth[...]))
        late_grad(4, mm(picked_t[:ranks, :], grad_rate), step)
        late_grad(6, mm(picked_t[ranks:, :], grad_inflow), step)

    @pl.when(step == count - 1)
    def _():
        onehot = onehot_ref[...]
        chosen = inner[...] * jnp.concatenate([onehot, onehot], axis=1)
        gi[...] = chosen.astype(BF16)
        gi_t[...] = flipped(chosen)

    @pl.when(step == count)
    def _():
        for piece in range(low.shape[0]):
            lanes = slice(piece * tile, (piece + 1) * tile)
            shrink = jnp.concatenate(
                [
                    stack_ranks(core, sd_own[:, lanes], sd_oth[:, lanes]),
                    stack_ranks(core, si_own[:, lanes], si_oth[:, lanes]),
                ],
                axis=0,
            )
            grad = partial[:, lanes] + mm(gi[...], shrink)
            partial[:, lanes] = grad
            for s in range(seqs):
                firsts = [grad[s * steps + i * SEGS : s * steps + i * SEGS + 1, :] for i in range(HALO)]
                heads[piece, s * HALO : (s + 1) * HALO, :] = jnp.concatenate(firsts, axis=0)
            both = mm(gi_t[...], low[piece])
            late_grad(5, both[:ranks, :], piece)
            late_grad(7, both[ranks:, :], piece)
            head_copy(piece).start()

    @pl.when(jnp.logical_and(step > count, step <= 2 * count))
    def _():
        piece = step - count - 1
        at = pl.multiple_of(piece * tile, 128)
        head_copy(piece).wait()
        cols = pl.ds(at, tile)

        def filtered(s):
            at_run = lambda i: partial[row_at(s * steps, i * SEGS, SEGS), cols]
            rim = inbox[piece, row_at(s * HALO, 0, HALO), :]
            runs = {seg + k: shift_in(at_run(k), rim[k : k + 1, :], False) for k in range(lags)}
            for i in range(lags):
                runs[i] = at_run(i)
            for i in range(0, seg, 2):
                totals = []
                for k in (i, i + 1):
                    here = row_at(s * steps, k * SEGS, SEGS)
                    if k + lags < seg:
                        runs[k + lags] = at_run(k + lags)
                    total = taps_ref[0:1, :] * runs[k]
                    for lag in range(1, lags + 1):
                        total = total + taps_ref[lag : lag + 1, :] * runs[k + lag] * masks_ref[here, lags + lag - 1 : lags + lag]
                    totals.append(total)
                low[piece, row_at(s * steps, i * SEGS, 2 * SEGS), :] = jnp.concatenate(totals, axis=0).astype(BF16)

        per_sequence(seqs, filtered)
        grad = low[piece]
        inner_r[...] += mm_nt(grad, stack_ranks(core, er_own[...], er_oth[...]))
        late_grad(8, mm(picked_rt[...], grad), piece)

    @pl.when(step == 2 * count)
    def _():
        chosen = inner_r[...] * onehot_ref[...]
        late_grad(9, mm(flipped(chosen), normed_ref[...]))
        out_ref[...] = mm(chosen.astype(BF16), stack_ranks(core, sr_own[...], sr_oth[...])) + mm(
            gi_b_ref[...], stack_ranks(core, sb_own[...], sb_oth[...])
        )

    @pl.when(step > 2 * count)
    def _():
        left, right = halves(core, out_ref.shape[1])
        recur_grad, branch_grad = low[step - 2 * count - 1], pre_grad_ref[...]
        out_ref[:, left] += mm_nt(recur_grad, wr_own[...]) + mm_nt(branch_grad, wb_own[...])
        out_ref[:, right] += mm_nt(recur_grad, wr_oth[...]) + mm_nt(branch_grad, wb_oth[...])

    if reduce:

        @pl.when(step == 3 * count)
        def _():
            run(Links(), tail)


def indexed(shape, index, scalars):
    if scalars:
        return pl.BlockSpec(shape, index)
    return pl.BlockSpec(shape, lambda j: index(j, None))


def call(kernel, name, grid, core, ins, outs, scratch, flops, nbytes, collective=None):
    scalars = core is not None

    def still(shape):
        zeros = (0,) * len(shape)
        if scalars:
            return pl.BlockSpec(shape, lambda j, c: zeros, pipeline_mode=pl.Buffered(1))
        return pl.BlockSpec(shape, lambda j: zeros, pipeline_mode=pl.Buffered(1))

    in_specs, arrays = [], []
    for item in ins:
        if isinstance(item, tuple) and len(item) == 1:
            arrays.append(item[0])
            in_specs.append(pl.BlockSpec(memory_space=pl.ANY))
        elif isinstance(item, tuple) and len(item) == 2:
            arrays.append(item[0])
            in_specs.append(pl.BlockSpec(memory_space=item[1]))
        elif isinstance(item, tuple):
            arrays.append(item[0])
            in_specs.append(indexed(item[1], item[2], scalars))
        else:
            arrays.append(item)
            in_specs.append(still(item.shape))
    out_specs, shapes = [], []
    for item in outs:
        shapes.append(jax.ShapeDtypeStruct(item[0], item[1]))
        if len(item) == 3:
            out_specs.append(pl.BlockSpec(memory_space=pl.ANY))
        else:
            out_specs.append(indexed(item[2], item[3], scalars) if len(item) == 4 else still(item[0]))
    return pl.pallas_call(
        kernel,
        grid_spec=pltpu.PrefetchScalarGridSpec(
            num_scalar_prefetch=int(scalars), grid=(grid,), in_specs=in_specs, out_specs=out_specs, scratch_shapes=scratch
        ),
        out_shape=shapes,
        name=name,
        compiler_params=pltpu.CompilerParams(
            dimension_semantics=("arbitrary",), vmem_limit_bytes=67043328, collective_id=collective,
            has_side_effects=collective is not None,
        ),
        cost_estimate=pl.CostEstimate(flops=flops, bytes_accessed=nbytes, transcendentals=0),
    )(*([core] if scalars else []), *arrays)


def local(
    tokens, segment_ids, document_adapter, out_cotangent, mixer_gain, feed_gain, filter_taps, decay_param, *weights
):
    core = lax.axis_index("wshard").astype(jnp.int32).reshape(1)
    anywhere = pl.ANY
    at_once = (1, 8, 10, 11, 12, 14, 2, 3, 13, 15)
    with_mixer = (0, 9, 16, 17, 4, 5, 18, 19, 20, 21, 22, 23)
    with_branch = (6, 7)
    other = {}
    pair = lambda i: (weights[i], other[i])
    wr, sb, sr, er, sdec, sinf, bd, bi, edec, einf = [weights[i] for i in at_once]
    seqs, steps, width = tokens.shape
    rows = seqs * steps
    lru = filter_taps.shape[1]
    lags = filter_taps.shape[0] - 1
    ranks = 2 * sb.shape[0]
    feed = weights[5].shape[1]
    peers = lax.axis_size("seq")
    reach = peers // 4

    soft = jax.nn.softplus(-decay_param) * (-RATE_SCALE * LOG2_E)
    wider = lambda gain: jnp.pad(gain, (0, lru - width))
    params = jnp.stack([wider(mixer_gain), wider(feed_gain), soft, soft, soft, soft, soft, soft])
    tokens2 = tokens.reshape(rows, width)
    cot = out_cotangent.reshape(rows, width)

    tile = TILE
    count = lru // tile
    half = width // 2
    blocks = tile // bd.shape[1]
    block = bd.shape[1]
    early = lambda j: jnp.minimum(j, count - 1)
    late = lambda j: jnp.maximum(j - count, 0)
    flat = lambda r, at: ((r, tile), lambda j, c: (0, at(j)))

    def tiled(array, r, at):
        block_shape, index = flat(r, at)
        return (array, block_shape, index)

    def tiled_out(r, dtype, at, total=None):
        block_shape, index = flat(r, at)
        return ((r, total or lru), dtype, block_shape, index)

    def both(pair, r, at):
        return [tiled(pair[0], r, at), tiled(pair[1], r, at)]

    def gate_blocks(pair, at):
        index = lambda j, c: (at(j) % (count // 2), 0, 0)
        return [(pair[0], (blocks, block, block), index), (pair[1], (blocks, block, block), index)]

    half_ranks = ranks // 2
    ident = lambda j: j
    groups = seqs * SEGS
    def gate_half(array, at):
        return (array, (blocks, block, block), lambda j, c: (at(j) % (count // 2), 0, 0))

    dma = pltpu.SemaphoreType.DMA
    vm = lambda *shape: pltpu.VMEM(shape, BF16)
    vf = lambda *shape: pltpu.VMEM(shape, F32)
    with jax.named_scope("mixer_forward"):
        (normed, picked_br, picked_di, mixed, rate, inflow, held, span, ends, spans, summary, onehot_own, masks, tokens_in, *moved) = call(
            functools.partial(mixer_kernel, carried=len(with_mixer)), "mixer_forward", 2 * count, None,
            [tokens2, segment_ids, (document_adapter, pltpu.SMEM), params, tiled(filter_taps, lags + 1, early), tiled(params, 8, late),
             tiled(wr, half, early), sb, sr, tiled(er, half_ranks, early),
             tiled(sdec, half_ranks, early), tiled(sinf, half_ranks, early), gate_half(bd, late), gate_half(bi, late),
             tiled(edec, half_ranks, late), tiled(einf, half_ranks, late)]
            + [(weights[i],) for i in at_once + with_mixer],
            [((rows, width), BF16), ((rows, 2 * ranks), BF16), ((rows, 2 * ranks), BF16),
             tiled_out(rows, F32, early), tiled_out(rows, F32, late), tiled_out(rows, F32, late),
             tiled_out(rows, F32, late), tiled_out(rows, F32, late),
             tiled_out(groups, F32, late), tiled_out(groups, F32, late), tiled_out(2 * seqs, F32, late),
             ((rows, ranks), F32), ((rows, ranks), F32), ((rows, width), BF16)]
            + [(weights[i].shape, BF16, anywhere) for i in at_once + with_mixer],
            [vm(*weights[i].shape) for i in at_once]
            + [vm(rows + seqs * HALO, width), vm(rows + seqs * HALO, ranks), vf(rows, 2 * ranks), vm(rows, 2 * ranks),
               vf(rows, lru), vf(rows + seqs * HALO, tile),
               vm(seqs, 2 * HALO, width), pltpu.VMEM((2, seqs, steps), jnp.int32),
               dma((len(at_once) - 1,)), dma((len(at_once) - 1,)), dma((count,)), dma((count,)), dma((len(at_once),)),
               dma((seqs,)), dma((seqs,)), dma((2,)), dma((2,)), dma((len(with_mixer),)), dma((len(with_mixer),))],
            int(6e9), int(30e6), collective=2,
        )
    other.update(zip(at_once + with_mixer, moved))
    wr, bd, bi, sb, sr, er, sdec, edec, sinf, einf = [pair(i) for i in (1, 2, 3, 8, 10, 11, 12, 13, 14, 15)]
    wb, eb, so, eo, wo, wg = pair(0), pair(9), pair(16), pair(17), pair(4), pair(5)
    sg, eg, su, eu, sdn, edn = [pair(i) for i in (18, 19, 20, 21, 22, 23)]
    def own_rows(pair, at):
        part_of = lambda j, which: jnp.clip(at(j) - (count // 2) * which, 0, count // 2 - 1)
        return [
            (pair[0], (tile, width), lambda j, c: (part_of(j, lax.axis_index("wshard")), 0)),
            (pair[1], (tile, width), lambda j, c: (part_of(j, 1 - lax.axis_index("wshard")), 0)),
        ]

    with jax.named_scope("branch_and_output_forward"):
        branch_pre, state, merged, carry, residual, second, picked_o, *moved = call(
            functools.partial(branch_output_kernel, carried=len(with_branch)), "branch_output_forward", 2 * count, None,
            [summary, normed, (picked_br, (rows, ranks), lambda j, c: (0, 0))] + both(wb, half, early)
            + both(eb, half_ranks, early)
            + [tiled(held, rows, late), tiled(span, rows, late),
               tiled(ends, groups, late), tiled(spans, groups, late), tokens_in, onehot_own, params]
            + own_rows(wo, late) + both(so, half_ranks, late) + list(eo) + [(weights[i],) for i in with_branch],
            [tiled_out(rows, F32, early), tiled_out(rows, F32, late), tiled_out(rows, BF16, late),
             tiled_out(2 * seqs, F32, late), ((rows, width), F32), ((rows, width), BF16), ((rows, ranks), BF16)]
            + [(weights[i].shape, BF16, anywhere) for i in with_branch],
            [pltpu.VMEM((rows, lru), F32), pltpu.VMEM((rows, width), F32), pltpu.VMEM((rows, ranks), F32),
             pltpu.VMEM((reach, 2 * seqs, lru), F32), pltpu.SemaphoreType.DMA((reach,)), pltpu.SemaphoreType.DMA((reach,)),
             pltpu.SemaphoreType.DMA((len(with_branch),)), pltpu.SemaphoreType.DMA((len(with_branch),))],
            int(8e9), int(45e6), collective=1,
        )
    other.update(zip(with_branch, moved))
    wu, wd = pair(6), pair(7)

    part = 256
    pieces = feed // (2 * part)

    def feed_cols(pair_item, r):
        return [
            (pair_item, (r, part), lambda j, c: (0, c[0] * pieces + j)),
            (pair_item, (r, part), lambda j, c: (0, (1 - c[0]) * pieces + j)),
        ]

    def feed_pair(pair, r):
        return feed_cols(pair[0], r) + feed_cols(pair[1], r)

    chips = ranks // 8
    grad_cols = ((2, chips, 16, feed // 4), BF16, (2, chips, 16, part // 2), lambda j, c: (0, 0, 0, j))
    grad_whole = ((2, chips, 16, width // 4), BF16)
    grad_lru = ((2, chips, 16, lru // 4), BF16)

    def grad_tile(at):
        return ((2, chips, 16, lru // 4), BF16, (2, chips, 16, tile // 4), lambda j, c: (0, 0, 0, at(j)))

    with jax.named_scope("feed_forward_both_ways"):
        result, grad_residual, grad_low, deg, deu, dsdn, dsg, dsu, dedn = call(
            functools.partial(feed_kernel, seqs=seqs), "feed_both_ways", pieces, core,
            [second, cot, residual, onehot_own, params] + feed_pair(wg, half) + feed_pair(wu, half)
            + [(wd[0], (part, width), lambda j, c: (j, 0)), (wd[1], (part, width), lambda j, c: (j, 0))]
            + list(sg) + list(su) + feed_pair(eg, half_ranks) + feed_pair(eu, half_ranks)
            + feed_pair(sdn, half_ranks) + list(edn),
            [((rows, width), BF16), ((rows, width), F32), ((rows, width), BF16),
             grad_cols, grad_cols, grad_cols, grad_whole, grad_whole, grad_whole],
            [pltpu.VMEM((rows, 2 * ranks), BF16), pltpu.VMEM((2 * ranks, rows), BF16),
             pltpu.VMEM((rows, ranks), BF16), pltpu.VMEM((ranks, rows), BF16),
             pltpu.VMEM((rows, width), F32), pltpu.VMEM((rows, ranks), F32), pltpu.VMEM((rows, width), F32),
             pltpu.VMEM((rows, 2 * ranks), F32), vm(rows, width)],
            int(50e9), int(60e6),
        )

    split = ("eg", "eu", "sdn")
    runs = dict(sb=width, eb=tile, sr=width, er=tile, sdec=tile, edec=tile, sinf=tile, einf=tile, so=tile, eo=width,
                sg=width, eg=2 * part, su=width, eu=2 * part, sdn=2 * part, edn=width)
    reduce = peers == 16 and ranks == 128
    grads = dict(eg=deg, eu=deu, sdn=dsdn, sg=dsg, su=dsu, edn=dedn)
    size_of = lambda k: (width if k in ("eo", "sb", "sr", "sg", "su", "edn") else feed if k in split else lru) // 4
    feed_sizes = [size_of(k) for k in FEED_ORDER]
    mixer_sizes = [size_of(k) for k in MIXER_ORDER]
    feed_grads = [(grads[k],) for k in FEED_ORDER] if reduce else []
    wide, narrow = sum(feed_sizes), sum(mixer_sizes)
    dma = pltpu.SemaphoreType.DMA
    vm = lambda *shape: pltpu.VMEM(shape, BF16)
    vf = lambda *shape: pltpu.VMEM(shape, F32)
    nf, nm = len(feed_sizes), len(mixer_sizes)

    with jax.named_scope("output_and_branch_backward"):
        (grad_state, bends, bspans, bstart, pre_grad, gi_b, dso, deo, dsb, deb, *halved) = call(
            functools.partial(branch_back_kernel, feed_sizes=feed_sizes if reduce else [], reduce=reduce),
            "output_branch_backward", count + 1, None,
            [grad_low, onehot_own, masks, tiled(params, 8, early), picked_o, tiled(branch_pre, rows, early),
             tiled(state, rows, early), tiled(merged, rows, early), tiled(rate, rows, early)]
            + own_rows(wo, early) + both(so, half_ranks, early) + list(eo)
            + [normed, (picked_br, (rows, ranks), lambda j, c: (0, 0))]
            + list(eb) + feed_grads,
            [tiled_out(rows, F32, early), tiled_out(groups, F32, early), tiled_out(groups, F32, early),
             ((2 * seqs, lru), F32), tiled_out(rows, BF16, early), ((rows, ranks), BF16),
             grad_tile(early), grad_whole, grad_whole, ((2, chips, 16, lru // 4), BF16)]
            + ([((8, 16, wide), F32)] if reduce else []),
            [vm(rows, ranks), vm(ranks, rows), vf(rows, tile),
             vm(rows, lru), vf(2 * seqs, lru), vf(reach, 2 * seqs, lru), dma((reach,)), dma((reach,))]
            + ([vm(16, 16, wide), vm(16, 16, wide), vm(8, 16, wide), vm(8, 16, wide)] + [dma((nf,))] * 5 if reduce else []),
            int(10e9), int(50e6), collective=3,
        )
    early_grads = dict(eo=deo, so=dso, eb=deb, sb=dsb)
    grads.update(early_grads)
    third = 3
    first_of = lambda j: jnp.minimum(j, count - 1)
    last = lambda j: jnp.clip(j - count - 1, 0, count - 1)
    dense = lambda j: jnp.clip(j - 2 * count - 1, 0, count - 1)
    with jax.named_scope("gates_and_recur_backward"):
        grad_normed, *late = call(
            functools.partial(recur_back_kernel, feed_sizes=feed_sizes, mixer_sizes=mixer_sizes, reduce=reduce),
            "gates_recur_backward", 3 * count + 1, None,
            [tiled(grad_state, rows, first_of), tiled(bends, groups, first_of), tiled(bspans, groups, first_of),
             tiled(bstart, 2 * seqs, first_of), tiled(carry, 2 * seqs, first_of), tiled(state, rows, first_of),
             tiled(mixed, rows, first_of), tiled(rate, rows, first_of), tiled(inflow, rows, first_of),
             masks, onehot_own, tiled(params, 8, first_of), picked_di]
            + gate_blocks(bd, first_of) + gate_blocks(bi, first_of)
            + both(edec, half_ranks, first_of) + both(einf, half_ranks, first_of)
            + list(sdec) + list(sinf)
            + [tiled(filter_taps, lags + 1, last), normed, (picked_br, (rows, ranks), lambda j, c: (0, 1)),
               *both(er, half_ranks, last)]
            + both(wr, half, dense) + list(sr) + [tiled(pre_grad, rows, dense), gi_b] + both(wb, half, dense) + list(sb)
            + ([halved[0]] + [(early_grads[k],) for k in MIXER_ORDER[:4]] if reduce else []),
            [((rows, width), F32)]
            + ([((16, wide + narrow), F32)] if reduce else
               [grad_tile(first_of), grad_lru, grad_tile(first_of), grad_lru, grad_tile(last), grad_whole]),
            [vf(rows, lru), vf(rows, 2 * ranks),
             vm(rows, 2 * ranks), vm(2 * ranks, rows), vm(2 * ranks, rows), vm(count, rows, tile),
             vf(rows, ranks), vm(ranks, rows), vf(count, seqs * HALO, tile), vf(count, seqs * HALO, tile),
             dma((count,)), dma((count,)), vm(rows, tile), vm(rows, tile)]
            + ([vf(4, 16, wide), vm(4, 16, wide), vm(4, 16, wide), vm(3, 16, wide), vm(3, 16, wide),
                dma((nf,)), dma((nf,)), dma((nf, 3)), dma((nf, 3)),
                vm(2, 16, 16, narrow), vm(16, 16, narrow), vm(8, 16, narrow), vm(8, 16, narrow),
                vf(4, 16, narrow), vm(4, 16, narrow), vm(4, 16, narrow), vm(3, 16, narrow), vm(3, 16, narrow)]
               + [dma((nm,))] * 7 + [dma((nm, 3))] * 2 if reduce else []),
            int(10e9), int(50e6), collective=4,
        )

    names = ("sb", "eb", "sr", "er", "sdec", "edec", "sinf", "einf", "so", "eo", "sg", "eg", "su", "eu", "sdn", "edn")
    all_names = [k for k in FEED_ORDER + MIXER_ORDER] if reduce else []
    all_sizes = feed_sizes + mixer_sizes if reduce else []
    by_rows = lambda array: (array, (steps, width), lambda j, c: (j, 0))
    with jax.named_scope("first_norm_backward"):
        grad_tokens, *sums = call(
            functools.partial(
                last_kernel, sizes=all_sizes, runs=[runs[k] for k in all_names], split=[k in split for k in all_names]
            ),
            "first_norm_backward", seqs, None,
            [by_rows(grad_normed), by_rows(grad_residual), by_rows(tokens_in), params] + late[: int(reduce)],
            [((rows, width), F32, (steps, width), lambda j, c: (j, 0))] + [((4, 4 * n), F32) for n in all_sizes],
            [vf(width // LANES, steps + SEGS * SEGS, LANES)], int(1e7), int(11e6),
        )
    with jax.named_scope("factor_gradients"):
        if reduce:
            summed = dict(zip(all_names, sums))
        else:
            grads.update(zip([k for k in MIXER_ORDER[4:]], late))
            summed = scatter_plain(grads, runs, split)
    return (result.reshape(seqs, steps, width), grad_tokens.reshape(seqs, steps, width)) + tuple(
        summed[k] for k in names
    )


def solution(mesh):
    split = P("wshard", None)
    in_specs = (
        (P("wshard", "seq", None), P("wshard", "seq"), split, P("wshard", "seq", None))
        + (P(),) * 4
        + (split, split, P("wshard", None, None), P("wshard", None, None))
        + (split,) * 20
    )
    out_specs = (P("wshard", "seq", None),) * 2 + (P(("seq", "wshard"), None),) * 16
    return jax.shard_map(local, mesh=mesh, in_specs=in_specs, out_specs=out_specs, check_vma=False)
```
